32 devices in a mesh: dp: 4 (over y, core), seq: 8 (over z, x).
Axes of the slice: x: 2, y: 2, z: 4, core: 2. Of those that a mesh axis runs over, the one named last changes fastest.
Arguments:
- tokens: bfloat16 [4, 3072, 1024], P('dp', 'seq'), may hold values from -6 to 6
- segment_ids: int32 [4, 3072], P('dp', 'seq'), may hold values from 0 to 7, never falling along the last dimension, each value on 1 to 1536 neighbouring positions
- first_gain: float32 [1024], replicated, may hold values from 0.1 to 1.9
- triple_weight: bfloat16 [1024, 3072], P('dp'), may hold values from -0.1875 to 0.1875
- head_scale: float32 [16], replicated, may hold values from 0.1 to 1.9
- output_weight: bfloat16 [1024, 1024], P('dp'), may hold values from -0.1875 to 0.1875
- post_gain: float32 [1024], replicated, may hold values from 0.1 to 1.9
- second_gain: float32 [1024], replicated, may hold values from 0.1 to 1.9
- up_weight: bfloat16 [1024, 4096], P('dp'), may hold values from -0.1875 to 0.1875
- mid_gain: float32 [4096], replicated, may hold values from 0.1 to 1.9
- down_weight: bfloat16 [4096, 1024], P('dp'), may hold values from -0.09375 to 0.09375
- cotangent: bfloat16 [4, 3072, 1024], P('dp', 'seq'), may hold values from -6 to 6
Outputs:
- layer_out: bfloat16 [4, 3072, 1024], P('dp', 'seq')
- grad_tokens: bfloat16 [4, 3072, 1024], P('dp', 'seq')
- grad_first: float32 [1024], P(('dp', 'seq'))
- grad_triple: float32 [1024, 3072], P(('dp', 'seq'))
- grad_scale: float32 [16], P('seq')
- grad_output: float32 [1024, 1024], P(('dp', 'seq'))
- grad_post: float32 [1024], P(('dp', 'seq'))
- grad_second: float32 [1024], P(('dp', 'seq'))
- grad_up: float32 [1024, 4096], P(('dp', 'seq'))
- grad_mid: float32 [4096], P(('dp', 'seq'))
- grad_down: float32 [4096, 1024], P(('dp', 'seq'))
The draws below stay inside these ranges and needn't reach their ends.
Inputs may be any that keep to these rules, and one draw needn't show every extreme that they name: `segment_ids`: within each sequence the ids never fall; each of the 8 documents holds 1 to 1536 tokens, and one holds exactly 1536.
All inputs are finite; a program needn't handle non-finite values.
Results may differ from the reference program's by a relative error of at most 0.014.
Values may be sent and summed in bfloat16 or wider, within the bound.
A program may use at most 192 MiB of HBM per device.

```python
import math
import jax
import jax.numpy as jnp
import numpy as np
from jax import lax

HEADS = 16
HEAD = 64
FF = 4096
DOCS = 8
D = 1024
LENGTH = 3072
SEQS = 4


def level_of(rng, dims, cuts, low, high):
    def one(dim, shards_of):
        draws = jax.random.uniform(jax.random.fold_in(jax.random.fold_in(rng, 6), dim), (shards_of,), jnp.float32, low / len(cuts), high / len(cuts))
        return jnp.repeat(jnp.exp(draws), dims[dim] // shards_of).reshape((-1,) + (1,) * (len(dims) - dim - 1))

    level = one(*cuts[0])
    for cut in cuts[1:]:
        level = level * one(*cut)
    return level


def profile(count, total, most, skew):
    portions = [(1 << 20) // math.isqrt(standing ** skew) + 1 for standing in range(2, count + 1)]
    surplus, counts = total - most - (count - 1), [1] * (count - 1)
    while surplus > 0:
        movable = [i for i in range(count - 1) if counts[i] < most]
        mass, left = sum([portions[i] for i in movable]), surplus
        for i in movable:
            addition = min(most - counts[i], max(1, left * portions[i] // mass), surplus)
            counts[i] = counts[i] + addition
            surplus = surplus - addition
    return np.array([most] + counts)


def ragged_sizes(rng, number_of, total, bound, skew):
    if number_of == 2:
        one = jax.random.randint(rng, (), max(1, total - bound), min(bound, total - 1) + 1)
        return jnp.stack([one, total - one])
    sizes = jnp.asarray(profile(number_of, total, bound, skew), jnp.int32)
    pairs = (number_of - 1) // 2
    giver, taker = sizes[1:1 + 2 * pairs:2], sizes[2:2 + 2 * pairs:2]
    room = jnp.minimum(giver - 1, bound - taker)
    shifted = jax.random.randint(jax.random.fold_in(rng, 1), (pairs,), 0, 1 << 20) % (room + 1)
    sizes = sizes.at[1:1 + 2 * pairs:2].set(giver - shifted).at[2:2 + 2 * pairs:2].set(taker + shifted)
    return sizes[jax.random.permutation(jax.random.fold_in(rng, 2), number_of)]


def centred(key, extent, deviation, reach, cuts=(), held_as=jnp.bfloat16):
    values = deviation * jax.random.normal(key, extent, jnp.float32)
    if cuts:
        values = values * level_of(key, extent, cuts, -0.22, 0.18)
    return jnp.clip(values, -reach, reach).astype(held_as)


def setup_inputs(seed: int = 0) -> dict:
    key_of = jax.random.split(jax.random.key(seed), 13)
    tokens = centred(key_of[0], (SEQS, LENGTH, D), 1.0, 6.0, ((0, 4), (1, 8)))
    segment_ids = jax.vmap(lambda own: jnp.searchsorted(jnp.cumsum(ragged_sizes(own, DOCS, LENGTH, LENGTH // 2, 2)), jnp.arange(LENGTH), side="right"))(jax.random.split(key_of[1], SEQS)).reshape((SEQS, LENGTH)).astype(jnp.int32)
    first_gain = jnp.clip(1.0 + 0.18 * jax.random.normal(key_of[2], (D,), jnp.float32), 0.1, 1.9)
    triple_weight = centred(key_of[3], (D, 3 * D), D ** -0.5, 0.1875, ((0, 4),))
    head_scale = jnp.clip(1.0 + 0.18 * jax.random.normal(key_of[4], (HEADS,), jnp.float32), 0.1, 1.9)
    output_weight = centred(key_of[5], (D, D), D ** -0.5, 0.1875, ((0, 4),))
    post_gain = jnp.clip(1.0 + 0.18 * jax.random.normal(key_of[6], (D,), jnp.float32), 0.1, 1.9)
    second_gain = jnp.clip(1.0 + 0.18 * jax.random.normal(key_of[7], (D,), jnp.float32), 0.1, 1.9)
    up_weight = centred(key_of[8], (D, FF), D ** -0.5, 0.1875, ((0, 4),))
    mid_gain = jnp.clip(1.0 + 0.18 * jax.random.normal(key_of[9], (FF,), jnp.float32), 0.1, 1.9)
    down_weight = centred(key_of[10], (FF, D), FF ** -0.5, 0.09375, ((0, 4),))
    cotangent = centred(key_of[11], (SEQS, LENGTH, D), 1.0, 6.0, ((0, 4), (1, 8)))
    return dict(tokens=tokens, segment_ids=segment_ids, first_gain=first_gain, triple_weight=triple_weight, head_scale=head_scale, output_weight=output_weight, post_gain=post_gain, second_gain=second_gain, up_weight=up_weight, mid_gain=mid_gain, down_weight=down_weight, cotangent=cotangent)


@jax.custom_vjp
def low(v):
    return lax.optimization_barrier(v.astype(jnp.bfloat16)).astype(jnp.float32)

@jax.custom_vjp
def low_back(v):
    return v

def low_keep(v):
    return (low(v), None)

def low_pass(kept, grad):
    return (grad,)

def back_keep(v):
    return (v, None)

def back_low(kept, grad):
    return (low(grad),)
low.defvjp(low_keep, low_pass)
low_back.defvjp(back_keep, back_low)

def matmul(left, right):
    return jnp.dot(left, right, precision=lax.Precision.HIGHEST, preferred_element_type=jnp.float32)

def layer_norm(values, gains):
    center = values - lax.optimization_barrier(jnp.mean(values, axis=-1, keepdims=True))
    spread = lax.optimization_barrier(jnp.mean(center * center, axis=-1, keepdims=True))
    return center * lax.rsqrt(spread + 1e-05) * gains

def one_head(queries, keys_all, values_all, doc_ids):
    length = queries.shape[0]
    block_rows = min(512, length)
    positions = jnp.arange(length, dtype=jnp.int32)

    def block_out(block_index):
        first_row = block_index * block_rows
        query_block = lax.dynamic_slice_in_dim(queries, first_row, block_rows, 0)
        query_docs = lax.dynamic_slice_in_dim(doc_ids, first_row, block_rows, 0)
        query_pos = first_row + jnp.arange(block_rows, dtype=jnp.int32)
        scores = low_back(matmul(query_block, keys_all.T) * HEAD ** (-0.5))
        allowed = (query_docs[:, None] == doc_ids[None, :]) & (query_pos[:, None] >= positions[None, :])
        scores = jnp.where(allowed, scores, -1e+30)
        weights = jax.nn.softmax(scores, axis=-1)
        return matmul(low(weights), values_all)
    outputs = lax.map(jax.checkpoint(block_out), jnp.arange(length // block_rows, dtype=jnp.int32))
    return outputs.reshape(length, queries.shape[1])

def forward(inputs, doc_ids, first_gain, triple_weight, head_scale, output_weight, post_gain, second_gain, up_weight, mid_gain, down_weight):
    length = inputs.shape[0]
    normed = low(layer_norm(inputs, first_gain))
    triple = low_back(low(matmul(normed, triple_weight)))
    queries = triple[:, :D].reshape(length, HEADS, HEAD).transpose(1, 0, 2)
    keys_all = triple[:, D:2 * D].reshape(length, HEADS, HEAD).transpose(1, 0, 2)
    values_all = triple[:, 2 * D:].reshape(length, HEADS, HEAD).transpose(1, 0, 2)
    attended = lax.map(lambda triplet: one_head(triplet[0], triplet[1], triplet[2], doc_ids), (queries, keys_all, values_all))
    attended = low_back(attended)
    scaled = low_back(low(attended * head_scale[:, None, None]))
    merged = scaled.transpose(1, 0, 2).reshape(length, D)
    projected = low_back(matmul(merged, output_weight))
    middle = inputs + layer_norm(projected, post_gain)
    normed_two = low(layer_norm(middle, second_gain))
    hidden = low_back(matmul(normed_two, up_weight))
    activated = low(layer_norm(jax.nn.gelu(hidden, approximate=True), mid_gain))
    return middle + matmul(activated, down_weight)

def reference(tokens, segment_ids, first_gain, triple_weight, head_scale, output_weight, post_gain, second_gain, up_weight, mid_gain, down_weight, cotangent):
    params = (first_gain.astype(jnp.float32), triple_weight.astype(jnp.float32), head_scale.astype(jnp.float32), output_weight.astype(jnp.float32), post_gain.astype(jnp.float32), second_gain.astype(jnp.float32), up_weight.astype(jnp.float32), mid_gain.astype(jnp.float32), down_weight.astype(jnp.float32))

    def per_sequence(running, sequence):
        seq_tokens, seq_docs, seq_cot = sequence

        def closed(inputs, *weights):
            return forward(inputs, seq_docs, *weights)
        result, pull = jax.vjp(closed, seq_tokens.astype(jnp.float32), *params)
        gradients = pull(seq_cot.astype(jnp.float32))
        running = tuple((before + gradient for before, gradient in zip(running, gradients[1:])))
        return (running, (result.astype(jnp.bfloat16), gradients[0].astype(jnp.bfloat16)))
    empty_sums = tuple((jnp.zeros_like(weight) for weight in params))
    sums, (outputs, grad_inputs) = lax.scan(per_sequence, empty_sums, (tokens, segment_ids, cotangent))
    return (outputs, grad_inputs, sums[0], sums[1], sums[2], sums[3], sums[4], sums[5], sums[6], sums[7], sums[8])
```

```python
import functools
import jax
import jax.numpy as jnp
from jax import lax
from jax.sharding import PartitionSpec as P
from jax.experimental import pallas as pl
from jax.experimental.pallas import tpu as pltpu

HEAD = 64
NEG = -1e30
BQ = 256


def nt(a, b):
    return lax.dot_general(a, b, (((1,), (1,)), ((), ())), preferred_element_type=jnp.float32)


def tn(a, b):
    return lax.dot_general(a, b, (((0,), (0,)), ((), ())), preferred_element_type=jnp.float32)


def stack_heads(block, heads):
    if heads == 1:
        return block
    lane = lax.broadcasted_iota(jnp.int32, block.shape, 1)
    zero = jnp.zeros_like(block)
    return jnp.concatenate(
        [jnp.where((lane >= h * HEAD) & (lane < (h + 1) * HEAD), block, zero) for h in range(heads)],
        axis=0,
    )


def unstack_heads(wide, heads):
    rows = wide.shape[1] // heads
    return jnp.concatenate(
        [wide[h * HEAD : (h + 1) * HEAD, h * rows : (h + 1) * rows] for h in range(heads)], axis=0
    )


def forward_kernel(heads, lo_ref, full_ref, q_ref, k_ref, v_ref, start_ref, scale_ref,
                   o_ref, u_ref, lse_ref, m_s, l_s, acc_s):
    i = pl.program_id(0)
    rows = q_ref.shape[0]
    wide = heads * rows
    queries = stack_heads(q_ref[...] * jnp.bfloat16(HEAD ** -0.5), heads)
    starts = jnp.concatenate([start_ref[0]] * heads, axis=1)
    m_s[...] = jnp.full_like(m_s, NEG)
    l_s[...] = jnp.zeros_like(l_s)
    acc_s[...] = jnp.zeros_like(acc_s)

    def step(j, masked, diagonal):
        at = pl.ds(pl.multiple_of(j * rows, rows), rows)
        scores = nt(k_ref[at, :], queries)
        if masked or diagonal:
            key = j * rows + lax.broadcasted_iota(jnp.int32, scores.shape, 0)
            allowed = key >= starts
            if diagonal:
                lane = lax.broadcasted_iota(jnp.int32, scores.shape, 1) & (rows - 1)
                allowed = allowed & (key <= i * rows + lane)
            scores = jnp.where(allowed, scores, NEG)
        before = m_s[...]
        highest = jnp.maximum(before, jnp.max(scores, axis=0, keepdims=True))
        weights = jnp.exp(scores - highest)
        fade = jnp.exp(before - highest)
        if masked:
            weights = jnp.where(scores > 0.5 * NEG, weights, 0.0)
        m_s[...] = highest
        l_s[...] = l_s[...] * fade + jnp.sum(weights, axis=0, keepdims=True)
        acc_s[...] = acc_s[...] * fade + tn(v_ref[at, :], weights.astype(jnp.bfloat16))

    step(i, False, True)
    full = jnp.minimum(full_ref[i], i)

    def plain(j, carry):
        step(j, False, False)
        return carry

    def edge(j, carry):
        step(j, True, False)
        return carry

    lax.fori_loop(full, i, plain, 0)
    lax.fori_loop(lo_ref[i], full, edge, 0)
    total = l_s[...]
    out = unstack_heads(acc_s[...] / total, heads).T
    o_ref[...] = out
    u_ref[...] = (out * scale_ref[...]).astype(jnp.bfloat16)
    lse_ref[0] = m_s[...] + jnp.log(total)


def attend_forward(queries, keys, values, bounds, starts, scale_wide):
    length, width = queries.shape
    heads = width // HEAD
    blocks = length // BQ
    whole = pl.BlockSpec((length, width), lambda i, *_: (0, 0))
    mine = pl.BlockSpec((BQ, width), lambda i, *_: (i, 0))
    return pl.pallas_call(
        functools.partial(forward_kernel, heads),
        out_shape=(
            jax.ShapeDtypeStruct((length, width), jnp.float32),
            jax.ShapeDtypeStruct((length, width), jnp.bfloat16),
            jax.ShapeDtypeStruct((blocks, 1, heads * BQ), jnp.float32),
        ),
        grid_spec=pltpu.PrefetchScalarGridSpec(
            num_scalar_prefetch=2,
            grid=(blocks,),
            in_specs=[
                mine,
                whole,
                whole,
                pl.BlockSpec((1, 1, BQ), lambda i, *_: (i, 0, 0)),
                pl.BlockSpec((1, width), lambda i, *_: (0, 0)),
            ],
            out_specs=(mine, mine, pl.BlockSpec((1, 1, heads * BQ), lambda i, *_: (i, 0, 0))),
            scratch_shapes=[
                pltpu.VMEM((1, heads * BQ), jnp.float32),
                pltpu.VMEM((1, heads * BQ), jnp.float32),
                pltpu.VMEM((width, heads * BQ), jnp.float32),
            ],
        ),
        cost_estimate=pl.CostEstimate(
            flops=length * length * width, bytes_accessed=16 * length * width, transcendentals=0
        ),
        name="attend_forward",
    )(bounds[0], bounds[1], queries, keys, values, starts.reshape(blocks, 1, BQ), scale_wide)


def backward_kernel(heads, hi_ref, full_ref, q_ref, k_ref, v_ref, o_ref, du_ref, start_ref, scale_ref, lse_ref,
                    dq_ref, dk_ref, dv_ref, ds_ref, qs_s, dos_s, delta_s, dqt_s, dk_s, dv_s):
    j = pl.program_id(0)
    rows = k_ref.shape[0]
    blocks = qs_s.shape[0]
    wide = heads * rows

    @pl.when(j == 0)
    def prepare():
        def one(i, total):
            at = pl.ds(pl.multiple_of(i * rows, rows), rows)
            qs_s[i] = stack_heads(q_ref[at, :] * jnp.bfloat16(HEAD ** -0.5), heads)
            grad = du_ref[at, :].astype(jnp.float32)
            out = o_ref[at, :]
            low = (grad * scale_ref[...]).astype(jnp.bfloat16)
            dos_s[i] = stack_heads(low, heads)
            inner = (low.astype(jnp.float32) * out).T
            delta_s[i] = jnp.concatenate(
                [jnp.sum(inner[h * HEAD : (h + 1) * HEAD], axis=0, keepdims=True) for h in range(heads)],
                axis=1,
            )
            return total + jnp.sum(grad * out, axis=0, keepdims=True)

        ds_ref[...] = lax.fori_loop(0, blocks, one, jnp.zeros(ds_ref.shape, jnp.float32))
        dqt_s[...] = jnp.zeros_like(dqt_s)

    keys, values = k_ref[...], v_ref[...]
    dk_s[...] = jnp.zeros_like(dk_s)
    dv_s[...] = jnp.zeros_like(dv_s)

    def step(i, masked, diagonal):
        queries, grads = qs_s[i], dos_s[i]
        scores = nt(keys, queries)
        if masked or diagonal:
            key = j * rows + lax.broadcasted_iota(jnp.int32, scores.shape, 0)
            starts = jnp.concatenate([start_ref[i]] * heads, axis=1)
            allowed = key >= starts
            if diagonal:
                lane = lax.broadcasted_iota(jnp.int32, scores.shape, 1) & (rows - 1)
                allowed = allowed & (key <= i * rows + lane)
            scores = jnp.where(allowed, scores, NEG)
        weights = jnp.exp(scores - lse_ref[i])
        pulls = nt(values, grads)
        low = (weights * (pulls - delta_s[i])).astype(jnp.bfloat16)
        dv_s[...] += jnp.dot(weights.astype(jnp.bfloat16), grads, preferred_element_type=jnp.float32)
        dk_s[...] += jnp.dot(low, queries, preferred_element_type=jnp.float32)
        dqt_s[i] += tn(keys, low)

    step(j, False, True)
    full = jnp.maximum(full_ref[j], j + 1)

    def plain(i, carry):
        step(i, False, False)
        return carry

    def edge(i, carry):
        step(i, True, False)
        return carry

    lax.fori_loop(j + 1, full, plain, 0)
    lax.fori_loop(full, hi_ref[j], edge, 0)
    dk_ref[...] = dk_s[...].astype(jnp.bfloat16)
    dv_ref[...] = dv_s[...].astype(jnp.bfloat16)

    @pl.when(j == blocks - 1)
    def finish():
        def one(i, carry):
            at = pl.ds(pl.multiple_of(i * rows, rows), rows)
            dq_ref[at, :] = (unstack_heads(dqt_s[i], heads).T * HEAD ** -0.5).astype(jnp.bfloat16)
            return carry

        lax.fori_loop(0, blocks, one, 0)


def attend_backward(queries, keys, values, outs, grads, bounds, starts, scale_wide, logsum):
    length, width = queries.shape
    heads = width // HEAD
    blocks = length // BQ
    whole = pl.BlockSpec((length, width), lambda i, *_: (0, 0))
    mine = pl.BlockSpec((BQ, width), lambda i, *_: (i, 0))
    return pl.pallas_call(
        functools.partial(backward_kernel, heads),
        out_shape=(jax.ShapeDtypeStruct((length, width), jnp.bfloat16),) * 3
        + (jax.ShapeDtypeStruct((1, width), jnp.float32),),
        grid_spec=pltpu.PrefetchScalarGridSpec(
            num_scalar_prefetch=2,
            grid=(blocks,),
            in_specs=[
                whole,
                mine,
                mine,
                whole,
                whole,
                pl.BlockSpec((blocks, 1, BQ), lambda i, *_: (0, 0, 0)),
                pl.BlockSpec((1, width), lambda i, *_: (0, 0)),
                pl.BlockSpec((blocks, 1, heads * BQ), lambda i, *_: (0, 0, 0)),
            ],
            out_specs=(whole, mine, mine, pl.BlockSpec((1, width), lambda i, *_: (0, 0))),
            scratch_shapes=[
                pltpu.VMEM((blocks, heads * BQ, width), jnp.bfloat16),
                pltpu.VMEM((blocks, heads * BQ, width), jnp.bfloat16),
                pltpu.VMEM((blocks, 1, heads * BQ), jnp.float32),
                pltpu.VMEM((blocks, width, heads * BQ), jnp.float32),
                pltpu.VMEM((BQ, width), jnp.float32),
                pltpu.VMEM((BQ, width), jnp.float32),
            ],
        ),
        cost_estimate=pl.CostEstimate(
            flops=3 * length * length * width, bytes_accessed=32 * length * width, transcendentals=0
        ),
        name="attend_backward",
    )(bounds[2], bounds[3], queries, keys, values, outs, grads, starts.reshape(blocks, 1, BQ), scale_wide, logsum)


def document_bounds(doc_ids):
    length = doc_ids.shape[0]
    blocks = length // BQ
    counts = jnp.sum(doc_ids[None, :] < jnp.arange(8, dtype=jnp.int32)[:, None], axis=1, dtype=jnp.int32)
    starts = jnp.sum(
        jnp.where(doc_ids[:, None] == jnp.arange(8, dtype=jnp.int32)[None, :], counts[None, :], 0), axis=1, dtype=jnp.int32
    )
    by_block = starts.reshape(blocks, BQ)
    low = by_block[:, 0] // BQ
    full = (by_block[:, BQ - 1] + BQ - 1) // BQ
    index = jnp.arange(blocks, dtype=jnp.int32)
    high = jnp.sum(low[None, :] <= index[:, None], axis=1, dtype=jnp.int32)
    full_high = jnp.sum(full[None, :] <= index[:, None], axis=1, dtype=jnp.int32)
    return (low, full, high, full_high), starts


def layer_norm(values, gains):
    center = values - jnp.mean(values, axis=-1, keepdims=True)
    spread = jnp.mean(center * center, axis=-1, keepdims=True)
    return center * lax.rsqrt(spread + 1e-05) * gains


def gelu_norm(hidden, gains):
    return layer_norm(jax.nn.gelu(hidden, approximate=True), gains)


def transposed_times(left, right):
    return lax.dot_general(
        left, right, (((0,), (0,)), ((), ())), preferred_element_type=jnp.float32
    )


def times_transposed(left, right):
    return lax.dot_general(
        left, right, (((1,), (1,)), ((), ())), preferred_element_type=jnp.float32
    )


def scatter_rows(partial, sizes):
    current = partial
    for axis, size in zip(("dp", "seq"), sizes):
        place = lax.axis_index(axis)
        bits = size.bit_length() - 1
        pieces = current.reshape((2,) * bits + (-1, current.shape[-1]))
        for bit in range(bits):
            at = bits - 1 - bit
            mine = (place >> bit) & 1
            give = lax.dynamic_index_in_dim(pieces, 1 - mine, at, keepdims=False)
            keep = lax.dynamic_index_in_dim(pieces, mine, at, keepdims=False)
            got = lax.ppermute(give, axis, [(i, i ^ (1 << bit)) for i in range(size)])
            pieces = (keep.astype(jnp.float32) + got.astype(jnp.float32)).astype(jnp.bfloat16)
        current = pieces
    return current.astype(jnp.float32)


def per_device(
    sizes,
    tokens,
    segment_ids,
    first_gain,
    triple_weight,
    head_scale,
    output_weight,
    post_gain,
    second_gain,
    up_weight,
    mid_gain,
    down_weight,
    cotangent,
):
    inputs = tokens[0].astype(jnp.float32)
    width = inputs.shape[1]
    doc_ids = lax.all_gather(segment_ids[0], "seq", axis=0, tiled=True)
    triple_full, output_full = (
        lax.all_gather(triple_weight, "dp", axis=0, tiled=True),
        lax.all_gather(output_weight, "dp", axis=0, tiled=True),
    )
    normed, pull_first = jax.vjp(layer_norm, inputs, first_gain)
    normed_low = normed.astype(jnp.bfloat16)
    triple = jnp.dot(normed_low, triple_full, preferred_element_type=jnp.float32).astype(
        jnp.bfloat16
    )
    queries, keys_all, values_all = (
        lax.all_to_all(triple[:, :width], "seq", split_axis=1, concat_axis=0, tiled=True),
        lax.all_to_all(
            triple[:, width : 2 * width], "seq", split_axis=1, concat_axis=0, tiled=True
        ),
        lax.all_to_all(triple[:, 2 * width :], "seq", split_axis=1, concat_axis=0, tiled=True),
    )
    heads_here = queries.shape[1] // HEAD
    own_scale = lax.dynamic_slice_in_dim(
        head_scale, lax.axis_index("seq") * heads_here, heads_here, 0
    )
    scale_wide = jnp.repeat(own_scale, HEAD)[None]
    bounds, starts = document_bounds(doc_ids)
    attended, scaled, logsum = attend_forward(
        queries, keys_all, values_all, bounds, starts, scale_wide
    )
    merged = lax.all_to_all(scaled, "seq", split_axis=0, concat_axis=1, tiled=True)
    projected = jnp.dot(merged, output_full, preferred_element_type=jnp.float32)
    post_normed, pull_post = jax.vjp(layer_norm, projected, post_gain)
    middle = inputs + post_normed
    second, pull_second = jax.vjp(layer_norm, middle, second_gain)
    second_low = second.astype(jnp.bfloat16)
    feed_up, feed_down = (
        lax.all_gather(up_weight, "dp", axis=0, tiled=True),
        lax.all_gather(down_weight, "dp", axis=0, tiled=True),
    )
    hidden = jnp.dot(second_low, feed_up, preferred_element_type=jnp.float32)
    activated, pull_mid = jax.vjp(gelu_norm, hidden, mid_gain)
    activated_low = activated.astype(jnp.bfloat16)
    layer_out = (
        middle + jnp.dot(activated_low, feed_down, preferred_element_type=jnp.float32)
    ).astype(jnp.bfloat16)
    upstream = cotangent[0]
    grad_act = times_transposed(upstream, feed_down)
    grad_hidden, grad_mid = pull_mid(grad_act)
    grad_hidden_low = grad_hidden.astype(jnp.bfloat16)
    grad_second_in = times_transposed(grad_hidden_low, feed_up)
    grad_middle_part, grad_second = pull_second(grad_second_in)
    grad_middle = upstream.astype(jnp.float32) + grad_middle_part
    grad_projected, grad_post = pull_post(grad_middle)
    grad_projected_low = grad_projected.astype(jnp.bfloat16)
    grad_merged = times_transposed(grad_projected_low, output_full).astype(jnp.bfloat16)
    grad_scaled = lax.all_to_all(
        grad_merged, "seq", split_axis=1, concat_axis=0, tiled=True
    )
    grad_queries, grad_keys, grad_values, scale_lanes = attend_backward(
        queries, keys_all, values_all, attended, grad_scaled, bounds, starts, scale_wide, logsum
    )
    scale_terms = jnp.sum(scale_lanes.reshape(heads_here, HEAD), axis=1)
    back_queries, back_keys, back_values = (
        lax.all_to_all(
            grad_queries.astype(jnp.bfloat16), "seq", split_axis=0, concat_axis=1, tiled=True
        ),
        lax.all_to_all(
            grad_keys.astype(jnp.bfloat16), "seq", split_axis=0, concat_axis=1, tiled=True
        ),
        lax.all_to_all(
            grad_values.astype(jnp.bfloat16), "seq", split_axis=0, concat_axis=1, tiled=True
        ),
    )
    grad_triple_act = jnp.concatenate((back_queries, back_keys, back_values), axis=1)
    grad_normed = times_transposed(grad_triple_act, triple_full)
    grad_input_part, grad_first = pull_first(grad_normed)
    grad_tokens = (grad_middle + grad_input_part).astype(jnp.bfloat16)
    low = jnp.bfloat16
    grad_down = scatter_rows(transposed_times(activated_low, upstream).astype(low), sizes)
    grad_up = scatter_rows(transposed_times(second_low, grad_hidden_low).astype(low), sizes)
    grad_output = scatter_rows(transposed_times(merged, grad_projected_low).astype(low), sizes)
    gains = jnp.concatenate(
        (
            grad_first[:, None],
            grad_post[:, None],
            grad_second[:, None],
            grad_mid.reshape(width, -1),
        ),
        axis=1,
    )
    gains = jnp.pad(gains, ((0, 0), (0, 128 - gains.shape[1])))
    grad_triple = scatter_rows(
        jnp.concatenate(
            (transposed_times(normed_low, grad_triple_act).astype(low), gains.astype(low)), axis=1
        ),
        sizes,
    )
    gain_sums = grad_triple[:, 3 * width :]
    grad_scale = lax.psum(scale_terms, "dp")
    return (
        layer_out[None],
        grad_tokens[None],
        gain_sums[:, 0],
        grad_triple[:, : 3 * width],
        grad_scale,
        grad_output,
        gain_sums[:, 1],
        gain_sums[:, 2],
        grad_up,
        gain_sums[:, 3 : 3 + mid_gain.shape[0] // width].reshape(-1),
        grad_down,
    )


def solution(mesh):
    placed = (
        P("dp", "seq", None),
        P("dp", "seq"),
        P(),
        P("dp", None),
        P(),
        P("dp", None),
        P(),
        P(),
        P("dp", None),
        P(),
        P("dp", None),
        P("dp", "seq", None),
    )
    return jax.shard_map(
        functools.partial(per_device, (mesh.shape["dp"], mesh.shape["seq"])),
        mesh=mesh,
        in_specs=placed,
        out_specs=(
            P("dp", "seq", None),
            P("dp", "seq", None),
            P(("dp", "seq")),
            P(("dp", "seq"), None),
            P("seq"),
            P(("dp", "seq"), None),
            P(("dp", "seq")),
            P(("dp", "seq")),
            P(("dp", "seq"), None),
            P(("dp", "seq")),
            P(("dp", "seq"), None),
        ),
        check_vma=False,
    )
```

```python
import functools
import jax
import jax.numpy as jnp
from jax import lax
from jax.sharding import PartitionSpec as P
from jax.experimental import pallas as pl
from jax.experimental.pallas import tpu as pltpu

HEAD = 64
NEG = -1e30
BQ = 256


def nt(a, b):
    return lax.dot_general(a, b, (((1,), (1,)), ((), ())), preferred_element_type=jnp.float32)


def tn(a, b):
    return lax.dot_general(a, b, (((0,), (0,)), ((), ())), preferred_element_type=jnp.float32)


def stack_heads(block, heads):
    if heads == 1:
        return block
    lane = lax.broadcasted_iota(jnp.int32, block.shape, 1)
    zero = jnp.zeros_like(block)
    return jnp.concatenate(
        [jnp.where((lane >= h * HEAD) & (lane < (h + 1) * HEAD), block, zero) for h in range(heads)],
        axis=0,
    )


def unstack_heads(wide, heads):
    rows = wide.shape[1] // heads
    return jnp.concatenate(
        [wide[h * HEAD : (h + 1) * HEAD, h * rows : (h + 1) * rows] for h in range(heads)], axis=0
    )


def forward_kernel(heads, lo_ref, full_ref, q_ref, k_ref, v_ref, start_ref, scale_ref,
                   o_ref, u_ref, lse_ref, m_s, l_s, acc_s):
    i = pl.program_id(0)
    rows = q_ref.shape[0]
    wide = heads * rows
    queries = stack_heads(q_ref[...] * jnp.bfloat16(HEAD ** -0.5), heads)
    starts = jnp.concatenate([start_ref[0]] * heads, axis=1)
    m_s[...] = jnp.full_like(m_s, NEG)
    l_s[...] = jnp.zeros_like(l_s)
    acc_s[...] = jnp.zeros_like(acc_s)

    def step(j, masked, diagonal):
        at = pl.ds(pl.multiple_of(j * rows, rows), rows)
        scores = nt(k_ref[at, :], queries)
        if masked or diagonal:
            key = j * rows + lax.broadcasted_iota(jnp.int32, scores.shape, 0)
            allowed = key >= starts
            if diagonal:
                lane = lax.broadcasted_iota(jnp.int32, scores.shape, 1) & (rows - 1)
                allowed = allowed & (key <= i * rows + lane)
            scores = jnp.where(allowed, scores, NEG)
        before = m_s[...]
        highest = jnp.maximum(before, jnp.max(scores, axis=0, keepdims=True))
        weights = jnp.exp(scores - highest)
        fade = jnp.exp(before - highest)
        if masked:
            weights = jnp.where(scores > 0.5 * NEG, weights, 0.0)
        m_s[...] = highest
        l_s[...] = l_s[...] * fade + jnp.sum(weights, axis=0, keepdims=True)
        acc_s[...] = acc_s[...] * fade + tn(v_ref[at, :], weights.astype(jnp.bfloat16))

    step(i, False, True)
    full = jnp.minimum(full_ref[i], i)

    def plain(j, carry):
        step(j, False, False)
        return carry

    def edge(j, carry):
        step(j, True, False)
        return carry

    lax.fori_loop(full, i, plain, 0)
    lax.fori_loop(lo_ref[i], full, edge, 0)
    total = l_s[...]
    out = unstack_heads(acc_s[...] / total, heads).T
    o_ref[...] = out
    u_ref[...] = (out * scale_ref[...]).astype(jnp.bfloat16)
    lse_ref[0] = m_s[...] + jnp.log(total)


def attend_forward(queries, keys, values, bounds, starts, scale_wide):
    length, width = queries.shape
    heads = width // HEAD
    blocks = length // BQ
    whole = pl.BlockSpec((length, width), lambda i, *_: (0, 0))
    mine = pl.BlockSpec((BQ, width), lambda i, *_: (i, 0))
    return pl.pallas_call(
        functools.partial(forward_kernel, heads),
        out_shape=(
            jax.ShapeDtypeStruct((length, width), jnp.float32),
            jax.ShapeDtypeStruct((length, width), jnp.bfloat16),
            jax.ShapeDtypeStruct((blocks, 1, heads * BQ), jnp.float32),
        ),
        grid_spec=pltpu.PrefetchScalarGridSpec(
            num_scalar_prefetch=2,
            grid=(blocks,),
            in_specs=[
                mine,
                whole,
                whole,
                pl.BlockSpec((1, 1, BQ), lambda i, *_: (i, 0, 0)),
                pl.BlockSpec((1, width), lambda i, *_: (0, 0)),
            ],
            out_specs=(mine, mine, pl.BlockSpec((1, 1, heads * BQ), lambda i, *_: (i, 0, 0))),
            scratch_shapes=[
                pltpu.VMEM((1, heads * BQ), jnp.float32),
                pltpu.VMEM((1, heads * BQ), jnp.float32),
                pltpu.VMEM((width, heads * BQ), jnp.float32),
            ],
        ),
        cost_estimate=pl.CostEstimate(
            flops=length * length * width, bytes_accessed=16 * length * width, transcendentals=0
        ),
        name="attend_forward",
    )(bounds[0], bounds[1], queries, keys, values, starts.reshape(blocks, 1, BQ), scale_wide)


def backward_kernel(heads, hi_ref, full_ref, q_ref, k_ref, v_ref, o_ref, du_ref, start_ref, scale_ref, lse_ref,
                    dq_ref, dk_ref, dv_ref, ds_ref, qs_s, dos_s, delta_s, dqt_s, dk_s, dv_s):
    j = pl.program_id(0)
    rows = k_ref.shape[0]
    blocks = qs_s.shape[0]
    wide = heads * rows

    @pl.when(j == 0)
    def prepare():
        def one(i, total):
            at = pl.ds(pl.multiple_of(i * rows, rows), rows)
            qs_s[i] = stack_heads(q_ref[at, :] * jnp.bfloat16(HEAD ** -0.5), heads)
            grad = du_ref[at, :].astype(jnp.float32)
            out = o_ref[at, :]
            low = (grad * scale_ref[...]).astype(jnp.bfloat16)
            dos_s[i] = stack_heads(low, heads)
            inner = (low.astype(jnp.float32) * out).T
            delta_s[i] = jnp.concatenate(
                [jnp.sum(inner[h * HEAD : (h + 1) * HEAD], axis=0, keepdims=True) for h in range(heads)],
                axis=1,
            )
            return total + jnp.sum(grad * out, axis=0, keepdims=True)

        ds_ref[...] = lax.fori_loop(0, blocks, one, jnp.zeros(ds_ref.shape, jnp.float32))
        dqt_s[...] = jnp.zeros_like(dqt_s)

    keys, values = k_ref[...], v_ref[...]
    dk_s[...] = jnp.zeros_like(dk_s)
    dv_s[...] = jnp.zeros_like(dv_s)

    def step(i, masked, diagonal):
        queries, grads = qs_s[i], dos_s[i]
        scores = nt(keys, queries)
        if masked or diagonal:
            key = j * rows + lax.broadcasted_iota(jnp.int32, scores.shape, 0)
            starts = jnp.concatenate([start_ref[i]] * heads, axis=1)
            allowed = key >= starts
            if diagonal:
                lane = lax.broadcasted_iota(jnp.int32, scores.shape, 1) & (rows - 1)
                allowed = allowed & (key <= i * rows + lane)
            scores = jnp.where(allowed, scores, NEG)
        weights = jnp.exp(scores - lse_ref[i])
        pulls = nt(values, grads)
        low = (weights * (pulls - delta_s[i])).astype(jnp.bfloat16)
        dv_s[...] += jnp.dot(weights.astype(jnp.bfloat16), grads, preferred_element_type=jnp.float32)
        dk_s[...] += jnp.dot(low, queries, preferred_element_type=jnp.float32)
        dqt_s[i] += tn(keys, low)

    step(j, False, True)
    full = jnp.maximum(full_ref[j], j + 1)

    def plain(i, carry):
        step(i, False, False)
        return carry

    def edge(i, carry):
        step(i, True, False)
        return carry

    lax.fori_loop(j + 1, full, plain, 0)
    lax.fori_loop(full, hi_ref[j], edge, 0)
    dk_ref[...] = dk_s[...].astype(jnp.bfloat16)
    dv_ref[...] = dv_s[...].astype(jnp.bfloat16)

    @pl.when(j == blocks - 1)
    def finish():
        def one(i, carry):
            at = pl.ds(pl.multiple_of(i * rows, rows), rows)
            dq_ref[at, :] = (unstack_heads(dqt_s[i], heads).T * HEAD ** -0.5).astype(jnp.bfloat16)
            return carry

        lax.fori_loop(0, blocks, one, 0)


def attend_backward(queries, keys, values, outs, grads, bounds, starts, scale_wide, logsum):
    length, width = queries.shape
    heads = width // HEAD
    blocks = length // BQ
    whole = pl.BlockSpec((length, width), lambda i, *_: (0, 0))
    mine = pl.BlockSpec((BQ, width), lambda i, *_: (i, 0))
    return pl.pallas_call(
        functools.partial(backward_kernel, heads),
        out_shape=(jax.ShapeDtypeStruct((length, width), jnp.bfloat16),) * 3
        + (jax.ShapeDtypeStruct((1, width), jnp.float32),),
        grid_spec=pltpu.PrefetchScalarGridSpec(
            num_scalar_prefetch=2,
            grid=(blocks,),
            in_specs=[
                whole,
                mine,
                mine,
                whole,
                whole,
                pl.BlockSpec((blocks, 1, BQ), lambda i, *_: (0, 0, 0)),
                pl.BlockSpec((1, width), lambda i, *_: (0, 0)),
                pl.BlockSpec((blocks, 1, heads * BQ), lambda i, *_: (0, 0, 0)),
            ],
            out_specs=(whole, mine, mine, pl.BlockSpec((1, width), lambda i, *_: (0, 0))),
            scratch_shapes=[
                pltpu.VMEM((blocks, heads * BQ, width), jnp.bfloat16),
                pltpu.VMEM((blocks, heads * BQ, width), jnp.bfloat16),
                pltpu.VMEM((blocks, 1, heads * BQ), jnp.float32),
                pltpu.VMEM((blocks, width, heads * BQ), jnp.float32),
                pltpu.VMEM((BQ, width), jnp.float32),
                pltpu.VMEM((BQ, width), jnp.float32),
            ],
        ),
        cost_estimate=pl.CostEstimate(
            flops=3 * length * length * width, bytes_accessed=32 * length * width, transcendentals=0
        ),
        name="attend_backward",
    )(bounds[2], bounds[3], queries, keys, values, outs, grads, starts.reshape(blocks, 1, BQ), scale_wide, logsum)


def document_bounds(doc_ids):
    length = doc_ids.shape[0]
    blocks = length // BQ
    counts = jnp.sum(doc_ids[None, :] < jnp.arange(8, dtype=jnp.int32)[:, None], axis=1, dtype=jnp.int32)
    starts = jnp.sum(
        jnp.where(doc_ids[:, None] == jnp.arange(8, dtype=jnp.int32)[None, :], counts[None, :], 0), axis=1, dtype=jnp.int32
    )
    by_block = starts.reshape(blocks, BQ)
    low = by_block[:, 0] // BQ
    full = (by_block[:, BQ - 1] + BQ - 1) // BQ
    index = jnp.arange(blocks, dtype=jnp.int32)
    high = jnp.sum(low[None, :] <= index[:, None], axis=1, dtype=jnp.int32)
    full_high = jnp.sum(full[None, :] <= index[:, None], axis=1, dtype=jnp.int32)
    return (low, full, high, full_high), starts


def layer_norm(values, gains):
    center = values - jnp.mean(values, axis=-1, keepdims=True)
    spread = jnp.mean(center * center, axis=-1, keepdims=True)
    return center * lax.rsqrt(spread + 1e-05) * gains


def gelu_norm(hidden, gains):
    return layer_norm(jax.nn.gelu(hidden, approximate=True), gains)


def transposed_times(left, right):
    return lax.dot_general(
        left, right, (((0,), (0,)), ((), ())), preferred_element_type=jnp.float32
    )


def times_transposed(left, right):
    return lax.dot_general(
        left, right, (((1,), (1,)), ((), ())), preferred_element_type=jnp.float32
    )


def scatter_rows(partial, sizes):
    current = partial
    for axis, size in zip(("dp", "seq"), sizes):
        place = lax.axis_index(axis)
        bits = size.bit_length() - 1
        pieces = current.reshape((2,) * bits + (-1, current.shape[-1]))
        for bit in range(bits):
            at = bits - 1 - bit
            mine = (place >> bit) & 1
            give = lax.dynamic_index_in_dim(pieces, 1 - mine, at, keepdims=False)
            keep = lax.dynamic_index_in_dim(pieces, mine, at, keepdims=False)
            got = lax.ppermute(give, axis, [(i, i ^ (1 << bit)) for i in range(size)])
            pieces = (keep.astype(jnp.float32) + got.astype(jnp.float32)).astype(jnp.bfloat16)
        current = pieces
    return current.astype(jnp.float32)


MESH = pl.DeviceIdType.MESH
LOW = jnp.bfloat16
BLOCK = 1024
VMEM_BYTES = 66_000_000


class Place:
    def __init__(self):
        self.dp, self.seq = lax.axis_index("dp"), lax.axis_index("seq")
        self.core, self.y = self.dp % 2, self.dp // 2
        self.x, self.z = self.seq % 2, self.seq // 2
        self.z0, self.z1 = self.z % 2, self.z // 2

    def core_partner(self):
        return (self.dp + 1 - 2 * self.core, self.seq)

    def y_partner(self):
        return (self.dp + 2 - 4 * self.y, self.seq)

    def x_partner(self):
        return (self.dp, self.seq + 1 - 2 * self.x)

    def near_partner(self):
        return (self.dp, self.seq + 2 - 4 * self.z0)

    def far_partner(self):
        return (self.dp, self.seq + 4 - 8 * self.z1)


def meet(devices):
    barrier = pltpu.get_barrier_semaphore()
    for device in devices:
        pl.semaphore_signal(barrier, inc=1, device_id=device, device_id_type=MESH)
    pl.semaphore_wait(barrier, len(devices))


def remote(source, target, send, receive, device):
    return pltpu.make_async_remote_copy(
        src_ref=source,
        dst_ref=target,
        send_sem=send,
        recv_sem=receive,
        device_id=device,
        device_id_type=MESH,
    )


class Scatter:
    def __init__(self, place, refs, sems, base, left, right, write):
        self.place, self.base, self.left, self.right, self.write = place, base, left, right, write
        self.whole, self.first, self.second, self.near, self.far = refs
        self.send, self.receive = sems
        self.rows, self.columns = self.whole.shape[-2:]

    def axes(self, p):
        place = self.place
        if p % 2 == 0:
            return place.y, place.x, place.y_partner(), place.x_partner()
        return place.x, place.y, place.x_partner(), place.y_partner()

    def copy(self, p, stage):
        place = self.place
        mine, other, partner, second = self.axes(p)
        if stage == 0:
            source, target, device = self.whole.at[p, 1 - mine], self.first.at[p], partner
        elif stage == 1:
            source, target, device = self.first.at[p, :, :, 1 - other], self.second.at[p], second
        elif stage == 2:
            source, target, device = self.second.at[p, :, 1 - place.z0], self.near.at[p], place.near_partner()
        else:
            source, target, device = self.near.at[p, 1 - place.z1], self.far.at[p], place.far_partner()
        index = self.base + p
        return remote(source, target, self.send.at[stage, index], self.receive.at[stage, index], device)

    def compute(self, p):
        left, right = self.left(p), self.right(p)
        rows = self.rows

        def one(y, carry):
            for half in range(2):
                span = 4 * rows
                at = pl.ds(pl.multiple_of(y * 8 * rows + half * span, 128), span)
                block = tn(left[:, at], right[...]).astype(LOW)
                for k in range(4):
                    x = k % 2
                    part = block[k * rows : (k + 1) * rows]
                    if p % 2 == 0:
                        self.whole[p, y, half, k // 2, x] = part
                    else:
                        self.whole[p, x, half, k // 2, y] = part
            return carry

        lax.fori_loop(0, 2, one, 0)
        self.copy(p, 0).start()

    def advance(self, p, stage):
        place = self.place
        mine, other, _, _ = self.axes(p)
        wide = jnp.float32
        self.copy(p, stage - 1).wait_recv()
        if stage == 1:

            def add(k, carry):
                a, b, s = k // 4, k // 2 % 2, k % 2
                total = self.first[p, a, b, s].astype(wide) + self.whole[p, mine, a, b, s].astype(wide)
                self.first[p, a, b, s] = total.astype(LOW)
                return carry

            lax.fori_loop(0, 8, add, 0)
        elif stage == 2:

            def add(z, carry):
                a, b = z // 2, z % 2
                total = self.second[p, a, b].astype(wide) + self.first[p, a, b, other].astype(wide)
                self.second[p, a, b] = total.astype(LOW)
                return carry

            lax.fori_loop(0, 4, add, 0)
        elif stage == 3:

            def add(a, carry):
                total = self.near[p, a].astype(wide) + self.second[p, a, place.z0].astype(wide)
                self.near[p, a] = total.astype(LOW)
                return carry

            lax.fori_loop(0, 2, add, 0)
        else:
            self.write(p, self.near[p, place.z1].astype(wide) + self.far[p].astype(wide))
            return
        self.copy(p, stage).start()

    def settle(self, p):
        for stage in range(4):
            self.copy(p, stage).wait_send()


def scatter_scratch(pieces, rows, columns):
    return [
        pltpu.VMEM((pieces, 2, 2, 2, 2, rows, columns), LOW),
        pltpu.VMEM((pieces, 2, 2, 2, rows, columns), LOW),
        pltpu.VMEM((pieces, 2, 2, rows, columns), LOW),
        pltpu.VMEM((pieces, 2, rows, columns), LOW),
        pltpu.VMEM((pieces, rows, columns), LOW),
    ]


def own_columns(source, core, columns):
    half = source.shape[1] // 2
    return [
        source.at[:, pl.ds(pl.multiple_of(y * half + core * columns, 128), columns)] for y in range(2)
    ]


def tail_kernel(
    dq, dk, dv, tokens, gain, middle, triple, act_down, act_up, act_out, act_in, g_down, g_up, g_out, gains,
    o_tokens, o_triple, o_out, o_up, o_down, o_gains,
    d_left, d_right, d_whole, d_first, d_second, d_near, d_far,
    e_left, e_right, e_whole, e_first, e_second, e_near, e_far,
    grad_s, gain_s, gain_r,
    local_sem, core_send, core_recv, a2a_send, a2a_recv, s_send, s_recv, gain_send, gain_recv,
):
    place = Place()
    partner = place.core_partner()
    peers = [(place.dp, (place.seq + k) % 8) for k in range(1, 8)]
    local, width = tokens.shape
    heads_width = dq.shape[1]
    meet(peers + [partner, place.y_partner()])

    moves = []
    column = pl.ds(pl.multiple_of(place.seq * heads_width, 128), heads_width)
    for t, source in enumerate((dv, dk, dq)):
        slot = 5 + (2 - t)
        for k in range(1, 8):
            peer = (place.seq + k) % 8
            rows = pl.ds(pl.multiple_of(peer * local, 128), local)
            move = remote(
                source.at[rows, :],
                e_right.at[slot, pl.ds(0, local), column],
                a2a_send.at[t, k - 1],
                a2a_recv.at[t, k - 1],
                (place.dp, peer),
            )
            move.start()
            moves.append(move)
        rows = pl.ds(pl.multiple_of(place.seq * local, 128), local)
        move = pltpu.make_async_copy(
            source.at[rows, :], e_right.at[slot, pl.ds(0, local), column], local_sem.at[t]
        )
        move.start()
        moves.append(move)

    def share(index, sources, targets):
        out = []
        for k, (ours, theirs, target) in enumerate(zip(*sources, targets)):
            here = pltpu.make_async_copy(ours, target.at[pl.ds(0, local), :], local_sem.at[3 + index + k])
            there = remote(
                theirs,
                target.at[pl.ds(local, local), :],
                core_send.at[index + k],
                core_recv.at[index + k],
                partner,
            )
            here.start()
            there.start()
            out += [here, there]
        return out

    def share_left(index, source, target):
        columns = source.shape[1] // 4
        ours = own_columns(source, place.core, columns)
        theirs = own_columns(source, 1 - place.core, columns)
        targets = [target.at[:, pl.ds(y * columns, columns)] for y in range(2)]
        return share(index, (ours, theirs), targets)

    ready = {}
    ready["down"] = share_left(0, act_down, d_left) + share(2, ([g_down], [g_down]), [d_right])
    ready["up"] = share_left(3, act_up, e_left.at[0])
    for k in range(4):
        part = g_up.at[:, pl.ds(k * BLOCK, BLOCK)]
        ready["up"] += share(5 + k, ([part], [part]), [e_right.at[k]])
    ready["out"] = share_left(9, act_out, e_left.at[1]) + share(11, ([g_out], [g_out]), [e_right.at[4]])
    ready["in"] = share_left(12, act_in, e_left.at[2])

    def write_down(p, value):
        o_down[:, pl.ds(p * 256, 256)] = value

    def write_rest(p, value):
        if p < 4:
            o_up[:, pl.ds(p * BLOCK, BLOCK)] = value
        elif p == 4:
            o_out[...] = value
        else:
            o_triple[:, pl.ds((p - 5) * BLOCK, BLOCK)] = value

    down = Scatter(
        place, (d_whole, d_first, d_second, d_near, d_far), (s_send, s_recv), 0,
        lambda p: d_left, lambda p: d_right.at[:, pl.ds(p * 256, 256)], write_down,
    )
    rest = Scatter(
        place, (e_whole, e_first, e_second, e_near, e_far), (s_send, s_recv), 4,
        lambda p: e_left.at[0 if p < 4 else 1 if p == 4 else 2], lambda p: e_right.at[p], write_rest,
    )
    order = [(down, k) for k in range(4)] + [(rest, k) for k in (0, 1, 2, 3, 4, 7, 6, 5)]

    def wait_all(copies):
        for copy in copies:
            copy.wait()

    lag = 2
    gain_s[...] = gains[...]

    def step(t):
        if t < len(order):
            engine, p = order[t]
            if t == 0:
                wait_all(ready["down"])
            if t == 4:
                wait_all(ready["up"])
            if t == 8:
                wait_all(ready["out"])
            engine.compute(p)
        for stage in (1, 2, 3, 4):
            at = t - stage * lag
            if 0 <= at < len(order):
                order[at][0].advance(order[at][1], stage)

    for t in range(9):
        step(t)

    wait_all(moves)
    back = [
        remote(
            e_right.at[5 + t, pl.ds(0, local), :],
            e_right.at[5 + t, pl.ds(local, local), :],
            core_send.at[14 + t],
            core_recv.at[14 + t],
            partner,
        )
        for t in range(3)
    ]
    for move in back:
        move.start()

    def columns_of(n, carry):
        rows = pl.ds(pl.multiple_of(n * 256, 256), 256)
        total = jnp.zeros((local, 256), jnp.float32)
        for t in range(3):
            total += nt(e_right[5 + t, pl.ds(0, local), :], triple[rows, pl.ds(t * width, width)])
        grad_s[:, rows] = total
        return carry

    wait_all(ready["in"])
    wait_all(back)
    step(9)
    step(10)
    step(11)
    lax.fori_loop(0, width // 256, columns_of, 0)
    step(12)

    def norm_rows(n, total):
        rows = pl.ds(pl.multiple_of(n * 128, 128), 128)
        values = tokens[rows, :].astype(jnp.float32)
        center = values - jnp.mean(values, axis=-1, keepdims=True)
        inverse = lax.rsqrt(jnp.mean(center * center, axis=-1, keepdims=True) + 1e-05)
        unit = center * inverse
        grad = grad_s[rows, :]
        scaled = grad * gain[...]
        pulled = inverse * (
            scaled
            - jnp.mean(scaled, axis=-1, keepdims=True)
            - unit * jnp.mean(scaled * unit, axis=-1, keepdims=True)
        )
        o_tokens[rows, :] = (middle[rows, :] + pulled).astype(LOW)
        return total + jnp.sum(grad * unit, axis=0, keepdims=True)

    gain_s[0:1, :] = lax.fori_loop(0, local // 128, norm_rows, jnp.zeros((1, width), jnp.float32))

    meets = (partner, place.y_partner(), place.x_partner(), place.near_partner(), place.far_partner())

    def gain_step(k):
        move = remote(gain_s, gain_r.at[k], gain_send.at[k], gain_recv.at[k], meets[k])
        return move

    for k in range(5):
        move = gain_step(k)
        move.start()
        step(13 + k)
        move.wait()
        gain_s[...] = gain_s[...] + gain_r[k]
        if k == 1:
            o_gains[7:8, :] = gain_s[7:8, 0:128]
    for t in range(18, len(order) + 4 * lag + 1):
        step(t)
    device = place.dp * 8 + place.seq
    pick = (
        lax.broadcasted_iota(jnp.int32, (width, 128), 0)
        == device * 32 + lax.broadcasted_iota(jnp.int32, (width, 128), 1)
    ).astype(jnp.float32)
    o_gains[0:3, :] = jnp.dot(
        gain_s[...], pick, preferred_element_type=jnp.float32, precision=lax.Precision.HIGHEST
    )[0:3]
    block = gain_s[:, pl.ds(pl.multiple_of((device % 8) * 128, 128), 128)]
    row = lax.broadcasted_iota(jnp.int32, block.shape, 0)
    o_gains[3:4, :] = jnp.sum(jnp.where(row == 3 + device // 8, block, 0.0), axis=0, keepdims=True)
    o_gains[4:7, :] = jnp.zeros((3, 128), jnp.float32)
    for engine, p in order:
        engine.settle(p)


def tail(dqkv, tokens, gain, middle, triple, acts, grads, gains):
    local, width = tokens.shape
    heads_width = dqkv[0].shape[1]
    hidden = acts[0].shape[1]
    any_spec = pl.BlockSpec(memory_space=pl.ANY)
    vmem = pl.BlockSpec(memory_space=pltpu.VMEM)
    wide = jnp.float32
    dma = pltpu.SemaphoreType.DMA
    return pl.pallas_call(
        tail_kernel,
        out_shape=(
            jax.ShapeDtypeStruct((local, width), LOW),
            jax.ShapeDtypeStruct((width // 32, 3 * width), wide),
            jax.ShapeDtypeStruct((width // 32, width), wide),
            jax.ShapeDtypeStruct((width // 32, hidden), wide),
            jax.ShapeDtypeStruct((hidden // 32, width), wide),
            jax.ShapeDtypeStruct((8, 128), wide),
        ),
        in_specs=[any_spec] * 3 + [vmem] * 4 + [any_spec] * 7 + [vmem],
        out_specs=(vmem,) * 6,
        scratch_shapes=[pltpu.VMEM((2 * local, hidden // 2), LOW), pltpu.VMEM((2 * local, width), LOW)]
        + scatter_scratch(4, 128, 256)
        + [pltpu.VMEM((3, 2 * local, width // 2), LOW), pltpu.VMEM((8, 2 * local, width), LOW)]
        + scatter_scratch(8, 32, 1024)
        + [
            pltpu.VMEM((local, width), wide),
            pltpu.VMEM((8, width), wide),
            pltpu.VMEM((5, 8, width), wide),
            dma((20,)),
            dma((20,)),
            dma((20,)),
            dma((3, 7)),
            dma((3, 7)),
            dma((4, 12)),
            dma((4, 12)),
            dma((5,)),
            dma((5,)),
        ],
        compiler_params=pltpu.CompilerParams(
            collective_id=3, has_side_effects=True, vmem_limit_bytes=VMEM_BYTES
        ),
        name="tail",
    )(*dqkv, tokens, gain.reshape(1, width), middle, triple, *acts, *grads, gains)


def per_device(
    sizes,
    tokens,
    segment_ids,
    first_gain,
    triple_weight,
    head_scale,
    output_weight,
    post_gain,
    second_gain,
    up_weight,
    mid_gain,
    down_weight,
    cotangent,
):
    inputs = tokens[0].astype(jnp.float32)
    width = inputs.shape[1]
    doc_ids = lax.all_gather(segment_ids[0], "seq", axis=0, tiled=True)
    triple_full, output_full = (
        lax.all_gather(triple_weight, "dp", axis=0, tiled=True),
        lax.all_gather(output_weight, "dp", axis=0, tiled=True),
    )
    normed, pull_first = jax.vjp(layer_norm, inputs, first_gain)
    normed_low = normed.astype(jnp.bfloat16)
    triple = jnp.dot(normed_low, triple_full, preferred_element_type=jnp.float32).astype(
        jnp.bfloat16
    )
    queries, keys_all, values_all = (
        lax.all_to_all(triple[:, :width], "seq", split_axis=1, concat_axis=0, tiled=True),
        lax.all_to_all(
            triple[:, width : 2 * width], "seq", split_axis=1, concat_axis=0, tiled=True
        ),
        lax.all_to_all(triple[:, 2 * width :], "seq", split_axis=1, concat_axis=0, tiled=True),
    )
    heads_here = queries.shape[1] // HEAD
    own_scale = lax.dynamic_slice_in_dim(
        head_scale, lax.axis_index("seq") * heads_here, heads_here, 0
    )
    scale_wide = jnp.repeat(own_scale, HEAD)[None]
    bounds, starts = document_bounds(doc_ids)
    attended, scaled, logsum = attend_forward(
        queries, keys_all, values_all, bounds, starts, scale_wide
    )
    merged = lax.all_to_all(scaled, "seq", split_axis=0, concat_axis=1, tiled=True)
    projected = jnp.dot(merged, output_full, preferred_element_type=jnp.float32)
    post_normed, pull_post = jax.vjp(layer_norm, projected, post_gain)
    middle = inputs + post_normed
    second, pull_second = jax.vjp(layer_norm, middle, second_gain)
    second_low = second.astype(jnp.bfloat16)
    feed_up, feed_down = (
        lax.all_gather(up_weight, "dp", axis=0, tiled=True),
        lax.all_gather(down_weight, "dp", axis=0, tiled=True),
    )
    hidden = jnp.dot(second_low, feed_up, preferred_element_type=jnp.float32)
    activated, pull_mid = jax.vjp(gelu_norm, hidden, mid_gain)
    activated_low = activated.astype(jnp.bfloat16)
    layer_out = (
        middle + jnp.dot(activated_low, feed_down, preferred_element_type=jnp.float32)
    ).astype(jnp.bfloat16)
    upstream = cotangent[0]
    grad_act = times_transposed(upstream, feed_down)
    grad_hidden, grad_mid = pull_mid(grad_act)
    grad_hidden_low = grad_hidden.astype(jnp.bfloat16)
    grad_second_in = times_transposed(grad_hidden_low, feed_up)
    grad_middle_part, grad_second = pull_second(grad_second_in)
    grad_middle = upstream.astype(jnp.float32) + grad_middle_part
    grad_projected, grad_post = pull_post(grad_middle)
    grad_projected_low = grad_projected.astype(jnp.bfloat16)
    grad_merged = times_transposed(grad_projected_low, output_full).astype(jnp.bfloat16)
    grad_scaled = lax.all_to_all(
        grad_merged, "seq", split_axis=1, concat_axis=0, tiled=True
    )
    grad_queries, grad_keys, grad_values, scale_lanes = attend_backward(
        queries, keys_all, values_all, attended, grad_scaled, bounds, starts, scale_wide, logsum
    )
    scale_terms = jnp.sum(scale_lanes.reshape(heads_here, HEAD), axis=1)
    back_queries, back_keys, back_values = (
        lax.all_to_all(
            grad_queries.astype(jnp.bfloat16), "seq", split_axis=0, concat_axis=1, tiled=True
        ),
        lax.all_to_all(
            grad_keys.astype(jnp.bfloat16), "seq", split_axis=0, concat_axis=1, tiled=True
        ),
        lax.all_to_all(
            grad_values.astype(jnp.bfloat16), "seq", split_axis=0, concat_axis=1, tiled=True
        ),
    )
    grad_triple_act = jnp.concatenate((back_queries, back_keys, back_values), axis=1)
    grad_normed = times_transposed(grad_triple_act, triple_full)
    grad_input_part, grad_first = pull_first(grad_normed)
    grad_tokens = (grad_middle + grad_input_part).astype(jnp.bfloat16)
    low = jnp.bfloat16
    grad_down = scatter_rows(transposed_times(activated_low, upstream).astype(low), sizes)
    grad_up = scatter_rows(transposed_times(second_low, grad_hidden_low).astype(low), sizes)
    grad_output = scatter_rows(transposed_times(merged, grad_projected_low).astype(low), sizes)
    gains = jnp.concatenate(
        (
            grad_first[:, None],
            grad_post[:, None],
            grad_second[:, None],
            grad_mid.reshape(width, -1),
        ),
        axis=1,
    )
    gains = jnp.pad(gains, ((0, 0), (0, 128 - gains.shape[1])))
    grad_triple = scatter_rows(
        jnp.concatenate(
            (transposed_times(normed_low, grad_triple_act).astype(low), gains.astype(low)), axis=1
        ),
        sizes,
    )
    gain_sums = grad_triple[:, 3 * width :]
    grad_scale = lax.psum(scale_terms, "dp")
    return (
        layer_out[None],
        grad_tokens[None],
        gain_sums[:, 0],
        grad_triple[:, : 3 * width],
        grad_scale,
        grad_output,
        gain_sums[:, 1],
        gain_sums[:, 2],
        grad_up,
        gain_sums[:, 3 : 3 + mid_gain.shape[0] // width].reshape(-1),
        grad_down,
    )


def per_device_chips(
    sizes,
    tokens,
    segment_ids,
    first_gain,
    triple_weight,
    head_scale,
    output_weight,
    post_gain,
    second_gain,
    up_weight,
    mid_gain,
    down_weight,
    cotangent,
):
    inputs = tokens[0].astype(jnp.float32)
    width = inputs.shape[1]
    doc_ids = lax.all_gather(segment_ids[0], "seq", axis=0, tiled=True)
    triple_full, output_full = (
        lax.all_gather(triple_weight, "dp", axis=0, tiled=True),
        lax.all_gather(output_weight, "dp", axis=0, tiled=True),
    )
    normed = layer_norm(inputs, first_gain)
    normed_low = normed.astype(jnp.bfloat16)
    triple = jnp.dot(normed_low, triple_full, preferred_element_type=jnp.float32).astype(
        jnp.bfloat16
    )
    queries, keys_all, values_all = (
        lax.all_to_all(triple[:, :width], "seq", split_axis=1, concat_axis=0, tiled=True),
        lax.all_to_all(
            triple[:, width : 2 * width], "seq", split_axis=1, concat_axis=0, tiled=True
        ),
        lax.all_to_all(triple[:, 2 * width :], "seq", split_axis=1, concat_axis=0, tiled=True),
    )
    heads_here = queries.shape[1] // HEAD
    own_scale = lax.dynamic_slice_in_dim(
        head_scale, lax.axis_index("seq") * heads_here, heads_here, 0
    )
    scale_wide = jnp.repeat(own_scale, HEAD)[None]
    bounds, starts = document_bounds(doc_ids)
    attended, scaled, logsum = attend_forward(
        queries, keys_all, values_all, bounds, starts, scale_wide
    )
    merged = lax.all_to_all(scaled, "seq", split_axis=0, concat_axis=1, tiled=True)
    projected = jnp.dot(merged, output_full, preferred_element_type=jnp.float32)
    post_normed, pull_post = jax.vjp(layer_norm, projected, post_gain)
    middle = inputs + post_normed
    second, pull_second = jax.vjp(layer_norm, middle, second_gain)
    second_low = second.astype(jnp.bfloat16)
    feed_up, feed_down = (
        lax.all_gather(up_weight, "dp", axis=0, tiled=True),
        lax.all_gather(down_weight, "dp", axis=0, tiled=True),
    )
    hidden = jnp.dot(second_low, feed_up, preferred_element_type=jnp.float32)
    activated, pull_mid = jax.vjp(gelu_norm, hidden, mid_gain)
    activated_low = activated.astype(jnp.bfloat16)
    layer_out = (
        middle + jnp.dot(activated_low, feed_down, preferred_element_type=jnp.float32)
    ).astype(jnp.bfloat16)
    upstream = cotangent[0]
    grad_act = times_transposed(upstream, feed_down)
    grad_hidden, grad_mid = pull_mid(grad_act)
    grad_hidden_low = grad_hidden.astype(jnp.bfloat16)
    grad_second_in = times_transposed(grad_hidden_low, feed_up)
    grad_middle_part, grad_second = pull_second(grad_second_in)
    grad_middle = upstream.astype(jnp.float32) + grad_middle_part
    grad_projected, grad_post = pull_post(grad_middle)
    grad_projected_low = grad_projected.astype(jnp.bfloat16)
    grad_merged = times_transposed(grad_projected_low, output_full).astype(jnp.bfloat16)
    grad_scaled = lax.all_to_all(
        grad_merged, "seq", split_axis=1, concat_axis=0, tiled=True
    )
    grad_queries, grad_keys, grad_values, scale_lanes = attend_backward(
        queries, keys_all, values_all, attended, grad_scaled, bounds, starts, scale_wide, logsum
    )
    grad_first_low = jnp.zeros((1, width), jnp.float32)
    gains = jnp.concatenate(
        (
            grad_first_low,
            grad_post[None],
            grad_second[None],
            grad_mid.reshape(-1, width),
            jnp.pad(scale_lanes, ((0, 0), (0, width - scale_lanes.shape[1]))),
        ),
        axis=0,
    )
    grad_tokens, grad_triple, grad_output, grad_up, grad_down, sums = tail(
        (grad_queries, grad_keys, grad_values),
        tokens[0],
        first_gain,
        grad_middle,
        triple_full,
        (activated_low, second_low, merged, normed_low),
        (upstream, grad_hidden_low, grad_projected_low),
        gains,
    )
    own = width // 32
    return (
        layer_out[None],
        grad_tokens[None],
        sums[0, :own],
        grad_triple,
        jnp.sum(sums[7].reshape(heads_here, HEAD), axis=1),
        grad_output,
        sums[1, :own],
        sums[2, :own],
        grad_up,
        sums[3],
        grad_down,
    )


def solution(mesh):
    placed = (
        P("dp", "seq", None),
        P("dp", "seq"),
        P(),
        P("dp", None),
        P(),
        P("dp", None),
        P(),
        P(),
        P("dp", None),
        P(),
        P("dp", None),
        P("dp", "seq", None),
    )
    sizes = (mesh.shape["dp"], mesh.shape["seq"])
    program = per_device_chips if sizes == (4, 8) else per_device
    return jax.shard_map(
        functools.partial(program, sizes),
        mesh=mesh,
        in_specs=placed,
        out_specs=(
            P("dp", "seq", None),
            P("dp", "seq", None),
            P(("dp", "seq")),
            P(("dp", "seq"), None),
            P("seq"),
            P(("dp", "seq"), None),
            P(("dp", "seq")),
            P(("dp", "seq")),
            P(("dp", "seq"), None),
            P(("dp", "seq")),
            P(("dp", "seq"), None),
        ),
        check_vma=False,
    )
```

```python
import functools
import jax
import jax.numpy as jnp
from jax import lax
from jax.sharding import PartitionSpec as P
from jax.experimental import pallas as pl
from jax.experimental.pallas import tpu as pltpu

HEAD = 64
NEG = -1e30
BQ = 256


def nt(a, b):
    return lax.dot_general(a, b, (((1,), (1,)), ((), ())), preferred_element_type=jnp.float32)


def tn(a, b):
    return lax.dot_general(a, b, (((0,), (0,)), ((), ())), preferred_element_type=jnp.float32)


def stack_heads(block, heads):
    if heads == 1:
        return block
    lane = lax.broadcasted_iota(jnp.int32, block.shape, 1)
    zero = jnp.zeros_like(block)
    return jnp.concatenate(
        [jnp.where((lane >= h * HEAD) & (lane < (h + 1) * HEAD), block, zero) for h in range(heads)],
        axis=0,
    )


def unstack_heads(wide, heads):
    rows = wide.shape[1] // heads
    return jnp.concatenate(
        [wide[h * HEAD : (h + 1) * HEAD, h * rows : (h + 1) * rows] for h in range(heads)], axis=0
    )


def forward_kernel(heads, first_ref, q_ref, k_ref, v_ref, start_ref, scale_ref,
                   o_ref, u_ref, lse_ref, m_s, l_s, acc_s):
    i = pl.program_id(0)
    rows = q_ref.shape[0]
    wide = heads * rows
    queries = stack_heads(q_ref[...] * jnp.bfloat16(HEAD ** -0.5), heads)
    starts = jnp.concatenate([start_ref[0]] * heads, axis=1)
    m_s[...] = jnp.full_like(m_s, NEG)
    l_s[...] = jnp.zeros_like(l_s)
    acc_s[...] = jnp.zeros_like(acc_s)

    def step(j, masked, diagonal):
        at = pl.ds(pl.multiple_of(j * rows, rows), rows)
        scores = nt(k_ref[at, :], queries)
        if masked or diagonal:
            key = j * rows + lax.broadcasted_iota(jnp.int32, scores.shape, 0)
            allowed = key >= starts
            if diagonal:
                lane = lax.broadcasted_iota(jnp.int32, scores.shape, 1) & (rows - 1)
                allowed = allowed & (key <= i * rows + lane)
            scores = jnp.where(allowed, scores, NEG)
        before = m_s[...]
        highest = jnp.maximum(before, jnp.max(scores, axis=0, keepdims=True))
        weights = jnp.exp(scores - highest)
        fade = jnp.exp(before - highest)
        if masked:
            weights = jnp.where(scores > 0.5 * NEG, weights, 0.0)
        m_s[...] = highest
        l_s[...] = l_s[...] * fade + jnp.sum(weights, axis=0, keepdims=True)
        acc_s[...] = acc_s[...] * fade + tn(v_ref[at, :], weights.astype(jnp.bfloat16))

    step(i, False, True)
    low = first_ref[i, 0, 0] // rows
    full = jnp.minimum((first_ref[i, 0, rows - 1] + rows - 1) // rows, i)

    def plain(j, carry):
        step(j, False, False)
        return carry

    def edge(j, carry):
        step(j, True, False)
        return carry

    lax.fori_loop(full, i, plain, 0)
    lax.fori_loop(low, full, edge, 0)
    total = l_s[...]
    out = unstack_heads(acc_s[...] / total, heads).T
    o_ref[...] = out
    u_ref[...] = (out * scale_ref[...]).astype(jnp.bfloat16)
    lse_ref[0] = m_s[...] + jnp.log(total)


def attend_forward(queries, keys, values, starts, scale_wide):
    length, width = queries.shape
    heads = width // HEAD
    blocks = length // BQ
    whole = pl.BlockSpec((length, width), lambda i, *_: (0, 0))
    mine = pl.BlockSpec((BQ, width), lambda i, *_: (i, 0))
    return pl.pallas_call(
        functools.partial(forward_kernel, heads),
        out_shape=(
            jax.ShapeDtypeStruct((length, width), jnp.float32),
            jax.ShapeDtypeStruct((length, width), jnp.bfloat16),
            jax.ShapeDtypeStruct((blocks, 1, heads * BQ), jnp.float32),
        ),
        grid_spec=pltpu.PrefetchScalarGridSpec(
            num_scalar_prefetch=1,
            grid=(blocks,),
            in_specs=[
                mine,
                whole,
                whole,
                pl.BlockSpec((1, 1, BQ), lambda i, *_: (i, 0, 0)),
                pl.BlockSpec((1, width), lambda i, *_: (0, 0)),
            ],
            out_specs=(mine, mine, pl.BlockSpec((1, 1, heads * BQ), lambda i, *_: (i, 0, 0))),
            scratch_shapes=[
                pltpu.VMEM((1, heads * BQ), jnp.float32),
                pltpu.VMEM((1, heads * BQ), jnp.float32),
                pltpu.VMEM((width, heads * BQ), jnp.float32),
            ],
        ),
        cost_estimate=pl.CostEstimate(
            flops=length * length * width, bytes_accessed=16 * length * width, transcendentals=0
        ),
        name="attend_forward",
    )(starts, queries, keys, values, starts, scale_wide)


def backward_kernel(heads, first_ref, q_ref, k_ref, v_ref, o_ref, du_ref, start_ref, scale_ref, lse_ref,
                    dq_ref, dk_ref, dv_ref, ds_ref, qs_s, dos_s, delta_s, dqt_s, dk_s, dv_s):
    j = pl.program_id(0)
    rows = k_ref.shape[0]
    blocks = qs_s.shape[0]
    wide = heads * rows

    @pl.when(j == 0)
    def prepare():
        def one(i, total):
            at = pl.ds(pl.multiple_of(i * rows, rows), rows)
            qs_s[i] = stack_heads(q_ref[at, :] * jnp.bfloat16(HEAD ** -0.5), heads)
            grad = du_ref[at, :].astype(jnp.float32)
            out = o_ref[at, :]
            low = (grad * scale_ref[...]).astype(jnp.bfloat16)
            dos_s[i] = stack_heads(low, heads)
            inner = (low.astype(jnp.float32) * out).T
            delta_s[i] = jnp.concatenate(
                [jnp.sum(inner[h * HEAD : (h + 1) * HEAD], axis=0, keepdims=True) for h in range(heads)],
                axis=1,
            )
            return total + jnp.sum(grad * out, axis=0, keepdims=True)

        ds_ref[...] = lax.fori_loop(0, blocks, one, jnp.zeros(ds_ref.shape, jnp.float32))
        dqt_s[...] = jnp.zeros_like(dqt_s)

    keys, values = k_ref[...], v_ref[...]
    dk_s[...] = jnp.zeros_like(dk_s)
    dv_s[...] = jnp.zeros_like(dv_s)

    def step(i, masked, diagonal):
        queries, grads = qs_s[i], dos_s[i]
        scores = nt(keys, queries)
        if masked or diagonal:
            key = j * rows + lax.broadcasted_iota(jnp.int32, scores.shape, 0)
            starts = jnp.concatenate([start_ref[i]] * heads, axis=1)
            allowed = key >= starts
            if diagonal:
                lane = lax.broadcasted_iota(jnp.int32, scores.shape, 1) & (rows - 1)
                allowed = allowed & (key <= i * rows + lane)
            scores = jnp.where(allowed, scores, NEG)
        weights = jnp.exp(scores - lse_ref[i])
        pulls = nt(values, grads)
        low = (weights * (pulls - delta_s[i])).astype(jnp.bfloat16)
        dv_s[...] += jnp.dot(weights.astype(jnp.bfloat16), grads, preferred_element_type=jnp.float32)
        dk_s[...] += jnp.dot(low, queries, preferred_element_type=jnp.float32)
        dqt_s[i] += tn(keys, low)

    step(j, False, True)
    high, full = jnp.int32(0), jnp.int32(0)
    for i in range(blocks):
        high += (first_ref[i, 0, 0] // rows <= j).astype(jnp.int32)
        full += ((first_ref[i, 0, rows - 1] + rows - 1) // rows <= j).astype(jnp.int32)
    full = jnp.maximum(full, j + 1)

    def plain(i, carry):
        step(i, False, False)
        return carry

    def edge(i, carry):
        step(i, True, False)
        return carry

    lax.fori_loop(j + 1, full, plain, 0)
    lax.fori_loop(full, high, edge, 0)
    dk_ref[...] = dk_s[...].astype(jnp.bfloat16)
    dv_ref[...] = dv_s[...].astype(jnp.bfloat16)

    @pl.when(j == blocks - 1)
    def finish():
        def one(i, carry):
            at = pl.ds(pl.multiple_of(i * rows, rows), rows)
            dq_ref[at, :] = (unstack_heads(dqt_s[i], heads).T * HEAD ** -0.5).astype(jnp.bfloat16)
            return carry

        lax.fori_loop(0, blocks, one, 0)


def attend_backward(queries, keys, values, outs, grads, starts, scale_wide, logsum):
    length, width = queries.shape
    heads = width // HEAD
    blocks = length // BQ
    whole = pl.BlockSpec((length, width), lambda i, *_: (0, 0))
    mine = pl.BlockSpec((BQ, width), lambda i, *_: (i, 0))
    return pl.pallas_call(
        functools.partial(backward_kernel, heads),
        out_shape=(jax.ShapeDtypeStruct((length, width), jnp.bfloat16),) * 3
        + (jax.ShapeDtypeStruct((1, width), jnp.float32),),
        grid_spec=pltpu.PrefetchScalarGridSpec(
            num_scalar_prefetch=1,
            grid=(blocks,),
            in_specs=[
                whole,
                mine,
                mine,
                whole,
                whole,
                pl.BlockSpec((blocks, 1, BQ), lambda i, *_: (0, 0, 0)),
                pl.BlockSpec((1, width), lambda i, *_: (0, 0)),
                pl.BlockSpec((blocks, 1, heads * BQ), lambda i, *_: (0, 0, 0)),
            ],
            out_specs=(whole, mine, mine, pl.BlockSpec((1, width), lambda i, *_: (0, 0))),
            scratch_shapes=[
                pltpu.VMEM((blocks, heads * BQ, width), jnp.bfloat16),
                pltpu.VMEM((blocks, heads * BQ, width), jnp.bfloat16),
                pltpu.VMEM((blocks, 1, heads * BQ), jnp.float32),
                pltpu.VMEM((blocks, width, heads * BQ), jnp.float32),
                pltpu.VMEM((BQ, width), jnp.float32),
                pltpu.VMEM((BQ, width), jnp.float32),
            ],
        ),
        cost_estimate=pl.CostEstimate(
            flops=3 * length * length * width, bytes_accessed=32 * length * width, transcendentals=0
        ),
        name="attend_backward",
    )(starts, queries, keys, values, outs, grads, starts, scale_wide, logsum)


def document_starts(doc_ids):
    length = doc_ids.shape[0]
    names = jnp.arange(8, dtype=jnp.int32)
    counts = jnp.sum(doc_ids[None, :] < names[:, None], axis=1, dtype=jnp.int32)
    starts = jnp.sum(
        jnp.where(doc_ids[:, None] == names[None, :], counts[None, :], 0), axis=1, dtype=jnp.int32
    )
    return starts.reshape(length // BQ, 1, BQ)


def layer_norm(values, gains):
    center = values - jnp.mean(values, axis=-1, keepdims=True)
    spread = jnp.mean(center * center, axis=-1, keepdims=True)
    return center * lax.rsqrt(spread + 1e-05) * gains


def gelu_norm(hidden, gains):
    return layer_norm(jax.nn.gelu(hidden, approximate=True), gains)


def transposed_times(left, right):
    return lax.dot_general(
        left, right, (((0,), (0,)), ((), ())), preferred_element_type=jnp.float32
    )


def times_transposed(left, right):
    return lax.dot_general(
        left, right, (((1,), (1,)), ((), ())), preferred_element_type=jnp.float32
    )


def scatter_rows(partial, sizes):
    current = partial
    for axis, size in zip(("dp", "seq"), sizes):
        place = lax.axis_index(axis)
        bits = size.bit_length() - 1
        pieces = current.reshape((2,) * bits + (-1, current.shape[-1]))
        for bit in range(bits):
            at = bits - 1 - bit
            mine = (place >> bit) & 1
            give = lax.dynamic_index_in_dim(pieces, 1 - mine, at, keepdims=False)
            keep = lax.dynamic_index_in_dim(pieces, mine, at, keepdims=False)
            got = lax.ppermute(give, axis, [(i, i ^ (1 << bit)) for i in range(size)])
            pieces = (keep.astype(jnp.float32) + got.astype(jnp.float32)).astype(jnp.bfloat16)
        current = pieces
    return current.astype(jnp.float32)


MESH = pl.DeviceIdType.MESH
LOW = jnp.bfloat16
BLOCK = 1024
VMEM_BYTES = 66_000_000


class Place:
    def __init__(self):
        self.dp, self.seq = lax.axis_index("dp"), lax.axis_index("seq")
        self.core, self.y = self.dp % 2, self.dp // 2
        self.x, self.z = self.seq % 2, self.seq // 2
        self.z0, self.z1 = self.z % 2, self.z // 2

    def core_partner(self):
        return (self.dp + 1 - 2 * self.core, self.seq)

    def y_partner(self):
        return (self.dp + 2 - 4 * self.y, self.seq)

    def x_partner(self):
        return (self.dp, self.seq + 1 - 2 * self.x)

    def near_partner(self):
        return (self.dp, self.seq + 2 - 4 * self.z0)

    def far_partner(self):
        return (self.dp, self.seq + 4 - 8 * self.z1)


def meet(devices):
    barrier = pltpu.get_barrier_semaphore()
    for device in devices:
        pl.semaphore_signal(barrier, inc=1, device_id=device, device_id_type=MESH)
    pl.semaphore_wait(barrier, len(devices))


def remote(source, target, send, receive, device):
    return pltpu.make_async_remote_copy(
        src_ref=source,
        dst_ref=target,
        send_sem=send,
        recv_sem=receive,
        device_id=device,
        device_id_type=MESH,
    )


def lanes_of(z, x, width):
    return pl.ds(pl.multiple_of((z * 2 + x) * width, 128), width)


def rows_of(z, x, local):
    return pl.ds(pl.multiple_of((z * 2 + x) * local, 128), local)


class ToHeads:
    def __init__(self, place, part, target, relay, sems, keep_sem):
        self.place, self.target, self.relay, self.sems = place, target, relay, sems
        x_send, x_recv, z_send, z_recv = sems
        local, width = relay.shape[-2:]
        rows = rows_of(place.z, place.x, local)
        self.moves, self.sends = [], []
        for k in (2, 1, 3, 0):
            source = part.at[:, lanes_of((place.z + k) % 4, 1 - place.x, width)]
            landing = target.at[rows, :] if k == 0 else relay.at[k - 1]
            move = remote(source, landing, x_send.at[k], x_recv.at[k], place.x_partner())
            move.start()
            (self.moves if k == 0 else self.sends).append(move)
        for k in (2, 1, 3):
            z = (place.z + k) % 4
            source = part.at[:, lanes_of(z, place.x, width)]
            move = remote(
                source, target.at[rows, :], z_send.at[k - 1], z_recv.at[k - 1], (place.dp, z * 2 + place.x)
            )
            move.start()
            self.moves.append(move)
        source = part.at[:, lanes_of(place.z, place.x, width)]
        move = pltpu.make_async_copy(source, target.at[rows, :], keep_sem)
        move.start()
        self.moves.append(move)

    def pass_on(self):
        place, local = self.place, self.relay.shape[-2]
        x_send, x_recv, z_send, z_recv = self.sems
        rows = rows_of(place.z, 1 - place.x, local)
        for k in (2, 1, 3):
            here = self.relay.at[k - 1]
            remote(here, here, x_send.at[k], x_recv.at[k], place.x_partner()).wait_recv()
            device = (place.dp, (place.z + k) % 4 * 2 + place.x)
            move = remote(here, self.target.at[rows, :], z_send.at[k + 2], z_recv.at[k + 2], device)
            move.start()
            self.moves.append(move)

    def finish(self):
        for move in self.moves:
            move.wait()
        for move in self.sends:
            move.wait_send()


class ToTokens:
    def __init__(self, place, source, target, relay, sems, keep_sem):
        self.place, self.target, self.relay, self.sems = place, target, relay, sems
        x_send, x_recv, z_send, z_recv = sems
        local, width = relay.shape[-2:]
        self.moves, self.sends = [], []
        lanes = lanes_of(place.z, place.x, width)
        for x, first in ((1 - place.x, 0), (place.x, 3)):
            for k in (2, 1, 3):
                z, index = (place.z + k) % 4, first + k - 1
                landing = relay.at[k - 1] if first == 0 else target.at[:, lanes]
                move = remote(
                    source.at[rows_of(z, x, local), :],
                    landing,
                    z_send.at[index],
                    z_recv.at[index],
                    (place.dp, z * 2 + place.x),
                )
                move.start()
                (self.sends if first == 0 else self.moves).append(move)
        move = remote(
            source.at[rows_of(place.z, 1 - place.x, local), :],
            target.at[:, lanes],
            x_send.at[0],
            x_recv.at[0],
            place.x_partner(),
        )
        move.start()
        self.moves.append(move)
        move = pltpu.make_async_copy(
            source.at[rows_of(place.z, place.x, local), :], target.at[:, lanes], keep_sem
        )
        move.start()
        self.moves.append(move)

    def pass_on(self):
        place, width = self.place, self.relay.shape[-1]
        x_send, x_recv, z_send, z_recv = self.sems
        for k in (2, 1, 3):
            here = self.relay.at[k - 1]
            remote(here, here, z_send.at[k - 1], z_recv.at[k - 1], place.near_partner()).wait_recv()
            lanes = lanes_of((place.z + 4 - k) % 4, place.x, width)
            move = remote(here, self.target.at[:, lanes], x_send.at[k], x_recv.at[k], place.x_partner())
            move.start()
            self.moves.append(move)

    def finish(self):
        for move in self.moves:
            move.wait()
        for move in self.sends:
            move.wait_send()


def exchange_sems(count):
    dma = pltpu.SemaphoreType.DMA
    return [dma((count, 4)), dma((count, 4)), dma((count, 6)), dma((count, 6))]


def share(place, index, ours, theirs, target, local, here_sem, core_send, core_recv):
    here = pltpu.make_async_copy(ours, target.at[pl.ds(0, local), :], here_sem.at[index])
    there = remote(
        theirs, target.at[pl.ds(local, local), :], core_send.at[index], core_recv.at[index], place.core_partner()
    )
    here.start()
    there.start()
    return [here, there]


def share_left(place, index, source, target, local, *sems):
    half = source.shape[1] // 2
    columns = half // 2
    out = []
    for y in range(2):
        ours, theirs = (
            source.at[pl.ds(0, local), pl.ds(pl.multiple_of(y * half + core * columns, 128), columns)]
            for core in (place.core, 1 - place.core)
        )
        out += share(place, index + y, ours, theirs, target.at[:, pl.ds(y * columns, columns)], local, *sems)
    return out


def wait_all(copies):
    for copy in copies:
        copy.wait()


def norm_parts(values):
    center = values - jnp.mean(values, axis=-1, keepdims=True)
    inverse = lax.rsqrt(jnp.mean(center * center, axis=-1, keepdims=True) + 1e-05)
    return center * inverse, inverse


def norm_pull(grad, unit, inverse, gain):
    scaled = grad * gain
    return inverse * (
        scaled
        - jnp.mean(scaled, axis=-1, keepdims=True)
        - unit * jnp.mean(scaled * unit, axis=-1, keepdims=True)
    )


class Scatter:
    def __init__(self, place, refs, sems, base, left, right, write):
        self.place, self.base, self.left, self.right, self.write = place, base, left, right, write
        self.whole, self.first, self.second, self.near, self.far = refs
        self.send, self.receive = sems
        self.rows, self.columns = self.whole.shape[-2:]

    def axes(self, p):
        place = self.place
        if p % 2 == 0:
            return place.y, place.x, place.y_partner(), place.x_partner()
        return place.x, place.y, place.x_partner(), place.y_partner()

    def copy(self, p, stage):
        place = self.place
        mine, other, partner, second = self.axes(p)
        if stage == 0:
            source, target, device = self.whole.at[p, 1 - mine], self.first.at[p], partner
        elif stage == 1:
            source, target, device = self.first.at[p, :, :, 1 - other], self.second.at[p], second
        elif stage == 2:
            source, target, device = self.second.at[p, :, 1 - place.z0], self.near.at[p], place.near_partner()
        else:
            source, target, device = self.near.at[p, 1 - place.z1], self.far.at[p], place.far_partner()
        index = self.base + p
        return remote(source, target, self.send.at[stage, index], self.receive.at[stage, index], device)

    def compute(self, p):
        left, right = self.left(p), self.right(p)
        rows = self.rows

        def one(y, carry):
            for half in range(2):
                span = 4 * rows
                at = pl.ds(pl.multiple_of(y * 8 * rows + half * span, 128), span)
                block = tn(left[:, at], right[...]).astype(LOW)
                for k in range(4):
                    x = k % 2
                    part = block[k * rows : (k + 1) * rows]
                    if p % 2 == 0:
                        self.whole[p, y, half, k // 2, x] = part
                    else:
                        self.whole[p, x, half, k // 2, y] = part
            return carry

        lax.fori_loop(0, 2, one, 0)
        self.copy(p, 0).start()

    def advance(self, p, stage):
        place = self.place
        mine, other, _, _ = self.axes(p)
        wide = jnp.float32
        self.copy(p, stage - 1).wait_recv()
        if stage == 1:

            def add(k, carry):
                a, b, s = k // 4, k // 2 % 2, k % 2
                total = self.first[p, a, b, s].astype(wide) + self.whole[p, mine, a, b, s].astype(wide)
                self.first[p, a, b, s] = total.astype(LOW)
                return carry

            lax.fori_loop(0, 8, add, 0)
        elif stage == 2:

            def add(z, carry):
                a, b = z // 2, z % 2
                total = self.second[p, a, b].astype(wide) + self.first[p, a, b, other].astype(wide)
                self.second[p, a, b] = total.astype(LOW)
                return carry

            lax.fori_loop(0, 4, add, 0)
        elif stage == 3:

            def add(a, carry):
                total = self.near[p, a].astype(wide) + self.second[p, a, place.z0].astype(wide)
                self.near[p, a] = total.astype(LOW)
                return carry

            lax.fori_loop(0, 2, add, 0)
        else:
            self.write(p, self.near[p, place.z1].astype(wide) + self.far[p].astype(wide))
            return
        self.copy(p, stage).start()

    def settle(self, p):
        for stage in range(4):
            self.copy(p, stage).wait_send()


def scatter_scratch(pieces, rows, columns):
    return [
        pltpu.VMEM((pieces, 2, 2, 2, 2, rows, columns), LOW),
        pltpu.VMEM((pieces, 2, 2, 2, rows, columns), LOW),
        pltpu.VMEM((pieces, 2, 2, rows, columns), LOW),
        pltpu.VMEM((pieces, 2, rows, columns), LOW),
        pltpu.VMEM((pieces, rows, columns), LOW),
    ]


class Gather:
    def __init__(self, place, sems):
        self.place = place
        self.send, self.receive = sems

    def copies(self, index, own, full, rows, shared):
        place = self.place
        across = place.dp + 2 - 4 * place.y
        half = rows // 2

        def move(kind, source, target, device):
            return remote(source, target, self.send.at[kind, index], self.receive.at[kind, index], device)

        out = [move(0, own, full(place.dp, 0, rows), place.core_partner())]
        if shared:
            first = place.x * half
            out.append(
                move(1, own.at[pl.ds(pl.multiple_of(first, half), half), :],
                     full(place.dp, first, half), place.y_partner())
            )
            landed = full(across, first, half)
            out.append(move(2, landed, landed, place.x_partner()))
        else:
            out.append(move(1, own, full(place.dp, 0, rows), place.y_partner()))
            out.append(None)
        landed = full(across, 0, rows)
        out.append(move(3, landed, landed, place.core_partner()))
        return out


def front_kernel(
    tokens, gain, ids, w_triple, w_out, w_up,
    o_v, o_k, o_q, o_normed, o_starts, o_triple, o_out, o_up,
    triple_s, part_s, ids_s, bounce, relay, send, receive, x_send, x_recv, z_send, z_recv, ids_send, ids_recv, local_sem,
):
    place = Place()
    exchange_sem = (x_send, x_recv, z_send, z_recv)
    local, width = tokens.shape
    heads_width = o_v.shape[1]
    meet([(place.dp, (place.seq + k) % 8) for k in range(1, 8)] + [place.core_partner(), place.y_partner()])
    gather = Gather(place, (send, receive))

    def columns(weight, rows, column):
        at = pl.ds(column * width, width)

        def full(d, first, count):
            return weight.at[pl.ds(pl.multiple_of(d * rows + first, 128), count), at]

        return full

    plans = []
    for n, t in enumerate((2, 1, 0)):
        plans.append((w_triple.at[:, pl.ds(t * width, width)], columns(triple_s, 256, t)))
    plans.append((w_out, columns(o_out, 256, 0)))
    for k in range(w_up.shape[1] // width):
        plans.append((w_up.at[:, pl.ds(k * width, width)], columns(o_up, 256, k)))
    alone = (3,)
    chunks = [
        gather.copies(n, own, full, 256, n not in alone) for n, (own, full) in enumerate(plans)
    ]
    mine = []
    for n, (own, full) in enumerate(plans):
        chunks[n][1].start()
        chunks[n][0].start()
        target = full(place.dp, 0, 256) if n < 3 else bounce.at[n - 3]
        copy = pltpu.make_async_copy(own, target, local_sem.at[n])
        copy.start()
        mine.append(copy)
        if n == 0:
            news = []
            for k in range(1, 8):
                peer = (place.dp, (place.seq + k) % 8)
                move = remote(ids, ids_s.at[place.seq], ids_send.at[k - 1], ids_recv.at[k - 1], peer)
                move.start()
                news.append(move)
            ids_s[pl.ds(place.seq, 1)] = ids[...].reshape(1, 1, local)

    def norm_rows(n, carry):
        rows = pl.ds(pl.multiple_of(n * 128, 128), 128)
        values = tokens[rows, :].astype(jnp.float32)
        o_normed[rows, :] = (norm_parts(values)[0] * gain[...]).astype(LOW)
        return carry

    lax.fori_loop(0, local // 128, norm_rows, 0)
    moves = []
    exchanges = []

    def project(n):
        t, target = (2, 1, 0)[n], (o_v, o_k, o_q)[n]

        def one(c, carry):
            at = pl.ds(pl.multiple_of(c * 256, 256), 256)
            from_at = pl.ds(pl.multiple_of(t * width + c * 256, 256), 256)
            part_s[n, :, at] = jnp.dot(
                o_normed[...], triple_s[:, from_at], preferred_element_type=jnp.float32
            ).astype(LOW)
            return carry

        lax.fori_loop(0, width // 256, one, 0)
        exchange = ToHeads(
            place, part_s.at[n], target, relay.at[n], [sem.at[n] for sem in exchange_sem], local_sem.at[12 + n]
        )
        exchanges.append(exchange)
        save = pltpu.make_async_copy(
            triple_s.at[:, pl.ds(t * width, width)], o_triple.at[:, pl.ds(t * width, width)], local_sem.at[15 + n]
        )
        save.start()
        moves.append(save)

    def forward(n):
        if chunks[n][2] is not None:
            chunks[n][1].wait_recv()
            chunks[n][2].start()

    def across(n):
        (chunks[n][1] if chunks[n][2] is None else chunks[n][2]).wait_recv()
        chunks[n][3].start()

    def finish(n):
        chunks[n][0].wait_recv()
        chunks[n][3].wait_recv()
        if n < 3:
            mine[n].wait()
            project(n)

    def put_back(n):
        mine[n].wait()
        copy = pltpu.make_async_copy(bounce.at[n - 3], plans[n][1](place.dp, 0, 256), local_sem.at[n])
        copy.start()
        moves.append(copy)

    count = len(chunks)
    forward(0)
    for n in range(count):
        if n + 1 < count:
            forward(n + 1)
        across(n)
        if n < 3:
            finish(n)
        else:
            put_back(n)
        if 0 < n < 4:
            exchanges[n - 1].pass_on()
        if n == 4:
            for move in news:
                move.wait()
            every = ids_s[...]
            starts = jnp.zeros_like(every)
            for d in range(1, 8):
                before = jnp.sum((every < d).astype(jnp.int32), axis=2, keepdims=True)
                before = jnp.sum(before, axis=0, keepdims=True)
                starts = jnp.where(every == d, before, starts)
            for b in range(o_starts.shape[0]):
                for piece in range(BQ // 128):
                    at = b * BQ + piece * 128
                    o_starts[b, :, pl.ds(piece * 128, 128)] = starts[
                        at // local, :, at % local : at % local + 128
                    ]
    for n in range(3, count):
        finish(n)
    for move in moves:
        move.wait()
    for exchange in exchanges:
        exchange.finish()
    for chunk in chunks:
        for copy in chunk:
            if copy is not None:
                copy.wait_send()


def front(tokens, gain, ids, w_triple, w_out, w_up):
    local, width = tokens.shape
    heads_width = width // 8
    length = local * 8
    hidden = w_up.shape[1]
    any_spec = pl.BlockSpec(memory_space=pl.ANY)
    vmem = pl.BlockSpec(memory_space=pltpu.VMEM)
    dma = pltpu.SemaphoreType.DMA
    one = jax.ShapeDtypeStruct((length, heads_width), LOW)
    return pl.pallas_call(
        front_kernel,
        out_shape=(
            one, one, one,
            jax.ShapeDtypeStruct((local, width), LOW),
            jax.ShapeDtypeStruct((length // BQ, 1, BQ), jnp.int32),
            jax.ShapeDtypeStruct((width, 3 * width), LOW),
            jax.ShapeDtypeStruct((width, width), LOW),
            jax.ShapeDtypeStruct((width, hidden), LOW),
        ),
        in_specs=[vmem] * 3 + [any_spec] * 3,
        out_specs=(any_spec,) * 3 + (vmem,) * 2 + (any_spec,) * 3,
        scratch_shapes=[
            pltpu.VMEM((width, 3 * width), LOW),
            pltpu.VMEM((3, local, width), LOW),
            pltpu.VMEM((8, 1, local), jnp.int32),
            pltpu.VMEM((1 + hidden // width, 256, width), LOW),
            pltpu.VMEM((3, 3, local, heads_width), LOW),
            dma((4, 8)),
            dma((4, 8)),
            *exchange_sems(3),
            dma((7,)),
            dma((7,)),
            dma((20,)),
        ],
        compiler_params=pltpu.CompilerParams(
            collective_id=1, has_side_effects=True, vmem_limit_bytes=VMEM_BYTES
        ),
        name="front",
    )(tokens, gain.reshape(1, width), ids, w_triple, w_out, w_up)


def middle_kernel(
    u, tokens, cotangent, post_gain, second_gain, mid_gain, w_out, w_up, w_down,
    o_layer, o_middle, o_heads, o_merged, o_second, o_hidden, o_projected, o_gains, o_down,
    out_s, up_s, down_s, merged_s, second_s, unit_s, slope_s, act_s, hidden_s, projected_s, middle_s, far_s,
    inverse_s, inner_s, relay, grad_s,
    d_left, d_right, d_whole, d_first, d_second, d_near, d_far,
    local_sem, g_send, g_recv, core_send, core_recv, x_send, x_recv, z_send, z_recv, s_send, s_recv,
):
    place = Place()
    local, width = tokens.shape
    hidden = mid_gain.shape[1]
    wide = jnp.float32
    column_peers = [(place.dp, (place.z + k) % 4 * 2 + place.x) for k in range(1, 4)]
    meet(column_peers + [place.x_partner(), place.core_partner(), place.y_partner()])
    exchange_sem = (x_send, x_recv, z_send, z_recv)

    inbound = ToTokens(place, u, merged_s, relay.at[0], [sem.at[0] for sem in exchange_sem], local_sem.at[0])
    gather = Gather(place, (g_send, g_recv))
    alone = (0, 1)
    chunks, mine = [], []
    for k in range(4):

        def full(d, first, count, k=k):
            return down_s.at[pl.ds(pl.multiple_of(d * 1024 + k * 256 + first, 128), count), :]

        own = w_down.at[pl.ds(k * 256, 256), :]
        chunks.append(gather.copies(k, own, full, 256, k not in alone))
        chunks[k][1].start()
        chunks[k][0].start()
        mine.append(pltpu.make_async_copy(own, full(place.dp, 0, 256), local_sem.at[1 + k]))
        mine[k].start()
    loads = [
        pltpu.make_async_copy(w_out, out_s, local_sem.at[5]),
        pltpu.make_async_copy(w_up, up_s, local_sem.at[6]),
    ]
    for load in loads:
        load.start()
    sems = (local_sem, core_send, core_recv)
    right = share(place, 7, cotangent, cotangent, d_right, local, *sems)
    saves = []

    def save(source, target, index):
        copy = pltpu.make_async_copy(source, target, local_sem.at[index])
        copy.start()
        saves.append(copy)

    def across(k):
        (chunks[k][1] if chunks[k][2] is None else chunks[k][2]).wait_recv()
        chunks[k][3].start()

    def forward(k):
        chunks[k][1].wait_recv()
        chunks[k][2].start()

    gain = mid_gain[...]
    part_one = gain.astype(LOW)
    left_over = gain - part_one.astype(wide)
    part_two = left_over.astype(LOW)
    part_three = (left_over - part_two.astype(wide)).astype(LOW)
    row = lax.broadcasted_iota(jnp.int32, (16, hidden), 0)
    parts = jnp.where(row == 0, part_one.astype(wide), jnp.where(row == 1, part_two.astype(wide), part_three.astype(wide)))
    act_s[pl.ds(local, 16), :] = jnp.where(row < 3, parts, 0.0).astype(LOW)

    inbound.pass_on()
    across(0)
    forward(2)
    inbound.finish()
    wait_all(loads)
    save(merged_s, o_merged, 8)

    def blocks(count, body):
        def one(n, carry):
            body(n)
            return carry

        lax.fori_loop(0, count, one, 0)

    def span(n, size):
        return pl.ds(pl.multiple_of(n * size, size), size)

    def project(n):
        at = span(n, 256)
        far_s[:, at] = jnp.dot(merged_s[...], out_s[:, at], preferred_element_type=wide)

    blocks(width // 256, project)

    def norms(n):
        rows = span(n, 128)
        unit, inverse = norm_parts(far_s[rows, :])
        far_s[rows, :] = unit
        inverse_s[rows, :] = jnp.broadcast_to(inverse, (128, 128))
        middle = tokens[rows, :].astype(wide) + unit * post_gain[...]
        middle_s[rows, :] = middle
        second_s[rows, :] = (norm_parts(middle)[0] * second_gain[...]).astype(LOW)

    blocks(local // 128, norms)
    save(second_s, o_second, 9)

    def grow(n):
        at = span(n, 256)
        z = jnp.dot(second_s[...], up_s[:, at], preferred_element_type=wide)
        root = 0.7978845608028654
        square = z * z
        bent = jnp.tanh(root * z * (1.0 + 0.044715 * square))
        half = 0.5 * (1.0 + bent)
        unit_s[:, at] = z * half
        slope_s[:, at] = half + 0.5 * root * z * (1.0 - bent * bent) * (1.0 + 3.0 * 0.044715 * square)

    half_way = hidden // 512

    def grow_from(first):
        def body(n):
            grow(n + first)

        return body

    blocks(half_way, grow_from(0))
    across(1)
    across(2)
    forward(3)
    blocks(half_way, grow_from(half_way))

    def hidden_norm(n):
        rows = span(n, 32)
        unit, inverse = norm_parts(unit_s[rows, :])
        unit_s[rows, :] = unit
        inner_s[rows, :] = jnp.broadcast_to(inverse, (32, 128))
        act_s[rows, :] = (unit * gain).astype(LOW)

    blocks(local // 32, hidden_norm)
    left = share_left(place, 10, act_s, d_left, local, *sems)
    across(3)
    for k in range(4):
        chunks[k][0].wait_recv()
        chunks[k][3].wait_recv()
        mine[k].wait()

    def shrink(n):
        at = span(n, 256)
        total = jnp.dot(act_s[...], down_s[:, at], preferred_element_type=wide)
        low = cotangent[:, at].astype(wide)
        value = total[:local]
        o_layer[:, at] = (middle_s[:, at] + value).astype(LOW)
        weight = jnp.sum(total[local:], axis=0, keepdims=True)
        first = jnp.sum(low * weight, axis=1, keepdims=True) * (1.0 / hidden)
        second = jnp.sum(low * value, axis=1, keepdims=True) * (1.0 / hidden)
        grad_s[0] = grad_s[0] + jnp.broadcast_to(first, (local, 128))
        grad_s[1] = grad_s[1] + jnp.broadcast_to(second, (local, 128))

    grad_s[...] = jnp.zeros_like(grad_s)
    blocks(width // 256, shrink)

    def write_down(p, value):
        o_down[:, pl.ds(p * 256, 256)] = value

    down = Scatter(
        place, (d_whole, d_first, d_second, d_near, d_far), (s_send, s_recv), 0,
        lambda p: d_left, lambda p: d_right.at[:, pl.ds(p * 256, 256)], write_down,
    )
    wait_all(right)
    wait_all(left)
    for p in range(4):
        down.compute(p)

    def pull_hidden(n):
        at = span(n, 256)
        grad = nt(cotangent[...], down_s[at, :])
        unit = unit_s[:, at]
        o_gains[3:4, at] = jnp.sum(grad * unit, axis=0, keepdims=True)
        pulled = grad * mid_gain[:, at] - grad_s[0][:, 0:1] - unit * grad_s[1][:, 0:1]
        hidden_s[:, at] = (inner_s[:, 0:1] * pulled * slope_s[:, at]).astype(LOW)

    blocks(hidden // 256, pull_hidden)
    save(hidden_s, o_hidden, 15)
    for p in range(2):
        down.advance(p, 1)

    def pull_second(n):
        at = span(n, 256)
        o_middle[:, at] = nt(hidden_s[...], up_s[at, :])

    blocks(width // 256, pull_second)

    def pull_norms(n, totals):
        rows = span(n, 128)
        grad = o_middle[rows, :]
        unit, inverse = norm_parts(middle_s[rows, :])
        grad_middle = cotangent[rows, :].astype(wide) + norm_pull(grad, unit, inverse, second_gain[...])
        o_middle[rows, :] = grad_middle
        outer = far_s[rows, :]
        projected_s[rows, :] = norm_pull(grad_middle, outer, inverse_s[rows, 0:1], post_gain[...]).astype(LOW)
        return (
            totals[0] + jnp.sum(grad_middle * outer, axis=0, keepdims=True),
            totals[1] + jnp.sum(grad * unit, axis=0, keepdims=True),
        )

    nothing = jnp.zeros((1, width), wide)
    post, second = lax.fori_loop(0, local // 128, pull_norms, (nothing, nothing))
    o_gains[1:2, 0:width] = post
    o_gains[2:3, 0:width] = second
    save(projected_s, o_projected, 16)

    def pull_merged(n):
        at = span(n, 256)
        merged_s[:, at] = nt(projected_s[...], out_s[at, :]).astype(LOW)

    saves[0].wait()
    blocks(width // 256, pull_merged)
    outbound = ToHeads(
        place, merged_s, o_heads, relay.at[1], [sem.at[1] for sem in exchange_sem], local_sem.at[17]
    )
    down.advance(2, 1)
    down.advance(0, 2)
    down.advance(1, 2)
    outbound.pass_on()
    down.advance(3, 1)
    down.advance(2, 2)
    down.advance(0, 3)
    down.advance(1, 3)
    down.advance(3, 2)
    for p in range(4):
        if p > 1:
            down.advance(p, 3)
    for p in range(4):
        down.advance(p, 4)
    outbound.finish()
    wait_all(saves[1:])
    for p in range(4):
        down.settle(p)
    for chunk in chunks:
        for copy in chunk:
            if copy is not None:
                copy.wait_send()


def middle(u, tokens, cotangent, post_gain, second_gain, mid_gain, w_out, w_up, w_down):
    local, width = tokens.shape
    hidden = w_up.shape[1]
    any_spec = pl.BlockSpec(memory_space=pl.ANY)
    vmem = pl.BlockSpec(memory_space=pltpu.VMEM)
    dma = pltpu.SemaphoreType.DMA
    wide = jnp.float32
    act = jax.ShapeDtypeStruct((local, width), LOW)
    return pl.pallas_call(
        middle_kernel,
        out_shape=(
            act,
            jax.ShapeDtypeStruct((local, width), wide),
            jax.ShapeDtypeStruct((local * 8, width // 8), LOW),
            act,
            act,
            jax.ShapeDtypeStruct((local, hidden), LOW),
            act,
            jax.ShapeDtypeStruct((8, hidden), wide),
            jax.ShapeDtypeStruct((hidden // 32, width), wide),
        ),
        in_specs=[any_spec] + [vmem] * 5 + [any_spec] * 3,
        out_specs=(vmem,) * 2 + (any_spec,) * 5 + (vmem,) * 2,
        scratch_shapes=[
            pltpu.VMEM((width, width), LOW),
            pltpu.VMEM((width, hidden), LOW),
            pltpu.VMEM((hidden, width), LOW),
            pltpu.VMEM((local, width), LOW),
            pltpu.VMEM((local, width), LOW),
            pltpu.VMEM((local, hidden), wide),
            pltpu.VMEM((local, hidden), wide),
            pltpu.VMEM((local + 16, hidden), LOW),
            pltpu.VMEM((local, hidden), LOW),
            pltpu.VMEM((local, width), LOW),
            pltpu.VMEM((local, width), wide),
            pltpu.VMEM((local, width), wide),
            pltpu.VMEM((local, 128), wide),
            pltpu.VMEM((local, 128), wide),
            pltpu.VMEM((2, 3, local, width // 8), LOW),
            pltpu.VMEM((2, local, 128), wide),
            pltpu.VMEM((2 * local, hidden // 2), LOW),
            pltpu.VMEM((2 * local, width), LOW),
            *scatter_scratch(4, 128, 256),
            dma((20,)),
            dma((4, 4)),
            dma((4, 4)),
            dma((20,)),
            dma((20,)),
            *exchange_sems(2),
            dma((4, 4)),
            dma((4, 4)),
        ],
        compiler_params=pltpu.CompilerParams(
            collective_id=2, has_side_effects=True, vmem_limit_bytes=VMEM_BYTES
        ),
        name="middle",
    )(
        u, tokens, cotangent, post_gain.reshape(1, width), second_gain.reshape(1, width),
        mid_gain.reshape(1, hidden), w_out, w_up, w_down,
    )


def tail_kernel(
    dq, dk, dv, tokens, gain, middle, triple, act_up, act_out, act_in, g_up, g_out, gains, scales,
    o_tokens, o_triple, o_out, o_up, o_gains,
    e_left, e_right, e_whole, e_first, e_second, e_near, e_far,
    grad_s, gain_s, gain_r, relay,
    local_sem, core_send, core_recv, x_send, x_recv, z_send, z_recv, s_send, s_recv, gain_send, gain_recv,
):
    place = Place()
    partner = place.core_partner()
    column_peers = [(place.dp, (place.z + k) % 4 * 2 + place.x) for k in range(1, 4)]
    local, width = tokens.shape
    heads_width = dq.shape[1]
    meet(column_peers + [place.x_partner(), partner, place.y_partner()])

    def start_exchange(t):
        return ToTokens(
            place, (dv, dk, dq)[t], e_right.at[7 - t, pl.ds(0, local), :], relay.at[t],
            [sem.at[t] for sem in (x_send, x_recv, z_send, z_recv)], local_sem.at[13 + t],
        )

    exchanges = [start_exchange(0), start_exchange(1)]

    sems = (local_sem, core_send, core_recv)
    ready = {"up": share_left(place, 0, act_up, e_left.at[0], local, *sems)}
    for k in range(4):
        part = g_up.at[:, pl.ds(k * BLOCK, BLOCK)]
        ready["up"] += share(place, 2 + k, part, part, e_right.at[k], local, *sems)
    ready["out"] = share_left(place, 6, act_out, e_left.at[1], local, *sems)
    ready["out"] += share(place, 8, g_out, g_out, e_right.at[4], local, *sems)
    ready["in"] = share_left(place, 9, act_in, e_left.at[2], local, *sems)

    def write_rest(p, value):
        if p < 4:
            o_up[:, pl.ds(p * BLOCK, BLOCK)] = value
        elif p == 4:
            o_out[...] = value
        else:
            o_triple[:, pl.ds((p - 5) * BLOCK, BLOCK)] = value

    rest = Scatter(
        place, (e_whole, e_first, e_second, e_near, e_far), (s_send, s_recv), 0,
        lambda p: e_left.at[0 if p < 4 else 1 if p == 4 else 2], lambda p: e_right.at[p], write_rest,
    )
    order = [(rest, k) for k in (0, 1, 2, 3, 4, 7, 6, 5)]
    gain_s[...] = gains[...]
    gain_s[7:8, 0:128] = scales[...]
    marks = {"compute": 0, 1: 0, 2: 0, 3: 0, 4: 0}

    def advance(stage, upto):
        while marks[stage] < min(upto, len(order)):
            engine, p = order[marks[stage]]
            engine.advance(p, stage) if stage != "compute" else engine.compute(p)
            marks[stage] += 1

    wait_all(ready["up"])
    advance("compute", 2)
    advance(1, 1)
    exchanges[0].pass_on()
    advance("compute", 3)
    advance(1, 2)
    advance(2, 1)
    exchanges.append(start_exchange(2))
    wait_all(ready["out"])
    advance("compute", 4)
    advance(1, 3)
    exchanges[1].pass_on()
    advance("compute", 5)
    advance(1, 4)
    advance(2, 2)
    exchanges[2].pass_on()

    for exchange in exchanges:
        exchange.finish()
    back = [
        remote(
            e_right.at[5 + t, pl.ds(0, local), :], e_right.at[5 + t, pl.ds(local, local), :],
            core_send.at[11 + t], core_recv.at[11 + t], partner,
        )
        for t in range(3)
    ]
    for move in back:
        move.start()

    def columns_of(n, carry):
        rows = pl.ds(pl.multiple_of(n * 256, 256), 256)
        total = jnp.zeros((local, 256), jnp.float32)
        for t in range(3):
            total += nt(e_right[5 + t, pl.ds(0, local), :], triple[rows, pl.ds(t * width, width)])
        grad_s[:, rows] = total
        return carry

    wait_all(ready["in"])
    wait_all(back)
    advance("compute", 8)
    advance(1, 5)
    advance(2, 4)
    lax.fori_loop(0, width // 256, columns_of, 0)
    advance(3, 2)
    advance(1, 6)

    def norm_rows(n, total):
        rows = pl.ds(pl.multiple_of(n * 128, 128), 128)
        unit, inverse = norm_parts(tokens[rows, :].astype(jnp.float32))
        grad = grad_s[rows, :]
        pulled = norm_pull(grad, unit, inverse, gain[...])
        o_tokens[rows, :] = (middle[rows, :] + pulled).astype(LOW)
        return total + jnp.sum(grad * unit, axis=0, keepdims=True)

    gain_s[0:1, :] = lax.fori_loop(0, local // 128, norm_rows, jnp.zeros((1, width), jnp.float32))

    meets = (partner, place.y_partner(), place.x_partner(), place.near_partner(), place.far_partner())

    for k in range(5):
        move = remote(gain_s, gain_r.at[k], gain_send.at[k], gain_recv.at[k], meets[k])
        move.start()
        advance(1, 7 + k // 2)
        advance(2, 5 + k // 2)
        advance(3, 3 + k // 2)
        advance(4, 1 + k // 2)
        move.wait()
        gain_s[...] = gain_s[...] + gain_r[k]
        if k == 1:
            o_gains[7:8, :] = gain_s[7:8, 0:128]
    for n in range(8):
        advance(2, n + 1)
        advance(3, n)
        advance(4, n - 1)
    advance(3, 8)
    advance(4, 8)
    device = place.dp * 8 + place.seq
    pick = (
        lax.broadcasted_iota(jnp.int32, (width, 128), 0)
        == device * 32 + lax.broadcasted_iota(jnp.int32, (width, 128), 1)
    ).astype(jnp.float32)
    o_gains[0:3, :] = jnp.dot(
        gain_s[...], pick, preferred_element_type=jnp.float32, precision=lax.Precision.HIGHEST
    )[0:3]
    block = gain_s[:, pl.ds(pl.multiple_of((device % 8) * 128, 128), 128)]
    row = lax.broadcasted_iota(jnp.int32, block.shape, 0)
    o_gains[3:4, :] = jnp.sum(jnp.where(row == 3 + device // 8, block, 0.0), axis=0, keepdims=True)
    o_gains[4:7, :] = jnp.zeros((3, 128), jnp.float32)
    for engine, p in order:
        engine.settle(p)


def tail(dqkv, tokens, gain, middle, triple, acts, grads, gains, scales):
    local, width = tokens.shape
    heads_width = dqkv[0].shape[1]
    hidden = grads[0].shape[1]
    any_spec = pl.BlockSpec(memory_space=pl.ANY)
    vmem = pl.BlockSpec(memory_space=pltpu.VMEM)
    wide = jnp.float32
    dma = pltpu.SemaphoreType.DMA
    return pl.pallas_call(
        tail_kernel,
        out_shape=(
            jax.ShapeDtypeStruct((local, width), LOW),
            jax.ShapeDtypeStruct((width // 32, 3 * width), wide),
            jax.ShapeDtypeStruct((width // 32, width), wide),
            jax.ShapeDtypeStruct((width // 32, hidden), wide),
            jax.ShapeDtypeStruct((8, 128), wide),
        ),
        in_specs=[any_spec] * 3 + [vmem] * 4 + [any_spec] * 5 + [vmem] * 2,
        out_specs=(vmem,) * 5,
        scratch_shapes=[pltpu.VMEM((3, 2 * local, width // 2), LOW), pltpu.VMEM((8, 2 * local, width), LOW)]
        + scatter_scratch(8, 32, 1024)
        + [
            pltpu.VMEM((local, width), wide),
            pltpu.VMEM((8, width), wide),
            pltpu.VMEM((5, 8, width), wide),
            pltpu.VMEM((3, 3, local, heads_width), LOW),
            dma((20,)),
            dma((20,)),
            dma((20,)),
            *exchange_sems(3),
            dma((4, 8)),
            dma((4, 8)),
            dma((5,)),
            dma((5,)),
        ],
        compiler_params=pltpu.CompilerParams(
            collective_id=3, has_side_effects=True, vmem_limit_bytes=VMEM_BYTES
        ),
        name="tail",
    )(*dqkv, tokens, gain.reshape(1, width), middle, triple, *acts, *grads, gains, scales)


def per_device(
    sizes,
    tokens,
    segment_ids,
    first_gain,
    triple_weight,
    head_scale,
    output_weight,
    post_gain,
    second_gain,
    up_weight,
    mid_gain,
    down_weight,
    cotangent,
):
    inputs = tokens[0].astype(jnp.float32)
    width = inputs.shape[1]
    doc_ids = lax.all_gather(segment_ids[0], "seq", axis=0, tiled=True)
    triple_full, output_full = (
        lax.all_gather(triple_weight, "dp", axis=0, tiled=True),
        lax.all_gather(output_weight, "dp", axis=0, tiled=True),
    )
    normed, pull_first = jax.vjp(layer_norm, inputs, first_gain)
    normed_low = normed.astype(jnp.bfloat16)
    triple = jnp.dot(normed_low, triple_full, preferred_element_type=jnp.float32).astype(
        jnp.bfloat16
    )
    queries, keys_all, values_all = (
        lax.all_to_all(triple[:, :width], "seq", split_axis=1, concat_axis=0, tiled=True),
        lax.all_to_all(
            triple[:, width : 2 * width], "seq", split_axis=1, concat_axis=0, tiled=True
        ),
        lax.all_to_all(triple[:, 2 * width :], "seq", split_axis=1, concat_axis=0, tiled=True),
    )
    heads_here = queries.shape[1] // HEAD
    own_scale = lax.dynamic_slice_in_dim(
        head_scale, lax.axis_index("seq") * heads_here, heads_here, 0
    )
    scale_wide = jnp.repeat(own_scale, HEAD)[None]
    starts = document_starts(doc_ids)
    attended, scaled, logsum = attend_forward(
        queries, keys_all, values_all, starts, scale_wide
    )
    merged = lax.all_to_all(scaled, "seq", split_axis=0, concat_axis=1, tiled=True)
    projected = jnp.dot(merged, output_full, preferred_element_type=jnp.float32)
    post_normed, pull_post = jax.vjp(layer_norm, projected, post_gain)
    middle = inputs + post_normed
    second, pull_second = jax.vjp(layer_norm, middle, second_gain)
    second_low = second.astype(jnp.bfloat16)
    feed_up, feed_down = (
        lax.all_gather(up_weight, "dp", axis=0, tiled=True),
        lax.all_gather(down_weight, "dp", axis=0, tiled=True),
    )
    hidden = jnp.dot(second_low, feed_up, preferred_element_type=jnp.float32)
    activated, pull_mid = jax.vjp(gelu_norm, hidden, mid_gain)
    activated_low = activated.astype(jnp.bfloat16)
    layer_out = (
        middle + jnp.dot(activated_low, feed_down, preferred_element_type=jnp.float32)
    ).astype(jnp.bfloat16)
    upstream = cotangent[0]
    grad_act = times_transposed(upstream, feed_down)
    grad_hidden, grad_mid = pull_mid(grad_act)
    grad_hidden_low = grad_hidden.astype(jnp.bfloat16)
    grad_second_in = times_transposed(grad_hidden_low, feed_up)
    grad_middle_part, grad_second = pull_second(grad_second_in)
    grad_middle = upstream.astype(jnp.float32) + grad_middle_part
    grad_projected, grad_post = pull_post(grad_middle)
    grad_projected_low = grad_projected.astype(jnp.bfloat16)
    grad_merged = times_transposed(grad_projected_low, output_full).astype(jnp.bfloat16)
    grad_scaled = lax.all_to_all(
        grad_merged, "seq", split_axis=1, concat_axis=0, tiled=True
    )
    grad_queries, grad_keys, grad_values, scale_lanes = attend_backward(
        queries, keys_all, values_all, attended, grad_scaled, starts, scale_wide, logsum
    )
    scale_terms = jnp.sum(scale_lanes.reshape(heads_here, HEAD), axis=1)
    back_queries, back_keys, back_values = (
        lax.all_to_all(
            grad_queries.astype(jnp.bfloat16), "seq", split_axis=0, concat_axis=1, tiled=True
        ),
        lax.all_to_all(
            grad_keys.astype(jnp.bfloat16), "seq", split_axis=0, concat_axis=1, tiled=True
        ),
        lax.all_to_all(
            grad_values.astype(jnp.bfloat16), "seq", split_axis=0, concat_axis=1, tiled=True
        ),
    )
    grad_triple_act = jnp.concatenate((back_queries, back_keys, back_values), axis=1)
    grad_normed = times_transposed(grad_triple_act, triple_full)
    grad_input_part, grad_first = pull_first(grad_normed)
    grad_tokens = (grad_middle + grad_input_part).astype(jnp.bfloat16)
    low = jnp.bfloat16
    grad_down = scatter_rows(transposed_times(activated_low, upstream).astype(low), sizes)
    grad_up = scatter_rows(transposed_times(second_low, grad_hidden_low).astype(low), sizes)
    grad_output = scatter_rows(transposed_times(merged, grad_projected_low).astype(low), sizes)
    gains = jnp.concatenate(
        (
            grad_first[:, None],
            grad_post[:, None],
            grad_second[:, None],
            grad_mid.reshape(width, -1),
        ),
        axis=1,
    )
    gains = jnp.pad(gains, ((0, 0), (0, 128 - gains.shape[1])))
    grad_triple = scatter_rows(
        jnp.concatenate(
            (transposed_times(normed_low, grad_triple_act).astype(low), gains.astype(low)), axis=1
        ),
        sizes,
    )
    gain_sums = grad_triple[:, 3 * width :]
    grad_scale = lax.psum(scale_terms, "dp")
    return (
        layer_out[None],
        grad_tokens[None],
        gain_sums[:, 0],
        grad_triple[:, : 3 * width],
        grad_scale,
        grad_output,
        gain_sums[:, 1],
        gain_sums[:, 2],
        grad_up,
        gain_sums[:, 3 : 3 + mid_gain.shape[0] // width].reshape(-1),
        grad_down,
    )


def per_device_chips(
    sizes,
    tokens,
    segment_ids,
    first_gain,
    triple_weight,
    head_scale,
    output_weight,
    post_gain,
    second_gain,
    up_weight,
    mid_gain,
    down_weight,
    cotangent,
):
    width, hidden = tokens.shape[2], up_weight.shape[1]
    heads_here = width // HEAD // sizes[1]
    own_scale = lax.dynamic_slice_in_dim(
        head_scale, lax.axis_index("seq") * heads_here, heads_here, 0
    )
    scale_wide = jnp.repeat(own_scale, HEAD)[None]
    values, keys, queries, normed, starts, triple_full, output_full, up_full = front(
        tokens[0], first_gain, segment_ids, triple_weight, output_weight, up_weight
    )
    attended, scaled, logsum = attend_forward(queries, keys, values, starts, scale_wide)
    layer_out, grad_middle, grad_scaled, merged, second, grad_hidden, grad_projected, gains, grad_down = middle(
        scaled, tokens[0], cotangent[0], post_gain, second_gain, mid_gain, output_full, up_full, down_weight
    )
    grad_queries, grad_keys, grad_values, scale_lanes = attend_backward(
        queries, keys, values, attended, grad_scaled, starts, scale_wide, logsum
    )
    gains = jnp.concatenate(
        (gains[:3, :width], gains[3].reshape(-1, width), jnp.zeros((1, width), jnp.float32)), axis=0
    )
    grad_tokens, grad_triple, grad_output, grad_up, sums = tail(
        (grad_queries, grad_keys, grad_values),
        tokens[0],
        first_gain,
        grad_middle,
        triple_full,
        (second, merged, normed),
        (grad_hidden, grad_projected),
        gains,
        scale_lanes,
    )
    own = width // 32
    return (
        layer_out[None],
        grad_tokens[None],
        sums[0, :own],
        grad_triple,
        jnp.sum(sums[7].reshape(heads_here, HEAD), axis=1),
        grad_output,
        sums[1, :own],
        sums[2, :own],
        grad_up,
        sums[3],
        grad_down,
    )


def solution(mesh):
    placed = (
        P("dp", "seq", None),
        P("dp", "seq"),
        P(),
        P("dp", None),
        P(),
        P("dp", None),
        P(),
        P(),
        P("dp", None),
        P(),
        P("dp", None),
        P("dp", "seq", None),
    )
    sizes = (mesh.shape["dp"], mesh.shape["seq"])
    program = per_device_chips if sizes == (4, 8) else per_device
    return jax.shard_map(
        functools.partial(program, sizes),
        mesh=mesh,
        in_specs=placed,
        out_specs=(
            P("dp", "seq", None),
            P("dp", "seq", None),
            P(("dp", "seq")),
            P(("dp", "seq"), None),
            P("seq"),
            P(("dp", "seq"), None),
            P(("dp", "seq")),
            P(("dp", "seq")),
            P(("dp", "seq"), None),
            P(("dp", "seq")),
            P(("dp", "seq"), None),
        ),
        check_vma=False,
    )
```

```python
import functools
import jax
import jax.numpy as jnp
from jax import lax
from jax.sharding import PartitionSpec as P
from jax.experimental import pallas as pl
from jax.experimental.pallas import tpu as pltpu

HEAD = 64
NEG = -1e30
BQ = 256
QB = 512
KB = 512
WIDE = 1


def nt(a, b):
    return lax.dot_general(a, b, (((1,), (1,)), ((), ())), preferred_element_type=jnp.float32)


def tn(a, b):
    return lax.dot_general(a, b, (((0,), (0,)), ((), ())), preferred_element_type=jnp.float32)


def stack_heads(block, heads):
    if heads == 1:
        return block
    lane = lax.broadcasted_iota(jnp.int32, block.shape, 1)
    zero = jnp.zeros_like(block)
    return jnp.concatenate(
        [jnp.where((lane >= h * HEAD) & (lane < (h + 1) * HEAD), block, zero) for h in range(heads)],
        axis=0,
    )


def unstack_heads(wide, heads):
    rows = wide.shape[1] // heads
    return jnp.concatenate(
        [wide[h * HEAD : (h + 1) * HEAD, h * rows : (h + 1) * rows] for h in range(heads)], axis=0
    )


def forward_kernel(heads, first_ref, q_ref, k_ref, v_ref, start_ref, scale_ref,
                   o_ref, u_ref, lse_ref, m_s, l_s, acc_s):
    rows, step_rows = QB, KB
    ratio = rows // step_rows

    def one(i, carry):
        mine = pl.ds(pl.multiple_of(i * rows, rows), rows)
        queries = stack_heads(q_ref[mine, :] * jnp.bfloat16(HEAD ** -0.5), heads)
        starts = jnp.concatenate([start_ref[i * (rows // BQ) + k] for k in range(rows // BQ)] * heads, axis=1)

        def step(j, count, masked, diagonal):
            at = pl.ds(pl.multiple_of(j * step_rows, step_rows), count * step_rows)
            scores = nt(k_ref[at, :], queries)
            if masked or diagonal:
                key = j * step_rows + lax.broadcasted_iota(jnp.int32, scores.shape, 0)
                allowed = key >= starts
                if diagonal:
                    lane = lax.broadcasted_iota(jnp.int32, scores.shape, 1) & (rows - 1)
                    allowed = allowed & (key <= i * rows + lane)
                scores = jnp.where(allowed, scores, NEG)
            highest = jnp.max(scores, axis=0, keepdims=True)
            if not diagonal:
                before = m_s[...]
                highest = jnp.maximum(before, highest)
                fade = jnp.exp(before - highest)
            weights = jnp.exp(scores - highest)
            total = jnp.sum(weights, axis=0, keepdims=True)
            part = tn(v_ref[at, :], weights.astype(jnp.bfloat16))
            m_s[...] = highest
            if diagonal:
                l_s[...] = total
                acc_s[...] = part
            else:
                l_s[...] = l_s[...] * fade + total
                acc_s[...] = acc_s[...] * fade + part

        step(i * ratio, ratio, False, True)
        low = first_ref[i * (rows // BQ), 0, 0] // step_rows
        last = first_ref[i * (rows // BQ) + rows // BQ - 1, 0, BQ - 1]
        full = jnp.minimum((last + step_rows - 1) // step_rows, i * ratio)
        pairs = (i * ratio - full) // WIDE

        def wide(n, carry):
            step(i * ratio - WIDE * (n + 1), WIDE, False, False)
            return carry

        def plain(j, carry):
            step(j, 1, False, False)
            return carry

        def edge(j, carry):
            step(j, 1, True, False)
            return carry

        lax.fori_loop(0, pairs, wide, 0)
        lax.fori_loop(full, i * ratio - WIDE * pairs, plain, 0)
        lax.fori_loop(low, full, edge, 0)
        total = l_s[...]
        out = unstack_heads(acc_s[...] * (1.0 / total), heads).T
        o_ref[mine, :] = out
        u_ref[mine, :] = (out * scale_ref[...]).astype(jnp.bfloat16)
        logsum = m_s[...] + jnp.log(total)
        for k in range(rows // BQ):
            lse_ref[i * (rows // BQ) + k] = jnp.concatenate(
                [logsum[:, h * rows + k * BQ : h * rows + (k + 1) * BQ] for h in range(heads)], axis=1
            )
        return carry

    lax.fori_loop(0, q_ref.shape[0] // rows, one, 0)


def attend_forward(queries, keys, values, starts, scale_wide):
    length, width = queries.shape
    heads = width // HEAD
    blocks = length // BQ
    vmem = pl.BlockSpec(memory_space=pltpu.VMEM)
    return pl.pallas_call(
        functools.partial(forward_kernel, heads),
        out_shape=(
            jax.ShapeDtypeStruct((length, width), jnp.float32),
            jax.ShapeDtypeStruct((length, width), jnp.bfloat16),
            jax.ShapeDtypeStruct((blocks, 1, heads * BQ), jnp.float32),
        ),
        in_specs=[pl.BlockSpec(memory_space=pltpu.SMEM)] + [vmem] * 5,
        out_specs=(vmem,) * 3,
        scratch_shapes=[
            pltpu.VMEM((1, heads * QB), jnp.float32),
            pltpu.VMEM((1, heads * QB), jnp.float32),
            pltpu.VMEM((width, heads * QB), jnp.float32),
        ],
        cost_estimate=pl.CostEstimate(
            flops=length * length * width, bytes_accessed=16 * length * width, transcendentals=0
        ),
        name="attend_forward",
    )(starts, queries, keys, values, starts, scale_wide)


def backward_kernel(heads, first_ref, q_ref, k_ref, v_ref, o_ref, du_ref, start_ref, scale_ref, lse_ref,
                    dq_ref, dk_ref, dv_ref, ds_ref, qs_s, dos_s, delta_s, dqt_s, dk_s, dv_s):
    rows = BQ
    blocks = qs_s.shape[0]

    def prepare(i, total):
        at = pl.ds(pl.multiple_of(i * rows, rows), rows)
        qs_s[i] = stack_heads(q_ref[at, :] * jnp.bfloat16(HEAD ** -0.5), heads)
        grad = du_ref[at, :].astype(jnp.float32)
        out = o_ref[at, :]
        low = (grad * scale_ref[...]).astype(jnp.bfloat16)
        dos_s[i] = stack_heads(low, heads)
        inner = (low.astype(jnp.float32) * out).T
        delta_s[i] = jnp.concatenate(
            [jnp.sum(inner[h * HEAD : (h + 1) * HEAD], axis=0, keepdims=True) for h in range(heads)],
            axis=1,
        )
        return total + jnp.sum(grad * out, axis=0, keepdims=True)

    ds_ref[...] = lax.fori_loop(0, blocks, prepare, jnp.zeros(ds_ref.shape, jnp.float32))

    def one(j, carry):
        mine = pl.ds(pl.multiple_of(j * rows, rows), rows)
        keys, values = k_ref[mine, :], v_ref[mine, :]

        def step(i, masked, diagonal):
            queries, grads = qs_s[i], dos_s[i]
            scores = nt(keys, queries)
            if masked or diagonal:
                key = j * rows + lax.broadcasted_iota(jnp.int32, scores.shape, 0)
                starts = jnp.concatenate([start_ref[i]] * heads, axis=1)
                allowed = key >= starts
                if diagonal:
                    lane = lax.broadcasted_iota(jnp.int32, scores.shape, 1) & (rows - 1)
                    allowed = allowed & (key <= i * rows + lane)
                scores = jnp.where(allowed, scores, NEG)
            weights = jnp.exp(scores - lse_ref[i])
            pulls = nt(values, grads)
            low = (weights * (pulls - delta_s[i])).astype(jnp.bfloat16)
            part_v = jnp.dot(weights.astype(jnp.bfloat16), grads, preferred_element_type=jnp.float32)
            part_k = jnp.dot(low, queries, preferred_element_type=jnp.float32)
            part_q = tn(keys, low)
            if diagonal:
                dv_s[...] = part_v
                dk_s[...] = part_k
            else:
                dv_s[...] += part_v
                dk_s[...] += part_k
            return part_q

        high, full = jnp.int32(0), jnp.int32(0)
        for i in range(blocks):
            high += (first_ref[i, 0, 0] // rows <= j).astype(jnp.int32)
            full += ((first_ref[i, 0, rows - 1] + rows - 1) // rows <= j).astype(jnp.int32)
        full = jnp.maximum(full, j + 1)

        def plain(i, carry):
            dqt_s[i] += step(i, False, False)
            return carry

        def edge(i, carry):
            dqt_s[i] += step(i, True, False)
            return carry

        dqt_s[j] = step(j, False, True)
        lax.fori_loop(j + 1, full, plain, 0)
        lax.fori_loop(full, high, edge, 0)
        dk_ref[mine, :] = dk_s[...].astype(jnp.bfloat16)
        dv_ref[mine, :] = dv_s[...].astype(jnp.bfloat16)
        return carry

    lax.fori_loop(0, blocks, lambda n, carry: one(blocks - 1 - n, carry), 0)

    def finish(i, carry):
        at = pl.ds(pl.multiple_of(i * rows, rows), rows)
        dq_ref[at, :] = (unstack_heads(dqt_s[i], heads).T * HEAD ** -0.5).astype(jnp.bfloat16)
        return carry

    lax.fori_loop(0, blocks, finish, 0)


def attend_backward(queries, keys, values, outs, grads, starts, scale_wide, logsum):
    length, width = queries.shape
    heads = width // HEAD
    blocks = length // BQ
    vmem = pl.BlockSpec(memory_space=pltpu.VMEM)
    return pl.pallas_call(
        functools.partial(backward_kernel, heads),
        out_shape=(jax.ShapeDtypeStruct((length, width), jnp.bfloat16),) * 3
        + (jax.ShapeDtypeStruct((1, width), jnp.float32),),
        in_specs=[pl.BlockSpec(memory_space=pltpu.SMEM)] + [vmem] * 8,
        out_specs=(vmem,) * 4,
        scratch_shapes=[
            pltpu.VMEM((blocks, heads * BQ, width), jnp.bfloat16),
            pltpu.VMEM((blocks, heads * BQ, width), jnp.bfloat16),
            pltpu.VMEM((blocks, 1, heads * BQ), jnp.float32),
            pltpu.VMEM((blocks, width, heads * BQ), jnp.float32),
            pltpu.VMEM((BQ, width), jnp.float32),
            pltpu.VMEM((BQ, width), jnp.float32),
        ],
        cost_estimate=pl.CostEstimate(
            flops=3 * length * length * width, bytes_accessed=32 * length * width, transcendentals=0
        ),
        name="attend_backward",
    )(starts, queries, keys, values, outs, grads, starts, scale_wide, logsum)


def document_starts(doc_ids):
    length = doc_ids.shape[0]
    names = jnp.arange(8, dtype=jnp.int32)
    counts = jnp.sum(doc_ids[None, :] < names[:, None], axis=1, dtype=jnp.int32)
    starts = jnp.sum(
        jnp.where(doc_ids[:, None] == names[None, :], counts[None, :], 0), axis=1, dtype=jnp.int32
    )
    return starts.reshape(length // BQ, 1, BQ)


def layer_norm(values, gains):
    center = values - jnp.mean(values, axis=-1, keepdims=True)
    spread = jnp.mean(center * center, axis=-1, keepdims=True)
    return center * lax.rsqrt(spread + 1e-05) * gains


def gelu_norm(hidden, gains):
    return layer_norm(jax.nn.gelu(hidden, approximate=True), gains)


def transposed_times(left, right):
    return lax.dot_general(
        left, right, (((0,), (0,)), ((), ())), preferred_element_type=jnp.float32
    )


def times_transposed(left, right):
    return lax.dot_general(
        left, right, (((1,), (1,)), ((), ())), preferred_element_type=jnp.float32
    )


def scatter_rows(partial, sizes):
    current = partial
    for axis, size in zip(("dp", "seq"), sizes):
        place = lax.axis_index(axis)
        bits = size.bit_length() - 1
        pieces = current.reshape((2,) * bits + (-1, current.shape[-1]))
        for bit in range(bits):
            at = bits - 1 - bit
            mine = (place >> bit) & 1
            give = lax.dynamic_index_in_dim(pieces, 1 - mine, at, keepdims=False)
            keep = lax.dynamic_index_in_dim(pieces, mine, at, keepdims=False)
            got = lax.ppermute(give, axis, [(i, i ^ (1 << bit)) for i in range(size)])
            pieces = (keep.astype(jnp.float32) + got.astype(jnp.float32)).astype(jnp.bfloat16)
        current = pieces
    return current.astype(jnp.float32)


MESH = pl.DeviceIdType.MESH
LOW = jnp.bfloat16
BLOCK = 1024
VMEM_BYTES = 66_000_000


class Place:
    def __init__(self):
        self.dp, self.seq = lax.axis_index("dp"), lax.axis_index("seq")
        self.core, self.y = self.dp % 2, self.dp // 2
        self.x, self.z = self.seq % 2, self.seq // 2
        self.z0, self.z1 = self.z % 2, self.z // 2

    def core_partner(self):
        return (self.dp + 1 - 2 * self.core, self.seq)

    def y_partner(self):
        return (self.dp + 2 - 4 * self.y, self.seq)

    def x_partner(self):
        return (self.dp, self.seq + 1 - 2 * self.x)

    def near_partner(self):
        return (self.dp, self.seq + 2 - 4 * self.z0)

    def far_partner(self):
        return (self.dp, self.seq + 4 - 8 * self.z1)


def meet(devices):
    barrier = pltpu.get_barrier_semaphore()
    for device in devices:
        pl.semaphore_signal(barrier, inc=1, device_id=device, device_id_type=MESH)
    pl.semaphore_wait(barrier, len(devices))


def remote(source, target, send, receive, device):
    return pltpu.make_async_remote_copy(
        src_ref=source,
        dst_ref=target,
        send_sem=send,
        recv_sem=receive,
        device_id=device,
        device_id_type=MESH,
    )


def lanes_of(z, x, width):
    return pl.ds(pl.multiple_of((z * 2 + x) * width, 128), width)


def rows_of(z, x, local):
    return pl.ds(pl.multiple_of((z * 2 + x) * local, 128), local)


class ToHeads:
    def __init__(self, place, part, target, relay, sems, keep_sem):
        self.place, self.target, self.relay, self.sems = place, target, relay, sems
        x_send, x_recv, z_send, z_recv = sems
        local, width = relay.shape[-2:]
        rows = rows_of(place.z, place.x, local)
        self.moves, self.sends = [], []
        for k in (2, 1, 3, 0):
            source = part.at[:, lanes_of((place.z + k) % 4, 1 - place.x, width)]
            landing = target.at[rows, :] if k == 0 else relay.at[k - 1]
            move = remote(source, landing, x_send.at[k], x_recv.at[k], place.x_partner())
            move.start()
            (self.moves if k == 0 else self.sends).append(move)
        for k in (2, 1, 3):
            z = (place.z + k) % 4
            source = part.at[:, lanes_of(z, place.x, width)]
            move = remote(
                source, target.at[rows, :], z_send.at[k - 1], z_recv.at[k - 1], (place.dp, z * 2 + place.x)
            )
            move.start()
            self.moves.append(move)
        source = part.at[:, lanes_of(place.z, place.x, width)]
        move = pltpu.make_async_copy(source, target.at[rows, :], keep_sem)
        move.start()
        self.moves.append(move)

    def pass_on(self):
        place, local = self.place, self.relay.shape[-2]
        x_send, x_recv, z_send, z_recv = self.sems
        rows = rows_of(place.z, 1 - place.x, local)
        for k in (2, 1, 3):
            here = self.relay.at[k - 1]
            remote(here, here, x_send.at[k], x_recv.at[k], place.x_partner()).wait_recv()
            device = (place.dp, (place.z + k) % 4 * 2 + place.x)
            move = remote(here, self.target.at[rows, :], z_send.at[k + 2], z_recv.at[k + 2], device)
            move.start()
            self.moves.append(move)

    def finish(self):
        for move in self.moves:
            move.wait()
        for move in self.sends:
            move.wait_send()


class ToTokens:
    def __init__(self, place, source, target, relay, sems, keep_sem):
        self.place, self.target, self.relay, self.sems = place, target, relay, sems
        x_send, x_recv, z_send, z_recv = sems
        local, width = relay.shape[-2:]
        self.moves, self.sends = [], []
        lanes = lanes_of(place.z, place.x, width)
        for x, first in ((1 - place.x, 0), (place.x, 3)):
            for k in (2, 1, 3):
                z, index = (place.z + k) % 4, first + k - 1
                landing = relay.at[k - 1] if first == 0 else target.at[:, lanes]
                move = remote(
                    source.at[rows_of(z, x, local), :],
                    landing,
                    z_send.at[index],
                    z_recv.at[index],
                    (place.dp, z * 2 + place.x),
                )
                move.start()
                (self.sends if first == 0 else self.moves).append(move)
        move = remote(
            source.at[rows_of(place.z, 1 - place.x, local), :],
            target.at[:, lanes],
            x_send.at[0],
            x_recv.at[0],
            place.x_partner(),
        )
        move.start()
        self.moves.append(move)
        move = pltpu.make_async_copy(
            source.at[rows_of(place.z, place.x, local), :], target.at[:, lanes], keep_sem
        )
        move.start()
        self.moves.append(move)

    def pass_on(self):
        place, width = self.place, self.relay.shape[-1]
        x_send, x_recv, z_send, z_recv = self.sems
        for k in (2, 1, 3):
            here = self.relay.at[k - 1]
            remote(here, here, z_send.at[k - 1], z_recv.at[k - 1], place.near_partner()).wait_recv()
            lanes = lanes_of((place.z + 4 - k) % 4, place.x, width)
            move = remote(here, self.target.at[:, lanes], x_send.at[k], x_recv.at[k], place.x_partner())
            move.start()
            self.moves.append(move)

    def finish(self):
        for move in self.moves:
            move.wait()
        for move in self.sends:
            move.wait_send()


def exchange_sems(count):
    dma = pltpu.SemaphoreType.DMA
    return [dma((count, 4)), dma((count, 4)), dma((count, 6)), dma((count, 6))]


def share(place, index, ours, theirs, target, local, here_sem, core_send, core_recv):
    here = pltpu.make_async_copy(ours, target.at[pl.ds(0, local), :], here_sem.at[index])
    there = remote(
        theirs, target.at[pl.ds(local, local), :], core_send.at[index], core_recv.at[index], place.core_partner()
    )
    here.start()
    there.start()
    return [here, there]


def share_left(place, index, source, target, local, *sems):
    half = source.shape[1] // 2
    columns = half // 2
    out = []
    for y in range(2):
        ours, theirs = (
            source.at[pl.ds(0, local), pl.ds(pl.multiple_of(y * half + core * columns, 128), columns)]
            for core in (place.core, 1 - place.core)
        )
        out += share(place, index + y, ours, theirs, target.at[:, pl.ds(y * columns, columns)], local, *sems)
    return out


def wait_all(copies):
    for copy in copies:
        copy.wait()


def norm_parts(values):
    center = values - jnp.mean(values, axis=-1, keepdims=True)
    inverse = lax.rsqrt(jnp.mean(center * center, axis=-1, keepdims=True) + 1e-05)
    return center * inverse, inverse


def norm_pull(grad, unit, inverse, gain):
    scaled = grad * gain
    return inverse * (
        scaled
        - jnp.mean(scaled, axis=-1, keepdims=True)
        - unit * jnp.mean(scaled * unit, axis=-1, keepdims=True)
    )


class Scatter:
    def __init__(self, place, refs, sems, x_first, left, right, write):
        self.place, self.x_first, self.left, self.right, self.write = place, x_first, left, right, write
        self.whole, self.first, self.second, self.near, self.far = refs
        self.send, self.receive = sems
        self.rows, self.columns = self.whole.shape[-2:]

    def axes(self, p):
        place = self.place
        if p not in self.x_first:
            return place.y, place.x, place.y_partner(), place.x_partner()
        return place.x, place.y, place.x_partner(), place.y_partner()

    def copy(self, p, stage):
        place = self.place
        mine, other, partner, second = self.axes(p)
        if stage == 0:
            source, target, device = self.whole.at[p, 1 - mine], self.first.at[p], partner
        elif stage == 1:
            source, target, device = self.first.at[p, :, :, 1 - other], self.second.at[p], second
        elif stage == 2:
            source, target, device = self.second.at[p, :, 1 - place.z0], self.near.at[p], place.near_partner()
        else:
            source, target, device = self.near.at[p, 1 - place.z1], self.far.at[p], place.far_partner()
        index = p
        return remote(source, target, self.send.at[stage, index], self.receive.at[stage, index], device)

    def compute(self, p):
        left, right = self.left(p), self.right(p)
        rows = self.rows

        def one(y, carry):
            for half in range(2):
                span = 4 * rows
                at = pl.ds(pl.multiple_of(y * 8 * rows + half * span, 128), span)
                block = tn(left[:, at], right[...]).astype(LOW)
                for k in range(4):
                    x = k % 2
                    part = block[k * rows : (k + 1) * rows]
                    if p not in self.x_first:
                        self.whole[p, y, half, k // 2, x] = part
                    else:
                        self.whole[p, x, half, k // 2, y] = part
            return carry

        lax.fori_loop(0, 2, one, 0)
        self.copy(p, 0).start()

    def advance(self, p, stage):
        place = self.place
        mine, other, _, _ = self.axes(p)
        wide = jnp.float32
        self.copy(p, stage - 1).wait_recv()
        if stage == 1:

            def add(k, carry):
                a, b, s = k // 4, k // 2 % 2, k % 2
                total = self.first[p, a, b, s].astype(wide) + self.whole[p, mine, a, b, s].astype(wide)
                self.first[p, a, b, s] = total.astype(LOW)
                return carry

            lax.fori_loop(0, 8, add, 0)
        elif stage == 2:

            def add(z, carry):
                a, b = z // 2, z % 2
                total = self.second[p, a, b].astype(wide) + self.first[p, a, b, other].astype(wide)
                self.second[p, a, b] = total.astype(LOW)
                return carry

            lax.fori_loop(0, 4, add, 0)
        elif stage == 3:

            def add(a, carry):
                total = self.near[p, a].astype(wide) + self.second[p, a, place.z0].astype(wide)
                self.near[p, a] = total.astype(LOW)
                return carry

            lax.fori_loop(0, 2, add, 0)
        else:
            self.write(p, self.near[p, place.z1].astype(wide) + self.far[p].astype(wide))
            return
        self.copy(p, stage).start()

    def settle(self, p):
        for stage in range(4):
            self.copy(p, stage).wait_send()


def scatter_scratch(pieces, rows, columns):
    return [
        pltpu.VMEM((pieces, 2, 2, 2, 2, rows, columns), LOW),
        pltpu.VMEM((pieces, 2, 2, 2, rows, columns), LOW),
        pltpu.VMEM((pieces, 2, 2, rows, columns), LOW),
        pltpu.VMEM((pieces, 2, rows, columns), LOW),
        pltpu.VMEM((pieces, rows, columns), LOW),
    ]


class Gather:
    def __init__(self, place, sems):
        self.place = place
        self.send, self.receive = sems

    def copies(self, index, own, full, rows, shared):
        place = self.place
        across = place.dp + 2 - 4 * place.y
        half = rows // 2

        def move(kind, source, target, device):
            return remote(source, target, self.send.at[kind, index], self.receive.at[kind, index], device)

        out = [move(0, own, full(place.dp, 0, rows), place.core_partner())]
        if shared:
            first = place.x * half
            out.append(
                move(1, own.at[pl.ds(pl.multiple_of(first, half), half), :],
                     full(place.dp, first, half), place.y_partner())
            )
            landed = full(across, first, half)
            out.append(move(2, landed, landed, place.x_partner()))
        else:
            out.append(move(1, own, full(place.dp, 0, rows), place.y_partner()))
            out.append(None)
        landed = full(across, 0, rows)
        out.append(move(3, landed, landed, place.core_partner()))
        return out


def front_kernel(
    tokens, gain, ids, w_triple, w_out, w_up,
    o_v, o_k, o_q, o_normed, o_starts, o_triple, o_out, o_up,
    triple_s, part_s, ids_s, bounce, relay, send, receive, x_send, x_recv, z_send, z_recv, ids_send, ids_recv, local_sem,
):
    place = Place()
    exchange_sem = (x_send, x_recv, z_send, z_recv)
    local, width = tokens.shape
    heads_width = o_v.shape[1]
    meet([(place.dp, (place.seq + k) % 8) for k in range(1, 8)] + [place.core_partner(), place.y_partner()])
    gather = Gather(place, (send, receive))

    def columns(weight, rows, column):
        at = pl.ds(column * width, width)

        def full(d, first, count):
            return weight.at[pl.ds(pl.multiple_of(d * rows + first, 128), count), at]

        return full

    plans = []
    for n, t in enumerate((2, 1, 0)):
        plans.append((w_triple.at[:, pl.ds(t * width, width)], columns(triple_s, 256, t)))
    plans.append((w_out, columns(o_out, 256, 0)))
    for k in range(w_up.shape[1] // width):
        plans.append((w_up.at[:, pl.ds(k * width, width)], columns(o_up, 256, k)))
    alone = (3,)
    chunks = [
        gather.copies(n, own, full, 256, n not in alone) for n, (own, full) in enumerate(plans)
    ]
    mine = []
    for n, (own, full) in enumerate(plans):
        chunks[n][1].start()
        chunks[n][0].start()
        target = full(place.dp, 0, 256) if n < 3 else bounce.at[n - 3]
        copy = pltpu.make_async_copy(own, target, local_sem.at[n])
        copy.start()
        mine.append(copy)
        if n == 0:
            news = []
            for k in range(1, 8):
                peer = (place.dp, (place.seq + k) % 8)
                move = remote(ids, ids_s.at[place.seq], ids_send.at[k - 1], ids_recv.at[k - 1], peer)
                move.start()
                news.append(move)
            ids_s[pl.ds(place.seq, 1)] = ids[...].reshape(1, 1, local)

    def norm_rows(n, carry):
        rows = pl.ds(pl.multiple_of(n * 128, 128), 128)
        values = tokens[rows, :].astype(jnp.float32)
        o_normed[rows, :] = (norm_parts(values)[0] * gain[...]).astype(LOW)
        return carry

    lax.fori_loop(0, local // 128, norm_rows, 0)
    moves = []
    exchanges = []

    def project(n):
        t, target = (2, 1, 0)[n], (o_v, o_k, o_q)[n]

        def one(c, carry):
            at = pl.ds(pl.multiple_of(c * 256, 256), 256)
            from_at = pl.ds(pl.multiple_of(t * width + c * 256, 256), 256)
            part_s[n, :, at] = jnp.dot(
                o_normed[...], triple_s[:, from_at], preferred_element_type=jnp.float32
            ).astype(LOW)
            return carry

        lax.fori_loop(0, width // 256, one, 0)
        exchange = ToHeads(
            place, part_s.at[n], target, relay.at[n], [sem.at[n] for sem in exchange_sem], local_sem.at[12 + n]
        )
        exchanges.append(exchange)
        save = pltpu.make_async_copy(
            triple_s.at[:, pl.ds(t * width, width)], o_triple.at[:, pl.ds(t * width, width)], local_sem.at[15 + n]
        )
        save.start()
        moves.append(save)

    def forward(n):
        if chunks[n][2] is not None:
            chunks[n][1].wait_recv()
            chunks[n][2].start()

    def across(n):
        (chunks[n][1] if chunks[n][2] is None else chunks[n][2]).wait_recv()
        chunks[n][3].start()

    def finish(n):
        chunks[n][0].wait_recv()
        chunks[n][3].wait_recv()
        if n < 3:
            mine[n].wait()
            project(n)

    def put_back(n):
        mine[n].wait()
        copy = pltpu.make_async_copy(bounce.at[n - 3], plans[n][1](place.dp, 0, 256), local_sem.at[n])
        copy.start()
        moves.append(copy)

    count = len(chunks)
    forward(0)
    for n in range(count):
        if n + 1 < count:
            forward(n + 1)
        across(n)
        if n < 3:
            finish(n)
        else:
            put_back(n)
        if 0 < n < 4:
            exchanges[n - 1].pass_on()
        if n == 4:
            for move in news:
                move.wait()
            every = ids_s[...]
            starts = jnp.zeros_like(every)
            for d in range(1, 8):
                before = jnp.sum((every < d).astype(jnp.int32), axis=2, keepdims=True)
                before = jnp.sum(before, axis=0, keepdims=True)
                starts = jnp.where(every == d, before, starts)
            for b in range(o_starts.shape[0]):
                for piece in range(BQ // 128):
                    at = b * BQ + piece * 128
                    o_starts[b, :, pl.ds(piece * 128, 128)] = starts[
                        at // local, :, at % local : at % local + 128
                    ]
    for n in range(3, count):
        finish(n)
    for move in moves:
        move.wait()
    for exchange in exchanges:
        exchange.finish()
    for chunk in chunks:
        for copy in chunk:
            if copy is not None:
                copy.wait_send()


def front(tokens, gain, ids, w_triple, w_out, w_up):
    local, width = tokens.shape
    heads_width = width // 8
    length = local * 8
    hidden = w_up.shape[1]
    any_spec = pl.BlockSpec(memory_space=pl.ANY)
    vmem = pl.BlockSpec(memory_space=pltpu.VMEM)
    dma = pltpu.SemaphoreType.DMA
    one = jax.ShapeDtypeStruct((length, heads_width), LOW)
    return pl.pallas_call(
        front_kernel,
        out_shape=(
            one, one, one,
            jax.ShapeDtypeStruct((local, width), LOW),
            jax.ShapeDtypeStruct((length // BQ, 1, BQ), jnp.int32),
            jax.ShapeDtypeStruct((width, 3 * width), LOW),
            jax.ShapeDtypeStruct((width, width), LOW),
            jax.ShapeDtypeStruct((width, hidden), LOW),
        ),
        in_specs=[vmem] * 3 + [any_spec] * 3,
        out_specs=(any_spec,) * 3 + (vmem,) * 2 + (any_spec,) * 3,
        scratch_shapes=[
            pltpu.VMEM((width, 3 * width), LOW),
            pltpu.VMEM((3, local, width), LOW),
            pltpu.VMEM((8, 1, local), jnp.int32),
            pltpu.VMEM((1 + hidden // width, 256, width), LOW),
            pltpu.VMEM((3, 3, local, heads_width), LOW),
            dma((4, 8)),
            dma((4, 8)),
            *exchange_sems(3),
            dma((7,)),
            dma((7,)),
            dma((20,)),
        ],
        compiler_params=pltpu.CompilerParams(
            collective_id=1, has_side_effects=True, vmem_limit_bytes=VMEM_BYTES
        ),
        name="front",
    )(tokens, gain.reshape(1, width), ids, w_triple, w_out, w_up)


MIDDLE_ALONE = (0, 2, 3)
MIDDLE_X_FIRST = (1, 3)
MIDDLE_ORDER = (
    1100, 600, 1200, 1300, 1400, 700, 701, 702, 602, 501, 703, 1500, 601, 3, 603, 0, 800, 801,
    1, 802, 900, 901, 103, 100, 2, 902, 903, 203, 1000, 1001, 101, 303, 1600, 200, 1700, 102,
    300, 403, 201, 1800, 400, 202, 301, 302, 1900, 401, 402,
)


def middle_kernel(
    u, tokens, cotangent, post_gain, second_gain, mid_gain, w_out, w_up, w_down,
    o_layer, o_middle, o_heads, o_merged, o_second, o_hidden, o_projected, o_gains, o_down,
    out_s, up_s, down_s, merged_s, second_s, unit_s, slope_s, act_s, hidden_s, projected_s, middle_s, far_s,
    inverse_s, inner_s, relay, grad_s,
    d_left, d_right, d_whole, d_first, d_second, d_near, d_far,
    local_sem, g_send, g_recv, core_send, core_recv, x_send, x_recv, z_send, z_recv, s_send, s_recv,
):
    place = Place()
    local, width = tokens.shape
    hidden = mid_gain.shape[1]
    wide = jnp.float32
    column_peers = [(place.dp, (place.z + k) % 4 * 2 + place.x) for k in range(1, 4)]
    meet(column_peers + [place.x_partner(), place.core_partner(), place.y_partner()])
    exchange_sem = (x_send, x_recv, z_send, z_recv)

    inbound = ToTokens(place, u, merged_s, relay.at[0], [sem.at[0] for sem in exchange_sem], local_sem.at[0])
    gather = Gather(place, (g_send, g_recv))
    alone = MIDDLE_ALONE
    chunks, mine = [], []
    for k in range(4):

        def full(d, first, count, k=k):
            return down_s.at[pl.ds(pl.multiple_of(d * 1024 + k * 256 + first, 128), count), :]

        own = w_down.at[pl.ds(k * 256, 256), :]
        chunks.append(gather.copies(k, own, full, 256, k not in alone))
        chunks[k][1].start()
        chunks[k][0].start()
        mine.append(pltpu.make_async_copy(own, full(place.dp, 0, 256), local_sem.at[1 + k]))
        mine[k].start()
    loads = [
        pltpu.make_async_copy(w_out, out_s, local_sem.at[5]),
        pltpu.make_async_copy(w_up, up_s, local_sem.at[6]),
    ]
    for load in loads:
        load.start()
    sems = (local_sem, core_send, core_recv)
    right = share(place, 7, cotangent, cotangent, d_right, local, *sems)
    saves = []

    def save(source, target, index):
        copy = pltpu.make_async_copy(source, target, local_sem.at[index])
        copy.start()
        saves.append(copy)

    def across(k):
        (chunks[k][1] if chunks[k][2] is None else chunks[k][2]).wait_recv()
        chunks[k][3].start()

    def forward(k):
        chunks[k][1].wait_recv()
        chunks[k][2].start()

    gain = mid_gain[...]
    part_one = gain.astype(LOW)
    left_over = gain - part_one.astype(wide)
    part_two = left_over.astype(LOW)
    part_three = (left_over - part_two.astype(wide)).astype(LOW)
    row = lax.broadcasted_iota(jnp.int32, (16, hidden), 0)
    parts = jnp.where(row == 0, part_one.astype(wide), jnp.where(row == 1, part_two.astype(wide), part_three.astype(wide)))
    act_s[pl.ds(local, 16), :] = jnp.where(row < 3, parts, 0.0).astype(LOW)

    def blocks(first, count, body):
        def one(n, carry):
            body(n + first)
            return carry

        lax.fori_loop(0, count, one, 0)

    def span(n, size):
        return pl.ds(pl.multiple_of(n * size, size), size)

    later = {}

    def arrive(_):
        inbound.finish()
        wait_all(loads)
        save(merged_s, o_merged, 8)

    def project(n):
        at = span(n, 256)
        far_s[:, at] = jnp.dot(merged_s[...], out_s[:, at], preferred_element_type=wide)

    def norms(n):
        rows = span(n, 128)
        unit, inverse = norm_parts(far_s[rows, :])
        far_s[rows, :] = unit
        inverse_s[rows, :] = jnp.broadcast_to(inverse, (128, 128))
        middle = tokens[rows, :].astype(wide) + unit * post_gain[...]
        middle_s[rows, :] = middle
        second_s[rows, :] = (norm_parts(middle)[0] * second_gain[...]).astype(LOW)

    def grow(n):
        at = span(n, 256)
        z = jnp.dot(second_s[...], up_s[:, at], preferred_element_type=wide)
        root = 0.7978845608028654
        square = z * z
        bent = jnp.tanh(root * z * (1.0 + 0.044715 * square))
        half = 0.5 * (1.0 + bent)
        unit_s[:, at] = z * half
        slope_s[:, at] = half + 0.5 * root * z * (1.0 - bent * bent) * (1.0 + 3.0 * 0.044715 * square)

    def hidden_norm(n):
        rows = span(n, 32)
        unit, inverse = norm_parts(unit_s[rows, :])
        unit_s[rows, :] = unit
        inner_s[rows, :] = jnp.broadcast_to(inverse, (32, 128))
        act_s[rows, :] = (unit * gain).astype(LOW)

    def settle_weights():
        for k in range(4):
            chunks[k][0].wait_recv()
            chunks[k][3].wait_recv()
            mine[k].wait()
        grad_s[...] = jnp.zeros_like(grad_s)

    def shrink(n):
        at = span(n, 256)
        total = jnp.dot(act_s[...], down_s[:, at], preferred_element_type=wide)
        low = cotangent[:, at].astype(wide)
        value = total[:local]
        o_layer[:, at] = (middle_s[:, at] + value).astype(LOW)
        weight = jnp.sum(total[local:], axis=0, keepdims=True)
        first = jnp.sum(low * weight, axis=1, keepdims=True) * (1.0 / hidden)
        second = jnp.sum(low * value, axis=1, keepdims=True) * (1.0 / hidden)
        grad_s[0] = grad_s[0] + jnp.broadcast_to(first, (local, 128))
        grad_s[1] = grad_s[1] + jnp.broadcast_to(second, (local, 128))

    def write_down(p, value):
        o_down[:, pl.ds(p * 256, 256)] = value

    down = Scatter(
        place, (d_whole, d_first, d_second, d_near, d_far), (s_send, s_recv), MIDDLE_X_FIRST,
        lambda p: d_left, lambda p: d_right.at[:, pl.ds(p * 256, 256)], write_down,
    )

    def pull_hidden(n):
        at = span(n, 256)
        grad = nt(cotangent[...], down_s[at, :])
        unit = unit_s[:, at]
        o_gains[3:4, at] = jnp.sum(grad * unit, axis=0, keepdims=True)
        pulled = grad * mid_gain[:, at] - grad_s[0][:, 0:1] - unit * grad_s[1][:, 0:1]
        hidden_s[:, at] = (inner_s[:, 0:1] * pulled * slope_s[:, at]).astype(LOW)

    def pull_second(n):
        at = span(n, 256)
        o_middle[:, at] = nt(hidden_s[...], up_s[at, :])

    def pull_norms(n, totals):
        rows = span(n, 128)
        grad = o_middle[rows, :]
        unit, inverse = norm_parts(middle_s[rows, :])
        grad_middle = cotangent[rows, :].astype(wide) + norm_pull(grad, unit, inverse, second_gain[...])
        o_middle[rows, :] = grad_middle
        outer = far_s[rows, :]
        projected_s[rows, :] = norm_pull(grad_middle, outer, inverse_s[rows, 0:1], post_gain[...]).astype(LOW)
        return (
            totals[0] + jnp.sum(grad_middle * outer, axis=0, keepdims=True),
            totals[1] + jnp.sum(grad * unit, axis=0, keepdims=True),
        )

    def pull_merged(n):
        at = span(n, 256)
        merged_s[:, at] = nt(projected_s[...], out_s[at, :]).astype(LOW)

    def compute(p):
        if later.get("left"):
            wait_all(right)
            wait_all(later.pop("left"))
        down.compute(p)

    def do_norms(_):
        blocks(0, local // 128, norms)
        save(second_s, o_second, 9)

    def do_hidden_norm(_):
        blocks(0, local // 32, hidden_norm)
        later["left"] = share_left(place, 10, act_s, d_left, local, *sems)

    def do_shrink(n):
        if n == 0:
            settle_weights()
        else:
            blocks((n - 1) * 2, 2, shrink)

    def do_pull_hidden(n):
        blocks(n * (hidden // 1024), hidden // 1024, pull_hidden)
        if n == 3:
            save(hidden_s, o_hidden, 15)

    def do_pull_norms(_):
        nothing = jnp.zeros((1, width), wide)
        post, second = lax.fori_loop(0, local // 128, pull_norms, (nothing, nothing))
        o_gains[1:2, 0:width] = post
        o_gains[2:3, 0:width] = second
        save(projected_s, o_projected, 16)

    def do_pull_merged(_):
        saves[0].wait()
        blocks(0, width // 256, pull_merged)
        later["out"] = ToHeads(
            place, merged_s, o_heads, relay.at[1], [sem.at[1] for sem in exchange_sem], local_sem.at[17]
        )

    act = (
        compute,
        lambda p: down.advance(p, 1),
        lambda p: down.advance(p, 2),
        lambda p: down.advance(p, 3),
        lambda p: down.advance(p, 4),
        forward,
        across,
        lambda n: blocks(n * (hidden // 1024), hidden // 1024, grow),
        do_shrink,
        do_pull_hidden,
        lambda n: blocks(n * 2, 2, pull_second),
        lambda n: inbound.pass_on(),
        arrive,
        lambda n: blocks(0, width // 256, project),
        do_norms,
        do_hidden_norm,
        do_pull_norms,
        do_pull_merged,
        lambda n: later["out"].pass_on(),
        lambda n: later["out"].finish(),
    )
    for code in MIDDLE_ORDER:
        act[code // 100](code % 100)
    wait_all(saves[1:])
    for p in range(4):
        down.settle(p)
    for chunk in chunks:
        for copy in chunk:
            if copy is not None:
                copy.wait_send()


def middle(u, tokens, cotangent, post_gain, second_gain, mid_gain, w_out, w_up, w_down):
    local, width = tokens.shape
    hidden = w_up.shape[1]
    any_spec = pl.BlockSpec(memory_space=pl.ANY)
    vmem = pl.BlockSpec(memory_space=pltpu.VMEM)
    dma = pltpu.SemaphoreType.DMA
    wide = jnp.float32
    act = jax.ShapeDtypeStruct((local, width), LOW)
    return pl.pallas_call(
        middle_kernel,
        out_shape=(
            act,
            jax.ShapeDtypeStruct((local, width), wide),
            jax.ShapeDtypeStruct((local * 8, width // 8), LOW),
            act,
            act,
            jax.ShapeDtypeStruct((local, hidden), LOW),
            act,
            jax.ShapeDtypeStruct((8, hidden), wide),
            jax.ShapeDtypeStruct((hidden // 32, width), wide),
        ),
        in_specs=[any_spec] + [vmem] * 5 + [any_spec] * 3,
        out_specs=(vmem,) * 2 + (any_spec,) * 5 + (vmem,) * 2,
        scratch_shapes=[
            pltpu.VMEM((width, width), LOW),
            pltpu.VMEM((width, hidden), LOW),
            pltpu.VMEM((hidden, width), LOW),
            pltpu.VMEM((local, width), LOW),
            pltpu.VMEM((local, width), LOW),
            pltpu.VMEM((local, hidden), wide),
            pltpu.VMEM((local, hidden), wide),
            pltpu.VMEM((local + 16, hidden), LOW),
            pltpu.VMEM((local, hidden), LOW),
            pltpu.VMEM((local, width), LOW),
            pltpu.VMEM((local, width), wide),
            pltpu.VMEM((local, width), wide),
            pltpu.VMEM((local, 128), wide),
            pltpu.VMEM((local, 128), wide),
            pltpu.VMEM((2, 3, local, width // 8), LOW),
            pltpu.VMEM((2, local, 128), wide),
            pltpu.VMEM((2 * local, hidden // 2), LOW),
            pltpu.VMEM((2 * local, width), LOW),
            *scatter_scratch(4, 128, 256),
            dma((20,)),
            dma((4, 4)),
            dma((4, 4)),
            dma((20,)),
            dma((20,)),
            *exchange_sems(2),
            dma((4, 4)),
            dma((4, 4)),
        ],
        compiler_params=pltpu.CompilerParams(
            collective_id=2, has_side_effects=True, vmem_limit_bytes=VMEM_BYTES
        ),
        name="middle",
    )(
        u, tokens, cotangent, post_gain.reshape(1, width), second_gain.reshape(1, width),
        mid_gain.reshape(1, hidden), w_out, w_up, w_down,
    )


HALF = 512
X_FIRST = (1, 3, 5, 12, 13)
TAIL_ORDER = (
    0, 3, 7, 9, 500, 1, 100, 2, 103, 4, 5, 600, 700, 15, 101, 501, 200, 107, 102, 109,
    8, 203, 6, 105, 14, 601, 303, 502, 701, 12, 104, 115, 201, 207, 300, 202, 13, 209, 108, 602,
    702, 800, 900, 302, 106, 205, 309, 112, 301, 11, 204, 305, 402, 400, 901, 215, 304, 401, 307, 405,
    212, 403, 114, 10, 409, 113, 315, 208, 111, 404, 312, 206, 902, 415, 308, 407, 306, 412, 214, 110,
    408, 213, 211, 406, 314, 313, 210, 311, 310, 414, 413, 411, 410,
)


def tail_kernel(
    dq, dk, dv, tokens, gain, middle, triple, act_up, act_out, act_in, g_up, g_out, gains, scales,
    o_tokens, o_triple, o_out, o_up, o_gains,
    e_left, e_right, e_whole, e_first, e_second, e_near, e_far,
    grad_s, gain_s, gain_r, relay,
    local_sem, core_send, core_recv, x_send, x_recv, z_send, z_recv, s_send, s_recv, gain_send, gain_recv,
):
    place = Place()
    partner = place.core_partner()
    local, width = tokens.shape
    heads_width = dq.shape[1]
    seq_peers = [(place.dp, (place.seq + k) % 8) for k in range(1, 8)]
    dp_peers = [((place.dp + k) % 4, place.seq) for k in range(1, 4)]
    meet(seq_peers + dp_peers)

    def start_exchange(t):
        return ToTokens(
            place, (dv, dk, dq)[t], e_right.at[7 - t, pl.ds(0, local), :], relay.at[t],
            [sem.at[t] for sem in (x_send, x_recv, z_send, z_recv)], local_sem.at[13 + t],
        )

    exchanges = [start_exchange(t) for t in range(3)]

    sems = (local_sem, core_send, core_recv)
    ready = {"up": share_left(place, 0, act_up, e_left.at[0], local, *sems)}
    for k in range(4):
        part = g_up.at[:, pl.ds(k * BLOCK, BLOCK)]
        ready[k] = share(place, 2 + k, part, part, e_right.at[k], local, *sems)
    ready["out"] = share_left(place, 6, act_out, e_left.at[1], local, *sems)
    ready["out"] += share(place, 8, g_out, g_out, e_right.at[4], local, *sems)
    ready["in"] = share_left(place, 9, act_in, e_left.at[2], local, *sems)

    def write(p, value):
        at = pl.ds(p % 2 * HALF, HALF)
        if p < 8:
            o_up[:, pl.ds(p * HALF, HALF)] = value
        elif p < 10:
            o_out[:, at] = value
        else:
            o_triple[:, pl.ds((p - 10) * HALF, HALF)] = value

    engine = Scatter(
        place, (e_whole, e_first, e_second, e_near, e_far), (s_send, s_recv), X_FIRST,
        lambda p: e_left.at[0 if p < 8 else 1 if p < 10 else 2],
        lambda p: e_right.at[p // 2, :, pl.ds(p % 2 * HALF, HALF)], write,
    )
    gain_s[...] = gains[...]
    gain_s[7:8, 0:128] = scales[...]
    def bring_back(t):
        exchanges[t].finish()
        slot = e_right.at[7 - t]
        move = remote(
            slot.at[pl.ds(0, local), :], slot.at[pl.ds(local, local), :],
            core_send.at[11 + t], core_recv.at[11 + t], partner,
        )
        move.start()
        return move

    def pull_normed(t):
        def one(n, carry):
            rows = pl.ds(pl.multiple_of(n * 256, 256), 256)
            part = nt(e_right[7 - t, pl.ds(0, local), :], triple[rows, pl.ds((2 - t) * width, width)])
            grad_s[:, rows] = part if t == 0 else grad_s[:, rows] + part
            return carry

        lax.fori_loop(0, width // 256, one, 0)

    def norm_rows(n, total):
        rows = pl.ds(pl.multiple_of(n * 128, 128), 128)
        unit, inverse = norm_parts(tokens[rows, :].astype(jnp.float32))
        grad = grad_s[rows, :]
        pulled = norm_pull(grad, unit, inverse, gain[...])
        o_tokens[rows, :] = (middle[rows, :] + pulled).astype(LOW)
        return total + jnp.sum(grad * unit, axis=0, keepdims=True)

    def pull_norm(_):
        gain_s[0:1, :] = lax.fori_loop(0, local // 128, norm_rows, jnp.zeros((1, width), jnp.float32))

    def gain_moves(peers, first):
        out = [
            remote(gain_s, gain_r.at[first + k], gain_send.at[first + k], gain_recv.at[first + k], peer)
            for k, peer in enumerate(peers)
        ]
        for move in out:
            move.start()
        return out

    gain_steps = {}

    def sum_gains(step):
        if step == 0:
            gain_steps[0] = gain_moves(dp_peers, 0)
        elif step == 1:
            wait_all(gain_steps[0])
            gain_s[...] = gain_s[...] + gain_r[0] + gain_r[1] + gain_r[2]
            o_gains[7:8, :] = gain_s[7:8, 0:128]
            gain_steps[1] = gain_moves(seq_peers, 3)
        else:
            wait_all(gain_steps[1])
            total = gain_s[...]
            for k in range(7):
                total = total + gain_r[3 + k]
            gain_s[...] = total

    backs, waited = {}, set()

    def need(key):
        if key not in waited:
            wait_all(ready[key])
            waited.add(key)

    def compute(p):
        need("up" if p < 8 else "out" if p < 10 else "in")
        if p < 8:
            need(p // 2)
        elif p >= 10 and 7 - p // 2 in backs:
            backs.pop(7 - p // 2).wait()
        engine.compute(p)

    def bring(t):
        backs[t] = bring_back(t)

    act = (
        compute,
        lambda p: engine.advance(p, 1),
        lambda p: engine.advance(p, 2),
        lambda p: engine.advance(p, 3),
        lambda p: engine.advance(p, 4),
        lambda t: exchanges[t].pass_on(),
        bring,
        pull_normed,
        pull_norm,
        sum_gains,
    )
    for code in TAIL_ORDER:
        act[code // 100](code % 100)
    device = place.dp * 8 + place.seq
    pick = (
        lax.broadcasted_iota(jnp.int32, (width, 128), 0)
        == device * 32 + lax.broadcasted_iota(jnp.int32, (width, 128), 1)
    ).astype(jnp.float32)
    o_gains[0:3, :] = jnp.dot(
        gain_s[...], pick, preferred_element_type=jnp.float32, precision=lax.Precision.HIGHEST
    )[0:3]
    block = gain_s[:, pl.ds(pl.multiple_of((device % 8) * 128, 128), 128)]
    row = lax.broadcasted_iota(jnp.int32, block.shape, 0)
    o_gains[3:4, :] = jnp.sum(jnp.where(row == 3 + device // 8, block, 0.0), axis=0, keepdims=True)
    o_gains[4:7, :] = jnp.zeros((3, 128), jnp.float32)
    for p in range(16):
        engine.settle(p)


def tail(dqkv, tokens, gain, middle, triple, acts, grads, gains, scales):
    local, width = tokens.shape
    heads_width = dqkv[0].shape[1]
    hidden = grads[0].shape[1]
    any_spec = pl.BlockSpec(memory_space=pl.ANY)
    vmem = pl.BlockSpec(memory_space=pltpu.VMEM)
    wide = jnp.float32
    dma = pltpu.SemaphoreType.DMA
    return pl.pallas_call(
        tail_kernel,
        out_shape=(
            jax.ShapeDtypeStruct((local, width), LOW),
            jax.ShapeDtypeStruct((width // 32, 3 * width), wide),
            jax.ShapeDtypeStruct((width // 32, width), wide),
            jax.ShapeDtypeStruct((width // 32, hidden), wide),
            jax.ShapeDtypeStruct((8, 128), wide),
        ),
        in_specs=[any_spec] * 3 + [vmem] * 4 + [any_spec] * 5 + [vmem] * 2,
        out_specs=(vmem,) * 5,
        scratch_shapes=[pltpu.VMEM((3, 2 * local, width // 2), LOW), pltpu.VMEM((8, 2 * local, width), LOW)]
        + scatter_scratch(16, 32, HALF)
        + [
            pltpu.VMEM((local, width), wide),
            pltpu.VMEM((8, width), wide),
            pltpu.VMEM((10, 8, width), wide),
            pltpu.VMEM((3, 3, local, heads_width), LOW),
            dma((20,)),
            dma((20,)),
            dma((20,)),
            *exchange_sems(3),
            dma((4, 16)),
            dma((4, 16)),
            dma((10,)),
            dma((10,)),
        ],
        compiler_params=pltpu.CompilerParams(
            collective_id=3, has_side_effects=True, vmem_limit_bytes=VMEM_BYTES
        ),
        name="tail",
    )(*dqkv, tokens, gain.reshape(1, width), middle, triple, *acts, *grads, gains, scales)


def per_device(
    sizes,
    tokens,
    segment_ids,
    first_gain,
    triple_weight,
    head_scale,
    output_weight,
    post_gain,
    second_gain,
    up_weight,
    mid_gain,
    down_weight,
    cotangent,
):
    inputs = tokens[0].astype(jnp.float32)
    width = inputs.shape[1]
    doc_ids = lax.all_gather(segment_ids[0], "seq", axis=0, tiled=True)
    triple_full, output_full = (
        lax.all_gather(triple_weight, "dp", axis=0, tiled=True),
        lax.all_gather(output_weight, "dp", axis=0, tiled=True),
    )
    normed, pull_first = jax.vjp(layer_norm, inputs, first_gain)
    normed_low = normed.astype(jnp.bfloat16)
    triple = jnp.dot(normed_low, triple_full, preferred_element_type=jnp.float32).astype(
        jnp.bfloat16
    )
    queries, keys_all, values_all = (
        lax.all_to_all(triple[:, :width], "seq", split_axis=1, concat_axis=0, tiled=True),
        lax.all_to_all(
            triple[:, width : 2 * width], "seq", split_axis=1, concat_axis=0, tiled=True
        ),
        lax.all_to_all(triple[:, 2 * width :], "seq", split_axis=1, concat_axis=0, tiled=True),
    )
    heads_here = queries.shape[1] // HEAD
    own_scale = lax.dynamic_slice_in_dim(
        head_scale, lax.axis_index("seq") * heads_here, heads_here, 0
    )
    scale_wide = jnp.repeat(own_scale, HEAD)[None]
    starts = document_starts(doc_ids)
    attended, scaled, logsum = attend_forward(
        queries, keys_all, values_all, starts, scale_wide
    )
    merged = lax.all_to_all(scaled, "seq", split_axis=0, concat_axis=1, tiled=True)
    projected = jnp.dot(merged, output_full, preferred_element_type=jnp.float32)
    post_normed, pull_post = jax.vjp(layer_norm, projected, post_gain)
    middle = inputs + post_normed
    second, pull_second = jax.vjp(layer_norm, middle, second_gain)
    second_low = second.astype(jnp.bfloat16)
    feed_up, feed_down = (
        lax.all_gather(up_weight, "dp", axis=0, tiled=True),
        lax.all_gather(down_weight, "dp", axis=0, tiled=True),
    )
    hidden = jnp.dot(second_low, feed_up, preferred_element_type=jnp.float32)
    activated, pull_mid = jax.vjp(gelu_norm, hidden, mid_gain)
    activated_low = activated.astype(jnp.bfloat16)
    layer_out = (
        middle + jnp.dot(activated_low, feed_down, preferred_element_type=jnp.float32)
    ).astype(jnp.bfloat16)
    upstream = cotangent[0]
    grad_act = times_transposed(upstream, feed_down)
    grad_hidden, grad_mid = pull_mid(grad_act)
    grad_hidden_low = grad_hidden.astype(jnp.bfloat16)
    grad_second_in = times_transposed(grad_hidden_low, feed_up)
    grad_middle_part, grad_second = pull_second(grad_second_in)
    grad_middle = upstream.astype(jnp.float32) + grad_middle_part
    grad_projected, grad_post = pull_post(grad_middle)
    grad_projected_low = grad_projected.astype(jnp.bfloat16)
    grad_merged = times_transposed(grad_projected_low, output_full).astype(jnp.bfloat16)
    grad_scaled = lax.all_to_all(
        grad_merged, "seq", split_axis=1, concat_axis=0, tiled=True
    )
    grad_queries, grad_keys, grad_values, scale_lanes = attend_backward(
        queries, keys_all, values_all, attended, grad_scaled, starts, scale_wide, logsum
    )
    scale_terms = jnp.sum(scale_lanes.reshape(heads_here, HEAD), axis=1)
    back_queries, back_keys, back_values = (
        lax.all_to_all(
            grad_queries.astype(jnp.bfloat16), "seq", split_axis=0, concat_axis=1, tiled=True
        ),
        lax.all_to_all(
            grad_keys.astype(jnp.bfloat16), "seq", split_axis=0, concat_axis=1, tiled=True
        ),
        lax.all_to_all(
            grad_values.astype(jnp.bfloat16), "seq", split_axis=0, concat_axis=1, tiled=True
        ),
    )
    grad_triple_act = jnp.concatenate((back_queries, back_keys, back_values), axis=1)
    grad_normed = times_transposed(grad_triple_act, triple_full)
    grad_input_part, grad_first = pull_first(grad_normed)
    grad_tokens = (grad_middle + grad_input_part).astype(jnp.bfloat16)
    low = jnp.bfloat16
    grad_down = scatter_rows(transposed_times(activated_low, upstream).astype(low), sizes)
    grad_up = scatter_rows(transposed_times(second_low, grad_hidden_low).astype(low), sizes)
    grad_output = scatter_rows(transposed_times(merged, grad_projected_low).astype(low), sizes)
    gains = jnp.concatenate(
        (
            grad_first[:, None],
            grad_post[:, None],
            grad_second[:, None],
            grad_mid.reshape(width, -1),
        ),
        axis=1,
    )
    gains = jnp.pad(gains, ((0, 0), (0, 128 - gains.shape[1])))
    grad_triple = scatter_rows(
        jnp.concatenate(
            (transposed_times(normed_low, grad_triple_act).astype(low), gains.astype(low)), axis=1
        ),
        sizes,
    )
    gain_sums = grad_triple[:, 3 * width :]
    grad_scale = lax.psum(scale_terms, "dp")
    return (
        layer_out[None],
        grad_tokens[None],
        gain_sums[:, 0],
        grad_triple[:, : 3 * width],
        grad_scale,
        grad_output,
        gain_sums[:, 1],
        gain_sums[:, 2],
        grad_up,
        gain_sums[:, 3 : 3 + mid_gain.shape[0] // width].reshape(-1),
        grad_down,
    )


def per_device_chips(
    sizes,
    tokens,
    segment_ids,
    first_gain,
    triple_weight,
    head_scale,
    output_weight,
    post_gain,
    second_gain,
    up_weight,
    mid_gain,
    down_weight,
    cotangent,
):
    width, hidden = tokens.shape[2], up_weight.shape[1]
    heads_here = width // HEAD // sizes[1]
    own_scale = lax.dynamic_slice_in_dim(
        head_scale, lax.axis_index("seq") * heads_here, heads_here, 0
    )
    scale_wide = jnp.repeat(own_scale, HEAD)[None]
    values, keys, queries, normed, starts, triple_full, output_full, up_full = front(
        tokens[0], first_gain, segment_ids, triple_weight, output_weight, up_weight
    )
    attended, scaled, logsum = attend_forward(queries, keys, values, starts, scale_wide)
    layer_out, grad_middle, grad_scaled, merged, second, grad_hidden, grad_projected, gains, grad_down = middle(
        scaled, tokens[0], cotangent[0], post_gain, second_gain, mid_gain, output_full, up_full, down_weight
    )
    grad_queries, grad_keys, grad_values, scale_lanes = attend_backward(
        queries, keys, values, attended, grad_scaled, starts, scale_wide, logsum
    )
    gains = jnp.concatenate(
        (gains[:3, :width], gains[3].reshape(-1, width), jnp.zeros((1, width), jnp.float32)), axis=0
    )
    grad_tokens, grad_triple, grad_output, grad_up, sums = tail(
        (grad_queries, grad_keys, grad_values),
        tokens[0],
        first_gain,
        grad_middle,
        triple_full,
        (second, merged, normed),
        (grad_hidden, grad_projected),
        gains,
        scale_lanes,
    )
    own = width // 32
    return (
        layer_out[None],
        grad_tokens[None],
        sums[0, :own],
        grad_triple,
        jnp.sum(sums[7].reshape(heads_here, HEAD), axis=1),
        grad_output,
        sums[1, :own],
        sums[2, :own],
        grad_up,
        sums[3],
        grad_down,
    )


def solution(mesh):
    placed = (
        P("dp", "seq", None),
        P("dp", "seq"),
        P(),
        P("dp", None),
        P(),
        P("dp", None),
        P(),
        P(),
        P("dp", None),
        P(),
        P("dp", None),
        P("dp", "seq", None),
    )
    sizes = (mesh.shape["dp"], mesh.shape["seq"])
    program = per_device_chips if sizes == (4, 8) else per_device
    return jax.shard_map(
        functools.partial(program, sizes),
        mesh=mesh,
        in_specs=placed,
        out_specs=(
            P("dp", "seq", None),
            P("dp", "seq", None),
            P(("dp", "seq")),
            P(("dp", "seq"), None),
            P("seq"),
            P(("dp", "seq"), None),
            P(("dp", "seq")),
            P(("dp", "seq")),
            P(("dp", "seq"), None),
            P(("dp", "seq")),
            P(("dp", "seq"), None),
        ),
        check_vma=False,
    )
```

```python
import functools
import jax
import jax.numpy as jnp
from jax import lax
from jax.sharding import PartitionSpec as P
from jax.experimental import pallas as pl
from jax.experimental.pallas import tpu as pltpu

HEAD = 64
NEG = -1e30
BQ = 256
QB = 1024
KB = 512


def nt(a, b):
    return lax.dot_general(a, b, (((1,), (1,)), ((), ())), preferred_element_type=jnp.float32)


def tn(a, b):
    return lax.dot_general(a, b, (((0,), (0,)), ((), ())), preferred_element_type=jnp.float32)


def stack_heads(block, heads):
    if heads == 1:
        return block
    lane = lax.broadcasted_iota(jnp.int32, block.shape, 1)
    zero = jnp.zeros_like(block)
    return jnp.concatenate(
        [jnp.where((lane >= h * HEAD) & (lane < (h + 1) * HEAD), block, zero) for h in range(heads)],
        axis=0,
    )


def unstack_heads(wide, heads):
    rows = wide.shape[1] // heads
    return jnp.concatenate(
        [wide[h * HEAD : (h + 1) * HEAD, h * rows : (h + 1) * rows] for h in range(heads)], axis=0
    )


def scale_row(scale_ref, width):
    heads = width // HEAD
    first = lax.axis_index("seq") * heads
    lane = lax.broadcasted_iota(jnp.int32, (1, width), 1)
    row = jnp.full((1, width), scale_ref[first], jnp.float32)
    for h in range(1, heads):
        row = jnp.where(lane >= h * HEAD, scale_ref[first + h], row)
    return row


def forward_kernel(heads, first_ref, q_ref, k_ref, v_ref, start_ref, scale_ref,
                   o_ref, u_ref, lse_ref, m_s, l_s, acc_s):
    rows, step_rows = QB, KB
    scale = scale_row(scale_ref, q_ref.shape[1])
    ratio = rows // step_rows

    def one(i, carry):
        mine = pl.ds(pl.multiple_of(i * rows, rows), rows)
        queries = stack_heads(q_ref[mine, :] * jnp.bfloat16(HEAD ** -0.5), heads)
        starts = jnp.concatenate([start_ref[i * (rows // BQ) + k] for k in range(rows // BQ)] * heads, axis=1)

        def scores_of(j, count, queries, starts):
            at = pl.ds(pl.multiple_of(j * BQ, BQ), count)
            scores = nt(k_ref[at, :], queries)
            if starts is not None:
                key = j * BQ + lax.broadcasted_iota(jnp.int32, scores.shape, 0)
                scores = jnp.where(key >= starts, scores, NEG)
            return at, scores

        def fold(at, scores, columns):
            before = m_s[:, columns]
            highest = jnp.maximum(before, jnp.max(scores, axis=0, keepdims=True))
            fade = jnp.exp(before - highest)
            weights = jnp.exp(scores - highest)
            m_s[:, columns] = highest
            l_s[:, columns] = l_s[:, columns] * fade + jnp.sum(weights, axis=0, keepdims=True)
            acc_s[:, columns] = acc_s[:, columns] * fade + tn(v_ref[at, :], weights.astype(jnp.bfloat16))

        def step(j, masked):
            at, scores = scores_of(j * (step_rows // BQ), step_rows, queries, starts if masked else None)
            fold(at, scores, slice(None))

        for k in range(rows // BQ):
            wide = rows - k * BQ
            late = [slice(h * rows + k * BQ, (h + 1) * rows) for h in range(heads)]
            some = queries if k == 0 else jnp.concatenate([queries[c] for c in late], axis=0)
            start = starts if k == 0 else jnp.concatenate([starts[:, c] for c in late], axis=1)
            at, scores = scores_of(i * (rows // BQ) + k, BQ, some, start)
            key = lax.broadcasted_iota(jnp.int32, scores.shape, 0)
            for h in range(heads):
                part = scores[:, h * wide : (h + 1) * wide]
                lane = lax.broadcasted_iota(jnp.int32, part.shape, 1)
                part = jnp.where(key[:, :wide] <= lane, part, NEG)
                if k == 0:
                    highest = jnp.max(part, axis=0, keepdims=True)
                    weights = jnp.exp(part - highest)
                    m_s[:, late[h]] = highest
                    l_s[:, late[h]] = jnp.sum(weights, axis=0, keepdims=True)
                    acc_s[:, late[h]] = tn(v_ref[at, :], weights.astype(jnp.bfloat16))
                else:
                    fold(at, part, late[h])

        low = first_ref[i * (rows // BQ), 0, 0] // step_rows
        last = first_ref[i * (rows // BQ) + rows // BQ - 1, 0, BQ - 1]
        full = jnp.minimum((last + step_rows - 1) // step_rows, i * ratio)

        def plain(j, carry):
            step(j, False)
            return carry

        def edge(j, carry):
            step(j, True)
            return carry

        lax.fori_loop(full, i * ratio, plain, 0)
        lax.fori_loop(low, full, edge, 0)
        total = l_s[...]
        out = unstack_heads(acc_s[...] * (1.0 / total), heads).T
        o_ref[mine, :] = out
        u_ref[mine, :] = (out * scale).astype(jnp.bfloat16)
        logsum = m_s[...] + jnp.log(total)
        for k in range(rows // BQ):
            lse_ref[i * (rows // BQ) + k] = jnp.concatenate(
                [logsum[:, h * rows + k * BQ : h * rows + (k + 1) * BQ] for h in range(heads)], axis=1
            )
        return carry

    lax.fori_loop(0, q_ref.shape[0] // rows, one, 0)


def attend_forward(queries, keys, values, starts, scales):
    length, width = queries.shape
    heads = width // HEAD
    vmem = pl.BlockSpec(memory_space=pltpu.VMEM)
    return pl.pallas_call(
        functools.partial(forward_kernel, heads),
        out_shape=(
            jax.ShapeDtypeStruct((length, width), jnp.float32),
            jax.ShapeDtypeStruct((length, width), jnp.bfloat16),
            jax.ShapeDtypeStruct((length // BQ, 1, heads * BQ), jnp.float32),
        ),
        in_specs=[pl.BlockSpec(memory_space=pltpu.SMEM)] + [vmem] * 4 + [pl.BlockSpec(memory_space=pltpu.SMEM)],
        out_specs=(vmem,) * 3,
        scratch_shapes=[
            pltpu.VMEM((1, heads * QB), jnp.float32),
            pltpu.VMEM((1, heads * QB), jnp.float32),
            pltpu.VMEM((width, heads * QB), jnp.float32),
        ],
        cost_estimate=pl.CostEstimate(
            flops=length * length * width, bytes_accessed=16 * length * width, transcendentals=0
        ),
        name="attend_forward",
    )(starts, queries, keys, values, starts, scales)


def backward_kernel(heads, first_ref, q_ref, k_ref, v_ref, o_ref, du_ref, start_ref, scale_ref, lse_ref,
                    dq_ref, dk_ref, dv_ref, ds_ref, qs_s, dos_s, delta_s, dqt_s, dk_s, dv_s):
    rows, group = BQ, 1
    blocks = qs_s.shape[0]
    scale = scale_row(scale_ref, q_ref.shape[1])

    def prepare(i, total):
        at = pl.ds(pl.multiple_of(i * rows, rows), rows)
        qs_s[i] = stack_heads(q_ref[at, :] * jnp.bfloat16(HEAD ** -0.5), heads)
        grad = du_ref[at, :].astype(jnp.float32)
        out = o_ref[at, :]
        low = (grad * scale).astype(jnp.bfloat16)
        dos_s[i] = stack_heads(low, heads)
        inner = (low.astype(jnp.float32) * out).T
        delta_s[i] = jnp.concatenate(
            [jnp.sum(inner[h * HEAD : (h + 1) * HEAD], axis=0, keepdims=True) for h in range(heads)],
            axis=1,
        )
        dqt_s[i] = jnp.zeros(dqt_s.shape[1:], jnp.float32)
        return total + jnp.sum(grad * out, axis=0, keepdims=True)

    ds_ref[...] = lax.fori_loop(0, blocks, prepare, jnp.zeros(ds_ref.shape, jnp.float32))

    def one(j, carry):
        mine = pl.ds(pl.multiple_of(j * BQ, BQ), BQ)
        keys, values = k_ref[mine, :], v_ref[mine, :]

        def step(i, masked, diagonal):
            queries, grads = qs_s[i], dos_s[i]
            scores = nt(keys, queries)
            if masked or diagonal:
                key = j * BQ + lax.broadcasted_iota(jnp.int32, scores.shape, 0)
                starts = jnp.concatenate([start_ref[i * group + k] for k in range(group)] * heads, axis=1)
                allowed = key >= starts
                if diagonal:
                    lane = lax.broadcasted_iota(jnp.int32, scores.shape, 1) & (rows - 1)
                    allowed = allowed & (key <= i * rows + lane)
                scores = jnp.where(allowed, scores, NEG)
            weights = jnp.exp(scores - lse_ref[i])
            pulls = nt(values, grads)
            low = (weights * (pulls - delta_s[i])).astype(jnp.bfloat16)
            part_v = jnp.dot(weights.astype(jnp.bfloat16), grads, preferred_element_type=jnp.float32)
            part_k = jnp.dot(low, queries, preferred_element_type=jnp.float32)
            part_q = tn(keys, low)
            if diagonal:
                dv_s[...] = part_v
                dk_s[...] = part_k
            else:
                dv_s[...] += part_v
                dk_s[...] += part_k
            return part_q

        high, full = jnp.int32(0), jnp.int32(0)
        for i in range(blocks):
            high += (first_ref[i * group, 0, 0] // BQ <= j).astype(jnp.int32)
            full += (first_ref[i * group + group - 1, 0, BQ - 1] <= j * BQ).astype(jnp.int32)
        own = j // group
        full = jnp.maximum(full, own + 1)

        def plain(i, carry):
            dqt_s[i] += step(i, False, False)
            return carry

        def edge(i, carry):
            dqt_s[i] += step(i, True, False)
            return carry

        dqt_s[own] += step(own, False, True)
        lax.fori_loop(own + 1, full, plain, 0)
        lax.fori_loop(full, high, edge, 0)
        dk_ref[mine, :] = dk_s[...].astype(jnp.bfloat16)
        dv_ref[mine, :] = dv_s[...].astype(jnp.bfloat16)
        return carry

    lax.fori_loop(0, blocks * group, one, 0)

    def finish(i, carry):
        at = pl.ds(pl.multiple_of(i * rows, rows), rows)
        dq_ref[at, :] = (unstack_heads(dqt_s[i], heads).T * HEAD ** -0.5).astype(jnp.bfloat16)
        return carry

    lax.fori_loop(0, blocks, finish, 0)


def attend_backward(queries, keys, values, outs, grads, starts, scales, logsum):
    length, width = queries.shape
    heads = width // HEAD
    blocks = length // BQ
    vmem = pl.BlockSpec(memory_space=pltpu.VMEM)
    return pl.pallas_call(
        functools.partial(backward_kernel, heads),
        out_shape=(jax.ShapeDtypeStruct((length, width), jnp.bfloat16),) * 3
        + (jax.ShapeDtypeStruct((1, width), jnp.float32),),
        in_specs=[pl.BlockSpec(memory_space=pltpu.SMEM)] + [vmem] * 6 + [pl.BlockSpec(memory_space=pltpu.SMEM), vmem],
        out_specs=(vmem,) * 4,
        scratch_shapes=[
            pltpu.VMEM((blocks, heads * BQ, width), jnp.bfloat16),
            pltpu.VMEM((blocks, heads * BQ, width), jnp.bfloat16),
            pltpu.VMEM((blocks, 1, heads * BQ), jnp.float32),
            pltpu.VMEM((blocks, width, heads * BQ), jnp.float32),
            pltpu.VMEM((BQ, width), jnp.float32),
            pltpu.VMEM((BQ, width), jnp.float32),
        ],
        cost_estimate=pl.CostEstimate(
            flops=3 * length * length * width, bytes_accessed=32 * length * width, transcendentals=0
        ),
        name="attend_backward",
    )(starts, queries, keys, values, outs, grads, starts, scales, logsum)


def document_starts(doc_ids):
    length = doc_ids.shape[0]
    names = jnp.arange(8, dtype=jnp.int32)
    counts = jnp.sum(doc_ids[None, :] < names[:, None], axis=1, dtype=jnp.int32)
    starts = jnp.sum(
        jnp.where(doc_ids[:, None] == names[None, :], counts[None, :], 0), axis=1, dtype=jnp.int32
    )
    return starts.reshape(length // BQ, 1, BQ)


def layer_norm(values, gains):
    center = values - jnp.mean(values, axis=-1, keepdims=True)
    spread = jnp.mean(center * center, axis=-1, keepdims=True)
    return center * lax.rsqrt(spread + 1e-05) * gains


def gelu_norm(hidden, gains):
    return layer_norm(jax.nn.gelu(hidden, approximate=True), gains)


def transposed_times(left, right):
    return lax.dot_general(
        left, right, (((0,), (0,)), ((), ())), preferred_element_type=jnp.float32
    )


def times_transposed(left, right):
    return lax.dot_general(
        left, right, (((1,), (1,)), ((), ())), preferred_element_type=jnp.float32
    )


def scatter_rows(partial, sizes):
    current = partial
    for axis, size in zip(("dp", "seq"), sizes):
        place = lax.axis_index(axis)
        bits = size.bit_length() - 1
        pieces = current.reshape((2,) * bits + (-1, current.shape[-1]))
        for bit in range(bits):
            at = bits - 1 - bit
            mine = (place >> bit) & 1
            give = lax.dynamic_index_in_dim(pieces, 1 - mine, at, keepdims=False)
            keep = lax.dynamic_index_in_dim(pieces, mine, at, keepdims=False)
            got = lax.ppermute(give, axis, [(i, i ^ (1 << bit)) for i in range(size)])
            pieces = (keep.astype(jnp.float32) + got.astype(jnp.float32)).astype(jnp.bfloat16)
        current = pieces
    return current.astype(jnp.float32)


MESH = pl.DeviceIdType.MESH
LOW = jnp.bfloat16
BLOCK = 1024
VMEM_BYTES = 66_000_000


class Place:
    def __init__(self):
        self.dp, self.seq = lax.axis_index("dp"), lax.axis_index("seq")
        self.core, self.y = self.dp % 2, self.dp // 2
        self.x, self.z = self.seq % 2, self.seq // 2
        self.z0, self.z1 = self.z % 2, self.z // 2

    def core_partner(self):
        return (self.dp + 1 - 2 * self.core, self.seq)

    def y_partner(self):
        return (self.dp + 2 - 4 * self.y, self.seq)

    def x_partner(self):
        return (self.dp, self.seq + 1 - 2 * self.x)

    def near_partner(self):
        return (self.dp, self.seq + 2 - 4 * self.z0)

    def far_partner(self):
        return (self.dp, self.seq + 4 - 8 * self.z1)


def meet(devices):
    barrier = pltpu.get_barrier_semaphore()
    for device in devices:
        pl.semaphore_signal(barrier, inc=1, device_id=device, device_id_type=MESH)
    pl.semaphore_wait(barrier, len(devices))


def remote(source, target, send, receive, device):
    return pltpu.make_async_remote_copy(
        src_ref=source,
        dst_ref=target,
        send_sem=send,
        recv_sem=receive,
        device_id=device,
        device_id_type=MESH,
    )


def lanes_of(z, x, width):
    return pl.ds(pl.multiple_of((z * 2 + x) * width, 128), width)


def rows_of(z, x, local):
    return pl.ds(pl.multiple_of((z * 2 + x) * local, 128), local)


class ToHeads:
    def __init__(self, place, part, target, relay, sems, keep_sem):
        self.place, self.target, self.relay, self.sems = place, target, relay, sems
        x_send, x_recv, z_send, z_recv = sems
        local, width = relay.shape[-2:]
        rows = rows_of(place.z, place.x, local)
        self.moves, self.sends = [], []
        for k in (2, 1, 3, 0):
            source = part.at[:, lanes_of((place.z + k) % 4, 1 - place.x, width)]
            landing = target.at[rows, :] if k == 0 else relay.at[k - 1]
            move = remote(source, landing, x_send.at[k], x_recv.at[k], place.x_partner())
            move.start()
            (self.moves if k == 0 else self.sends).append(move)
        for k in (2, 1, 3):
            z = (place.z + k) % 4
            source = part.at[:, lanes_of(z, place.x, width)]
            move = remote(
                source, target.at[rows, :], z_send.at[k - 1], z_recv.at[k - 1], (place.dp, z * 2 + place.x)
            )
            move.start()
            self.moves.append(move)
        source = part.at[:, lanes_of(place.z, place.x, width)]
        move = pltpu.make_async_copy(source, target.at[rows, :], keep_sem)
        move.start()
        self.moves.append(move)

    def pass_on(self):
        place, local = self.place, self.relay.shape[-2]
        x_send, x_recv, z_send, z_recv = self.sems
        rows = rows_of(place.z, 1 - place.x, local)
        for k in (2, 1, 3):
            here = self.relay.at[k - 1]
            remote(here, here, x_send.at[k], x_recv.at[k], place.x_partner()).wait_recv()
            device = (place.dp, (place.z + k) % 4 * 2 + place.x)
            move = remote(here, self.target.at[rows, :], z_send.at[k + 2], z_recv.at[k + 2], device)
            move.start()
            self.moves.append(move)

    def finish(self):
        for move in self.moves:
            move.wait()
        for move in self.sends:
            move.wait_send()


class ToTokens:
    def __init__(self, place, source, target, relay, sems, keep_sem):
        self.place, self.target, self.relay, self.sems = place, target, relay, sems
        x_send, x_recv, z_send, z_recv = sems
        local, width = relay.shape[-2:]
        self.moves, self.sends = [], []
        lanes = lanes_of(place.z, place.x, width)
        for x, first in ((1 - place.x, 0), (place.x, 3)):
            for k in (2, 1, 3):
                z, index = (place.z + k) % 4, first + k - 1
                landing = relay.at[k - 1] if first == 0 else target.at[:, lanes]
                move = remote(
                    source.at[rows_of(z, x, local), :],
                    landing,
                    z_send.at[index],
                    z_recv.at[index],
                    (place.dp, z * 2 + place.x),
                )
                move.start()
                (self.sends if first == 0 else self.moves).append(move)
        move = remote(
            source.at[rows_of(place.z, 1 - place.x, local), :],
            target.at[:, lanes],
            x_send.at[0],
            x_recv.at[0],
            place.x_partner(),
        )
        move.start()
        self.moves.append(move)
        move = pltpu.make_async_copy(
            source.at[rows_of(place.z, place.x, local), :], target.at[:, lanes], keep_sem
        )
        move.start()
        self.moves.append(move)

    def pass_on(self):
        place, width = self.place, self.relay.shape[-1]
        x_send, x_recv, z_send, z_recv = self.sems
        for k in (2, 1, 3):
            here = self.relay.at[k - 1]
            remote(here, here, z_send.at[k - 1], z_recv.at[k - 1], place.near_partner()).wait_recv()
            lanes = lanes_of((place.z + 4 - k) % 4, place.x, width)
            move = remote(here, self.target.at[:, lanes], x_send.at[k], x_recv.at[k], place.x_partner())
            move.start()
            self.moves.append(move)

    def finish(self):
        for move in self.moves:
            move.wait()
        for move in self.sends:
            move.wait_send()


def exchange_sems(count):
    dma = pltpu.SemaphoreType.DMA
    return [dma((count, 4)), dma((count, 4)), dma((count, 6)), dma((count, 6))]


def share(place, index, ours, theirs, target, local, here_sem, core_send, core_recv):
    here = pltpu.make_async_copy(ours, target.at[pl.ds(0, local), :], here_sem.at[index])
    there = remote(
        theirs, target.at[pl.ds(local, local), :], core_send.at[index], core_recv.at[index], place.core_partner()
    )
    here.start()
    there.start()
    return [here, there]


def share_left(place, index, source, target, local, *sems):
    half = source.shape[1] // 2
    columns = half // 2
    out = []
    for y in range(2):
        ours, theirs = (
            source.at[pl.ds(0, local), pl.ds(pl.multiple_of(y * half + core * columns, 128), columns)]
            for core in (place.core, 1 - place.core)
        )
        out += share(place, index + y, ours, theirs, target.at[:, pl.ds(y * columns, columns)], local, *sems)
    return out


def wait_all(copies):
    for copy in copies:
        copy.wait()


def norm_parts(values):
    center = values - jnp.mean(values, axis=-1, keepdims=True)
    inverse = lax.rsqrt(jnp.mean(center * center, axis=-1, keepdims=True) + 1e-05)
    return center * inverse, inverse


def norm_pull(grad, unit, inverse, gain):
    scaled = grad * gain
    return inverse * (
        scaled
        - jnp.mean(scaled, axis=-1, keepdims=True)
        - unit * jnp.mean(scaled * unit, axis=-1, keepdims=True)
    )


class Scatter:
    def __init__(self, place, refs, sems, x_first, left, right, write):
        self.place, self.x_first, self.left, self.right, self.write = place, x_first, left, right, write
        self.whole, self.first, self.second, self.near, self.far = refs
        self.send, self.receive = sems
        self.rows, self.columns = self.whole.shape[-2:]

    def axes(self, p):
        place = self.place
        if p not in self.x_first:
            return place.y, place.x, place.y_partner(), place.x_partner()
        return place.x, place.y, place.x_partner(), place.y_partner()

    def copy(self, p, stage):
        place = self.place
        mine, other, partner, second = self.axes(p)
        if stage == 0:
            source, target, device = self.whole.at[p, 1 - mine], self.first.at[p], partner
        elif stage == 1:
            source, target, device = self.first.at[p, :, :, 1 - other], self.second.at[p], second
        elif stage == 2:
            source, target, device = self.second.at[p, :, 1 - place.z0], self.near.at[p], place.near_partner()
        else:
            source, target, device = self.near.at[p, 1 - place.z1], self.far.at[p], place.far_partner()
        index = p
        return remote(source, target, self.send.at[stage, index], self.receive.at[stage, index], device)

    def compute(self, p):
        left, right = self.left(p), self.right(p)
        rows = self.rows

        def one(y, carry):
            for half in range(2):
                span = 4 * rows
                at = pl.ds(pl.multiple_of(y * 8 * rows + half * span, 128), span)
                block = tn(left[:, at], right[...]).astype(LOW)
                for k in range(4):
                    x = k % 2
                    part = block[k * rows : (k + 1) * rows]
                    if p not in self.x_first:
                        self.whole[p, y, half, k // 2, x] = part
                    else:
                        self.whole[p, x, half, k // 2, y] = part
            return carry

        lax.fori_loop(0, 2, one, 0)
        self.copy(p, 0).start()

    def advance(self, p, stage):
        place = self.place
        mine, other, _, _ = self.axes(p)
        wide = jnp.float32
        self.copy(p, stage - 1).wait_recv()
        if stage == 1:

            def add(k, carry):
                a, b, s = k // 4, k // 2 % 2, k % 2
                total = self.first[p, a, b, s].astype(wide) + self.whole[p, mine, a, b, s].astype(wide)
                self.first[p, a, b, s] = total.astype(LOW)
                return carry

            lax.fori_loop(0, 8, add, 0)
        elif stage == 2:

            def add(z, carry):
                a, b = z // 2, z % 2
                total = self.second[p, a, b].astype(wide) + self.first[p, a, b, other].astype(wide)
                self.second[p, a, b] = total.astype(LOW)
                return carry

            lax.fori_loop(0, 4, add, 0)
        elif stage == 3:

            def add(a, carry):
                total = self.near[p, a].astype(wide) + self.second[p, a, place.z0].astype(wide)
                self.near[p, a] = total.astype(LOW)
                return carry

            lax.fori_loop(0, 2, add, 0)
        else:
            self.write(p, self.near[p, place.z1].astype(wide) + self.far[p].astype(wide))
            return
        self.copy(p, stage).start()

    def settle(self, p):
        for stage in range(4):
            self.copy(p, stage).wait_send()


def scatter_scratch(pieces, rows, columns):
    return [
        pltpu.VMEM((pieces, 2, 2, 2, 2, rows, columns), LOW),
        pltpu.VMEM((pieces, 2, 2, 2, rows, columns), LOW),
        pltpu.VMEM((pieces, 2, 2, rows, columns), LOW),
        pltpu.VMEM((pieces, 2, rows, columns), LOW),
        pltpu.VMEM((pieces, rows, columns), LOW),
    ]


class Gather:
    def __init__(self, place, sems):
        self.place = place
        self.send, self.receive = sems

    def copies(self, index, own, full, rows, shared):
        place = self.place
        across = place.dp + 2 - 4 * place.y
        half = rows // 2

        def move(kind, source, target, device):
            return remote(source, target, self.send.at[kind, index], self.receive.at[kind, index], device)

        out = [move(0, own, full(place.dp, 0, rows), place.core_partner())]
        if shared:
            first = place.x * half
            out.append(
                move(1, own.at[pl.ds(pl.multiple_of(first, half), half), :],
                     full(place.dp, first, half), place.y_partner())
            )
            landed = full(across, first, half)
            out.append(move(2, landed, landed, place.x_partner()))
        else:
            out.append(move(1, own, full(place.dp, 0, rows), place.y_partner()))
            out.append(None)
        landed = full(across, 0, rows)
        out.append(move(3, landed, landed, place.core_partner()))
        return out


FRONT_ALONE = (0, 2, 5, 7)
FRONT_ORDER = (
    500, 200, 0, 101, 300, 600, 202, 2, 201, 1, 103, 104, 302, 301, 205, 203, 106, 204,
    206, 207, 405, 403, 404, 406, 407,
)


def front_kernel(
    tokens, gain, ids, w_triple, w_out, w_up,
    o_v, o_k, o_q, o_normed, o_starts, o_triple, o_out, o_up,
    triple_s, part_s, ids_s, bounce, relay, send, receive, x_send, x_recv, z_send, z_recv, ids_send, ids_recv, local_sem,
):
    place = Place()
    exchange_sem = (x_send, x_recv, z_send, z_recv)
    local, width = tokens.shape
    heads_width = o_v.shape[1]
    meet([(place.dp, (place.seq + k) % 8) for k in range(1, 8)] + [place.core_partner(), place.y_partner()])
    gather = Gather(place, (send, receive))

    def columns(weight, rows, column):
        at = pl.ds(column * width, width)

        def full(d, first, count):
            return weight.at[pl.ds(pl.multiple_of(d * rows + first, 128), count), at]

        return full

    plans = []
    for n, t in enumerate((2, 1, 0)):
        plans.append((w_triple.at[:, pl.ds(t * width, width)], columns(triple_s, 256, t)))
    plans.append((w_out, columns(o_out, 256, 0)))
    for k in range(w_up.shape[1] // width):
        plans.append((w_up.at[:, pl.ds(k * width, width)], columns(o_up, 256, k)))
    alone = FRONT_ALONE
    chunks = [
        gather.copies(n, own, full, 256, n not in alone) for n, (own, full) in enumerate(plans)
    ]
    mine = []
    for n, (own, full) in enumerate(plans):
        chunks[n][1].start()
        chunks[n][0].start()
        target = full(place.dp, 0, 256) if n < 3 else bounce.at[n - 3]
        copy = pltpu.make_async_copy(own, target, local_sem.at[n])
        copy.start()
        mine.append(copy)
        if n == 0:
            news = []
            for k in range(1, 8):
                peer = (place.dp, (place.seq + k) % 8)
                move = remote(ids, ids_s.at[place.seq], ids_send.at[k - 1], ids_recv.at[k - 1], peer)
                move.start()
                news.append(move)
            ids_s[pl.ds(place.seq, 1)] = ids[...].reshape(1, 1, local)

    def norm_rows(n, carry):
        rows = pl.ds(pl.multiple_of(n * 128, 128), 128)
        values = tokens[rows, :].astype(jnp.float32)
        o_normed[rows, :] = (norm_parts(values)[0] * gain[...]).astype(LOW)
        return carry

    moves = []
    exchanges = {}

    def project(n):
        t, target = (2, 1, 0)[n], (o_v, o_k, o_q)[n]

        def one(c, carry):
            at = pl.ds(pl.multiple_of(c * 256, 256), 256)
            from_at = pl.ds(pl.multiple_of(t * width + c * 256, 256), 256)
            part_s[n, :, at] = jnp.dot(
                o_normed[...], triple_s[:, from_at], preferred_element_type=jnp.float32
            ).astype(LOW)
            return carry

        lax.fori_loop(0, width // 256, one, 0)
        exchange = ToHeads(
            place, part_s.at[n], target, relay.at[n], [sem.at[n] for sem in exchange_sem], local_sem.at[12 + n]
        )
        exchanges[n] = exchange
        save = pltpu.make_async_copy(
            triple_s.at[:, pl.ds(t * width, width)], o_triple.at[:, pl.ds(t * width, width)], local_sem.at[15 + n]
        )
        save.start()
        moves.append(save)

    def forward(n):
        if chunks[n][2] is not None:
            chunks[n][1].wait_recv()
            chunks[n][2].start()

    def across(n):
        (chunks[n][1] if chunks[n][2] is None else chunks[n][2]).wait_recv()
        chunks[n][3].start()

    def finish(n):
        chunks[n][0].wait_recv()
        chunks[n][3].wait_recv()
        mine[n].wait()
        project(n)

    def put_back(n):
        chunks[n][0].wait_recv()
        chunks[n][3].wait_recv()
        mine[n].wait()
        copy = pltpu.make_async_copy(bounce.at[n - 3], plans[n][1](place.dp, 0, 256), local_sem.at[n])
        copy.start()
        moves.append(copy)

    def document_starts_here(_):
        for move in news:
            move.wait()
        every = ids_s[...]
        starts = jnp.zeros_like(every)
        for d in range(1, 8):
            before = jnp.sum((every < d).astype(jnp.int32), axis=2, keepdims=True)
            before = jnp.sum(before, axis=0, keepdims=True)
            starts = jnp.where(every == d, before, starts)
        for b in range(o_starts.shape[0]):
            for piece in range(BQ // 128):
                at = b * BQ + piece * 128
                o_starts[b, :, pl.ds(piece * 128, 128)] = starts[
                    at // local, :, at % local : at % local + 128
                ]

    act = (
        finish, forward, across, lambda n: exchanges[n].pass_on(), put_back,
        lambda n: lax.fori_loop(0, local // 128, norm_rows, 0), document_starts_here,
    )
    for code in FRONT_ORDER:
        act[code // 100](code % 100)
    for move in moves:
        move.wait()
    for exchange in exchanges.values():
        exchange.finish()
    for chunk in chunks:
        for copy in chunk:
            if copy is not None:
                copy.wait_send()


def front(tokens, gain, ids, w_triple, w_out, w_up):
    local, width = tokens.shape
    heads_width = width // 8
    length = local * 8
    hidden = w_up.shape[1]
    any_spec = pl.BlockSpec(memory_space=pl.ANY)
    vmem = pl.BlockSpec(memory_space=pltpu.VMEM)
    dma = pltpu.SemaphoreType.DMA
    one = jax.ShapeDtypeStruct((length, heads_width), LOW)
    return pl.pallas_call(
        front_kernel,
        out_shape=(
            one, one, one,
            jax.ShapeDtypeStruct((local, width), LOW),
            jax.ShapeDtypeStruct((length // BQ, 1, BQ), jnp.int32),
            jax.ShapeDtypeStruct((width, 3 * width), LOW),
            jax.ShapeDtypeStruct((width, width), LOW),
            jax.ShapeDtypeStruct((width, hidden), LOW),
        ),
        in_specs=[vmem] * 3 + [any_spec] * 3,
        out_specs=(any_spec,) * 3 + (vmem,) * 2 + (any_spec,) * 3,
        scratch_shapes=[
            pltpu.VMEM((width, 3 * width), LOW),
            pltpu.VMEM((3, local, width), LOW),
            pltpu.VMEM((8, 1, local), jnp.int32),
            pltpu.VMEM((1 + hidden // width, 256, width), LOW),
            pltpu.VMEM((3, 3, local, heads_width), LOW),
            dma((4, 8)),
            dma((4, 8)),
            *exchange_sems(3),
            dma((7,)),
            dma((7,)),
            dma((20,)),
        ],
        compiler_params=pltpu.CompilerParams(
            collective_id=1, has_side_effects=True, vmem_limit_bytes=VMEM_BYTES
        ),
        name="front",
    )(tokens, gain.reshape(1, width), ids, w_triple, w_out, w_up)


MIDDLE_ALONE = (3,)
MIDDLE_X_FIRST = (0, 2)
MIDDLE_ORDER = (
    1100, 500, 501, 502, 1200, 1300, 1400, 700, 701, 702, 703, 1500, 603, 601, 600, 2, 602, 0,
    1, 800, 801, 802, 900, 901, 902, 102, 903, 1000, 101, 3, 1001, 202, 1600, 1700, 100, 302,
    201, 103, 1800, 200, 301, 402, 203, 1900, 300, 303, 401, 400, 403,
)


def middle_kernel(
    u, tokens, cotangent, post_gain, second_gain, mid_gain, w_out, w_up, w_down,
    o_layer, o_grad, o_heads, o_merged, o_second, o_hidden, o_projected, o_gains, o_down,
    out_s, up_s, down_s, merged_s, second_s, unit_s, slope_s, act_s, hidden_s, projected_s, middle_s, far_s,
    layer_s, o_middle, inverse_s, inner_s, relay, grad_s,
    d_left, d_right, d_whole, d_first, d_second, d_near, d_far,
    local_sem, g_send, g_recv, core_send, core_recv, x_send, x_recv, z_send, z_recv, s_send, s_recv,
):
    place = Place()
    local, width = tokens.shape
    hidden = mid_gain.shape[1]
    wide = jnp.float32
    column_peers = [(place.dp, (place.z + k) % 4 * 2 + place.x) for k in range(1, 4)]
    meet(column_peers + [place.x_partner(), place.core_partner(), place.y_partner()])
    exchange_sem = (x_send, x_recv, z_send, z_recv)

    inbound = ToTokens(place, u, merged_s, relay.at[0], [sem.at[0] for sem in exchange_sem], local_sem.at[0])
    gather = Gather(place, (g_send, g_recv))
    alone = MIDDLE_ALONE
    chunks, mine = [], []
    for k in range(4):

        def full(d, first, count, k=k):
            return down_s.at[pl.ds(pl.multiple_of(d * 1024 + k * 256 + first, 128), count), :]

        own = w_down.at[pl.ds(k * 256, 256), :]
        chunks.append(gather.copies(k, own, full, 256, k not in alone))
        chunks[k][1].start()
        chunks[k][0].start()
        mine.append(pltpu.make_async_copy(own, full(place.dp, 0, 256), local_sem.at[1 + k]))
        mine[k].start()
    loads = [
        pltpu.make_async_copy(w_out, out_s, local_sem.at[5]),
        pltpu.make_async_copy(w_up, up_s, local_sem.at[6]),
    ]
    for load in loads:
        load.start()
    sems = (local_sem, core_send, core_recv)
    right = share(place, 7, cotangent, cotangent, d_right, local, *sems)
    saves = []

    def save(source, target, index):
        copy = pltpu.make_async_copy(source, target, local_sem.at[index])
        copy.start()
        saves.append(copy)

    def across(k):
        (chunks[k][1] if chunks[k][2] is None else chunks[k][2]).wait_recv()
        chunks[k][3].start()

    def forward(k):
        chunks[k][1].wait_recv()
        chunks[k][2].start()

    gain = mid_gain[...]
    part_one = gain.astype(LOW)
    left_over = gain - part_one.astype(wide)
    part_two = left_over.astype(LOW)
    part_three = (left_over - part_two.astype(wide)).astype(LOW)
    row = lax.broadcasted_iota(jnp.int32, (16, hidden), 0)
    parts = jnp.where(row == 0, part_one.astype(wide), jnp.where(row == 1, part_two.astype(wide), part_three.astype(wide)))
    act_s[pl.ds(local, 16), :] = jnp.where(row < 3, parts, 0.0).astype(LOW)

    def blocks(first, count, body):
        def one(n, carry):
            body(n + first)
            return carry

        lax.fori_loop(0, count, one, 0)

    def span(n, size):
        return pl.ds(pl.multiple_of(n * size, size), size)

    later = {}

    def arrive(_):
        inbound.finish()
        wait_all(loads)
        save(merged_s, o_merged, 8)

    def project(n):
        at = span(n, 512)
        far_s[:, at] = jnp.dot(merged_s[...], out_s[:, at], preferred_element_type=wide)

    def norms(n):
        rows = span(n, 128)
        unit, inverse = norm_parts(far_s[rows, :])
        far_s[rows, :] = unit
        inverse_s[rows, :] = jnp.broadcast_to(inverse, (128, 128))
        middle = tokens[rows, :].astype(wide) + unit * post_gain[...]
        middle_s[rows, :] = middle
        second_s[rows, :] = (norm_parts(middle)[0] * second_gain[...]).astype(LOW)

    def grow(n):
        at = span(n, 512)
        z = jnp.dot(second_s[...], up_s[:, at], preferred_element_type=wide)
        root = 0.7978845608028654
        square = z * z
        half = 0.5 + 0.5 * jnp.tanh(z * (root + (root * 0.044715) * square))
        value = z * half
        unit_s[:, at] = value
        slope_s[:, at] = half + (value - value * half) * (2.0 * root + (6.0 * root * 0.044715) * square)

    def hidden_norm(n):
        rows = span(n, 64)
        unit, inverse = norm_parts(unit_s[rows, :])
        unit_s[rows, :] = unit
        inner_s[rows, :] = jnp.broadcast_to(inverse, (64, 128))
        act_s[rows, :] = (unit * gain).astype(LOW)

    def settle_weights():
        for k in range(4):
            chunks[k][0].wait_recv()
            chunks[k][3].wait_recv()
            mine[k].wait()
        grad_s[...] = jnp.zeros_like(grad_s)

    def shrink(n):
        at = span(n, 512)
        total = jnp.dot(act_s[...], down_s[:, at], preferred_element_type=wide)
        low = cotangent[:, at].astype(wide)
        value = total[:local]
        layer_s[:, at] = (middle_s[:, at] + value).astype(LOW)
        weight = jnp.sum(total[local:], axis=0, keepdims=True)
        first = jnp.sum(low * weight, axis=1, keepdims=True) * (1.0 / hidden)
        second = jnp.sum(low * value, axis=1, keepdims=True) * (1.0 / hidden)
        grad_s[0] = grad_s[0] + jnp.broadcast_to(first, (local, 128))
        grad_s[1] = grad_s[1] + jnp.broadcast_to(second, (local, 128))

    def write_down(p, value):
        o_down[:, pl.ds(p * 256, 256)] = value

    down = Scatter(
        place, (d_whole, d_first, d_second, d_near, d_far), (s_send, s_recv), MIDDLE_X_FIRST,
        lambda p: d_left, lambda p: d_right.at[:, pl.ds(p * 256, 256)], write_down,
    )

    def pull_hidden(n):
        at = span(n, 512)
        grad = nt(cotangent[...], down_s[at, :])
        unit = unit_s[:, at]
        o_gains[3:4, at] = jnp.sum(grad * unit, axis=0, keepdims=True)
        pulled = grad * mid_gain[:, at] - grad_s[0][:, 0:1] - unit * grad_s[1][:, 0:1]
        hidden_s[:, at] = (inner_s[:, 0:1] * pulled * slope_s[:, at]).astype(LOW)

    def pull_second(n):
        at = span(n, 512)
        o_middle[:, at] = nt(hidden_s[...], up_s[at, :])

    def pull_norms(n, totals):
        rows = span(n, 128)
        grad = o_middle[rows, :]
        unit, inverse = norm_parts(middle_s[rows, :])
        grad_middle = cotangent[rows, :].astype(wide) + norm_pull(grad, unit, inverse, second_gain[...])
        o_middle[rows, :] = grad_middle
        outer = far_s[rows, :]
        projected_s[rows, :] = norm_pull(grad_middle, outer, inverse_s[rows, 0:1], post_gain[...]).astype(LOW)
        return (
            totals[0] + jnp.sum(grad_middle * outer, axis=0, keepdims=True),
            totals[1] + jnp.sum(grad * unit, axis=0, keepdims=True),
        )

    def pull_merged(n):
        at = span(n, 512)
        merged_s[:, at] = nt(projected_s[...], out_s[at, :]).astype(LOW)

    def compute(p):
        if later.get("left"):
            wait_all(right)
            wait_all(later.pop("left"))
        down.compute(p)

    def do_norms(_):
        blocks(0, local // 128, norms)
        save(second_s, o_second, 9)

    def do_hidden_norm(_):
        blocks(0, local // 64, hidden_norm)
        later["left"] = share_left(place, 10, act_s, d_left, local, *sems)

    def do_shrink(n):
        if n == 0:
            settle_weights()
        else:
            blocks(n - 1, 1, shrink)
        if n == 2:
            save(layer_s, o_layer, 18)

    def do_pull_hidden(n):
        blocks(n * (hidden // 2048), hidden // 2048, pull_hidden)
        if n == 3:
            save(hidden_s, o_hidden, 15)

    def do_pull_norms(_):
        nothing = jnp.zeros((1, width), wide)
        post, second = lax.fori_loop(0, local // 128, pull_norms, (nothing, nothing))
        o_gains[1:2, 0:width] = post
        o_gains[2:3, 0:width] = second
        save(projected_s, o_projected, 16)
        save(o_middle, o_grad, 19)

    def do_pull_merged(_):
        saves[0].wait()
        blocks(0, width // 512, pull_merged)
        later["out"] = ToHeads(
            place, merged_s, o_heads, relay.at[1], [sem.at[1] for sem in exchange_sem], local_sem.at[17]
        )

    act = (
        compute,
        lambda p: down.advance(p, 1),
        lambda p: down.advance(p, 2),
        lambda p: down.advance(p, 3),
        lambda p: down.advance(p, 4),
        forward,
        across,
        lambda n: blocks(n * (hidden // 2048), hidden // 2048, grow),
        do_shrink,
        do_pull_hidden,
        lambda n: blocks(n, 1, pull_second),
        lambda n: inbound.pass_on(),
        arrive,
        lambda n: blocks(0, width // 512, project),
        do_norms,
        do_hidden_norm,
        do_pull_norms,
        do_pull_merged,
        lambda n: later["out"].pass_on(),
        lambda n: later["out"].finish(),
    )
    for code in MIDDLE_ORDER:
        act[code // 100](code % 100)
    wait_all(saves[1:])
    for p in range(4):
        down.settle(p)
    for chunk in chunks:
        for copy in chunk:
            if copy is not None:
                copy.wait_send()


def middle(u, tokens, cotangent, post_gain, second_gain, mid_gain, w_out, w_up, w_down):
    local, width = tokens.shape
    hidden = w_up.shape[1]
    any_spec = pl.BlockSpec(memory_space=pl.ANY)
    vmem = pl.BlockSpec(memory_space=pltpu.VMEM)
    dma = pltpu.SemaphoreType.DMA
    wide = jnp.float32
    act = jax.ShapeDtypeStruct((local, width), LOW)
    return pl.pallas_call(
        middle_kernel,
        out_shape=(
            act,
            jax.ShapeDtypeStruct((local, width), wide),
            jax.ShapeDtypeStruct((local * 8, width // 8), LOW),
            act,
            act,
            jax.ShapeDtypeStruct((local, hidden), LOW),
            act,
            jax.ShapeDtypeStruct((8, hidden), wide),
            jax.ShapeDtypeStruct((hidden // 32, width), wide),
        ),
        in_specs=[any_spec] + [vmem] * 5 + [any_spec] * 3,
        out_specs=(any_spec,) * 7 + (vmem,) * 2,
        scratch_shapes=[
            pltpu.VMEM((width, width), LOW),
            pltpu.VMEM((width, hidden), LOW),
            pltpu.VMEM((hidden, width), LOW),
            pltpu.VMEM((local, width), LOW),
            pltpu.VMEM((local, width), LOW),
            pltpu.VMEM((local, hidden), wide),
            pltpu.VMEM((local, hidden), wide),
            pltpu.VMEM((local + 16, hidden), LOW),
            pltpu.VMEM((local, hidden), LOW),
            pltpu.VMEM((local, width), LOW),
            pltpu.VMEM((local, width), wide),
            pltpu.VMEM((local, width), wide),
            pltpu.VMEM((local, width), LOW),
            pltpu.VMEM((local, width), wide),
            pltpu.VMEM((local, 128), wide),
            pltpu.VMEM((local, 128), wide),
            pltpu.VMEM((2, 3, local, width // 8), LOW),
            pltpu.VMEM((2, local, 128), wide),
            pltpu.VMEM((2 * local, hidden // 2), LOW),
            pltpu.VMEM((2 * local, width), LOW),
            *scatter_scratch(4, 128, 256),
            dma((20,)),
            dma((4, 4)),
            dma((4, 4)),
            dma((20,)),
            dma((20,)),
            *exchange_sems(2),
            dma((4, 4)),
            dma((4, 4)),
        ],
        compiler_params=pltpu.CompilerParams(
            collective_id=2, has_side_effects=True, vmem_limit_bytes=VMEM_BYTES
        ),
        name="middle",
    )(
        u, tokens, cotangent, post_gain.reshape(1, width), second_gain.reshape(1, width),
        mid_gain.reshape(1, hidden), w_out, w_up, w_down,
    )


HALF = 512
X_FIRST = (0, 3, 8, 13)
TAIL_ORDER = (
    1, 2, 0, 4, 500, 6, 7, 9, 101, 8, 5, 100, 3, 102, 600, 700, 15, 501, 201, 14,
    104, 108, 106, 103, 107, 202, 109, 302, 601, 502, 701, 301, 105, 12, 13, 200, 206, 204, 207, 402,
    300, 209, 115, 307, 306, 304, 309, 400, 602, 702, 208, 114, 800, 900, 205, 308, 11, 10, 203, 305,
    901, 303, 215, 409, 405, 112, 404, 406, 408, 407, 113, 214, 111, 212, 902, 314, 315, 403, 211, 110,
    312, 414, 213, 311, 415, 210, 412, 313, 401, 310, 411, 413, 410,
)


def tail_kernel(
    dq, dk, dv, tokens, gain, middle_in, triple_in, act_up, act_out, act_in, g_up, g_out, gains, scales,
    o_tokens, o_triple, o_out, o_up, o_gains,
    e_left, e_right, e_whole, e_first, e_second, e_near, e_far,
    triple, middle, tokens_s, grad_s, gain_s, gain_r, relay,
    local_sem, core_send, core_recv, x_send, x_recv, z_send, z_recv, s_send, s_recv, gain_send, gain_recv,
):
    place = Place()
    partner = place.core_partner()
    local, width = tokens.shape
    heads_width = dq.shape[1]
    seq_peers = [(place.dp, (place.seq + k) % 8) for k in range(1, 8)]
    dp_peers = [((place.dp + k) % 4, place.seq) for k in range(1, 4)]
    meet(seq_peers + dp_peers)

    def start_exchange(t):
        return ToTokens(
            place, (dv, dk, dq)[t], e_right.at[7 - t, pl.ds(0, local), :], relay.at[t],
            [sem.at[t] for sem in (x_send, x_recv, z_send, z_recv)], local_sem.at[13 + t],
        )

    exchanges = [start_exchange(t) for t in range(3)]

    load_triple = pltpu.make_async_copy(triple_in, triple, local_sem.at[16])
    load_middle = pltpu.make_async_copy(middle_in, middle, local_sem.at[17])

    sems = (local_sem, core_send, core_recv)
    ready = {"up": share_left(place, 0, act_up, e_left.at[0], local, *sems)}
    for k in range(4):
        part = g_up.at[:, pl.ds(k * BLOCK, BLOCK)]
        ready[k] = share(place, 2 + k, part, part, e_right.at[k], local, *sems)
    ready["out"] = share_left(place, 6, act_out, e_left.at[1], local, *sems)
    ready["out"] += share(place, 8, g_out, g_out, e_right.at[4], local, *sems)
    ready["in"] = share_left(place, 9, act_in, e_left.at[2], local, *sems)
    load_triple.start()
    load_middle.start()

    def write(p, value):
        at = pl.ds(p % 2 * HALF, HALF)
        if p < 8:
            o_up[:, pl.ds(p * HALF, HALF)] = value
        elif p < 10:
            o_out[:, at] = value
        else:
            o_triple[:, pl.ds((p - 10) * HALF, HALF)] = value

    engine = Scatter(
        place, (e_whole, e_first, e_second, e_near, e_far), (s_send, s_recv), X_FIRST,
        lambda p: e_left.at[0 if p < 8 else 1 if p < 10 else 2],
        lambda p: e_right.at[p // 2, :, pl.ds(p % 2 * HALF, HALF)], write,
    )
    gain_s[0:3, :] = gains[0:3, 0:width]
    for k in range(gains.shape[1] // width):
        gain_s[3 + k : 4 + k, :] = gains[3:4, pl.ds(k * width, width)]
    gain_s[7:8, :] = jnp.zeros((1, width), jnp.float32)
    gain_s[7:8, 0:128] = scales[...]
    def bring_back(t):
        exchanges[t].finish()
        slot = e_right.at[7 - t]
        move = remote(
            slot.at[pl.ds(0, local), :], slot.at[pl.ds(local, local), :],
            core_send.at[11 + t], core_recv.at[11 + t], partner,
        )
        move.start()
        return move

    def pull_normed(t):
        if t == 0:
            load_triple.wait()

        def one(n, carry):
            rows = pl.ds(pl.multiple_of(n * 256, 256), 256)
            part = nt(e_right[7 - t, pl.ds(0, local), :], triple[rows, pl.ds((2 - t) * width, width)])
            grad_s[:, rows] = part if t == 0 else grad_s[:, rows] + part
            return carry

        lax.fori_loop(0, width // 256, one, 0)

    def norm_rows(n, total):
        rows = pl.ds(pl.multiple_of(n * 128, 128), 128)
        unit, inverse = norm_parts(tokens[rows, :].astype(jnp.float32))
        grad = grad_s[rows, :]
        pulled = norm_pull(grad, unit, inverse, gain[...])
        tokens_s[rows, :] = (middle[rows, :] + pulled).astype(LOW)
        return total + jnp.sum(grad * unit, axis=0, keepdims=True)

    save_tokens = pltpu.make_async_copy(tokens_s, o_tokens, local_sem.at[18])

    def pull_norm(_):
        load_middle.wait()
        gain_s[0:1, :] = lax.fori_loop(0, local // 128, norm_rows, jnp.zeros((1, width), jnp.float32))
        save_tokens.start()

    def gain_moves(peers, first):
        out = [
            remote(gain_s, gain_r.at[first + k], gain_send.at[first + k], gain_recv.at[first + k], peer)
            for k, peer in enumerate(peers)
        ]
        for move in out:
            move.start()
        return out

    gain_steps = {}

    def sum_gains(step):
        if step == 0:
            gain_steps[0] = gain_moves(dp_peers, 0)
        elif step == 1:
            wait_all(gain_steps[0])
            gain_s[...] = gain_s[...] + gain_r[0] + gain_r[1] + gain_r[2]
            o_gains[7:8, :] = gain_s[7:8, 0:128]
            gain_steps[1] = gain_moves(seq_peers, 3)
        else:
            wait_all(gain_steps[1])
            total = gain_s[...]
            for k in range(7):
                total = total + gain_r[3 + k]
            gain_s[...] = total
            device = place.dp * 8 + place.seq
            pick = (
                lax.broadcasted_iota(jnp.int32, (width, 128), 0)
                == device * 32 + lax.broadcasted_iota(jnp.int32, (width, 128), 1)
            ).astype(jnp.float32)
            o_gains[0:3, :] = jnp.dot(
                gain_s[...], pick, preferred_element_type=jnp.float32, precision=lax.Precision.HIGHEST
            )[0:3]
            block = gain_s[:, pl.ds(pl.multiple_of((device % 8) * 128, 128), 128)]
            row = lax.broadcasted_iota(jnp.int32, block.shape, 0)
            o_gains[3:4, :] = jnp.sum(jnp.where(row == 3 + device // 8, block, 0.0), axis=0, keepdims=True)

    backs, waited = {}, set()

    def need(key):
        if key not in waited:
            wait_all(ready[key])
            waited.add(key)

    def compute(p):
        need("up" if p < 8 else "out" if p < 10 else "in")
        if p < 8:
            need(p // 2)
        elif p >= 10 and 7 - p // 2 in backs:
            backs.pop(7 - p // 2).wait()
        engine.compute(p)

    def bring(t):
        backs[t] = bring_back(t)

    act = (
        compute,
        lambda p: engine.advance(p, 1),
        lambda p: engine.advance(p, 2),
        lambda p: engine.advance(p, 3),
        lambda p: engine.advance(p, 4),
        lambda t: exchanges[t].pass_on(),
        bring,
        pull_normed,
        pull_norm,
        sum_gains,
    )
    for code in TAIL_ORDER:
        act[code // 100](code % 100)
    o_gains[4:7, :] = jnp.zeros((3, 128), jnp.float32)
    save_tokens.wait()
    for p in range(16):
        engine.settle(p)


def tail(dqkv, tokens, gain, middle, triple, acts, grads, gains, scales):
    local, width = tokens.shape
    heads_width = dqkv[0].shape[1]
    hidden = grads[0].shape[1]
    any_spec = pl.BlockSpec(memory_space=pl.ANY)
    vmem = pl.BlockSpec(memory_space=pltpu.VMEM)
    wide = jnp.float32
    dma = pltpu.SemaphoreType.DMA
    return pl.pallas_call(
        tail_kernel,
        out_shape=(
            jax.ShapeDtypeStruct((local, width), LOW),
            jax.ShapeDtypeStruct((width // 32, 3 * width), wide),
            jax.ShapeDtypeStruct((width // 32, width), wide),
            jax.ShapeDtypeStruct((width // 32, hidden), wide),
            jax.ShapeDtypeStruct((8, 128), wide),
        ),
        in_specs=[any_spec] * 3 + [vmem] * 2 + [any_spec] * 7 + [vmem] * 2,
        out_specs=(any_spec,) + (vmem,) * 4,
        scratch_shapes=[pltpu.VMEM((3, 2 * local, width // 2), LOW), pltpu.VMEM((8, 2 * local, width), LOW)]
        + scatter_scratch(16, 32, HALF)
        + [
            pltpu.VMEM((width, 3 * width), LOW),
            pltpu.VMEM((local, width), wide),
            pltpu.VMEM((local, width), LOW),
            pltpu.VMEM((local, width), wide),
            pltpu.VMEM((8, width), wide),
            pltpu.VMEM((10, 8, width), wide),
            pltpu.VMEM((3, 3, local, heads_width), LOW),
            dma((20,)),
            dma((20,)),
            dma((20,)),
            *exchange_sems(3),
            dma((4, 16)),
            dma((4, 16)),
            dma((10,)),
            dma((10,)),
        ],
        compiler_params=pltpu.CompilerParams(
            collective_id=3, has_side_effects=True, vmem_limit_bytes=VMEM_BYTES
        ),
        name="tail",
    )(*dqkv, tokens, gain.reshape(1, width), middle, triple, *acts, *grads, gains, scales)


def finish_kernel(count, *refs):
    ins, outs = refs[: count + 1], refs[count + 1 :]
    for k in range(count):
        outs[k][...] = ins[k][...]
    sums = ins[count]
    for row in range(3):
        outs[count + row][...] = sums[row, 0 : outs[count + row].shape[0]]
    outs[count + 3][...] = sums[3]
    row = sums[7:8, :]
    lane = lax.broadcasted_iota(jnp.int32, row.shape, 1)
    heads = outs[count + 4].shape[1]
    for h in range(heads):
        own = (lane >= h * HEAD) & (lane < (h + 1) * HEAD)
        outs[count + 4][:, h : h + 1] = jnp.sum(jnp.where(own, row, 0.0), axis=1, keepdims=True)


def finish(arrays, sums, own, heads):
    vmem = pl.BlockSpec(memory_space=pltpu.VMEM)
    wide = jnp.float32
    shapes = [jax.ShapeDtypeStruct(a.shape, a.dtype) for a in arrays]
    shapes += [jax.ShapeDtypeStruct((own,), wide)] * 3 + [jax.ShapeDtypeStruct((sums.shape[1],), wide), jax.ShapeDtypeStruct((1, heads), wide)]
    return pl.pallas_call(
        functools.partial(finish_kernel, len(arrays)),
        out_shape=tuple(shapes),
        in_specs=[vmem] * (len(arrays) + 1),
        out_specs=(vmem,) * len(shapes),
        name="finish",
    )(*arrays, sums)


def per_device(
    sizes,
    tokens,
    segment_ids,
    first_gain,
    triple_weight,
    head_scale,
    output_weight,
    post_gain,
    second_gain,
    up_weight,
    mid_gain,
    down_weight,
    cotangent,
):
    inputs = tokens[0].astype(jnp.float32)
    width = inputs.shape[1]
    doc_ids = lax.all_gather(segment_ids[0], "seq", axis=0, tiled=True)
    triple_full, output_full = (
        lax.all_gather(triple_weight, "dp", axis=0, tiled=True),
        lax.all_gather(output_weight, "dp", axis=0, tiled=True),
    )
    normed, pull_first = jax.vjp(layer_norm, inputs, first_gain)
    normed_low = normed.astype(jnp.bfloat16)
    triple = jnp.dot(normed_low, triple_full, preferred_element_type=jnp.float32).astype(
        jnp.bfloat16
    )
    queries, keys_all, values_all = (
        lax.all_to_all(triple[:, :width], "seq", split_axis=1, concat_axis=0, tiled=True),
        lax.all_to_all(
            triple[:, width : 2 * width], "seq", split_axis=1, concat_axis=0, tiled=True
        ),
        lax.all_to_all(triple[:, 2 * width :], "seq", split_axis=1, concat_axis=0, tiled=True),
    )
    heads_here = queries.shape[1] // HEAD
    starts = document_starts(doc_ids)
    attended, scaled, logsum = attend_forward(
        queries, keys_all, values_all, starts, head_scale
    )
    merged = lax.all_to_all(scaled, "seq", split_axis=0, concat_axis=1, tiled=True)
    projected = jnp.dot(merged, output_full, preferred_element_type=jnp.float32)
    post_normed, pull_post = jax.vjp(layer_norm, projected, post_gain)
    middle = inputs + post_normed
    second, pull_second = jax.vjp(layer_norm, middle, second_gain)
    second_low = second.astype(jnp.bfloat16)
    feed_up, feed_down = (
        lax.all_gather(up_weight, "dp", axis=0, tiled=True),
        lax.all_gather(down_weight, "dp", axis=0, tiled=True),
    )
    hidden = jnp.dot(second_low, feed_up, preferred_element_type=jnp.float32)
    activated, pull_mid = jax.vjp(gelu_norm, hidden, mid_gain)
    activated_low = activated.astype(jnp.bfloat16)
    layer_out = (
        middle + jnp.dot(activated_low, feed_down, preferred_element_type=jnp.float32)
    ).astype(jnp.bfloat16)
    upstream = cotangent[0]
    grad_act = times_transposed(upstream, feed_down)
    grad_hidden, grad_mid = pull_mid(grad_act)
    grad_hidden_low = grad_hidden.astype(jnp.bfloat16)
    grad_second_in = times_transposed(grad_hidden_low, feed_up)
    grad_middle_part, grad_second = pull_second(grad_second_in)
    grad_middle = upstream.astype(jnp.float32) + grad_middle_part
    grad_projected, grad_post = pull_post(grad_middle)
    grad_projected_low = grad_projected.astype(jnp.bfloat16)
    grad_merged = times_transposed(grad_projected_low, output_full).astype(jnp.bfloat16)
    grad_scaled = lax.all_to_all(
        grad_merged, "seq", split_axis=1, concat_axis=0, tiled=True
    )
    grad_queries, grad_keys, grad_values, scale_lanes = attend_backward(
        queries, keys_all, values_all, attended, grad_scaled, starts, head_scale, logsum
    )
    scale_terms = jnp.sum(scale_lanes.reshape(heads_here, HEAD), axis=1)
    back_queries, back_keys, back_values = (
        lax.all_to_all(
            grad_queries.astype(jnp.bfloat16), "seq", split_axis=0, concat_axis=1, tiled=True
        ),
        lax.all_to_all(
            grad_keys.astype(jnp.bfloat16), "seq", split_axis=0, concat_axis=1, tiled=True
        ),
        lax.all_to_all(
            grad_values.astype(jnp.bfloat16), "seq", split_axis=0, concat_axis=1, tiled=True
        ),
    )
    grad_triple_act = jnp.concatenate((back_queries, back_keys, back_values), axis=1)
    grad_normed = times_transposed(grad_triple_act, triple_full)
    grad_input_part, grad_first = pull_first(grad_normed)
    grad_tokens = (grad_middle + grad_input_part).astype(jnp.bfloat16)
    low = jnp.bfloat16
    grad_down = scatter_rows(transposed_times(activated_low, upstream).astype(low), sizes)
    grad_up = scatter_rows(transposed_times(second_low, grad_hidden_low).astype(low), sizes)
    grad_output = scatter_rows(transposed_times(merged, grad_projected_low).astype(low), sizes)
    gains = jnp.concatenate(
        (
            grad_first[:, None],
            grad_post[:, None],
            grad_second[:, None],
            grad_mid.reshape(width, -1),
        ),
        axis=1,
    )
    gains = jnp.pad(gains, ((0, 0), (0, 128 - gains.shape[1])))
    grad_triple = scatter_rows(
        jnp.concatenate(
            (transposed_times(normed_low, grad_triple_act).astype(low), gains.astype(low)), axis=1
        ),
        sizes,
    )
    gain_sums = grad_triple[:, 3 * width :]
    grad_scale = lax.psum(scale_terms, "dp")
    return (
        layer_out[None],
        grad_tokens[None],
        gain_sums[:, 0],
        grad_triple[:, : 3 * width],
        grad_scale,
        grad_output,
        gain_sums[:, 1],
        gain_sums[:, 2],
        grad_up,
        gain_sums[:, 3 : 3 + mid_gain.shape[0] // width].reshape(-1),
        grad_down,
    )


def per_device_chips(
    sizes,
    tokens,
    segment_ids,
    first_gain,
    triple_weight,
    head_scale,
    output_weight,
    post_gain,
    second_gain,
    up_weight,
    mid_gain,
    down_weight,
    cotangent,
):
    width, hidden = tokens.shape[2], up_weight.shape[1]
    heads_here = width // HEAD // sizes[1]
    values, keys, queries, normed, starts, triple_full, output_full, up_full = front(
        tokens[0], first_gain, segment_ids, triple_weight, output_weight, up_weight
    )
    attended, scaled, logsum = attend_forward(queries, keys, values, starts, head_scale)
    layer_out, grad_middle, grad_scaled, merged, second_low, grad_hidden, grad_projected, gains, grad_down = middle(
        scaled, tokens[0], cotangent[0], post_gain, second_gain, mid_gain, output_full, up_full, down_weight
    )
    grad_queries, grad_keys, grad_values, scale_lanes = attend_backward(
        queries, keys, values, attended, grad_scaled, starts, head_scale, logsum
    )
    grad_tokens, grad_triple, grad_output, grad_up, sums = tail(
        (grad_queries, grad_keys, grad_values),
        tokens[0],
        first_gain,
        grad_middle,
        triple_full,
        (second_low, merged, normed),
        (grad_hidden, grad_projected),
        gains,
        scale_lanes,
    )
    layer_out, grad_tokens, grad_triple, grad_output, grad_up, grad_down, first, post, second, mid, scale = finish(
        (layer_out, grad_tokens, grad_triple, grad_output, grad_up, grad_down), sums, width // 32, heads_here
    )
    return (
        layer_out[None],
        grad_tokens[None],
        first,
        grad_triple,
        scale[0],
        grad_output,
        post,
        second,
        grad_up,
        mid,
        grad_down,
    )


def solution(mesh):
    placed = (
        P("dp", "seq", None),
        P("dp", "seq"),
        P(),
        P("dp", None),
        P(),
        P("dp", None),
        P(),
        P(),
        P("dp", None),
        P(),
        P("dp", None),
        P("dp", "seq", None),
    )
    sizes = (mesh.shape["dp"], mesh.shape["seq"])
    program = per_device_chips if sizes == (4, 8) else per_device
    return jax.shard_map(
        functools.partial(program, sizes),
        mesh=mesh,
        in_specs=placed,
        out_specs=(
            P("dp", "seq", None),
            P("dp", "seq", None),
            P(("dp", "seq")),
            P(("dp", "seq"), None),
            P("seq"),
            P(("dp", "seq"), None),
            P(("dp", "seq")),
            P(("dp", "seq")),
            P(("dp", "seq"), None),
            P(("dp", "seq")),
            P(("dp", "seq"), None),
        ),
        check_vma=False,
    )
```

```python
import functools
import jax
import jax.numpy as jnp
from jax import lax
from jax.sharding import PartitionSpec as P
from jax.experimental import pallas as pl
from jax.experimental.pallas import tpu as pltpu

HEAD = 64
NEG = -1e30
BQ = 256
QB = 1024
KB = 512


def nt(a, b):
    return lax.dot_general(a, b, (((1,), (1,)), ((), ())), preferred_element_type=jnp.float32)


def tn(a, b):
    return lax.dot_general(a, b, (((0,), (0,)), ((), ())), preferred_element_type=jnp.float32)


def stack_heads(block, heads):
    if heads == 1:
        return block
    lane = lax.broadcasted_iota(jnp.int32, block.shape, 1)
    zero = jnp.zeros_like(block)
    return jnp.concatenate(
        [jnp.where((lane >= h * HEAD) & (lane < (h + 1) * HEAD), block, zero) for h in range(heads)],
        axis=0,
    )


def unstack_heads(wide, heads):
    rows = wide.shape[1] // heads
    return jnp.concatenate(
        [wide[h * HEAD : (h + 1) * HEAD, h * rows : (h + 1) * rows] for h in range(heads)], axis=0
    )


def scale_row(scale_ref, width):
    heads = width // HEAD
    first = lax.axis_index("seq") * heads
    lane = lax.broadcasted_iota(jnp.int32, (1, width), 1)
    row = jnp.full((1, width), scale_ref[first], jnp.float32)
    for h in range(1, heads):
        row = jnp.where(lane >= h * HEAD, scale_ref[first + h], row)
    return row


def forward_kernel(heads, first_ref, q_ref, k_ref, v_ref, start_ref, scale_ref,
                   o_ref, u_ref, lse_ref, m_s, l_s, acc_s):
    rows, step_rows = QB, KB
    scale = scale_row(scale_ref, q_ref.shape[1])
    ratio = rows // step_rows

    def one(i, carry):
        mine = pl.ds(pl.multiple_of(i * rows, rows), rows)
        queries = stack_heads(q_ref[mine, :] * jnp.bfloat16(HEAD ** -0.5), heads)
        starts = jnp.concatenate([start_ref[i * (rows // BQ) + k] for k in range(rows // BQ)] * heads, axis=1)

        def scores_of(j, count, queries, starts):
            at = pl.ds(pl.multiple_of(j * BQ, BQ), count)
            scores = nt(k_ref[at, :], queries)
            if starts is not None:
                key = j * BQ + lax.broadcasted_iota(jnp.int32, scores.shape, 0)
                scores = jnp.where(key >= starts, scores, NEG)
            return at, scores

        def fold(at, scores, columns):
            before = m_s[:, columns]
            highest = jnp.maximum(before, jnp.max(scores, axis=0, keepdims=True))
            fade = jnp.exp(before - highest)
            weights = jnp.exp(scores - highest)
            m_s[:, columns] = highest
            l_s[:, columns] = l_s[:, columns] * fade + jnp.sum(weights, axis=0, keepdims=True)
            acc_s[:, columns] = acc_s[:, columns] * fade + tn(v_ref[at, :], weights.astype(jnp.bfloat16))

        def step(j, masked):
            at, scores = scores_of(j * (step_rows // BQ), step_rows, queries, starts if masked else None)
            fold(at, scores, slice(None))

        for k in range(rows // BQ):
            wide = rows - k * BQ
            late = [slice(h * rows + k * BQ, (h + 1) * rows) for h in range(heads)]
            some = queries if k == 0 else jnp.concatenate([queries[c] for c in late], axis=0)
            start = starts if k == 0 else jnp.concatenate([starts[:, c] for c in late], axis=1)
            at, scores = scores_of(i * (rows // BQ) + k, BQ, some, start)
            key = lax.broadcasted_iota(jnp.int32, scores.shape, 0)
            for h in range(heads):
                part = scores[:, h * wide : (h + 1) * wide]
                lane = lax.broadcasted_iota(jnp.int32, part.shape, 1)
                part = jnp.where(key[:, :wide] <= lane, part, NEG)
                if k == 0:
                    highest = jnp.max(part, axis=0, keepdims=True)
                    weights = jnp.exp(part - highest)
                    m_s[:, late[h]] = highest
                    l_s[:, late[h]] = jnp.sum(weights, axis=0, keepdims=True)
                    acc_s[:, late[h]] = tn(v_ref[at, :], weights.astype(jnp.bfloat16))
                else:
                    fold(at, part, late[h])

        low = first_ref[i * (rows // BQ), 0, 0] // step_rows
        last = first_ref[i * (rows // BQ) + rows // BQ - 1, 0, BQ - 1]
        full = jnp.minimum((last + step_rows - 1) // step_rows, i * ratio)

        def plain(j, carry):
            step(j, False)
            return carry

        def edge(j, carry):
            step(j, True)
            return carry

        lax.fori_loop(full, i * ratio, plain, 0)
        lax.fori_loop(low, full, edge, 0)
        total = l_s[...]
        out = unstack_heads(acc_s[...] * (1.0 / total), heads).T
        o_ref[mine, :] = out
        u_ref[mine, :] = (out * scale).astype(jnp.bfloat16)
        logsum = m_s[...] + jnp.log(total)
        for k in range(rows // BQ):
            lse_ref[i * (rows // BQ) + k] = jnp.concatenate(
                [logsum[:, h * rows + k * BQ : h * rows + (k + 1) * BQ] for h in range(heads)], axis=1
            )
        return carry

    lax.fori_loop(0, q_ref.shape[0] // rows, one, 0)


def attend_forward(queries, keys, values, starts, scales):
    length, width = queries.shape
    heads = width // HEAD
    vmem = pl.BlockSpec(memory_space=pltpu.VMEM)
    return pl.pallas_call(
        functools.partial(forward_kernel, heads),
        out_shape=(
            jax.ShapeDtypeStruct((length, width), jnp.float32),
            jax.ShapeDtypeStruct((length, width), jnp.bfloat16),
            jax.ShapeDtypeStruct((length // BQ, 1, heads * BQ), jnp.float32),
        ),
        in_specs=[pl.BlockSpec(memory_space=pltpu.SMEM)] + [vmem] * 4 + [pl.BlockSpec(memory_space=pltpu.SMEM)],
        out_specs=(vmem,) * 3,
        scratch_shapes=[
            pltpu.VMEM((1, heads * QB), jnp.float32),
            pltpu.VMEM((1, heads * QB), jnp.float32),
            pltpu.VMEM((width, heads * QB), jnp.float32),
        ],
        cost_estimate=pl.CostEstimate(
            flops=length * length * width, bytes_accessed=16 * length * width, transcendentals=0
        ),
        name="attend_forward",
    )(starts, queries, keys, values, starts, scales)


def backward_kernel(heads, first_ref, q_ref, k_ref, v_ref, o_ref, du_ref, start_ref, scale_ref, lse_ref,
                    dq_ref, dk_ref, dv_ref, ds_ref, qs_s, dos_s, delta_s, dqt_s, dk_s, dv_s):
    rows, group = BQ, 1
    blocks = qs_s.shape[0]
    scale = scale_row(scale_ref, q_ref.shape[1])

    def prepare(i, total):
        at = pl.ds(pl.multiple_of(i * rows, rows), rows)
        qs_s[i] = stack_heads(q_ref[at, :] * jnp.bfloat16(HEAD ** -0.5), heads)
        grad = du_ref[at, :].astype(jnp.float32)
        out = o_ref[at, :]
        low = (grad * scale).astype(jnp.bfloat16)
        dos_s[i] = stack_heads(low, heads)
        inner = (low.astype(jnp.float32) * out).T
        delta_s[i] = jnp.concatenate(
            [jnp.sum(inner[h * HEAD : (h + 1) * HEAD], axis=0, keepdims=True) for h in range(heads)],
            axis=1,
        )
        dqt_s[i] = jnp.zeros(dqt_s.shape[1:], jnp.float32)
        return total + jnp.sum(grad * out, axis=0, keepdims=True)

    ds_ref[...] = lax.fori_loop(0, blocks, prepare, jnp.zeros(ds_ref.shape, jnp.float32))

    def one(j, carry):
        mine = pl.ds(pl.multiple_of(j * BQ, BQ), BQ)
        keys, values = k_ref[mine, :], v_ref[mine, :]

        def step(i, masked, diagonal):
            queries, grads = qs_s[i], dos_s[i]
            scores = nt(keys, queries)
            if masked or diagonal:
                key = j * BQ + lax.broadcasted_iota(jnp.int32, scores.shape, 0)
                starts = jnp.concatenate([start_ref[i * group + k] for k in range(group)] * heads, axis=1)
                allowed = key >= starts
                if diagonal:
                    lane = lax.broadcasted_iota(jnp.int32, scores.shape, 1) & (rows - 1)
                    allowed = allowed & (key <= i * rows + lane)
                scores = jnp.where(allowed, scores, NEG)
            weights = jnp.exp(scores - lse_ref[i])
            pulls = nt(values, grads)
            low = (weights * (pulls - delta_s[i])).astype(jnp.bfloat16)
            part_v = jnp.dot(weights.astype(jnp.bfloat16), grads, preferred_element_type=jnp.float32)
            part_k = jnp.dot(low, queries, preferred_element_type=jnp.float32)
            part_q = tn(keys, low)
            if diagonal:
                dv_s[...] = part_v
                dk_s[...] = part_k
            else:
                dv_s[...] += part_v
                dk_s[...] += part_k
            return part_q

        high, full = jnp.int32(0), jnp.int32(0)
        for i in range(blocks):
            high += (first_ref[i * group, 0, 0] // BQ <= j).astype(jnp.int32)
            full += (first_ref[i * group + group - 1, 0, BQ - 1] <= j * BQ).astype(jnp.int32)
        own = j // group
        full = jnp.maximum(full, own + 1)

        def plain(i, carry):
            dqt_s[i] += step(i, False, False)
            return carry

        def edge(i, carry):
            dqt_s[i] += step(i, True, False)
            return carry

        dqt_s[own] += step(own, False, True)
        lax.fori_loop(own + 1, full, plain, 0)
        lax.fori_loop(full, high, edge, 0)
        dk_ref[mine, :] = dk_s[...].astype(jnp.bfloat16)
        dv_ref[mine, :] = dv_s[...].astype(jnp.bfloat16)
        return carry

    lax.fori_loop(0, blocks * group, one, 0)

    def finish(i, carry):
        at = pl.ds(pl.multiple_of(i * rows, rows), rows)
        dq_ref[at, :] = (unstack_heads(dqt_s[i], heads).T * HEAD ** -0.5).astype(jnp.bfloat16)
        return carry

    lax.fori_loop(0, blocks, finish, 0)


def attend_backward(queries, keys, values, outs, grads, starts, scales, logsum):
    length, width = queries.shape
    heads = width // HEAD
    blocks = length // BQ
    vmem = pl.BlockSpec(memory_space=pltpu.VMEM)
    return pl.pallas_call(
        functools.partial(backward_kernel, heads),
        out_shape=(jax.ShapeDtypeStruct((length, width), jnp.bfloat16),) * 3
        + (jax.ShapeDtypeStruct((1, width), jnp.float32),),
        in_specs=[pl.BlockSpec(memory_space=pltpu.SMEM)] + [vmem] * 6 + [pl.BlockSpec(memory_space=pltpu.SMEM), vmem],
        out_specs=(vmem,) * 4,
        scratch_shapes=[
            pltpu.VMEM((blocks, heads * BQ, width), jnp.bfloat16),
            pltpu.VMEM((blocks, heads * BQ, width), jnp.bfloat16),
            pltpu.VMEM((blocks, 1, heads * BQ), jnp.float32),
            pltpu.VMEM((blocks, width, heads * BQ), jnp.float32),
            pltpu.VMEM((BQ, width), jnp.float32),
            pltpu.VMEM((BQ, width), jnp.float32),
        ],
        cost_estimate=pl.CostEstimate(
            flops=3 * length * length * width, bytes_accessed=32 * length * width, transcendentals=0
        ),
        name="attend_backward",
    )(starts, queries, keys, values, outs, grads, starts, scales, logsum)


def document_starts(doc_ids):
    length = doc_ids.shape[0]
    names = jnp.arange(8, dtype=jnp.int32)
    counts = jnp.sum(doc_ids[None, :] < names[:, None], axis=1, dtype=jnp.int32)
    starts = jnp.sum(
        jnp.where(doc_ids[:, None] == names[None, :], counts[None, :], 0), axis=1, dtype=jnp.int32
    )
    return starts.reshape(length // BQ, 1, BQ)


def layer_norm(values, gains):
    center = values - jnp.mean(values, axis=-1, keepdims=True)
    spread = jnp.mean(center * center, axis=-1, keepdims=True)
    return center * lax.rsqrt(spread + 1e-05) * gains


def gelu_norm(hidden, gains):
    return layer_norm(jax.nn.gelu(hidden, approximate=True), gains)


def transposed_times(left, right):
    return lax.dot_general(
        left, right, (((0,), (0,)), ((), ())), preferred_element_type=jnp.float32
    )


def times_transposed(left, right):
    return lax.dot_general(
        left, right, (((1,), (1,)), ((), ())), preferred_element_type=jnp.float32
    )


def scatter_rows(partial, sizes):
    current = partial
    for axis, size in zip(("dp", "seq"), sizes):
        place = lax.axis_index(axis)
        bits = size.bit_length() - 1
        pieces = current.reshape((2,) * bits + (-1, current.shape[-1]))
        for bit in range(bits):
            at = bits - 1 - bit
            mine = (place >> bit) & 1
            give = lax.dynamic_index_in_dim(pieces, 1 - mine, at, keepdims=False)
            keep = lax.dynamic_index_in_dim(pieces, mine, at, keepdims=False)
            got = lax.ppermute(give, axis, [(i, i ^ (1 << bit)) for i in range(size)])
            pieces = (keep.astype(jnp.float32) + got.astype(jnp.float32)).astype(jnp.bfloat16)
        current = pieces
    return current.astype(jnp.float32)


MESH = pl.DeviceIdType.MESH
LOW = jnp.bfloat16
BLOCK = 1024
VMEM_BYTES = 66_000_000


class Place:
    def __init__(self):
        self.dp, self.seq = lax.axis_index("dp"), lax.axis_index("seq")
        self.core, self.y = self.dp % 2, self.dp // 2
        self.x, self.z = self.seq % 2, self.seq // 2
        self.z0, self.z1 = self.z % 2, self.z // 2

    def core_partner(self):
        return (self.dp + 1 - 2 * self.core, self.seq)

    def y_partner(self):
        return (self.dp + 2 - 4 * self.y, self.seq)

    def x_partner(self):
        return (self.dp, self.seq + 1 - 2 * self.x)

    def near_partner(self):
        return (self.dp, self.seq + 2 - 4 * self.z0)

    def far_partner(self):
        return (self.dp, self.seq + 4 - 8 * self.z1)


def meet(devices):
    barrier = pltpu.get_barrier_semaphore()
    for device in devices:
        pl.semaphore_signal(barrier, inc=1, device_id=device, device_id_type=MESH)
    pl.semaphore_wait(barrier, len(devices))


def remote(source, target, send, receive, device):
    return pltpu.make_async_remote_copy(
        src_ref=source,
        dst_ref=target,
        send_sem=send,
        recv_sem=receive,
        device_id=device,
        device_id_type=MESH,
    )


def lanes_of(z, x, width):
    return pl.ds(pl.multiple_of((z * 2 + x) * width, 128), width)


def rows_of(z, x, local):
    return pl.ds(pl.multiple_of((z * 2 + x) * local, 128), local)


class ToHeads:
    def __init__(self, place, part, target, relay, sems, keep_sem):
        self.place, self.part, self.target, self.relay, self.sems = place, part, target, relay, sems
        self.keep_sem, self.moves, self.sends = keep_sem, [], []

    def other(self, m):
        place = self.place
        low = place.z0 + (m % 2) * (1 - 2 * place.z0)
        high = place.z1 + (m // 2) * (1 - 2 * place.z1)
        return high * 2 + low

    def start(self, steps=(2, 3, 1, 0)):
        place = self.place
        x_send, x_recv, z_send, z_recv = self.sems
        local, width = self.relay.shape[-2:]
        rows = rows_of(place.z, place.x, local)
        for m in steps:
            source = self.part.at[:, lanes_of(self.other(m), 1 - place.x, width)]
            landing = self.target.at[rows, :] if m == 0 else self.relay.at[m - 1]
            move = remote(source, landing, x_send.at[m], x_recv.at[m], place.x_partner())
            move.start()
            (self.moves if m == 0 else self.sends).append(move)
        for m in steps:
            z = self.other(m)
            source = self.part.at[:, lanes_of(z, place.x, width)]
            if m == 0:
                move = pltpu.make_async_copy(source, self.target.at[rows, :], self.keep_sem)
            else:
                device = (place.dp, z * 2 + place.x)
                move = remote(source, self.target.at[rows, :], z_send.at[m - 1], z_recv.at[m - 1], device)
            move.start()
            self.moves.append(move)

    def pass_on(self, steps=(2, 3, 1)):
        place, local = self.place, self.relay.shape[-2]
        x_send, x_recv, z_send, z_recv = self.sems
        rows = rows_of(place.z, 1 - place.x, local)
        for m in steps:
            here = self.relay.at[m - 1]
            remote(here, here, x_send.at[m], x_recv.at[m], place.x_partner()).wait_recv()
            device = (place.dp, self.other(m) * 2 + place.x)
            move = remote(here, self.target.at[rows, :], z_send.at[m + 2], z_recv.at[m + 2], device)
            move.start()
            self.moves.append(move)

    def finish(self):
        for move in self.moves:
            move.wait()
        for move in self.sends:
            move.wait_send()


class ToTokens:
    def __init__(self, place, source, target, relay, sems, keep_sem):
        self.place, self.target, self.relay, self.sems = place, target, relay, sems
        x_send, x_recv, z_send, z_recv = sems
        local, width = relay.shape[-2:]
        self.moves, self.sends = [], []
        lanes = lanes_of(place.z, place.x, width)
        for x, first in ((1 - place.x, 0), (place.x, 3)):
            for k in (2, 1, 3):
                z, index = (place.z + k) % 4, first + k - 1
                landing = relay.at[k - 1] if first == 0 else target.at[:, lanes]
                move = remote(
                    source.at[rows_of(z, x, local), :],
                    landing,
                    z_send.at[index],
                    z_recv.at[index],
                    (place.dp, z * 2 + place.x),
                )
                move.start()
                (self.sends if first == 0 else self.moves).append(move)
        move = remote(
            source.at[rows_of(place.z, 1 - place.x, local), :],
            target.at[:, lanes],
            x_send.at[0],
            x_recv.at[0],
            place.x_partner(),
        )
        move.start()
        self.moves.append(move)
        move = pltpu.make_async_copy(
            source.at[rows_of(place.z, place.x, local), :], target.at[:, lanes], keep_sem
        )
        move.start()
        self.moves.append(move)

    def pass_on(self):
        place, width = self.place, self.relay.shape[-1]
        x_send, x_recv, z_send, z_recv = self.sems
        for k in (2, 1, 3):
            here = self.relay.at[k - 1]
            remote(here, here, z_send.at[k - 1], z_recv.at[k - 1], place.near_partner()).wait_recv()
            lanes = lanes_of((place.z + 4 - k) % 4, place.x, width)
            move = remote(here, self.target.at[:, lanes], x_send.at[k], x_recv.at[k], place.x_partner())
            move.start()
            self.moves.append(move)

    def finish(self):
        for move in self.moves:
            move.wait()
        for move in self.sends:
            move.wait_send()


def exchange_sems(count):
    dma = pltpu.SemaphoreType.DMA
    return [dma((count, 4)), dma((count, 4)), dma((count, 6)), dma((count, 6))]


def share(place, index, ours, theirs, target, local, here_sem, core_send, core_recv):
    here = pltpu.make_async_copy(ours, target.at[pl.ds(0, local), :], here_sem.at[index])
    there = remote(
        theirs, target.at[pl.ds(local, local), :], core_send.at[index], core_recv.at[index], place.core_partner()
    )
    here.start()
    there.start()
    return [here, there]


def share_left(place, index, source, target, local, *sems):
    half = source.shape[1] // 2
    columns = half // 2
    out = []
    for y in range(2):
        ours, theirs = (
            source.at[pl.ds(0, local), pl.ds(pl.multiple_of(y * half + core * columns, 128), columns)]
            for core in (place.core, 1 - place.core)
        )
        out += share(place, index + y, ours, theirs, target.at[:, pl.ds(y * columns, columns)], local, *sems)
    return out


def wait_all(copies):
    for copy in copies:
        copy.wait()


def norm_parts(values):
    center = values - jnp.mean(values, axis=-1, keepdims=True)
    inverse = lax.rsqrt(jnp.mean(center * center, axis=-1, keepdims=True) + 1e-05)
    return center * inverse, inverse


def norm_pull(grad, unit, inverse, gain):
    scaled = grad * gain
    return inverse * (
        scaled
        - jnp.mean(scaled, axis=-1, keepdims=True)
        - unit * jnp.mean(scaled * unit, axis=-1, keepdims=True)
    )


class Scatter:
    def __init__(self, place, refs, sems, x_first, left, right, write):
        self.place, self.x_first, self.left, self.right, self.write = place, x_first, left, right, write
        self.whole, self.first, self.second, self.near, self.far = refs
        self.send, self.receive = sems
        self.rows, self.columns = self.whole.shape[-2:]

    def axes(self, p):
        place = self.place
        if p not in self.x_first:
            return place.y, place.x, place.y_partner(), place.x_partner()
        return place.x, place.y, place.x_partner(), place.y_partner()

    def copy(self, p, stage):
        place = self.place
        mine, other, partner, second = self.axes(p)
        if stage == 0:
            source, target, device = self.whole.at[p, 1 - mine], self.first.at[p], partner
        elif stage == 1:
            source, target, device = self.first.at[p, :, :, 1 - other], self.second.at[p], second
        elif stage == 2:
            source, target, device = self.second.at[p, :, 1 - place.z0], self.near.at[p], place.near_partner()
        else:
            source, target, device = self.near.at[p, 1 - place.z1], self.far.at[p], place.far_partner()
        index = p
        return remote(source, target, self.send.at[stage, index], self.receive.at[stage, index], device)

    def compute(self, p):
        left, right = self.left(p), self.right(p)
        rows = self.rows

        def one(y, carry):
            for half in range(2):
                span = 4 * rows
                at = pl.ds(pl.multiple_of(y * 8 * rows + half * span, 128), span)
                block = tn(left[:, at], right[...]).astype(LOW)
                for k in range(4):
                    x = k % 2
                    part = block[k * rows : (k + 1) * rows]
                    if p not in self.x_first:
                        self.whole[p, y, half, k // 2, x] = part
                    else:
                        self.whole[p, x, half, k // 2, y] = part
            return carry

        lax.fori_loop(0, 2, one, 0)
        self.copy(p, 0).start()

    def advance(self, p, stage):
        place = self.place
        mine, other, _, _ = self.axes(p)
        wide = jnp.float32
        self.copy(p, stage - 1).wait_recv()
        if stage == 1:

            def add(k, carry):
                a, b, s = k // 4, k // 2 % 2, k % 2
                total = self.first[p, a, b, s].astype(wide) + self.whole[p, mine, a, b, s].astype(wide)
                self.first[p, a, b, s] = total.astype(LOW)
                return carry

            lax.fori_loop(0, 8, add, 0)
        elif stage == 2:

            def add(z, carry):
                a, b = z // 2, z % 2
                total = self.second[p, a, b].astype(wide) + self.first[p, a, b, other].astype(wide)
                self.second[p, a, b] = total.astype(LOW)
                return carry

            lax.fori_loop(0, 4, add, 0)
        elif stage == 3:

            def add(a, carry):
                total = self.near[p, a].astype(wide) + self.second[p, a, place.z0].astype(wide)
                self.near[p, a] = total.astype(LOW)
                return carry

            lax.fori_loop(0, 2, add, 0)
        else:
            self.write(p, self.near[p, place.z1].astype(wide) + self.far[p].astype(wide))
            return
        self.copy(p, stage).start()

    def settle(self, p):
        for stage in range(4):
            self.copy(p, stage).wait_send()


def scatter_scratch(pieces, rows, columns):
    return [
        pltpu.VMEM((pieces, 2, 2, 2, 2, rows, columns), LOW),
        pltpu.VMEM((pieces, 2, 2, 2, rows, columns), LOW),
        pltpu.VMEM((pieces, 2, 2, rows, columns), LOW),
        pltpu.VMEM((pieces, 2, rows, columns), LOW),
        pltpu.VMEM((pieces, rows, columns), LOW),
    ]


class Gather:
    def __init__(self, place, sems):
        self.place = place
        self.send, self.receive = sems

    def copies(self, index, own, full, rows, shared):
        place = self.place
        across = place.dp + 2 - 4 * place.y
        half = rows // 2

        def move(kind, source, target, device):
            return remote(source, target, self.send.at[kind, index], self.receive.at[kind, index], device)

        out = [move(0, own, full(place.dp, 0, rows), place.core_partner())]
        if shared:
            first = place.x * half
            out.append(
                move(1, own.at[pl.ds(pl.multiple_of(first, half), half), :],
                     full(place.dp, first, half), place.y_partner())
            )
            landed = full(across, first, half)
            out.append(move(2, landed, landed, place.x_partner()))
        else:
            out.append(move(1, own, full(place.dp, 0, rows), place.y_partner()))
            out.append(None)
        landed = full(across, 0, rows)
        out.append(move(3, landed, landed, place.core_partner()))
        return out


FRONT_ALONE = (0, 2, 5, 8)
FRONT_ORDER = (
    500, 200, 101, 0, 201, 1, 300, 600, 202, 301, 2, 103, 104, 302, 203, 3, 205, 204,
    106, 303, 107, 206, 208, 207, 405, 406, 404, 408, 407,
)


def front_kernel(
    tokens, gain, ids, w_triple, w_out, w_up,
    o_v, o_k, o_q, o_normed, o_starts, o_triple, o_out, o_up,
    triple_s, part_s, ids_s, bounce, relay, send, receive, x_send, x_recv, z_send, z_recv, ids_send, ids_recv, local_sem,
):
    place = Place()
    exchange_sem = (x_send, x_recv, z_send, z_recv)
    local, width = tokens.shape
    heads_width = o_v.shape[1]
    meet([(place.dp, (place.seq + k) % 8) for k in range(1, 8)] + [place.core_partner(), place.y_partner()])
    gather = Gather(place, (send, receive))

    def columns(weight, at):
        def full(d, first, count):
            return weight.at[pl.ds(pl.multiple_of(d * 256 + first, 128), count), at]

        return full

    half = width // 2
    spans = [
        (2 * width + (1 - place.z1) * half, half), (2 * width + place.z1 * half, half), (width, width), (0, width)
    ]
    spans = [(pl.multiple_of(first, 512), count) for first, count in spans]
    plans = []
    for first, count in spans:
        plans.append((w_triple.at[:, pl.ds(first, count)], columns(triple_s, pl.ds(first, count))))
    plans.append((w_out, columns(o_out, pl.ds(0, width))))
    for k in range(w_up.shape[1] // width):
        plans.append((w_up.at[:, pl.ds(k * width, width)], columns(o_up, pl.ds(k * width, width))))
    alone = FRONT_ALONE
    chunks = [
        gather.copies(n, own, full, 256, n not in alone) for n, (own, full) in enumerate(plans)
    ]
    mine = []
    for n, (own, full) in enumerate(plans):
        chunks[n][1].start()
        chunks[n][0].start()
        target = full(place.dp, 0, 256) if n < 4 else bounce.at[n - 4]
        copy = pltpu.make_async_copy(own, target, local_sem.at[n])
        copy.start()
        mine.append(copy)
        if n == 0:
            news = []
            for k in range(1, 8):
                peer = (place.dp, (place.seq + k) % 8)
                move = remote(ids, ids_s.at[place.seq], ids_send.at[k - 1], ids_recv.at[k - 1], peer)
                move.start()
                news.append(move)
            ids_s[pl.ds(place.seq, 1)] = ids[...].reshape(1, 1, local)

    def norm_rows(n, carry):
        rows = pl.ds(pl.multiple_of(n * 128, 128), 128)
        values = tokens[rows, :].astype(jnp.float32)
        o_normed[rows, :] = (norm_parts(values)[0] * gain[...]).astype(LOW)
        return carry

    moves = []
    exchanges = [
        ToHeads(
            place, part_s.at[t], target, relay.at[t], [sem.at[t] for sem in exchange_sem], local_sem.at[12 + t]
        )
        for t, target in enumerate((o_v, o_k, o_q))
    ]
    far, near = (2, 3), (1, 0)
    steps = ((0, far), (0, near), (1, far + near), (2, far + near))

    def project(n):
        first, count = spans[n]
        t, reach = steps[n]

        def one(c, carry):
            from_at = pl.ds(pl.multiple_of(first + c * 256, 256), 256)
            at = pl.ds(pl.multiple_of(first - (2 - t) * width + c * 256, 256), 256)
            part_s[t, :, at] = jnp.dot(
                o_normed[...], triple_s[:, from_at], preferred_element_type=jnp.float32
            ).astype(LOW)
            return carry

        lax.fori_loop(0, count // 256, one, 0)
        exchanges[t].start(reach)
        at = pl.ds(first, count)
        save = pltpu.make_async_copy(triple_s.at[:, at], o_triple.at[:, at], local_sem.at[15 + n])
        save.start()
        moves.append(save)

    def pass_on(n):
        t, reach = steps[n]
        exchanges[t].pass_on(tuple(m for m in reach if m))

    def forward(n):
        if chunks[n][2] is not None:
            chunks[n][1].wait_recv()
            chunks[n][2].start()

    def across(n):
        (chunks[n][1] if chunks[n][2] is None else chunks[n][2]).wait_recv()
        chunks[n][3].start()

    def finish(n):
        chunks[n][0].wait_recv()
        chunks[n][3].wait_recv()
        mine[n].wait()
        project(n)

    def put_back(n):
        chunks[n][0].wait_recv()
        chunks[n][3].wait_recv()
        mine[n].wait()
        copy = pltpu.make_async_copy(bounce.at[n - 4], plans[n][1](place.dp, 0, 256), local_sem.at[n])
        copy.start()
        moves.append(copy)

    def document_starts_here(_):
        for move in news:
            move.wait()
        every = ids_s[...]
        starts = jnp.zeros_like(every)
        for d in range(1, 8):
            before = jnp.sum((every < d).astype(jnp.int32), axis=2, keepdims=True)
            before = jnp.sum(before, axis=0, keepdims=True)
            starts = jnp.where(every == d, before, starts)
        for b in range(o_starts.shape[0]):
            for piece in range(BQ // 128):
                at = b * BQ + piece * 128
                o_starts[b, :, pl.ds(piece * 128, 128)] = starts[
                    at // local, :, at % local : at % local + 128
                ]

    act = (
        finish, forward, across, pass_on, put_back,
        lambda n: lax.fori_loop(0, local // 128, norm_rows, 0), document_starts_here,
    )
    for code in FRONT_ORDER:
        act[code // 100](code % 100)
    for move in moves:
        move.wait()
    for exchange in exchanges:
        exchange.finish()
    for chunk in chunks:
        for copy in chunk:
            if copy is not None:
                copy.wait_send()


def front(tokens, gain, ids, w_triple, w_out, w_up):
    local, width = tokens.shape
    heads_width = width // 8
    length = local * 8
    hidden = w_up.shape[1]
    any_spec = pl.BlockSpec(memory_space=pl.ANY)
    vmem = pl.BlockSpec(memory_space=pltpu.VMEM)
    dma = pltpu.SemaphoreType.DMA
    one = jax.ShapeDtypeStruct((length, heads_width), LOW)
    return pl.pallas_call(
        front_kernel,
        out_shape=(
            one, one, one,
            jax.ShapeDtypeStruct((local, width), LOW),
            jax.ShapeDtypeStruct((length // BQ, 1, BQ), jnp.int32),
            jax.ShapeDtypeStruct((width, 3 * width), LOW),
            jax.ShapeDtypeStruct((width, width), LOW),
            jax.ShapeDtypeStruct((width, hidden), LOW),
        ),
        in_specs=[vmem] * 3 + [any_spec] * 3,
        out_specs=(any_spec,) * 3 + (vmem,) * 2 + (any_spec,) * 3,
        scratch_shapes=[
            pltpu.VMEM((width, 3 * width), LOW),
            pltpu.VMEM((3, local, width), LOW),
            pltpu.VMEM((8, 1, local), jnp.int32),
            pltpu.VMEM((1 + hidden // width, 256, width), LOW),
            pltpu.VMEM((3, 3, local, heads_width), LOW),
            dma((4, 9)),
            dma((4, 9)),
            *exchange_sems(3),
            dma((7,)),
            dma((7,)),
            dma((20,)),
        ],
        compiler_params=pltpu.CompilerParams(
            collective_id=1, has_side_effects=True, vmem_limit_bytes=VMEM_BYTES
        ),
        name="front",
    )(tokens, gain.reshape(1, width), ids, w_triple, w_out, w_up)


MIDDLE_ALONE = (1, 3)
MIDDLE_X_FIRST = (1, 3)
MIDDLE_ORDER = (
    1100, 500, 601, 1200, 1300, 1400, 700, 701, 502, 702, 703, 1500, 600, 602, 1, 603, 0, 3,
    800, 801, 802, 900, 901, 902, 903, 101, 2, 1000, 1001, 1600, 201, 1700, 103, 100, 301, 1800,
    102, 401, 203, 200, 303, 202, 1900, 300, 403, 302, 400, 402,
)


def middle_kernel(
    u, tokens, cotangent, post_gain, second_gain, mid_gain, w_out, w_up, w_down,
    o_layer, o_grad, o_heads, o_merged, o_second, o_hidden, o_projected, o_gains, o_down,
    out_s, up_s, down_s, merged_s, second_s, unit_s, slope_s, act_s, hidden_s, projected_s, middle_s, far_s,
    layer_s, o_middle, inverse_s, inner_s, relay, grad_s,
    d_left, d_right, d_whole, d_first, d_second, d_near, d_far,
    local_sem, g_send, g_recv, core_send, core_recv, x_send, x_recv, z_send, z_recv, s_send, s_recv,
):
    place = Place()
    local, width = tokens.shape
    hidden = mid_gain.shape[1]
    wide = jnp.float32
    column_peers = [(place.dp, (place.z + k) % 4 * 2 + place.x) for k in range(1, 4)]
    meet(column_peers + [place.x_partner(), place.core_partner(), place.y_partner()])
    exchange_sem = (x_send, x_recv, z_send, z_recv)

    inbound = ToTokens(place, u, merged_s, relay.at[0], [sem.at[0] for sem in exchange_sem], local_sem.at[0])
    gather = Gather(place, (g_send, g_recv))
    alone = MIDDLE_ALONE
    chunks, mine = [], []
    for k in range(4):

        def full(d, first, count, k=k):
            return down_s.at[pl.ds(pl.multiple_of(d * 1024 + k * 256 + first, 128), count), :]

        own = w_down.at[pl.ds(k * 256, 256), :]
        chunks.append(gather.copies(k, own, full, 256, k not in alone))
        chunks[k][1].start()
        chunks[k][0].start()
        mine.append(pltpu.make_async_copy(own, full(place.dp, 0, 256), local_sem.at[1 + k]))
        mine[k].start()
    loads = [
        pltpu.make_async_copy(w_out, out_s, local_sem.at[5]),
        pltpu.make_async_copy(w_up, up_s, local_sem.at[6]),
    ]
    for load in loads:
        load.start()
    sems = (local_sem, core_send, core_recv)
    right = share(place, 7, cotangent, cotangent, d_right, local, *sems)
    saves = []

    def save(source, target, index):
        copy = pltpu.make_async_copy(source, target, local_sem.at[index])
        copy.start()
        saves.append(copy)

    def across(k):
        (chunks[k][1] if chunks[k][2] is None else chunks[k][2]).wait_recv()
        chunks[k][3].start()

    def forward(k):
        chunks[k][1].wait_recv()
        chunks[k][2].start()

    gain = mid_gain[...]
    part_one = gain.astype(LOW)
    left_over = gain - part_one.astype(wide)
    part_two = left_over.astype(LOW)
    part_three = (left_over - part_two.astype(wide)).astype(LOW)
    row = lax.broadcasted_iota(jnp.int32, (16, hidden), 0)
    parts = jnp.where(row == 0, part_one.astype(wide), jnp.where(row == 1, part_two.astype(wide), part_three.astype(wide)))
    act_s[pl.ds(local, 16), :] = jnp.where(row < 3, parts, 0.0).astype(LOW)

    def blocks(first, count, body):
        def one(n, carry):
            body(n + first)
            return carry

        lax.fori_loop(0, count, one, 0)

    def span(n, size):
        return pl.ds(pl.multiple_of(n * size, size), size)

    later = {}

    def arrive(_):
        inbound.finish()
        wait_all(loads)
        save(merged_s, o_merged, 8)

    def project(n):
        at = span(n, 512)
        far_s[:, at] = jnp.dot(merged_s[...], out_s[:, at], preferred_element_type=wide)

    def norms(n):
        rows = span(n, 128)
        unit, inverse = norm_parts(far_s[rows, :])
        far_s[rows, :] = unit
        inverse_s[rows, :] = jnp.broadcast_to(inverse, (128, 128))
        middle = tokens[rows, :].astype(wide) + unit * post_gain[...]
        middle_s[rows, :] = middle
        second_s[rows, :] = (norm_parts(middle)[0] * second_gain[...]).astype(LOW)

    def grow(n):
        at = span(n, 512)
        z = jnp.dot(second_s[...], up_s[:, at], preferred_element_type=wide)
        root = 0.7978845608028654
        square = z * z
        half = 0.5 + 0.5 * jnp.tanh(z * (root + (root * 0.044715) * square))
        value = z * half
        unit_s[:, at] = value
        slope_s[:, at] = half + (value - value * half) * (2.0 * root + (6.0 * root * 0.044715) * square)

    def hidden_norm(n):
        rows = span(n, 64)
        unit, inverse = norm_parts(unit_s[rows, :])
        unit_s[rows, :] = unit
        inner_s[rows, :] = jnp.broadcast_to(inverse, (64, 128))
        act_s[rows, :] = (unit * gain).astype(LOW)

    def settle_weights():
        for k in range(4):
            chunks[k][0].wait_recv()
            chunks[k][3].wait_recv()
            mine[k].wait()
        grad_s[...] = jnp.zeros_like(grad_s)

    def shrink(n):
        at = span(n, 512)
        total = jnp.dot(act_s[...], down_s[:, at], preferred_element_type=wide)
        low = cotangent[:, at].astype(wide)
        value = total[:local]
        layer_s[:, at] = (middle_s[:, at] + value).astype(LOW)
        weight = jnp.sum(total[local:], axis=0, keepdims=True)
        first = jnp.sum(low * weight, axis=1, keepdims=True) * (1.0 / hidden)
        second = jnp.sum(low * value, axis=1, keepdims=True) * (1.0 / hidden)
        grad_s[0] = grad_s[0] + jnp.broadcast_to(first, (local, 128))
        grad_s[1] = grad_s[1] + jnp.broadcast_to(second, (local, 128))

    def write_down(p, value):
        o_down[:, pl.ds(p * 256, 256)] = value

    down = Scatter(
        place, (d_whole, d_first, d_second, d_near, d_far), (s_send, s_recv), MIDDLE_X_FIRST,
        lambda p: d_left, lambda p: d_right.at[:, pl.ds(p * 256, 256)], write_down,
    )

    def pull_hidden(n):
        at = span(n, 512)
        grad = nt(cotangent[...], down_s[at, :])
        unit = unit_s[:, at]
        o_gains[3:4, at] = jnp.sum(grad * unit, axis=0, keepdims=True)
        pulled = grad * mid_gain[:, at] - grad_s[0][:, 0:1] - unit * grad_s[1][:, 0:1]
        hidden_s[:, at] = (inner_s[:, 0:1] * pulled * slope_s[:, at]).astype(LOW)

    def pull_second(n):
        at = span(n, 512)
        o_middle[:, at] = nt(hidden_s[...], up_s[at, :])

    def pull_norms(n, totals):
        rows = span(n, 128)
        grad = o_middle[rows, :]
        unit, inverse = norm_parts(middle_s[rows, :])
        grad_middle = cotangent[rows, :].astype(wide) + norm_pull(grad, unit, inverse, second_gain[...])
        o_middle[rows, :] = grad_middle
        outer = far_s[rows, :]
        projected_s[rows, :] = norm_pull(grad_middle, outer, inverse_s[rows, 0:1], post_gain[...]).astype(LOW)
        return (
            totals[0] + jnp.sum(grad_middle * outer, axis=0, keepdims=True),
            totals[1] + jnp.sum(grad * unit, axis=0, keepdims=True),
        )

    def pull_merged(n):
        at = span(n, 512)
        merged_s[:, at] = nt(projected_s[...], out_s[at, :]).astype(LOW)

    def compute(p):
        if later.get("left"):
            wait_all(right)
            wait_all(later.pop("left"))
        down.compute(p)

    def do_norms(_):
        blocks(0, local // 128, norms)
        save(second_s, o_second, 9)

    def do_hidden_norm(_):
        blocks(0, local // 64, hidden_norm)
        later["left"] = share_left(place, 10, act_s, d_left, local, *sems)

    def do_shrink(n):
        if n == 0:
            settle_weights()
        else:
            blocks(n - 1, 1, shrink)
        if n == 2:
            save(layer_s, o_layer, 18)

    def do_pull_hidden(n):
        blocks(n * (hidden // 2048), hidden // 2048, pull_hidden)
        if n == 3:
            save(hidden_s, o_hidden, 15)

    def do_pull_norms(_):
        nothing = jnp.zeros((1, width), wide)
        post, second = lax.fori_loop(0, local // 128, pull_norms, (nothing, nothing))
        o_gains[1:2, 0:width] = post
        o_gains[2:3, 0:width] = second
        save(projected_s, o_projected, 16)
        save(o_middle, o_grad, 19)

    def do_pull_merged(_):
        saves[0].wait()
        blocks(0, width // 512, pull_merged)
        later["out"] = ToHeads(
            place, merged_s, o_heads, relay.at[1], [sem.at[1] for sem in exchange_sem], local_sem.at[17]
        )
        later["out"].start()

    act = (
        compute,
        lambda p: down.advance(p, 1),
        lambda p: down.advance(p, 2),
        lambda p: down.advance(p, 3),
        lambda p: down.advance(p, 4),
        forward,
        across,
        lambda n: blocks(n * (hidden // 2048), hidden // 2048, grow),
        do_shrink,
        do_pull_hidden,
        lambda n: blocks(n, 1, pull_second),
        lambda n: inbound.pass_on(),
        arrive,
        lambda n: blocks(0, width // 512, project),
        do_norms,
        do_hidden_norm,
        do_pull_norms,
        do_pull_merged,
        lambda n: later["out"].pass_on(),
        lambda n: later["out"].finish(),
    )
    for code in MIDDLE_ORDER:
        act[code // 100](code % 100)
    wait_all(saves[1:])
    for p in range(4):
        down.settle(p)
    for chunk in chunks:
        for copy in chunk:
            if copy is not None:
                copy.wait_send()


def middle(u, tokens, cotangent, post_gain, second_gain, mid_gain, w_out, w_up, w_down):
    local, width = tokens.shape
    hidden = w_up.shape[1]
    any_spec = pl.BlockSpec(memory_space=pl.ANY)
    vmem = pl.BlockSpec(memory_space=pltpu.VMEM)
    dma = pltpu.SemaphoreType.DMA
    wide = jnp.float32
    act = jax.ShapeDtypeStruct((local, width), LOW)
    return pl.pallas_call(
        middle_kernel,
        out_shape=(
            act,
            jax.ShapeDtypeStruct((local, width), wide),
            jax.ShapeDtypeStruct((local * 8, width // 8), LOW),
            act,
            act,
            jax.ShapeDtypeStruct((local, hidden), LOW),
            act,
            jax.ShapeDtypeStruct((8, hidden), wide),
            jax.ShapeDtypeStruct((hidden // 32, width), wide),
        ),
        in_specs=[any_spec] + [vmem] * 5 + [any_spec] * 3,
        out_specs=(any_spec,) * 7 + (vmem,) * 2,
        scratch_shapes=[
            pltpu.VMEM((width, width), LOW),
            pltpu.VMEM((width, hidden), LOW),
            pltpu.VMEM((hidden, width), LOW),
            pltpu.VMEM((local, width), LOW),
            pltpu.VMEM((local, width), LOW),
            pltpu.VMEM((local, hidden), wide),
            pltpu.VMEM((local, hidden), wide),
            pltpu.VMEM((local + 16, hidden), LOW),
            pltpu.VMEM((local, hidden), LOW),
            pltpu.VMEM((local, width), LOW),
            pltpu.VMEM((local, width), wide),
            pltpu.VMEM((local, width), wide),
            pltpu.VMEM((local, width), LOW),
            pltpu.VMEM((local, width), wide),
            pltpu.VMEM((local, 128), wide),
            pltpu.VMEM((local, 128), wide),
            pltpu.VMEM((2, 3, local, width // 8), LOW),
            pltpu.VMEM((2, local, 128), wide),
            pltpu.VMEM((2 * local, hidden // 2), LOW),
            pltpu.VMEM((2 * local, width), LOW),
            *scatter_scratch(4, 128, 256),
            dma((20,)),
            dma((4, 4)),
            dma((4, 4)),
            dma((20,)),
            dma((20,)),
            *exchange_sems(2),
            dma((4, 4)),
            dma((4, 4)),
        ],
        compiler_params=pltpu.CompilerParams(
            collective_id=2, has_side_effects=True, vmem_limit_bytes=VMEM_BYTES
        ),
        name="middle",
    )(
        u, tokens, cotangent, post_gain.reshape(1, width), second_gain.reshape(1, width),
        mid_gain.reshape(1, hidden), w_out, w_up, w_down,
    )


HALF = 512
X_FIRST = (0, 4, 6, 12)
TAIL_ORDER = (
    1, 2, 4, 5, 6, 9, 500, 7, 101, 0, 104, 8, 3, 102, 106, 600, 700, 501, 201, 14,
    15, 109, 105, 107, 100, 204, 601, 502, 701, 304, 301, 108, 12, 103, 205, 209, 202, 13, 206, 305,
    404, 309, 207, 401, 602, 702, 800, 900, 10, 405, 11, 306, 200, 115, 114, 307, 302, 208, 112, 409,
    300, 203, 901, 308, 407, 113, 215, 402, 400, 406, 303, 214, 110, 213, 902, 315, 210, 408, 111, 314,
    313, 212, 415, 310, 403, 414, 211, 413, 312, 311, 410, 412, 411,
)


def tail_kernel(
    dq, dk, dv, tokens, gain, middle_in, triple_in, act_up, act_out, act_in, g_up, g_out, gains, scales,
    o_tokens, o_triple, o_out, o_up, o_gains,
    e_left, e_right, e_whole, e_first, e_second, e_near, e_far,
    triple, middle, tokens_s, grad_s, gain_s, gain_r, relay,
    local_sem, core_send, core_recv, x_send, x_recv, z_send, z_recv, s_send, s_recv, gain_send, gain_recv,
):
    place = Place()
    partner = place.core_partner()
    local, width = tokens.shape
    heads_width = dq.shape[1]
    seq_peers = [(place.dp, (place.seq + k) % 8) for k in range(1, 8)]
    dp_peers = [((place.dp + k) % 4, place.seq) for k in range(1, 4)]
    meet(seq_peers + dp_peers)

    def start_exchange(t):
        return ToTokens(
            place, (dv, dk, dq)[t], e_right.at[7 - t, pl.ds(0, local), :], relay.at[t],
            [sem.at[t] for sem in (x_send, x_recv, z_send, z_recv)], local_sem.at[13 + t],
        )

    exchanges = [start_exchange(t) for t in range(3)]

    load_triple = pltpu.make_async_copy(triple_in, triple, local_sem.at[16])
    load_middle = pltpu.make_async_copy(middle_in, middle, local_sem.at[17])

    sems = (local_sem, core_send, core_recv)
    ready = {"up": share_left(place, 0, act_up, e_left.at[0], local, *sems)}
    for k in range(4):
        part = g_up.at[:, pl.ds(k * BLOCK, BLOCK)]
        ready[k] = share(place, 2 + k, part, part, e_right.at[k], local, *sems)
    ready["out"] = share_left(place, 6, act_out, e_left.at[1], local, *sems)
    ready["out"] += share(place, 8, g_out, g_out, e_right.at[4], local, *sems)
    ready["in"] = share_left(place, 9, act_in, e_left.at[2], local, *sems)
    load_triple.start()
    load_middle.start()

    def write(p, value):
        at = pl.ds(p % 2 * HALF, HALF)
        if p < 8:
            o_up[:, pl.ds(p * HALF, HALF)] = value
        elif p < 10:
            o_out[:, at] = value
        else:
            o_triple[:, pl.ds((p - 10) * HALF, HALF)] = value

    engine = Scatter(
        place, (e_whole, e_first, e_second, e_near, e_far), (s_send, s_recv), X_FIRST,
        lambda p: e_left.at[0 if p < 8 else 1 if p < 10 else 2],
        lambda p: e_right.at[p // 2, :, pl.ds(p % 2 * HALF, HALF)], write,
    )
    gain_s[0:3, :] = gains[0:3, 0:width]
    for k in range(gains.shape[1] // width):
        gain_s[3 + k : 4 + k, :] = gains[3:4, pl.ds(k * width, width)]
    gain_s[7:8, :] = jnp.zeros((1, width), jnp.float32)
    gain_s[7:8, 0:128] = scales[...]
    def bring_back(t):
        exchanges[t].finish()
        slot = e_right.at[7 - t]
        move = remote(
            slot.at[pl.ds(0, local), :], slot.at[pl.ds(local, local), :],
            core_send.at[11 + t], core_recv.at[11 + t], partner,
        )
        move.start()
        return move

    def pull_normed(t):
        if t == 0:
            load_triple.wait()

        def one(n, carry):
            rows = pl.ds(pl.multiple_of(n * 256, 256), 256)
            part = nt(e_right[7 - t, pl.ds(0, local), :], triple[rows, pl.ds((2 - t) * width, width)])
            grad_s[:, rows] = part if t == 0 else grad_s[:, rows] + part
            return carry

        lax.fori_loop(0, width // 256, one, 0)

    def norm_rows(n, total):
        rows = pl.ds(pl.multiple_of(n * 128, 128), 128)
        unit, inverse = norm_parts(tokens[rows, :].astype(jnp.float32))
        grad = grad_s[rows, :]
        pulled = norm_pull(grad, unit, inverse, gain[...])
        tokens_s[rows, :] = (middle[rows, :] + pulled).astype(LOW)
        return total + jnp.sum(grad * unit, axis=0, keepdims=True)

    save_tokens = pltpu.make_async_copy(tokens_s, o_tokens, local_sem.at[18])

    def pull_norm(_):
        load_middle.wait()
        gain_s[0:1, :] = lax.fori_loop(0, local // 128, norm_rows, jnp.zeros((1, width), jnp.float32))
        save_tokens.start()

    def gain_moves(peers, first):
        out = [
            remote(gain_s, gain_r.at[first + k], gain_send.at[first + k], gain_recv.at[first + k], peer)
            for k, peer in enumerate(peers)
        ]
        for move in out:
            move.start()
        return out

    gain_steps = {}

    def sum_gains(step):
        if step == 0:
            gain_steps[0] = gain_moves(dp_peers, 0)
        elif step == 1:
            wait_all(gain_steps[0])
            gain_s[...] = gain_s[...] + gain_r[0] + gain_r[1] + gain_r[2]
            o_gains[7:8, :] = gain_s[7:8, 0:128]
            gain_steps[1] = gain_moves(seq_peers, 3)
        else:
            wait_all(gain_steps[1])
            total = gain_s[...]
            for k in range(7):
                total = total + gain_r[3 + k]
            gain_s[...] = total
            device = place.dp * 8 + place.seq
            pick = (
                lax.broadcasted_iota(jnp.int32, (width, 128), 0)
                == device * 32 + lax.broadcasted_iota(jnp.int32, (width, 128), 1)
            ).astype(jnp.float32)
            o_gains[0:3, :] = jnp.dot(
                gain_s[...], pick, preferred_element_type=jnp.float32, precision=lax.Precision.HIGHEST
            )[0:3]
            block = gain_s[:, pl.ds(pl.multiple_of((device % 8) * 128, 128), 128)]
            row = lax.broadcasted_iota(jnp.int32, block.shape, 0)
            o_gains[3:4, :] = jnp.sum(jnp.where(row == 3 + device // 8, block, 0.0), axis=0, keepdims=True)

    backs, waited = {}, set()

    def need(key):
        if key not in waited:
            wait_all(ready[key])
            waited.add(key)

    def compute(p):
        need("up" if p < 8 else "out" if p < 10 else "in")
        if p < 8:
            need(p // 2)
        elif p >= 10 and 7 - p // 2 in backs:
            backs.pop(7 - p // 2).wait()
        engine.compute(p)

    def bring(t):
        backs[t] = bring_back(t)

    act = (
        compute,
        lambda p: engine.advance(p, 1),
        lambda p: engine.advance(p, 2),
        lambda p: engine.advance(p, 3),
        lambda p: engine.advance(p, 4),
        lambda t: exchanges[t].pass_on(),
        bring,
        pull_normed,
        pull_norm,
        sum_gains,
    )
    for code in TAIL_ORDER:
        act[code // 100](code % 100)
    o_gains[4:7, :] = jnp.zeros((3, 128), jnp.float32)
    save_tokens.wait()
    for p in range(16):
        engine.settle(p)


def tail(dqkv, tokens, gain, middle, triple, acts, grads, gains, scales):
    local, width = tokens.shape
    heads_width = dqkv[0].shape[1]
    hidden = grads[0].shape[1]
    any_spec = pl.BlockSpec(memory_space=pl.ANY)
    vmem = pl.BlockSpec(memory_space=pltpu.VMEM)
    wide = jnp.float32
    dma = pltpu.SemaphoreType.DMA
    return pl.pallas_call(
        tail_kernel,
        out_shape=(
            jax.ShapeDtypeStruct((local, width), LOW),
            jax.ShapeDtypeStruct((width // 32, 3 * width), wide),
            jax.ShapeDtypeStruct((width // 32, width), wide),
            jax.ShapeDtypeStruct((width // 32, hidden), wide),
            jax.ShapeDtypeStruct((8, 128), wide),
        ),
        in_specs=[any_spec] * 3 + [vmem] * 2 + [any_spec] * 7 + [vmem] * 2,
        out_specs=(any_spec,) + (vmem,) * 4,
        scratch_shapes=[pltpu.VMEM((3, 2 * local, width // 2), LOW), pltpu.VMEM((8, 2 * local, width), LOW)]
        + scatter_scratch(16, 32, HALF)
        + [
            pltpu.VMEM((width, 3 * width), LOW),
            pltpu.VMEM((local, width), wide),
            pltpu.VMEM((local, width), LOW),
            pltpu.VMEM((local, width), wide),
            pltpu.VMEM((8, width), wide),
            pltpu.VMEM((10, 8, width), wide),
            pltpu.VMEM((3, 3, local, heads_width), LOW),
            dma((20,)),
            dma((20,)),
            dma((20,)),
            *exchange_sems(3),
            dma((4, 16)),
            dma((4, 16)),
            dma((10,)),
            dma((10,)),
        ],
        compiler_params=pltpu.CompilerParams(
            collective_id=3, has_side_effects=True, vmem_limit_bytes=VMEM_BYTES
        ),
        name="tail",
    )(*dqkv, tokens, gain.reshape(1, width), middle, triple, *acts, *grads, gains, scales)


def finish_kernel(count, *refs):
    ins, outs = refs[: count + 1], refs[count + 1 :]
    for k in range(count):
        outs[k][...] = ins[k][...]
    sums = ins[count]
    for row in range(3):
        outs[count + row][...] = sums[row, 0 : outs[count + row].shape[0]]
    outs[count + 3][...] = sums[3]
    row = sums[7:8, :]
    lane = lax.broadcasted_iota(jnp.int32, row.shape, 1)
    heads = outs[count + 4].shape[1]
    for h in range(heads):
        own = (lane >= h * HEAD) & (lane < (h + 1) * HEAD)
        outs[count + 4][:, h : h + 1] = jnp.sum(jnp.where(own, row, 0.0), axis=1, keepdims=True)


def finish(arrays, sums, own, heads):
    vmem = pl.BlockSpec(memory_space=pltpu.VMEM)
    wide = jnp.float32
    shapes = [jax.ShapeDtypeStruct(a.shape, a.dtype) for a in arrays]
    shapes += [jax.ShapeDtypeStruct((own,), wide)] * 3 + [jax.ShapeDtypeStruct((sums.shape[1],), wide), jax.ShapeDtypeStruct((1, heads), wide)]
    return pl.pallas_call(
        functools.partial(finish_kernel, len(arrays)),
        out_shape=tuple(shapes),
        in_specs=[vmem] * (len(arrays) + 1),
        out_specs=(vmem,) * len(shapes),
        name="finish",
    )(*arrays, sums)


def per_device(
    sizes,
    tokens,
    segment_ids,
    first_gain,
    triple_weight,
    head_scale,
    output_weight,
    post_gain,
    second_gain,
    up_weight,
    mid_gain,
    down_weight,
    cotangent,
):
    inputs = tokens[0].astype(jnp.float32)
    width = inputs.shape[1]
    doc_ids = lax.all_gather(segment_ids[0], "seq", axis=0, tiled=True)
    triple_full, output_full = (
        lax.all_gather(triple_weight, "dp", axis=0, tiled=True),
        lax.all_gather(output_weight, "dp", axis=0, tiled=True),
    )
    normed, pull_first = jax.vjp(layer_norm, inputs, first_gain)
    normed_low = normed.astype(jnp.bfloat16)
    triple = jnp.dot(normed_low, triple_full, preferred_element_type=jnp.float32).astype(
        jnp.bfloat16
    )
    queries, keys_all, values_all = (
        lax.all_to_all(triple[:, :width], "seq", split_axis=1, concat_axis=0, tiled=True),
        lax.all_to_all(
            triple[:, width : 2 * width], "seq", split_axis=1, concat_axis=0, tiled=True
        ),
        lax.all_to_all(triple[:, 2 * width :], "seq", split_axis=1, concat_axis=0, tiled=True),
    )
    heads_here = queries.shape[1] // HEAD
    starts = document_starts(doc_ids)
    attended, scaled, logsum = attend_forward(
        queries, keys_all, values_all, starts, head_scale
    )
    merged = lax.all_to_all(scaled, "seq", split_axis=0, concat_axis=1, tiled=True)
    projected = jnp.dot(merged, output_full, preferred_element_type=jnp.float32)
    post_normed, pull_post = jax.vjp(layer_norm, projected, post_gain)
    middle = inputs + post_normed
    second, pull_second = jax.vjp(layer_norm, middle, second_gain)
    second_low = second.astype(jnp.bfloat16)
    feed_up, feed_down = (
        lax.all_gather(up_weight, "dp", axis=0, tiled=True),
        lax.all_gather(down_weight, "dp", axis=0, tiled=True),
    )
    hidden = jnp.dot(second_low, feed_up, preferred_element_type=jnp.float32)
    activated, pull_mid = jax.vjp(gelu_norm, hidden, mid_gain)
    activated_low = activated.astype(jnp.bfloat16)
    layer_out = (
        middle + jnp.dot(activated_low, feed_down, preferred_element_type=jnp.float32)
    ).astype(jnp.bfloat16)
    upstream = cotangent[0]
    grad_act = times_transposed(upstream, feed_down)
    grad_hidden, grad_mid = pull_mid(grad_act)
    grad_hidden_low = grad_hidden.astype(jnp.bfloat16)
    grad_second_in = times_transposed(grad_hidden_low, feed_up)
    grad_middle_part, grad_second = pull_second(grad_second_in)
    grad_middle = upstream.astype(jnp.float32) + grad_middle_part
    grad_projected, grad_post = pull_post(grad_middle)
    grad_projected_low = grad_projected.astype(jnp.bfloat16)
    grad_merged = times_transposed(grad_projected_low, output_full).astype(jnp.bfloat16)
    grad_scaled = lax.all_to_all(
        grad_merged, "seq", split_axis=1, concat_axis=0, tiled=True
    )
    grad_queries, grad_keys, grad_values, scale_lanes = attend_backward(
        queries, keys_all, values_all, attended, grad_scaled, starts, head_scale, logsum
    )
    scale_terms = jnp.sum(scale_lanes.reshape(heads_here, HEAD), axis=1)
    back_queries, back_keys, back_values = (
        lax.all_to_all(
            grad_queries.astype(jnp.bfloat16), "seq", split_axis=0, concat_axis=1, tiled=True
        ),
        lax.all_to_all(
            grad_keys.astype(jnp.bfloat16), "seq", split_axis=0, concat_axis=1, tiled=True
        ),
        lax.all_to_all(
            grad_values.astype(jnp.bfloat16), "seq", split_axis=0, concat_axis=1, tiled=True
        ),
    )
    grad_triple_act = jnp.concatenate((back_queries, back_keys, back_values), axis=1)
    grad_normed = times_transposed(grad_triple_act, triple_full)
    grad_input_part, grad_first = pull_first(grad_normed)
    grad_tokens = (grad_middle + grad_input_part).astype(jnp.bfloat16)
    low = jnp.bfloat16
    grad_down = scatter_rows(transposed_times(activated_low, upstream).astype(low), sizes)
    grad_up = scatter_rows(transposed_times(second_low, grad_hidden_low).astype(low), sizes)
    grad_output = scatter_rows(transposed_times(merged, grad_projected_low).astype(low), sizes)
    gains = jnp.concatenate(
        (
            grad_first[:, None],
            grad_post[:, None],
            grad_second[:, None],
            grad_mid.reshape(width, -1),
        ),
        axis=1,
    )
    gains = jnp.pad(gains, ((0, 0), (0, 128 - gains.shape[1])))
    grad_triple = scatter_rows(
        jnp.concatenate(
            (transposed_times(normed_low, grad_triple_act).astype(low), gains.astype(low)), axis=1
        ),
        sizes,
    )
    gain_sums = grad_triple[:, 3 * width :]
    grad_scale = lax.psum(scale_terms, "dp")
    return (
        layer_out[None],
        grad_tokens[None],
        gain_sums[:, 0],
        grad_triple[:, : 3 * width],
        grad_scale,
        grad_output,
        gain_sums[:, 1],
        gain_sums[:, 2],
        grad_up,
        gain_sums[:, 3 : 3 + mid_gain.shape[0] // width].reshape(-1),
        grad_down,
    )


def per_device_chips(
    sizes,
    tokens,
    segment_ids,
    first_gain,
    triple_weight,
    head_scale,
    output_weight,
    post_gain,
    second_gain,
    up_weight,
    mid_gain,
    down_weight,
    cotangent,
):
    width, hidden = tokens.shape[2], up_weight.shape[1]
    heads_here = width // HEAD // sizes[1]
    values, keys, queries, normed, starts, triple_full, output_full, up_full = front(
        tokens[0], first_gain, segment_ids, triple_weight, output_weight, up_weight
    )
    attended, scaled, logsum = attend_forward(queries, keys, values, starts, head_scale)
    layer_out, grad_middle, grad_scaled, merged, second_low, grad_hidden, grad_projected, gains, grad_down = middle(
        scaled, tokens[0], cotangent[0], post_gain, second_gain, mid_gain, output_full, up_full, down_weight
    )
    grad_queries, grad_keys, grad_values, scale_lanes = attend_backward(
        queries, keys, values, attended, grad_scaled, starts, head_scale, logsum
    )
    grad_tokens, grad_triple, grad_output, grad_up, sums = tail(
        (grad_queries, grad_keys, grad_values),
        tokens[0],
        first_gain,
        grad_middle,
        triple_full,
        (second_low, merged, normed),
        (grad_hidden, grad_projected),
        gains,
        scale_lanes,
    )
    layer_out, grad_tokens, grad_triple, grad_output, grad_up, grad_down, first, post, second, mid, scale = finish(
        (layer_out, grad_tokens, grad_triple, grad_output, grad_up, grad_down), sums, width // 32, heads_here
    )
    return (
        layer_out[None],
        grad_tokens[None],
        first,
        grad_triple,
        scale[0],
        grad_output,
        post,
        second,
        grad_up,
        mid,
        grad_down,
    )


def solution(mesh):
    placed = (
        P("dp", "seq", None),
        P("dp", "seq"),
        P(),
        P("dp", None),
        P(),
        P("dp", None),
        P(),
        P(),
        P("dp", None),
        P(),
        P("dp", None),
        P("dp", "seq", None),
    )
    sizes = (mesh.shape["dp"], mesh.shape["seq"])
    program = per_device_chips if sizes == (4, 8) else per_device
    return jax.shard_map(
        functools.partial(program, sizes),
        mesh=mesh,
        in_specs=placed,
        out_specs=(
            P("dp", "seq", None),
            P("dp", "seq", None),
            P(("dp", "seq")),
            P(("dp", "seq"), None),
            P("seq"),
            P(("dp", "seq"), None),
            P(("dp", "seq")),
            P(("dp", "seq")),
            P(("dp", "seq"), None),
            P(("dp", "seq")),
            P(("dp", "seq"), None),
        ),
        check_vma=False,
    )
```

```python
import functools
import jax
import jax.numpy as jnp
from jax import lax
from jax.sharding import PartitionSpec as P
from jax.experimental import pallas as pl
from jax.experimental.pallas import tpu as pltpu

HEAD = 64
NEG = -1e30
BQ = 256
QB = 1024
KB = 512


def nt(a, b):
    return lax.dot_general(a, b, (((1,), (1,)), ((), ())), preferred_element_type=jnp.float32)


def tn(a, b):
    return lax.dot_general(a, b, (((0,), (0,)), ((), ())), preferred_element_type=jnp.float32)


def stack_heads(block, heads):
    if heads == 1:
        return block
    lane = lax.broadcasted_iota(jnp.int32, block.shape, 1)
    zero = jnp.zeros_like(block)
    return jnp.concatenate(
        [jnp.where((lane >= h * HEAD) & (lane < (h + 1) * HEAD), block, zero) for h in range(heads)],
        axis=0,
    )


def unstack_heads(wide, heads):
    rows = wide.shape[1] // heads
    return jnp.concatenate(
        [wide[h * HEAD : (h + 1) * HEAD, h * rows : (h + 1) * rows] for h in range(heads)], axis=0
    )


def scale_row(scale_ref, width):
    heads = width // HEAD
    first = lax.axis_index("seq") * heads
    lane = lax.broadcasted_iota(jnp.int32, (1, width), 1)
    row = jnp.full((1, width), scale_ref[first], jnp.float32)
    for h in range(1, heads):
        row = jnp.where(lane >= h * HEAD, scale_ref[first + h], row)
    return row


def forward_kernel(heads, first_ref, q_ref, k_ref, v_ref, start_ref, scale_ref,
                   o_ref, u_ref, lse_ref, m_s, l_s, acc_s):
    rows, step_rows = QB, KB
    scale = scale_row(scale_ref, q_ref.shape[1])
    ratio = rows // step_rows

    def one(i, carry):
        mine = pl.ds(pl.multiple_of(i * rows, rows), rows)
        queries = stack_heads(q_ref[mine, :] * jnp.bfloat16(HEAD ** -0.5), heads)
        starts = jnp.concatenate([start_ref[i * (rows // BQ) + k] for k in range(rows // BQ)] * heads, axis=1)

        def scores_of(j, count, queries, starts):
            at = pl.ds(pl.multiple_of(j * BQ, BQ), count)
            scores = nt(k_ref[at, :], queries)
            if starts is not None:
                key = j * BQ + lax.broadcasted_iota(jnp.int32, scores.shape, 0)
                scores = jnp.where(key >= starts, scores, NEG)
            return at, scores

        def fold(at, scores, columns):
            before = m_s[:, columns]
            highest = jnp.maximum(before, jnp.max(scores, axis=0, keepdims=True))
            fade = jnp.exp(before - highest)
            weights = jnp.exp(scores - highest)
            m_s[:, columns] = highest
            l_s[:, columns] = l_s[:, columns] * fade + jnp.sum(weights, axis=0, keepdims=True)
            acc_s[:, columns] = acc_s[:, columns] * fade + tn(v_ref[at, :], weights.astype(jnp.bfloat16))

        def step(j, masked):
            at, scores = scores_of(j * (step_rows // BQ), step_rows, queries, starts if masked else None)
            fold(at, scores, slice(None))

        for k in range(rows // BQ):
            wide = rows - k * BQ
            late = [slice(h * rows + k * BQ, (h + 1) * rows) for h in range(heads)]
            some = queries if k == 0 else jnp.concatenate([queries[c] for c in late], axis=0)
            start = starts if k == 0 else jnp.concatenate([starts[:, c] for c in late], axis=1)
            at, scores = scores_of(i * (rows // BQ) + k, BQ, some, start)
            key = lax.broadcasted_iota(jnp.int32, scores.shape, 0)
            for h in range(heads):
                part = scores[:, h * wide : (h + 1) * wide]
                lane = lax.broadcasted_iota(jnp.int32, part.shape, 1)
                part = jnp.where(key[:, :wide] <= lane, part, NEG)
                if k == 0:
                    highest = jnp.max(part, axis=0, keepdims=True)
                    weights = jnp.exp(part - highest)
                    m_s[:, late[h]] = highest
                    l_s[:, late[h]] = jnp.sum(weights, axis=0, keepdims=True)
                    acc_s[:, late[h]] = tn(v_ref[at, :], weights.astype(jnp.bfloat16))
                else:
                    fold(at, part, late[h])

        low = first_ref[i * (rows // BQ), 0, 0] // step_rows
        last = first_ref[i * (rows // BQ) + rows // BQ - 1, 0, BQ - 1]
        full = jnp.minimum((last + step_rows - 1) // step_rows, i * ratio)

        def plain(j, carry):
            step(j, False)
            return carry

        def edge(j, carry):
            step(j, True)
            return carry

        lax.fori_loop(full, i * ratio, plain, 0)
        lax.fori_loop(low, full, edge, 0)
        total = l_s[...]
        out = unstack_heads(acc_s[...] * (1.0 / total), heads).T
        o_ref[mine, :] = out
        u_ref[mine, :] = (out * scale).astype(jnp.bfloat16)
        logsum = m_s[...] + jnp.log(total)
        for k in range(rows // BQ):
            lse_ref[i * (rows // BQ) + k] = jnp.concatenate(
                [logsum[:, h * rows + k * BQ : h * rows + (k + 1) * BQ] for h in range(heads)], axis=1
            )
        return carry

    lax.fori_loop(0, q_ref.shape[0] // rows, one, 0)


def attend_forward(queries, keys, values, starts, scales):
    length, width = queries.shape
    heads = width // HEAD
    vmem = pl.BlockSpec(memory_space=pltpu.VMEM)
    return pl.pallas_call(
        functools.partial(forward_kernel, heads),
        out_shape=(
            jax.ShapeDtypeStruct((length, width), jnp.float32),
            jax.ShapeDtypeStruct((length, width), jnp.bfloat16),
            jax.ShapeDtypeStruct((length // BQ, 1, heads * BQ), jnp.float32),
        ),
        in_specs=[pl.BlockSpec(memory_space=pltpu.SMEM)] + [vmem] * 4 + [pl.BlockSpec(memory_space=pltpu.SMEM)],
        out_specs=(vmem,) * 3,
        scratch_shapes=[
            pltpu.VMEM((1, heads * QB), jnp.float32),
            pltpu.VMEM((1, heads * QB), jnp.float32),
            pltpu.VMEM((width, heads * QB), jnp.float32),
        ],
        cost_estimate=pl.CostEstimate(
            flops=length * length * width, bytes_accessed=16 * length * width, transcendentals=0
        ),
        name="attend_forward",
    )(starts, queries, keys, values, starts, scales)


def backward_kernel(heads, first_ref, q_ref, k_ref, v_ref, o_ref, du_ref, start_ref, scale_ref, lse_ref,
                    dq_ref, dk_ref, dv_ref, ds_ref, qs_s, dos_s, delta_s, dqt_s, dk_s, dv_s):
    rows, group = BQ, 1
    blocks = qs_s.shape[0]
    scale = scale_row(scale_ref, q_ref.shape[1])

    def prepare(i, total):
        at = pl.ds(pl.multiple_of(i * rows, rows), rows)
        qs_s[i] = stack_heads(q_ref[at, :] * jnp.bfloat16(HEAD ** -0.5), heads)
        grad = du_ref[at, :].astype(jnp.float32)
        out = o_ref[at, :]
        low = (grad * scale).astype(jnp.bfloat16)
        dos_s[i] = stack_heads(low, heads)
        inner = (low.astype(jnp.float32) * out).T
        delta_s[i] = jnp.concatenate(
            [jnp.sum(inner[h * HEAD : (h + 1) * HEAD], axis=0, keepdims=True) for h in range(heads)],
            axis=1,
        )
        dqt_s[i] = jnp.zeros(dqt_s.shape[1:], jnp.float32)
        return total + jnp.sum(grad * out, axis=0, keepdims=True)

    ds_ref[...] = lax.fori_loop(0, blocks, prepare, jnp.zeros(ds_ref.shape, jnp.float32))

    def one(j, carry):
        mine = pl.ds(pl.multiple_of(j * BQ, BQ), BQ)
        keys, values = k_ref[mine, :], v_ref[mine, :]

        def step(i, masked, diagonal):
            queries, grads = qs_s[i], dos_s[i]
            scores = nt(keys, queries)
            if masked or diagonal:
                key = j * BQ + lax.broadcasted_iota(jnp.int32, scores.shape, 0)
                starts = jnp.concatenate([start_ref[i * group + k] for k in range(group)] * heads, axis=1)
                allowed = key >= starts
                if diagonal:
                    lane = lax.broadcasted_iota(jnp.int32, scores.shape, 1) & (rows - 1)
                    allowed = allowed & (key <= i * rows + lane)
                scores = jnp.where(allowed, scores, NEG)
            weights = jnp.exp(scores - lse_ref[i])
            pulls = nt(values, grads)
            low = (weights * (pulls - delta_s[i])).astype(jnp.bfloat16)
            part_v = jnp.dot(weights.astype(jnp.bfloat16), grads, preferred_element_type=jnp.float32)
            part_k = jnp.dot(low, queries, preferred_element_type=jnp.float32)
            part_q = tn(keys, low)
            if diagonal:
                dv_s[...] = part_v
                dk_s[...] = part_k
            else:
                dv_s[...] += part_v
                dk_s[...] += part_k
            return part_q

        high, full = jnp.int32(0), jnp.int32(0)
        for i in range(blocks):
            high += (first_ref[i * group, 0, 0] // BQ <= j).astype(jnp.int32)
            full += (first_ref[i * group + group - 1, 0, BQ - 1] <= j * BQ).astype(jnp.int32)
        own = j // group
        full = jnp.maximum(full, own + 1)

        def plain(i, carry):
            dqt_s[i] += step(i, False, False)
            return carry

        def edge(i, carry):
            dqt_s[i] += step(i, True, False)
            return carry

        dqt_s[own] += step(own, False, True)
        lax.fori_loop(own + 1, full, plain, 0)
        lax.fori_loop(full, high, edge, 0)
        dk_ref[mine, :] = dk_s[...].astype(jnp.bfloat16)
        dv_ref[mine, :] = dv_s[...].astype(jnp.bfloat16)
        return carry

    lax.fori_loop(0, blocks * group, one, 0)

    def finish(i, carry):
        at = pl.ds(pl.multiple_of(i * rows, rows), rows)
        dq_ref[at, :] = (unstack_heads(dqt_s[i], heads).T * HEAD ** -0.5).astype(jnp.bfloat16)
        return carry

    lax.fori_loop(0, blocks, finish, 0)


def attend_backward(queries, keys, values, outs, grads, starts, scales, logsum):
    length, width = queries.shape
    heads = width // HEAD
    blocks = length // BQ
    vmem = pl.BlockSpec(memory_space=pltpu.VMEM)
    return pl.pallas_call(
        functools.partial(backward_kernel, heads),
        out_shape=(jax.ShapeDtypeStruct((length, width), jnp.bfloat16),) * 3
        + (jax.ShapeDtypeStruct((1, width), jnp.float32),),
        in_specs=[pl.BlockSpec(memory_space=pltpu.SMEM)] + [vmem] * 6 + [pl.BlockSpec(memory_space=pltpu.SMEM), vmem],
        out_specs=(vmem,) * 4,
        scratch_shapes=[
            pltpu.VMEM((blocks, heads * BQ, width), jnp.bfloat16),
            pltpu.VMEM((blocks, heads * BQ, width), jnp.bfloat16),
            pltpu.VMEM((blocks, 1, heads * BQ), jnp.float32),
            pltpu.VMEM((blocks, width, heads * BQ), jnp.float32),
            pltpu.VMEM((BQ, width), jnp.float32),
            pltpu.VMEM((BQ, width), jnp.float32),
        ],
        cost_estimate=pl.CostEstimate(
            flops=3 * length * length * width, bytes_accessed=32 * length * width, transcendentals=0
        ),
        name="attend_backward",
    )(starts, queries, keys, values, outs, grads, starts, scales, logsum)


def document_starts(doc_ids):
    length = doc_ids.shape[0]
    names = jnp.arange(8, dtype=jnp.int32)
    counts = jnp.sum(doc_ids[None, :] < names[:, None], axis=1, dtype=jnp.int32)
    starts = jnp.sum(
        jnp.where(doc_ids[:, None] == names[None, :], counts[None, :], 0), axis=1, dtype=jnp.int32
    )
    return starts.reshape(length // BQ, 1, BQ)


def layer_norm(values, gains):
    center = values - jnp.mean(values, axis=-1, keepdims=True)
    spread = jnp.mean(center * center, axis=-1, keepdims=True)
    return center * lax.rsqrt(spread + 1e-05) * gains


def gelu_norm(hidden, gains):
    return layer_norm(jax.nn.gelu(hidden, approximate=True), gains)


def transposed_times(left, right):
    return lax.dot_general(
        left, right, (((0,), (0,)), ((), ())), preferred_element_type=jnp.float32
    )


def times_transposed(left, right):
    return lax.dot_general(
        left, right, (((1,), (1,)), ((), ())), preferred_element_type=jnp.float32
    )


def scatter_rows(partial, sizes):
    current = partial
    for axis, size in zip(("dp", "seq"), sizes):
        place = lax.axis_index(axis)
        bits = size.bit_length() - 1
        pieces = current.reshape((2,) * bits + (-1, current.shape[-1]))
        for bit in range(bits):
            at = bits - 1 - bit
            mine = (place >> bit) & 1
            give = lax.dynamic_index_in_dim(pieces, 1 - mine, at, keepdims=False)
            keep = lax.dynamic_index_in_dim(pieces, mine, at, keepdims=False)
            got = lax.ppermute(give, axis, [(i, i ^ (1 << bit)) for i in range(size)])
            pieces = (keep.astype(jnp.float32) + got.astype(jnp.float32)).astype(jnp.bfloat16)
        current = pieces
    return current.astype(jnp.float32)


MESH = pl.DeviceIdType.MESH
LOW = jnp.bfloat16
BLOCK = 1024
VMEM_BYTES = 66_000_000


class Place:
    def __init__(self):
        self.dp, self.seq = lax.axis_index("dp"), lax.axis_index("seq")
        self.core, self.y = self.dp % 2, self.dp // 2
        self.x, self.z = self.seq % 2, self.seq // 2
        self.z0, self.z1 = self.z % 2, self.z // 2

    def core_partner(self):
        return (self.dp + 1 - 2 * self.core, self.seq)

    def y_partner(self):
        return (self.dp + 2 - 4 * self.y, self.seq)

    def x_partner(self):
        return (self.dp, self.seq + 1 - 2 * self.x)

    def near_partner(self):
        return (self.dp, self.seq + 2 - 4 * self.z0)

    def far_partner(self):
        return (self.dp, self.seq + 4 - 8 * self.z1)


def meet(devices):
    barrier = pltpu.get_barrier_semaphore()
    for device in devices:
        pl.semaphore_signal(barrier, inc=1, device_id=device, device_id_type=MESH)
    pl.semaphore_wait(barrier, len(devices))


def remote(source, target, send, receive, device):
    return pltpu.make_async_remote_copy(
        src_ref=source,
        dst_ref=target,
        send_sem=send,
        recv_sem=receive,
        device_id=device,
        device_id_type=MESH,
    )


def lanes_of(z, x, width):
    return pl.ds(pl.multiple_of((z * 2 + x) * width, 128), width)


def rows_of(z, x, local):
    return pl.ds(pl.multiple_of((z * 2 + x) * local, 128), local)


class ToHeads:
    def __init__(self, place, part, target, relay, sems, keep_sem):
        self.place, self.part, self.target, self.relay, self.sems = place, part, target, relay, sems
        self.keep_sem, self.moves, self.sends = keep_sem, [], []

    def other(self, m):
        place = self.place
        low = place.z0 + (m % 2) * (1 - 2 * place.z0)
        high = place.z1 + (m // 2) * (1 - 2 * place.z1)
        return high * 2 + low

    def start(self, steps=(2, 3, 1, 0)):
        place = self.place
        x_send, x_recv, z_send, z_recv = self.sems
        local, width = self.relay.shape[-2:]
        rows = rows_of(place.z, place.x, local)
        for m in steps:
            source = self.part.at[:, lanes_of(self.other(m), 1 - place.x, width)]
            landing = self.target.at[rows, :] if m == 0 else self.relay.at[m - 1]
            move = remote(source, landing, x_send.at[m], x_recv.at[m], place.x_partner())
            move.start()
            (self.moves if m == 0 else self.sends).append(move)
        for m in steps:
            z = self.other(m)
            source = self.part.at[:, lanes_of(z, place.x, width)]
            if m == 0:
                move = pltpu.make_async_copy(source, self.target.at[rows, :], self.keep_sem)
            else:
                device = (place.dp, z * 2 + place.x)
                move = remote(source, self.target.at[rows, :], z_send.at[m - 1], z_recv.at[m - 1], device)
            move.start()
            self.moves.append(move)

    def pass_on(self, steps=(2, 3, 1)):
        place, local = self.place, self.relay.shape[-2]
        x_send, x_recv, z_send, z_recv = self.sems
        rows = rows_of(place.z, 1 - place.x, local)
        for m in steps:
            here = self.relay.at[m - 1]
            remote(here, here, x_send.at[m], x_recv.at[m], place.x_partner()).wait_recv()
            device = (place.dp, self.other(m) * 2 + place.x)
            move = remote(here, self.target.at[rows, :], z_send.at[m + 2], z_recv.at[m + 2], device)
            move.start()
            self.moves.append(move)

    def finish(self):
        for move in self.moves:
            move.wait()
        for move in self.sends:
            move.wait_send()


class ToTokens:
    def __init__(self, place, source, target, relay, sems, keep_sem, steps=(2, 1, 3)):
        self.place, self.target, self.relay, self.sems = place, target, relay, sems
        x_send, x_recv, z_send, z_recv = sems
        local, width = relay.shape[-2:]
        self.moves, self.sends = [], []
        lanes = lanes_of(place.z, place.x, width)
        for x, first in ((1 - place.x, 0), (place.x, 3)):
            for k in steps:
                z, index = (place.z + k) % 4, first + k - 1
                landing = relay.at[k - 1] if first == 0 else target.at[:, lanes]
                move = remote(
                    source.at[rows_of(z, x, local), :],
                    landing,
                    z_send.at[index],
                    z_recv.at[index],
                    (place.dp, z * 2 + place.x),
                )
                move.start()
                (self.sends if first == 0 else self.moves).append(move)
        move = remote(
            source.at[rows_of(place.z, 1 - place.x, local), :],
            target.at[:, lanes],
            x_send.at[0],
            x_recv.at[0],
            place.x_partner(),
        )
        move.start()
        self.moves.append(move)
        move = pltpu.make_async_copy(
            source.at[rows_of(place.z, place.x, local), :], target.at[:, lanes], keep_sem
        )
        move.start()
        self.moves.append(move)

    def pass_on(self):
        place, width = self.place, self.relay.shape[-1]
        x_send, x_recv, z_send, z_recv = self.sems
        for k in (2, 1, 3):
            here = self.relay.at[k - 1]
            remote(here, here, z_send.at[k - 1], z_recv.at[k - 1], place.near_partner()).wait_recv()
            lanes = lanes_of((place.z + 4 - k) % 4, place.x, width)
            move = remote(here, self.target.at[:, lanes], x_send.at[k], x_recv.at[k], place.x_partner())
            move.start()
            self.moves.append(move)

    def finish(self):
        for move in self.moves:
            move.wait()
        for move in self.sends:
            move.wait_send()


def exchange_sems(count):
    dma = pltpu.SemaphoreType.DMA
    return [dma((count, 4)), dma((count, 4)), dma((count, 6)), dma((count, 6))]


def share(place, index, ours, theirs, target, local, here_sem, core_send, core_recv):
    here = pltpu.make_async_copy(ours, target.at[pl.ds(0, local), :], here_sem.at[index])
    there = remote(
        theirs, target.at[pl.ds(local, local), :], core_send.at[index], core_recv.at[index], place.core_partner()
    )
    here.start()
    there.start()
    return [here, there]


def share_left(place, index, source, target, local, *sems):
    half = source.shape[1] // 2
    columns = half // 2
    out = []
    for y in range(2):
        ours, theirs = (
            source.at[pl.ds(0, local), pl.ds(pl.multiple_of(y * half + core * columns, 128), columns)]
            for core in (place.core, 1 - place.core)
        )
        out += share(place, index + y, ours, theirs, target.at[:, pl.ds(y * columns, columns)], local, *sems)
    return out


def wait_all(copies):
    for copy in copies:
        copy.wait()


def norm_parts(values):
    center = values - jnp.mean(values, axis=-1, keepdims=True)
    inverse = lax.rsqrt(jnp.mean(center * center, axis=-1, keepdims=True) + 1e-05)
    return center * inverse, inverse


def norm_pull(grad, unit, inverse, gain):
    scaled = grad * gain
    return inverse * (
        scaled
        - jnp.mean(scaled, axis=-1, keepdims=True)
        - unit * jnp.mean(scaled * unit, axis=-1, keepdims=True)
    )


class Scatter:
    def __init__(self, place, refs, sems, x_first, left, right, write):
        self.place, self.x_first, self.left, self.right, self.write = place, x_first, left, right, write
        self.whole, self.first, self.second, self.near, self.far = refs
        self.send, self.receive = sems
        self.rows, self.columns = self.whole.shape[-2:]

    def axes(self, p):
        place = self.place
        if p not in self.x_first:
            return place.y, place.x, place.y_partner(), place.x_partner()
        return place.x, place.y, place.x_partner(), place.y_partner()

    def copy(self, p, stage):
        place = self.place
        mine, other, partner, second = self.axes(p)
        if stage == 0:
            source, target, device = self.whole.at[p, 1 - mine], self.first.at[p], partner
        elif stage == 1:
            source, target, device = self.first.at[p, :, :, 1 - other], self.second.at[p], second
        elif stage == 2:
            source, target, device = self.second.at[p, :, 1 - place.z0], self.near.at[p], place.near_partner()
        else:
            source, target, device = self.near.at[p, 1 - place.z1], self.far.at[p], place.far_partner()
        index = p
        return remote(source, target, self.send.at[stage, index], self.receive.at[stage, index], device)

    def compute(self, p):
        left, right = self.left(p), self.right(p)
        rows = self.rows

        def one(y, carry):
            for half in range(2):
                span = 4 * rows
                at = pl.ds(pl.multiple_of(y * 8 * rows + half * span, 128), span)
                block = tn(left[:, at], right[...]).astype(LOW)
                for k in range(4):
                    x = k % 2
                    part = block[k * rows : (k + 1) * rows]
                    if p not in self.x_first:
                        self.whole[p, y, half, k // 2, x] = part
                    else:
                        self.whole[p, x, half, k // 2, y] = part
            return carry

        lax.fori_loop(0, 2, one, 0)
        self.copy(p, 0).start()

    def advance(self, p, stage):
        place = self.place
        mine, other, _, _ = self.axes(p)
        wide = jnp.float32
        self.copy(p, stage - 1).wait_recv()
        if stage == 1:

            def add(k, carry):
                a, b, s = k // 4, k // 2 % 2, k % 2
                total = self.first[p, a, b, s].astype(wide) + self.whole[p, mine, a, b, s].astype(wide)
                self.first[p, a, b, s] = total.astype(LOW)
                return carry

            lax.fori_loop(0, 8, add, 0)
        elif stage == 2:

            def add(z, carry):
                a, b = z // 2, z % 2
                total = self.second[p, a, b].astype(wide) + self.first[p, a, b, other].astype(wide)
                self.second[p, a, b] = total.astype(LOW)
                return carry

            lax.fori_loop(0, 4, add, 0)
        elif stage == 3:

            def add(a, carry):
                total = self.near[p, a].astype(wide) + self.second[p, a, place.z0].astype(wide)
                self.near[p, a] = total.astype(LOW)
                return carry

            lax.fori_loop(0, 2, add, 0)
        else:
            self.write(p, self.near[p, place.z1].astype(wide) + self.far[p].astype(wide))
            return
        self.copy(p, stage).start()

    def settle(self, p):
        for stage in range(4):
            self.copy(p, stage).wait_send()


def scatter_scratch(pieces, rows, columns):
    return [
        pltpu.VMEM((pieces, 2, 2, 2, 2, rows, columns), LOW),
        pltpu.VMEM((pieces, 2, 2, 2, rows, columns), LOW),
        pltpu.VMEM((pieces, 2, 2, rows, columns), LOW),
        pltpu.VMEM((pieces, 2, rows, columns), LOW),
        pltpu.VMEM((pieces, rows, columns), LOW),
    ]


class Gather:
    def __init__(self, place, sems):
        self.place = place
        self.send, self.receive = sems

    def copies(self, index, own, full, rows, shared):
        place = self.place
        across = place.dp + 2 - 4 * place.y
        half = rows // 2

        def move(kind, source, target, device):
            return remote(source, target, self.send.at[kind, index], self.receive.at[kind, index], device)

        out = [move(0, own, full(place.dp, 0, rows), place.core_partner())]
        if shared:
            first = place.x * half
            out.append(
                move(1, own.at[pl.ds(pl.multiple_of(first, half), half), :],
                     full(place.dp, first, half), place.y_partner())
            )
            landed = full(across, first, half)
            out.append(move(2, landed, landed, place.x_partner()))
        else:
            out.append(move(1, own, full(place.dp, 0, rows), place.y_partner()))
            out.append(None)
        landed = full(across, 0, rows)
        out.append(move(3, landed, landed, place.core_partner()))
        return out


FRONT_ALONE = (2, 5, 8)
FRONT_ORDER = (
    500, 100, 101, 200, 0, 201, 1, 300, 600, 202, 301, 2, 103, 104, 302, 203, 3, 205,
    204, 106, 303, 107, 404, 405, 206, 208, 207, 406, 408, 407,
)


def front_kernel(
    tokens, gain, ids, w_triple, w_out, w_up,
    o_v, o_k, o_q, o_normed, o_starts, o_triple, o_out, o_up,
    triple_s, part_s, ids_s, bounce, relay, send, receive, x_send, x_recv, z_send, z_recv, ids_send, ids_recv, local_sem,
):
    place = Place()
    exchange_sem = (x_send, x_recv, z_send, z_recv)
    local, width = tokens.shape
    heads_width = o_v.shape[1]
    meet([(place.dp, (place.seq + k) % 8) for k in range(1, 8)] + [place.core_partner(), place.y_partner()])
    gather = Gather(place, (send, receive))

    def columns(weight, at):
        def full(d, first, count):
            return weight.at[pl.ds(pl.multiple_of(d * 256 + first, 128), count), at]

        return full

    half = width // 2
    spans = [
        (2 * width + (1 - place.z1) * half, half), (2 * width + place.z1 * half, half), (width, width), (0, width)
    ]
    spans = [(pl.multiple_of(first, 512), count) for first, count in spans]
    plans = []
    for first, count in spans:
        plans.append((w_triple.at[:, pl.ds(first, count)], columns(triple_s, pl.ds(first, count))))
    plans.append((w_out, columns(o_out, pl.ds(0, width))))
    for k in range(w_up.shape[1] // width):
        plans.append((w_up.at[:, pl.ds(k * width, width)], columns(o_up, pl.ds(k * width, width))))
    alone = FRONT_ALONE
    chunks = [
        gather.copies(n, own, full, 256, n not in alone) for n, (own, full) in enumerate(plans)
    ]
    mine = []
    for n, (own, full) in enumerate(plans):
        chunks[n][1].start()
        chunks[n][0].start()
        target = full(place.dp, 0, 256) if n < 4 else bounce.at[n - 4]
        copy = pltpu.make_async_copy(own, target, local_sem.at[n])
        copy.start()
        mine.append(copy)
        if n == 0:
            news = []
            for k in range(1, 8):
                peer = (place.dp, (place.seq + k) % 8)
                move = remote(ids, ids_s.at[place.seq], ids_send.at[k - 1], ids_recv.at[k - 1], peer)
                move.start()
                news.append(move)
            ids_s[pl.ds(place.seq, 1)] = ids[...].reshape(1, 1, local)

    def norm_rows(n, carry):
        rows = pl.ds(pl.multiple_of(n * 128, 128), 128)
        values = tokens[rows, :].astype(jnp.float32)
        o_normed[rows, :] = (norm_parts(values)[0] * gain[...]).astype(LOW)
        return carry

    moves = []
    exchanges = [
        ToHeads(
            place, part_s.at[t], target, relay.at[t], [sem.at[t] for sem in exchange_sem], local_sem.at[12 + t]
        )
        for t, target in enumerate((o_v, o_k, o_q))
    ]
    far, near = (2, 3), (1, 0)
    steps = ((0, far), (0, near), (1, far + near), (2, far + near))

    def project(n):
        first, count = spans[n]
        t, reach = steps[n]

        def one(c, carry):
            from_at = pl.ds(pl.multiple_of(first + c * 256, 256), 256)
            at = pl.ds(pl.multiple_of(first - (2 - t) * width + c * 256, 256), 256)
            part_s[t, :, at] = jnp.dot(
                o_normed[...], triple_s[:, from_at], preferred_element_type=jnp.float32
            ).astype(LOW)
            return carry

        lax.fori_loop(0, count // 256, one, 0)
        exchanges[t].start(reach)
        at = pl.ds(first, count)
        save = pltpu.make_async_copy(triple_s.at[:, at], o_triple.at[:, at], local_sem.at[15 + n])
        save.start()
        moves.append(save)

    def pass_on(n):
        t, reach = steps[n]
        exchanges[t].pass_on(tuple(m for m in reach if m))

    def forward(n):
        if chunks[n][2] is not None:
            chunks[n][1].wait_recv()
            chunks[n][2].start()

    def across(n):
        (chunks[n][1] if chunks[n][2] is None else chunks[n][2]).wait_recv()
        chunks[n][3].start()

    def finish(n):
        chunks[n][0].wait_recv()
        chunks[n][3].wait_recv()
        mine[n].wait()
        project(n)

    def put_back(n):
        chunks[n][0].wait_recv()
        chunks[n][3].wait_recv()
        mine[n].wait()
        copy = pltpu.make_async_copy(bounce.at[n - 4], plans[n][1](place.dp, 0, 256), local_sem.at[n])
        copy.start()
        moves.append(copy)

    def document_starts_here(_):
        for move in news:
            move.wait()
        every = ids_s[...]
        starts = jnp.zeros_like(every)
        for d in range(1, 8):
            before = jnp.sum((every < d).astype(jnp.int32), axis=2, keepdims=True)
            before = jnp.sum(before, axis=0, keepdims=True)
            starts = jnp.where(every == d, before, starts)
        for b in range(o_starts.shape[0]):
            for piece in range(BQ // 128):
                at = b * BQ + piece * 128
                o_starts[b, :, pl.ds(piece * 128, 128)] = starts[
                    at // local, :, at % local : at % local + 128
                ]

    act = (
        finish, forward, across, pass_on, put_back,
        lambda n: lax.fori_loop(0, local // 128, norm_rows, 0), document_starts_here,
    )
    for code in FRONT_ORDER:
        act[code // 100](code % 100)
    for move in moves:
        move.wait()
    for exchange in exchanges:
        exchange.finish()
    for chunk in chunks:
        for copy in chunk:
            if copy is not None:
                copy.wait_send()


def front(tokens, gain, ids, w_triple, w_out, w_up):
    local, width = tokens.shape
    heads_width = width // 8
    length = local * 8
    hidden = w_up.shape[1]
    any_spec = pl.BlockSpec(memory_space=pl.ANY)
    vmem = pl.BlockSpec(memory_space=pltpu.VMEM)
    dma = pltpu.SemaphoreType.DMA
    one = jax.ShapeDtypeStruct((length, heads_width), LOW)
    return pl.pallas_call(
        front_kernel,
        out_shape=(
            one, one, one,
            jax.ShapeDtypeStruct((local, width), LOW),
            jax.ShapeDtypeStruct((length // BQ, 1, BQ), jnp.int32),
            jax.ShapeDtypeStruct((width, 3 * width), LOW),
            jax.ShapeDtypeStruct((width, width), LOW),
            jax.ShapeDtypeStruct((width, hidden), LOW),
        ),
        in_specs=[vmem] * 3 + [any_spec] * 3,
        out_specs=(any_spec,) * 3 + (vmem,) * 2 + (any_spec,) * 3,
        scratch_shapes=[
            pltpu.VMEM((width, 3 * width), LOW),
            pltpu.VMEM((3, local, width), LOW),
            pltpu.VMEM((8, 1, local), jnp.int32),
            pltpu.VMEM((1 + hidden // width, 256, width), LOW),
            pltpu.VMEM((3, 3, local, heads_width), LOW),
            dma((4, 9)),
            dma((4, 9)),
            *exchange_sems(3),
            dma((7,)),
            dma((7,)),
            dma((20,)),
        ],
        compiler_params=pltpu.CompilerParams(
            collective_id=1, has_side_effects=True, vmem_limit_bytes=VMEM_BYTES
        ),
        name="front",
    )(tokens, gain.reshape(1, width), ids, w_triple, w_out, w_up)


MIDDLE_ALONE = (1, 3)
MIDDLE_X_FIRST = (1, 3)
MIDDLE_ORDER = (
    1100, 500, 601, 1200, 1300, 1400, 700, 701, 502, 702, 703, 1500, 600, 602, 1, 603, 0, 3,
    800, 801, 802, 900, 901, 902, 903, 101, 2, 1000, 1001, 1600, 201, 1700, 103, 100, 301, 1800,
    102, 401, 203, 200, 303, 202, 1900, 300, 403, 302, 400, 402,
)


def middle_kernel(
    u, tokens, cotangent, post_gain, second_gain, mid_gain, w_out, w_up, w_down,
    o_layer, o_grad, o_heads, o_merged, o_second, o_hidden, o_projected, o_gains, o_down,
    out_s, up_s, down_s, merged_s, second_s, unit_s, slope_s, act_s, hidden_s, projected_s, middle_s, far_s,
    layer_s, o_middle, inverse_s, inner_s, relay, grad_s,
    d_left, d_right, d_whole, d_first, d_second, d_near, d_far,
    local_sem, g_send, g_recv, core_send, core_recv, x_send, x_recv, z_send, z_recv, s_send, s_recv,
):
    place = Place()
    local, width = tokens.shape
    hidden = mid_gain.shape[1]
    wide = jnp.float32
    column_peers = [(place.dp, (place.z + k) % 4 * 2 + place.x) for k in range(1, 4)]
    meet(column_peers + [place.x_partner(), place.core_partner(), place.y_partner()])
    exchange_sem = (x_send, x_recv, z_send, z_recv)

    inbound = ToTokens(
        place, u, merged_s, relay.at[0], [sem.at[0] for sem in exchange_sem], local_sem.at[0], (2, 3, 1)
    )
    gather = Gather(place, (g_send, g_recv))
    alone = MIDDLE_ALONE
    chunks, mine = [], []
    for k in range(4):

        def full(d, first, count, k=k):
            return down_s.at[pl.ds(pl.multiple_of(d * 1024 + k * 256 + first, 128), count), :]

        own = w_down.at[pl.ds(k * 256, 256), :]
        chunks.append(gather.copies(k, own, full, 256, k not in alone))
        chunks[k][1].start()
        chunks[k][0].start()
        mine.append(pltpu.make_async_copy(own, full(place.dp, 0, 256), local_sem.at[1 + k]))
        mine[k].start()
    loads = [
        pltpu.make_async_copy(w_out, out_s, local_sem.at[5]),
        pltpu.make_async_copy(w_up, up_s, local_sem.at[6]),
    ]
    for load in loads:
        load.start()
    sems = (local_sem, core_send, core_recv)
    right = share(place, 7, cotangent, cotangent, d_right, local, *sems)
    saves = []

    def save(source, target, index):
        copy = pltpu.make_async_copy(source, target, local_sem.at[index])
        copy.start()
        saves.append(copy)

    def across(k):
        (chunks[k][1] if chunks[k][2] is None else chunks[k][2]).wait_recv()
        chunks[k][3].start()

    def forward(k):
        chunks[k][1].wait_recv()
        chunks[k][2].start()

    gain = mid_gain[...]
    part_one = gain.astype(LOW)
    left_over = gain - part_one.astype(wide)
    part_two = left_over.astype(LOW)
    part_three = (left_over - part_two.astype(wide)).astype(LOW)
    row = lax.broadcasted_iota(jnp.int32, (16, hidden), 0)
    parts = jnp.where(row == 0, part_one.astype(wide), jnp.where(row == 1, part_two.astype(wide), part_three.astype(wide)))
    act_s[pl.ds(local, 16), :] = jnp.where(row < 3, parts, 0.0).astype(LOW)

    def blocks(first, count, body):
        def one(n, carry):
            body(n + first)
            return carry

        lax.fori_loop(0, count, one, 0)

    def span(n, size):
        return pl.ds(pl.multiple_of(n * size, size), size)

    later = {}

    def arrive(_):
        inbound.finish()
        wait_all(loads)
        save(merged_s, o_merged, 8)

    def project(n):
        at = span(n, 512)
        far_s[:, at] = jnp.dot(merged_s[...], out_s[:, at], preferred_element_type=wide)

    def norms(n):
        rows = span(n, 128)
        unit, inverse = norm_parts(far_s[rows, :])
        far_s[rows, :] = unit
        inverse_s[rows, :] = jnp.broadcast_to(inverse, (128, 128))
        middle = tokens[rows, :].astype(wide) + unit * post_gain[...]
        middle_s[rows, :] = middle
        second_s[rows, :] = (norm_parts(middle)[0] * second_gain[...]).astype(LOW)

    def grow(n):
        at = span(n, 512)
        z = jnp.dot(second_s[...], up_s[:, at], preferred_element_type=wide)
        root = 0.7978845608028654
        square = z * z
        half = 0.5 + 0.5 * jnp.tanh(z * (root + (root * 0.044715) * square))
        value = z * half
        unit_s[:, at] = value
        slope_s[:, at] = half + (value - value * half) * (2.0 * root + (6.0 * root * 0.044715) * square)

    def hidden_norm(n):
        rows = span(n, 64)
        unit, inverse = norm_parts(unit_s[rows, :])
        unit_s[rows, :] = unit
        inner_s[rows, :] = jnp.broadcast_to(inverse, (64, 128))
        act_s[rows, :] = (unit * gain).astype(LOW)

    def settle_weights():
        for k in range(4):
            chunks[k][0].wait_recv()
            chunks[k][3].wait_recv()
            mine[k].wait()
        grad_s[...] = jnp.zeros_like(grad_s)

    def shrink(n):
        at = span(n, 512)
        total = jnp.dot(act_s[...], down_s[:, at], preferred_element_type=wide)
        low = cotangent[:, at].astype(wide)
        value = total[:local]
        layer_s[:, at] = (middle_s[:, at] + value).astype(LOW)
        weight = jnp.sum(total[local:], axis=0, keepdims=True)
        first = jnp.sum(low * weight, axis=1, keepdims=True) * (1.0 / hidden)
        second = jnp.sum(low * value, axis=1, keepdims=True) * (1.0 / hidden)
        grad_s[0] = grad_s[0] + jnp.broadcast_to(first, (local, 128))
        grad_s[1] = grad_s[1] + jnp.broadcast_to(second, (local, 128))

    def write_down(p, value):
        o_down[:, pl.ds(p * 256, 256)] = value

    down = Scatter(
        place, (d_whole, d_first, d_second, d_near, d_far), (s_send, s_recv), MIDDLE_X_FIRST,
        lambda p: d_left, lambda p: d_right.at[:, pl.ds(p * 256, 256)], write_down,
    )

    def pull_hidden(n):
        at = span(n, 512)
        grad = nt(cotangent[...], down_s[at, :])
        unit = unit_s[:, at]
        o_gains[3:4, at] = jnp.sum(grad * unit, axis=0, keepdims=True)
        pulled = grad * mid_gain[:, at] - grad_s[0][:, 0:1] - unit * grad_s[1][:, 0:1]
        hidden_s[:, at] = (inner_s[:, 0:1] * pulled * slope_s[:, at]).astype(LOW)

    def pull_second(n):
        at = span(n, 512)
        o_middle[:, at] = nt(hidden_s[...], up_s[at, :])

    def pull_norms(n, totals):
        rows = span(n, 128)
        grad = o_middle[rows, :]
        unit, inverse = norm_parts(middle_s[rows, :])
        grad_middle = cotangent[rows, :].astype(wide) + norm_pull(grad, unit, inverse, second_gain[...])
        o_middle[rows, :] = grad_middle
        outer = far_s[rows, :]
        projected_s[rows, :] = norm_pull(grad_middle, outer, inverse_s[rows, 0:1], post_gain[...]).astype(LOW)
        return (
            totals[0] + jnp.sum(grad_middle * outer, axis=0, keepdims=True),
            totals[1] + jnp.sum(grad * unit, axis=0, keepdims=True),
        )

    def pull_merged(n):
        at = span(n, 512)
        merged_s[:, at] = nt(projected_s[...], out_s[at, :]).astype(LOW)

    def compute(p):
        if later.get("left"):
            wait_all(right)
            wait_all(later.pop("left"))
        down.compute(p)

    def do_norms(_):
        blocks(0, local // 128, norms)
        save(second_s, o_second, 9)

    def do_hidden_norm(_):
        blocks(0, local // 64, hidden_norm)
        later["left"] = share_left(place, 10, act_s, d_left, local, *sems)

    def do_shrink(n):
        if n == 0:
            settle_weights()
        else:
            blocks(n - 1, 1, shrink)
        if n == 2:
            save(layer_s, o_layer, 18)

    def do_pull_hidden(n):
        blocks(n * (hidden // 2048), hidden // 2048, pull_hidden)
        if n == 3:
            save(hidden_s, o_hidden, 15)

    def do_pull_norms(_):
        nothing = jnp.zeros((1, width), wide)
        post, second = lax.fori_loop(0, local // 128, pull_norms, (nothing, nothing))
        o_gains[1:2, 0:width] = post
        o_gains[2:3, 0:width] = second
        save(projected_s, o_projected, 16)
        save(o_middle, o_grad, 19)

    def do_pull_merged(_):
        saves[0].wait()
        blocks(0, width // 512, pull_merged)
        later["out"] = ToHeads(
            place, merged_s, o_heads, relay.at[1], [sem.at[1] for sem in exchange_sem], local_sem.at[17]
        )
        later["out"].start()

    act = (
        compute,
        lambda p: down.advance(p, 1),
        lambda p: down.advance(p, 2),
        lambda p: down.advance(p, 3),
        lambda p: down.advance(p, 4),
        forward,
        across,
        lambda n: blocks(n * (hidden // 2048), hidden // 2048, grow),
        do_shrink,
        do_pull_hidden,
        lambda n: blocks(n, 1, pull_second),
        lambda n: inbound.pass_on(),
        arrive,
        lambda n: blocks(0, width // 512, project),
        do_norms,
        do_hidden_norm,
        do_pull_norms,
        do_pull_merged,
        lambda n: later["out"].pass_on(),
        lambda n: later["out"].finish(),
    )
    for code in MIDDLE_ORDER:
        act[code // 100](code % 100)
    wait_all(saves[1:])
    for p in range(4):
        down.settle(p)
    for chunk in chunks:
        for copy in chunk:
            if copy is not None:
                copy.wait_send()


def middle(u, tokens, cotangent, post_gain, second_gain, mid_gain, w_out, w_up, w_down):
    local, width = tokens.shape
    hidden = w_up.shape[1]
    any_spec = pl.BlockSpec(memory_space=pl.ANY)
    vmem = pl.BlockSpec(memory_space=pltpu.VMEM)
    dma = pltpu.SemaphoreType.DMA
    wide = jnp.float32
    act = jax.ShapeDtypeStruct((local, width), LOW)
    return pl.pallas_call(
        middle_kernel,
        out_shape=(
            act,
            jax.ShapeDtypeStruct((local, width), wide),
            jax.ShapeDtypeStruct((local * 8, width // 8), LOW),
            act,
            act,
            jax.ShapeDtypeStruct((local, hidden), LOW),
            act,
            jax.ShapeDtypeStruct((8, hidden), wide),
            jax.ShapeDtypeStruct((hidden // 32, width), wide),
        ),
        in_specs=[any_spec] + [vmem] * 5 + [any_spec] * 3,
        out_specs=(any_spec,) * 7 + (vmem,) * 2,
        scratch_shapes=[
            pltpu.VMEM((width, width), LOW),
            pltpu.VMEM((width, hidden), LOW),
            pltpu.VMEM((hidden, width), LOW),
            pltpu.VMEM((local, width), LOW),
            pltpu.VMEM((local, width), LOW),
            pltpu.VMEM((local, hidden), wide),
            pltpu.VMEM((local, hidden), wide),
            pltpu.VMEM((local + 16, hidden), LOW),
            pltpu.VMEM((local, hidden), LOW),
            pltpu.VMEM((local, width), LOW),
            pltpu.VMEM((local, width), wide),
            pltpu.VMEM((local, width), wide),
            pltpu.VMEM((local, width), LOW),
            pltpu.VMEM((local, width), wide),
            pltpu.VMEM((local, 128), wide),
            pltpu.VMEM((local, 128), wide),
            pltpu.VMEM((2, 3, local, width // 8), LOW),
            pltpu.VMEM((2, local, 128), wide),
            pltpu.VMEM((2 * local, hidden // 2), LOW),
            pltpu.VMEM((2 * local, width), LOW),
            *scatter_scratch(4, 128, 256),
            dma((20,)),
            dma((4, 4)),
            dma((4, 4)),
            dma((20,)),
            dma((20,)),
            *exchange_sems(2),
            dma((4, 4)),
            dma((4, 4)),
        ],
        compiler_params=pltpu.CompilerParams(
            collective_id=2, has_side_effects=True, vmem_limit_bytes=VMEM_BYTES
        ),
        name="middle",
    )(
        u, tokens, cotangent, post_gain.reshape(1, width), second_gain.reshape(1, width),
        mid_gain.reshape(1, hidden), w_out, w_up, w_down,
    )


HALF = 512
X_FIRST = (2, 3, 9, 13)
TAIL_ORDER = (
    0, 2, 3, 4, 5, 7, 500, 6, 8, 100, 102, 1, 9, 104, 103, 105, 600, 700, 501, 14,
    15, 107, 200, 106, 109, 204, 205, 300, 108, 304, 502, 305, 601, 701, 12, 207, 101, 202, 203, 206,
    13, 307, 400, 404, 303, 208, 114, 602, 702, 800, 900, 306, 308, 403, 10, 201, 407, 209, 302, 11,
    115, 406, 301, 901, 112, 309, 214, 402, 401, 215, 408, 113, 405, 110, 212, 902, 314, 409, 210, 315,
    111, 312, 213, 414, 310, 211, 415, 313, 412, 311, 410, 413, 411,
)


def tail_kernel(
    dq, dk, dv, tokens, gain, middle_in, triple_in, act_up, act_out, act_in, g_up, g_out, gains, scales,
    o_tokens, o_triple, o_out, o_up, o_gains,
    e_left, e_right, e_whole, e_first, e_second, e_near, e_far,
    triple, middle, tokens_s, grad_s, gain_s, gain_r, relay,
    local_sem, core_send, core_recv, x_send, x_recv, z_send, z_recv, s_send, s_recv, gain_send, gain_recv,
):
    place = Place()
    partner = place.core_partner()
    local, width = tokens.shape
    heads_width = dq.shape[1]
    seq_peers = [(place.dp, (place.seq + k) % 8) for k in range(1, 8)]
    dp_peers = [((place.dp + k) % 4, place.seq) for k in range(1, 4)]
    meet(seq_peers + dp_peers)

    def start_exchange(t):
        return ToTokens(
            place, (dv, dk, dq)[t], e_right.at[7 - t, pl.ds(0, local), :], relay.at[t],
            [sem.at[t] for sem in (x_send, x_recv, z_send, z_recv)], local_sem.at[13 + t],
        )

    exchanges = [start_exchange(t) for t in range(3)]

    load_triple = pltpu.make_async_copy(triple_in, triple, local_sem.at[16])
    load_middle = pltpu.make_async_copy(middle_in, middle, local_sem.at[17])

    sems = (local_sem, core_send, core_recv)
    ready = {"up": share_left(place, 0, act_up, e_left.at[0], local, *sems)}
    for k in range(4):
        part = g_up.at[:, pl.ds(k * BLOCK, BLOCK)]
        ready[k] = share(place, 2 + k, part, part, e_right.at[k], local, *sems)
    ready["out"] = share_left(place, 6, act_out, e_left.at[1], local, *sems)
    ready["out"] += share(place, 8, g_out, g_out, e_right.at[4], local, *sems)
    ready["in"] = share_left(place, 9, act_in, e_left.at[2], local, *sems)
    load_triple.start()
    load_middle.start()

    def write(p, value):
        at = pl.ds(p % 2 * HALF, HALF)
        if p < 8:
            o_up[:, pl.ds(p * HALF, HALF)] = value
        elif p < 10:
            o_out[:, at] = value
        else:
            o_triple[:, pl.ds((p - 10) * HALF, HALF)] = value

    engine = Scatter(
        place, (e_whole, e_first, e_second, e_near, e_far), (s_send, s_recv), X_FIRST,
        lambda p: e_left.at[0 if p < 8 else 1 if p < 10 else 2],
        lambda p: e_right.at[p // 2, :, pl.ds(p % 2 * HALF, HALF)], write,
    )
    gain_s[0:3, :] = gains[0:3, 0:width]
    for k in range(gains.shape[1] // width):
        gain_s[3 + k : 4 + k, :] = gains[3:4, pl.ds(k * width, width)]
    gain_s[7:8, :] = jnp.zeros((1, width), jnp.float32)
    gain_s[7:8, 0:128] = scales[...]
    def bring_back(t):
        exchanges[t].finish()
        slot = e_right.at[7 - t]
        move = remote(
            slot.at[pl.ds(0, local), :], slot.at[pl.ds(local, local), :],
            core_send.at[11 + t], core_recv.at[11 + t], partner,
        )
        move.start()
        return move

    def pull_normed(t):
        if t == 0:
            load_triple.wait()

        def one(n, carry):
            rows = pl.ds(pl.multiple_of(n * 256, 256), 256)
            part = nt(e_right[7 - t, pl.ds(0, local), :], triple[rows, pl.ds((2 - t) * width, width)])
            grad_s[:, rows] = part if t == 0 else grad_s[:, rows] + part
            return carry

        lax.fori_loop(0, width // 256, one, 0)

    def norm_rows(n, total):
        rows = pl.ds(pl.multiple_of(n * 128, 128), 128)
        unit, inverse = norm_parts(tokens[rows, :].astype(jnp.float32))
        grad = grad_s[rows, :]
        pulled = norm_pull(grad, unit, inverse, gain[...])
        tokens_s[rows, :] = (middle[rows, :] + pulled).astype(LOW)
        return total + jnp.sum(grad * unit, axis=0, keepdims=True)

    save_tokens = pltpu.make_async_copy(tokens_s, o_tokens, local_sem.at[18])

    def pull_norm(_):
        load_middle.wait()
        gain_s[0:1, :] = lax.fori_loop(0, local // 128, norm_rows, jnp.zeros((1, width), jnp.float32))
        save_tokens.start()

    def gain_moves(peers, first):
        out = [
            remote(gain_s, gain_r.at[first + k], gain_send.at[first + k], gain_recv.at[first + k], peer)
            for k, peer in enumerate(peers)
        ]
        for move in out:
            move.start()
        return out

    gain_steps = {}

    def sum_gains(step):
        if step == 0:
            gain_steps[0] = gain_moves(dp_peers, 0)
        elif step == 1:
            wait_all(gain_steps[0])
            gain_s[...] = gain_s[...] + gain_r[0] + gain_r[1] + gain_r[2]
            o_gains[7:8, :] = gain_s[7:8, 0:128]
            gain_steps[1] = gain_moves(seq_peers, 3)
        else:
            wait_all(gain_steps[1])
            total = gain_s[...]
            for k in range(7):
                total = total + gain_r[3 + k]
            gain_s[...] = total
            device = place.dp * 8 + place.seq
            pick = (
                lax.broadcasted_iota(jnp.int32, (width, 128), 0)
                == device * 32 + lax.broadcasted_iota(jnp.int32, (width, 128), 1)
            ).astype(jnp.float32)
            o_gains[0:3, :] = jnp.dot(
                gain_s[...], pick, preferred_element_type=jnp.float32, precision=lax.Precision.HIGHEST
            )[0:3]
            block = gain_s[:, pl.ds(pl.multiple_of((device % 8) * 128, 128), 128)]
            row = lax.broadcasted_iota(jnp.int32, block.shape, 0)
            o_gains[3:4, :] = jnp.sum(jnp.where(row == 3 + device // 8, block, 0.0), axis=0, keepdims=True)

    backs, waited = {}, set()

    def need(key):
        if key not in waited:
            wait_all(ready[key])
            waited.add(key)

    def compute(p):
        need("up" if p < 8 else "out" if p < 10 else "in")
        if p < 8:
            need(p // 2)
        elif p >= 10 and 7 - p // 2 in backs:
            backs.pop(7 - p // 2).wait()
        engine.compute(p)

    def bring(t):
        backs[t] = bring_back(t)

    act = (
        compute,
        lambda p: engine.advance(p, 1),
        lambda p: engine.advance(p, 2),
        lambda p: engine.advance(p, 3),
        lambda p: engine.advance(p, 4),
        lambda t: exchanges[t].pass_on(),
        bring,
        pull_normed,
        pull_norm,
        sum_gains,
    )
    for code in TAIL_ORDER:
        act[code // 100](code % 100)
    o_gains[4:7, :] = jnp.zeros((3, 128), jnp.float32)
    save_tokens.wait()
    for p in range(16):
        engine.settle(p)


def tail(dqkv, tokens, gain, middle, triple, acts, grads, gains, scales):
    local, width = tokens.shape
    heads_width = dqkv[0].shape[1]
    hidden = grads[0].shape[1]
    any_spec = pl.BlockSpec(memory_space=pl.ANY)
    vmem = pl.BlockSpec(memory_space=pltpu.VMEM)
    wide = jnp.float32
    dma = pltpu.SemaphoreType.DMA
    return pl.pallas_call(
        tail_kernel,
        out_shape=(
            jax.ShapeDtypeStruct((local, width), LOW),
            jax.ShapeDtypeStruct((width // 32, 3 * width), wide),
            jax.ShapeDtypeStruct((width // 32, width), wide),
            jax.ShapeDtypeStruct((width // 32, hidden), wide),
            jax.ShapeDtypeStruct((8, 128), wide),
        ),
        in_specs=[any_spec] * 3 + [vmem] * 2 + [any_spec] * 7 + [vmem] * 2,
        out_specs=(any_spec,) + (vmem,) * 4,
        scratch_shapes=[pltpu.VMEM((3, 2 * local, width // 2), LOW), pltpu.VMEM((8, 2 * local, width), LOW)]
        + scatter_scratch(16, 32, HALF)
        + [
            pltpu.VMEM((width, 3 * width), LOW),
            pltpu.VMEM((local, width), wide),
            pltpu.VMEM((local, width), LOW),
            pltpu.VMEM((local, width), wide),
            pltpu.VMEM((8, width), wide),
            pltpu.VMEM((10, 8, width), wide),
            pltpu.VMEM((3, 3, local, heads_width), LOW),
            dma((20,)),
            dma((20,)),
            dma((20,)),
            *exchange_sems(3),
            dma((4, 16)),
            dma((4, 16)),
            dma((10,)),
            dma((10,)),
        ],
        compiler_params=pltpu.CompilerParams(
            collective_id=3, has_side_effects=True, vmem_limit_bytes=VMEM_BYTES
        ),
        name="tail",
    )(*dqkv, tokens, gain.reshape(1, width), middle, triple, *acts, *grads, gains, scales)


def finish_kernel(count, *refs):
    ins, outs = refs[: count + 1], refs[count + 1 :]
    for k in range(count):
        outs[k][...] = ins[k][...]
    sums = ins[count]
    for row in range(3):
        outs[count + row][...] = sums[row, 0 : outs[count + row].shape[0]]
    outs[count + 3][...] = sums[3]
    row = sums[7:8, :]
    lane = lax.broadcasted_iota(jnp.int32, row.shape, 1)
    heads = outs[count + 4].shape[1]
    for h in range(heads):
        own = (lane >= h * HEAD) & (lane < (h + 1) * HEAD)
        outs[count + 4][:, h : h + 1] = jnp.sum(jnp.where(own, row, 0.0), axis=1, keepdims=True)


def finish(arrays, sums, own, heads):
    vmem = pl.BlockSpec(memory_space=pltpu.VMEM)
    wide = jnp.float32
    shapes = [jax.ShapeDtypeStruct(a.shape, a.dtype) for a in arrays]
    shapes += [jax.ShapeDtypeStruct((own,), wide)] * 3 + [jax.ShapeDtypeStruct((sums.shape[1],), wide), jax.ShapeDtypeStruct((1, heads), wide)]
    return pl.pallas_call(
        functools.partial(finish_kernel, len(arrays)),
        out_shape=tuple(shapes),
        in_specs=[vmem] * (len(arrays) + 1),
        out_specs=(vmem,) * len(shapes),
        name="finish",
    )(*arrays, sums)


def per_device(
    sizes,
    tokens,
    segment_ids,
    first_gain,
    triple_weight,
    head_scale,
    output_weight,
    post_gain,
    second_gain,
    up_weight,
    mid_gain,
    down_weight,
    cotangent,
):
    inputs = tokens[0].astype(jnp.float32)
    width = inputs.shape[1]
    doc_ids = lax.all_gather(segment_ids[0], "seq", axis=0, tiled=True)
    triple_full, output_full = (
        lax.all_gather(triple_weight, "dp", axis=0, tiled=True),
        lax.all_gather(output_weight, "dp", axis=0, tiled=True),
    )
    normed, pull_first = jax.vjp(layer_norm, inputs, first_gain)
    normed_low = normed.astype(jnp.bfloat16)
    triple = jnp.dot(normed_low, triple_full, preferred_element_type=jnp.float32).astype(
        jnp.bfloat16
    )
    queries, keys_all, values_all = (
        lax.all_to_all(triple[:, :width], "seq", split_axis=1, concat_axis=0, tiled=True),
        lax.all_to_all(
            triple[:, width : 2 * width], "seq", split_axis=1, concat_axis=0, tiled=True
        ),
        lax.all_to_all(triple[:, 2 * width :], "seq", split_axis=1, concat_axis=0, tiled=True),
    )
    heads_here = queries.shape[1] // HEAD
    starts = document_starts(doc_ids)
    attended, scaled, logsum = attend_forward(
        queries, keys_all, values_all, starts, head_scale
    )
    merged = lax.all_to_all(scaled, "seq", split_axis=0, concat_axis=1, tiled=True)
    projected = jnp.dot(merged, output_full, preferred_element_type=jnp.float32)
    post_normed, pull_post = jax.vjp(layer_norm, projected, post_gain)
    middle = inputs + post_normed
    second, pull_second = jax.vjp(layer_norm, middle, second_gain)
    second_low = second.astype(jnp.bfloat16)
    feed_up, feed_down = (
        lax.all_gather(up_weight, "dp", axis=0, tiled=True),
        lax.all_gather(down_weight, "dp", axis=0, tiled=True),
    )
    hidden = jnp.dot(second_low, feed_up, preferred_element_type=jnp.float32)
    activated, pull_mid = jax.vjp(gelu_norm, hidden, mid_gain)
    activated_low = activated.astype(jnp.bfloat16)
    layer_out = (
        middle + jnp.dot(activated_low, feed_down, preferred_element_type=jnp.float32)
    ).astype(jnp.bfloat16)
    upstream = cotangent[0]
    grad_act = times_transposed(upstream, feed_down)
    grad_hidden, grad_mid = pull_mid(grad_act)
    grad_hidden_low = grad_hidden.astype(jnp.bfloat16)
    grad_second_in = times_transposed(grad_hidden_low, feed_up)
    grad_middle_part, grad_second = pull_second(grad_second_in)
    grad_middle = upstream.astype(jnp.float32) + grad_middle_part
    grad_projected, grad_post = pull_post(grad_middle)
    grad_projected_low = grad_projected.astype(jnp.bfloat16)
    grad_merged = times_transposed(grad_projected_low, output_full).astype(jnp.bfloat16)
    grad_scaled = lax.all_to_all(
        grad_merged, "seq", split_axis=1, concat_axis=0, tiled=True
    )
    grad_queries, grad_keys, grad_values, scale_lanes = attend_backward(
        queries, keys_all, values_all, attended, grad_scaled, starts, head_scale, logsum
    )
    scale_terms = jnp.sum(scale_lanes.reshape(heads_here, HEAD), axis=1)
    back_queries, back_keys, back_values = (
        lax.all_to_all(
            grad_queries.astype(jnp.bfloat16), "seq", split_axis=0, concat_axis=1, tiled=True
        ),
        lax.all_to_all(
            grad_keys.astype(jnp.bfloat16), "seq", split_axis=0, concat_axis=1, tiled=True
        ),
        lax.all_to_all(
            grad_values.astype(jnp.bfloat16), "seq", split_axis=0, concat_axis=1, tiled=True
        ),
    )
    grad_triple_act = jnp.concatenate((back_queries, back_keys, back_values), axis=1)
    grad_normed = times_transposed(grad_triple_act, triple_full)
    grad_input_part, grad_first = pull_first(grad_normed)
    grad_tokens = (grad_middle + grad_input_part).astype(jnp.bfloat16)
    low = jnp.bfloat16
    grad_down = scatter_rows(transposed_times(activated_low, upstream).astype(low), sizes)
    grad_up = scatter_rows(transposed_times(second_low, grad_hidden_low).astype(low), sizes)
    grad_output = scatter_rows(transposed_times(merged, grad_projected_low).astype(low), sizes)
    gains = jnp.concatenate(
        (
            grad_first[:, None],
            grad_post[:, None],
            grad_second[:, None],
            grad_mid.reshape(width, -1),
        ),
        axis=1,
    )
    gains = jnp.pad(gains, ((0, 0), (0, 128 - gains.shape[1])))
    grad_triple = scatter_rows(
        jnp.concatenate(
            (transposed_times(normed_low, grad_triple_act).astype(low), gains.astype(low)), axis=1
        ),
        sizes,
    )
    gain_sums = grad_triple[:, 3 * width :]
    grad_scale = lax.psum(scale_terms, "dp")
    return (
        layer_out[None],
        grad_tokens[None],
        gain_sums[:, 0],
        grad_triple[:, : 3 * width],
        grad_scale,
        grad_output,
        gain_sums[:, 1],
        gain_sums[:, 2],
        grad_up,
        gain_sums[:, 3 : 3 + mid_gain.shape[0] // width].reshape(-1),
        grad_down,
    )


def per_device_chips(
    sizes,
    tokens,
    segment_ids,
    first_gain,
    triple_weight,
    head_scale,
    output_weight,
    post_gain,
    second_gain,
    up_weight,
    mid_gain,
    down_weight,
    cotangent,
):
    width, hidden = tokens.shape[2], up_weight.shape[1]
    heads_here = width // HEAD // sizes[1]
    values, keys, queries, normed, starts, triple_full, output_full, up_full = front(
        tokens[0], first_gain, segment_ids, triple_weight, output_weight, up_weight
    )
    attended, scaled, logsum = attend_forward(queries, keys, values, starts, head_scale)
    layer_out, grad_middle, grad_scaled, merged, second_low, grad_hidden, grad_projected, gains, grad_down = middle(
        scaled, tokens[0], cotangent[0], post_gain, second_gain, mid_gain, output_full, up_full, down_weight
    )
    grad_queries, grad_keys, grad_values, scale_lanes = attend_backward(
        queries, keys, values, attended, grad_scaled, starts, head_scale, logsum
    )
    grad_tokens, grad_triple, grad_output, grad_up, sums = tail(
        (grad_queries, grad_keys, grad_values),
        tokens[0],
        first_gain,
        grad_middle,
        triple_full,
        (second_low, merged, normed),
        (grad_hidden, grad_projected),
        gains,
        scale_lanes,
    )
    layer_out, grad_tokens, grad_triple, grad_output, grad_up, grad_down, first, post, second, mid, scale = finish(
        (layer_out, grad_tokens, grad_triple, grad_output, grad_up, grad_down), sums, width // 32, heads_here
    )
    return (
        layer_out[None],
        grad_tokens[None],
        first,
        grad_triple,
        scale[0],
        grad_output,
        post,
        second,
        grad_up,
        mid,
        grad_down,
    )


def solution(mesh):
    placed = (
        P("dp", "seq", None),
        P("dp", "seq"),
        P(),
        P("dp", None),
        P(),
        P("dp", None),
        P(),
        P(),
        P("dp", None),
        P(),
        P("dp", None),
        P("dp", "seq", None),
    )
    sizes = (mesh.shape["dp"], mesh.shape["seq"])
    program = per_device_chips if sizes == (4, 8) else per_device
    return jax.shard_map(
        functools.partial(program, sizes),
        mesh=mesh,
        in_specs=placed,
        out_specs=(
            P("dp", "seq", None),
            P("dp", "seq", None),
            P(("dp", "seq")),
            P(("dp", "seq"), None),
            P("seq"),
            P(("dp", "seq"), None),
            P(("dp", "seq")),
            P(("dp", "seq")),
            P(("dp", "seq"), None),
            P(("dp", "seq")),
            P(("dp", "seq"), None),
        ),
        check_vma=False,
    )
```

```python
import functools
import jax
import jax.numpy as jnp
from jax import lax
from jax.sharding import PartitionSpec as P
from jax.experimental import pallas as pl
from jax.experimental.pallas import tpu as pltpu

HEAD = 64
NEG = -1e30
BQ = 256
QB = 1024
KB = 512


def nt(a, b):
    return lax.dot_general(a, b, (((1,), (1,)), ((), ())), preferred_element_type=jnp.float32)


def tn(a, b):
    return lax.dot_general(a, b, (((0,), (0,)), ((), ())), preferred_element_type=jnp.float32)


def stack_heads(block, heads):
    if heads == 1:
        return block
    lane = lax.broadcasted_iota(jnp.int32, block.shape, 1)
    zero = jnp.zeros_like(block)
    return jnp.concatenate(
        [jnp.where((lane >= h * HEAD) & (lane < (h + 1) * HEAD), block, zero) for h in range(heads)],
        axis=0,
    )


def unstack_heads(wide, heads):
    rows = wide.shape[1] // heads
    return jnp.concatenate(
        [wide[h * HEAD : (h + 1) * HEAD, h * rows : (h + 1) * rows] for h in range(heads)], axis=0
    )


def scale_row(scale_ref, width):
    heads = width // HEAD
    first = lax.axis_index("seq") * heads
    lane = lax.broadcasted_iota(jnp.int32, (1, width), 1)
    row = jnp.full((1, width), scale_ref[first], jnp.float32)
    for h in range(1, heads):
        row = jnp.where(lane >= h * HEAD, scale_ref[first + h], row)
    return row


def forward_kernel(heads, first_ref, q_ref, k_ref, v_ref, start_ref, scale_ref,
                   o_ref, u_ref, lse_ref, m_s, l_s, acc_s):
    rows, step_rows = QB, KB
    scale = scale_row(scale_ref, q_ref.shape[1])
    ratio = rows // step_rows

    def one(i, carry):
        mine = pl.ds(pl.multiple_of(i * rows, rows), rows)
        queries = stack_heads(q_ref[mine, :] * jnp.bfloat16(HEAD ** -0.5), heads)
        starts = jnp.concatenate([start_ref[i * (rows // BQ) + k] for k in range(rows // BQ)] * heads, axis=1)

        def scores_of(j, count, queries, starts):
            at = pl.ds(pl.multiple_of(j * BQ, BQ), count)
            scores = nt(k_ref[at, :], queries)
            if starts is not None:
                key = j * BQ + lax.broadcasted_iota(jnp.int32, scores.shape, 0)
                scores = jnp.where(key >= starts, scores, NEG)
            return at, scores

        def fold(at, scores, columns):
            before = m_s[:, columns]
            highest = jnp.maximum(before, jnp.max(scores, axis=0, keepdims=True))
            fade = jnp.exp(before - highest)
            weights = jnp.exp(scores - highest)
            m_s[:, columns] = highest
            l_s[:, columns] = l_s[:, columns] * fade + jnp.sum(weights, axis=0, keepdims=True)
            acc_s[:, columns] = acc_s[:, columns] * fade + tn(v_ref[at, :], weights.astype(jnp.bfloat16))

        def step(j, masked):
            at, scores = scores_of(j * (step_rows // BQ), step_rows, queries, starts if masked else None)
            fold(at, scores, slice(None))

        for k in range(rows // BQ):
            wide = rows - k * BQ
            late = [slice(h * rows + k * BQ, (h + 1) * rows) for h in range(heads)]
            some = queries if k == 0 else jnp.concatenate([queries[c] for c in late], axis=0)
            start = starts if k == 0 else jnp.concatenate([starts[:, c] for c in late], axis=1)
            at, scores = scores_of(i * (rows // BQ) + k, BQ, some, start)
            key = lax.broadcasted_iota(jnp.int32, scores.shape, 0)
            for h in range(heads):
                part = scores[:, h * wide : (h + 1) * wide]
                lane = lax.broadcasted_iota(jnp.int32, part.shape, 1)
                part = jnp.where(key[:, :wide] <= lane, part, NEG)
                if k == 0:
                    highest = jnp.max(part, axis=0, keepdims=True)
                    weights = jnp.exp(part - highest)
                    m_s[:, late[h]] = highest
                    l_s[:, late[h]] = jnp.sum(weights, axis=0, keepdims=True)
                    acc_s[:, late[h]] = tn(v_ref[at, :], weights.astype(jnp.bfloat16))
                else:
                    fold(at, part, late[h])

        low = first_ref[i * (rows // BQ), 0, 0] // step_rows
        last = first_ref[i * (rows // BQ) + rows // BQ - 1, 0, BQ - 1]
        full = jnp.minimum((last + step_rows - 1) // step_rows, i * ratio)

        def plain(j, carry):
            step(j, False)
            return carry

        def edge(j, carry):
            step(j, True)
            return carry

        lax.fori_loop(full, i * ratio, plain, 0)
        lax.fori_loop(low, full, edge, 0)
        total = l_s[...]
        out = unstack_heads(acc_s[...] * (1.0 / total), heads).T
        o_ref[mine, :] = out
        u_ref[mine, :] = (out * scale).astype(jnp.bfloat16)
        logsum = m_s[...] + jnp.log(total)
        for k in range(rows // BQ):
            lse_ref[i * (rows // BQ) + k] = jnp.concatenate(
                [logsum[:, h * rows + k * BQ : h * rows + (k + 1) * BQ] for h in range(heads)], axis=1
            )
        return carry

    lax.fori_loop(0, q_ref.shape[0] // rows, one, 0)


def attend_forward(queries, keys, values, starts, scales):
    length, width = queries.shape
    heads = width // HEAD
    vmem = pl.BlockSpec(memory_space=pltpu.VMEM)
    return pl.pallas_call(
        functools.partial(forward_kernel, heads),
        out_shape=(
            jax.ShapeDtypeStruct((length, width), jnp.float32),
            jax.ShapeDtypeStruct((length, width), jnp.bfloat16),
            jax.ShapeDtypeStruct((length // BQ, 1, heads * BQ), jnp.float32),
        ),
        in_specs=[pl.BlockSpec(memory_space=pltpu.SMEM)] + [vmem] * 4 + [pl.BlockSpec(memory_space=pltpu.SMEM)],
        out_specs=(vmem,) * 3,
        scratch_shapes=[
            pltpu.VMEM((1, heads * QB), jnp.float32),
            pltpu.VMEM((1, heads * QB), jnp.float32),
            pltpu.VMEM((width, heads * QB), jnp.float32),
        ],
        cost_estimate=pl.CostEstimate(
            flops=length * length * width, bytes_accessed=16 * length * width, transcendentals=0
        ),
        name="attend_forward",
    )(starts, queries, keys, values, starts, scales)


def backward_kernel(heads, count, first_ref, q_ref, k_ref, v_ref, o_ref, du_ref, start_ref, scale_ref, lse_ref, *refs):
    carried, refs = refs[:count], refs[count:]
    (dq_ref, dk_ref, dv_ref, ds_ref), refs = refs[:4], refs[4:]
    placed, refs = refs[:count], refs[count:]
    (qs_s, dos_s, delta_s, dqt_s, dk_s, dv_s), refs = refs[:6], refs[6:]
    held, sem = refs[:count], refs[count:]
    takes = [pltpu.make_async_copy(carried[n], held[n], sem[0].at[n]) for n in range(count)]
    puts = [pltpu.make_async_copy(held[n], placed[n], sem[0].at[count + n]) for n in range(count)]
    for copy in takes:
        copy.start()
    rows, group = BQ, 1
    blocks = qs_s.shape[0]
    scale = scale_row(scale_ref, q_ref.shape[1])

    def prepare(i, total):
        at = pl.ds(pl.multiple_of(i * rows, rows), rows)
        qs_s[i] = stack_heads(q_ref[at, :] * jnp.bfloat16(HEAD ** -0.5), heads)
        grad = du_ref[at, :].astype(jnp.float32)
        out = o_ref[at, :]
        low = (grad * scale).astype(jnp.bfloat16)
        dos_s[i] = stack_heads(low, heads)
        inner = (low.astype(jnp.float32) * out).T
        delta_s[i] = jnp.concatenate(
            [jnp.sum(inner[h * HEAD : (h + 1) * HEAD], axis=0, keepdims=True) for h in range(heads)],
            axis=1,
        )
        dqt_s[i] = jnp.zeros(dqt_s.shape[1:], jnp.float32)
        return total + jnp.sum(grad * out, axis=0, keepdims=True)

    ds_ref[...] = lax.fori_loop(0, blocks, prepare, jnp.zeros(ds_ref.shape, jnp.float32))
    for take, put in zip(takes, puts):
        take.wait()
        put.start()

    def one(j, carry):
        mine = pl.ds(pl.multiple_of(j * BQ, BQ), BQ)
        keys, values = k_ref[mine, :], v_ref[mine, :]

        def step(i, masked, diagonal):
            queries, grads = qs_s[i], dos_s[i]
            scores = nt(keys, queries)
            if masked or diagonal:
                key = j * BQ + lax.broadcasted_iota(jnp.int32, scores.shape, 0)
                starts = jnp.concatenate([start_ref[i * group + k] for k in range(group)] * heads, axis=1)
                allowed = key >= starts
                if diagonal:
                    lane = lax.broadcasted_iota(jnp.int32, scores.shape, 1) & (rows - 1)
                    allowed = allowed & (key <= i * rows + lane)
                scores = jnp.where(allowed, scores, NEG)
            weights = jnp.exp(scores - lse_ref[i])
            pulls = nt(values, grads)
            low = (weights * (pulls - delta_s[i])).astype(jnp.bfloat16)
            part_v = jnp.dot(weights.astype(jnp.bfloat16), grads, preferred_element_type=jnp.float32)
            part_k = jnp.dot(low, queries, preferred_element_type=jnp.float32)
            part_q = tn(keys, low)
            if diagonal:
                dv_s[...] = part_v
                dk_s[...] = part_k
            else:
                dv_s[...] += part_v
                dk_s[...] += part_k
            return part_q

        high, full = jnp.int32(0), jnp.int32(0)
        for i in range(blocks):
            high += (first_ref[i * group, 0, 0] // BQ <= j).astype(jnp.int32)
            full += (first_ref[i * group + group - 1, 0, BQ - 1] <= j * BQ).astype(jnp.int32)
        own = j // group
        full = jnp.maximum(full, own + 1)

        def plain(i, carry):
            dqt_s[i] += step(i, False, False)
            return carry

        def edge(i, carry):
            dqt_s[i] += step(i, True, False)
            return carry

        dqt_s[own] += step(own, False, True)
        lax.fori_loop(own + 1, full, plain, 0)
        lax.fori_loop(full, high, edge, 0)
        dk_ref[mine, :] = dk_s[...].astype(jnp.bfloat16)
        dv_ref[mine, :] = dv_s[...].astype(jnp.bfloat16)
        return carry

    lax.fori_loop(0, blocks * group, one, 0)

    def finish(i, carry):
        at = pl.ds(pl.multiple_of(i * rows, rows), rows)
        dq_ref[at, :] = (unstack_heads(dqt_s[i], heads).T * HEAD ** -0.5).astype(jnp.bfloat16)
        return carry

    lax.fori_loop(0, blocks, finish, 0)
    for put in puts:
        put.wait()


def attend_backward(queries, keys, values, outs, grads, starts, scales, logsum, carried=()):
    length, width = queries.shape
    heads = width // HEAD
    blocks = length // BQ
    vmem = pl.BlockSpec(memory_space=pltpu.VMEM)
    return pl.pallas_call(
        functools.partial(backward_kernel, heads, len(carried)),
        out_shape=(jax.ShapeDtypeStruct((length, width), jnp.bfloat16),) * 3
        + (jax.ShapeDtypeStruct((1, width), jnp.float32),)
        + tuple(jax.ShapeDtypeStruct(a.shape, a.dtype) for a in carried),
        in_specs=[pl.BlockSpec(memory_space=pltpu.SMEM)] + [vmem] * 6 + [pl.BlockSpec(memory_space=pltpu.SMEM), vmem]
        + [pl.BlockSpec(memory_space=pl.ANY)] * len(carried),
        out_specs=(vmem,) * 4 + (pl.BlockSpec(memory_space=pl.ANY),) * len(carried),
        scratch_shapes=[
            pltpu.VMEM((blocks, heads * BQ, width), jnp.bfloat16),
            pltpu.VMEM((blocks, heads * BQ, width), jnp.bfloat16),
            pltpu.VMEM((blocks, 1, heads * BQ), jnp.float32),
            pltpu.VMEM((blocks, width, heads * BQ), jnp.float32),
            pltpu.VMEM((BQ, width), jnp.float32),
            pltpu.VMEM((BQ, width), jnp.float32),
        ]
        + [pltpu.VMEM(a.shape, a.dtype) for a in carried]
        + ([pltpu.SemaphoreType.DMA((2 * len(carried),))] if carried else []),
        cost_estimate=pl.CostEstimate(
            flops=3 * length * length * width, bytes_accessed=32 * length * width, transcendentals=0
        ),
        name="attend_backward",
    )(starts, queries, keys, values, outs, grads, starts, scales, logsum, *carried)


def document_starts(doc_ids):
    length = doc_ids.shape[0]
    names = jnp.arange(8, dtype=jnp.int32)
    counts = jnp.sum(doc_ids[None, :] < names[:, None], axis=1, dtype=jnp.int32)
    starts = jnp.sum(
        jnp.where(doc_ids[:, None] == names[None, :], counts[None, :], 0), axis=1, dtype=jnp.int32
    )
    return starts.reshape(length // BQ, 1, BQ)


def layer_norm(values, gains):
    center = values - jnp.mean(values, axis=-1, keepdims=True)
    spread = jnp.mean(center * center, axis=-1, keepdims=True)
    return center * lax.rsqrt(spread + 1e-05) * gains


def gelu_norm(hidden, gains):
    return layer_norm(jax.nn.gelu(hidden, approximate=True), gains)


def transposed_times(left, right):
    return lax.dot_general(
        left, right, (((0,), (0,)), ((), ())), preferred_element_type=jnp.float32
    )


def times_transposed(left, right):
    return lax.dot_general(
        left, right, (((1,), (1,)), ((), ())), preferred_element_type=jnp.float32
    )


def scatter_rows(partial, sizes):
    current = partial
    for axis, size in zip(("dp", "seq"), sizes):
        place = lax.axis_index(axis)
        bits = size.bit_length() - 1
        pieces = current.reshape((2,) * bits + (-1, current.shape[-1]))
        for bit in range(bits):
            at = bits - 1 - bit
            mine = (place >> bit) & 1
            give = lax.dynamic_index_in_dim(pieces, 1 - mine, at, keepdims=False)
            keep = lax.dynamic_index_in_dim(pieces, mine, at, keepdims=False)
            got = lax.ppermute(give, axis, [(i, i ^ (1 << bit)) for i in range(size)])
            pieces = (keep.astype(jnp.float32) + got.astype(jnp.float32)).astype(jnp.bfloat16)
        current = pieces
    return current.astype(jnp.float32)


MESH = pl.DeviceIdType.MESH
LOW = jnp.bfloat16
BLOCK = 1024
VMEM_BYTES = 66_000_000


class Place:
    def __init__(self):
        self.dp, self.seq = lax.axis_index("dp"), lax.axis_index("seq")
        self.core, self.y = self.dp % 2, self.dp // 2
        self.x, self.z = self.seq % 2, self.seq // 2
        self.z0, self.z1 = self.z % 2, self.z // 2

    def core_partner(self):
        return (self.dp + 1 - 2 * self.core, self.seq)

    def y_partner(self):
        return (self.dp + 2 - 4 * self.y, self.seq)

    def x_partner(self):
        return (self.dp, self.seq + 1 - 2 * self.x)

    def near_partner(self):
        return (self.dp, self.seq + 2 - 4 * self.z0)

    def far_partner(self):
        return (self.dp, self.seq + 4 - 8 * self.z1)


def meet(devices):
    barrier = pltpu.get_barrier_semaphore()
    for device in devices:
        pl.semaphore_signal(barrier, inc=1, device_id=device, device_id_type=MESH)
    pl.semaphore_wait(barrier, len(devices))


def remote(source, target, send, receive, device):
    return pltpu.make_async_remote_copy(
        src_ref=source,
        dst_ref=target,
        send_sem=send,
        recv_sem=receive,
        device_id=device,
        device_id_type=MESH,
    )


def lanes_of(z, x, width):
    return pl.ds(pl.multiple_of((z * 2 + x) * width, 128), width)


def rows_of(z, x, local):
    return pl.ds(pl.multiple_of((z * 2 + x) * local, 128), local)


class ToHeads:
    def __init__(self, place, part, target, relay, sems, keep_sem):
        self.place, self.part, self.target, self.relay, self.sems = place, part, target, relay, sems
        self.keep_sem, self.moves, self.sends = keep_sem, [], []

    def other(self, m):
        place = self.place
        low = place.z0 + (m % 2) * (1 - 2 * place.z0)
        high = place.z1 + (m // 2) * (1 - 2 * place.z1)
        return high * 2 + low

    def start(self, steps=(2, 3, 1, 0)):
        place = self.place
        x_send, x_recv, z_send, z_recv = self.sems
        local, width = self.relay.shape[-2:]
        rows = rows_of(place.z, place.x, local)
        for m in steps:
            source = self.part.at[:, lanes_of(self.other(m), 1 - place.x, width)]
            landing = self.target.at[rows, :] if m == 0 else self.relay.at[m - 1]
            move = remote(source, landing, x_send.at[m], x_recv.at[m], place.x_partner())
            move.start()
            (self.moves if m == 0 else self.sends).append(move)
        for m in steps:
            z = self.other(m)
            source = self.part.at[:, lanes_of(z, place.x, width)]
            if m == 0:
                move = pltpu.make_async_copy(source, self.target.at[rows, :], self.keep_sem)
            else:
                device = (place.dp, z * 2 + place.x)
                move = remote(source, self.target.at[rows, :], z_send.at[m - 1], z_recv.at[m - 1], device)
            move.start()
            self.moves.append(move)

    def pass_on(self, steps=(2, 3, 1)):
        place, local = self.place, self.relay.shape[-2]
        x_send, x_recv, z_send, z_recv = self.sems
        rows = rows_of(place.z, 1 - place.x, local)
        for m in steps:
            here = self.relay.at[m - 1]
            remote(here, here, x_send.at[m], x_recv.at[m], place.x_partner()).wait_recv()
            device = (place.dp, self.other(m) * 2 + place.x)
            move = remote(here, self.target.at[rows, :], z_send.at[m + 2], z_recv.at[m + 2], device)
            move.start()
            self.moves.append(move)

    def finish(self):
        for move in self.moves:
            move.wait()
        for move in self.sends:
            move.wait_send()


class ToTokens:
    def __init__(self, place, source, target, relay, sems, keep_sem, steps=(2, 1, 3)):
        self.place, self.target, self.relay, self.sems = place, target, relay, sems
        x_send, x_recv, z_send, z_recv = sems
        local, width = relay.shape[-2:]
        self.moves, self.sends = [], []
        lanes = lanes_of(place.z, place.x, width)
        for x, first in ((1 - place.x, 0), (place.x, 3)):
            for k in steps:
                z, index = (place.z + k) % 4, first + k - 1
                landing = relay.at[k - 1] if first == 0 else target.at[:, lanes]
                move = remote(
                    source.at[rows_of(z, x, local), :],
                    landing,
                    z_send.at[index],
                    z_recv.at[index],
                    (place.dp, z * 2 + place.x),
                )
                move.start()
                (self.sends if first == 0 else self.moves).append(move)
        move = remote(
            source.at[rows_of(place.z, 1 - place.x, local), :],
            target.at[:, lanes],
            x_send.at[0],
            x_recv.at[0],
            place.x_partner(),
        )
        move.start()
        self.moves.append(move)
        move = pltpu.make_async_copy(
            source.at[rows_of(place.z, place.x, local), :], target.at[:, lanes], keep_sem
        )
        move.start()
        self.moves.append(move)

    def pass_on(self):
        place, width = self.place, self.relay.shape[-1]
        x_send, x_recv, z_send, z_recv = self.sems
        for k in (2, 1, 3):
            here = self.relay.at[k - 1]
            remote(here, here, z_send.at[k - 1], z_recv.at[k - 1], place.near_partner()).wait_recv()
            lanes = lanes_of((place.z + 4 - k) % 4, place.x, width)
            move = remote(here, self.target.at[:, lanes], x_send.at[k], x_recv.at[k], place.x_partner())
            move.start()
            self.moves.append(move)

    def finish(self):
        for move in self.moves:
            move.wait()
        for move in self.sends:
            move.wait_send()


def exchange_sems(count):
    dma = pltpu.SemaphoreType.DMA
    return [dma((count, 4)), dma((count, 4)), dma((count, 6)), dma((count, 6))]


def share(place, index, ours, theirs, target, local, here_sem, core_send, core_recv):
    here = pltpu.make_async_copy(ours, target.at[pl.ds(0, local), :], here_sem.at[index])
    there = remote(
        theirs, target.at[pl.ds(local, local), :], core_send.at[index], core_recv.at[index], place.core_partner()
    )
    here.start()
    there.start()
    return [here, there]


def share_left(place, index, source, target, local, *sems):
    half = source.shape[1] // 2
    columns = half // 2
    out = []
    for y in range(2):
        ours, theirs = (
            source.at[pl.ds(0, local), pl.ds(pl.multiple_of(y * half + core * columns, 128), columns)]
            for core in (place.core, 1 - place.core)
        )
        out += share(place, index + y, ours, theirs, target.at[:, pl.ds(y * columns, columns)], local, *sems)
    return out


def wait_all(copies):
    for copy in copies:
        copy.wait()


def norm_parts(values):
    center = values - jnp.mean(values, axis=-1, keepdims=True)
    inverse = lax.rsqrt(jnp.mean(center * center, axis=-1, keepdims=True) + 1e-05)
    return center * inverse, inverse


def norm_pull(grad, unit, inverse, gain):
    scaled = grad * gain
    return inverse * (
        scaled
        - jnp.mean(scaled, axis=-1, keepdims=True)
        - unit * jnp.mean(scaled * unit, axis=-1, keepdims=True)
    )


class Scatter:
    def __init__(self, place, refs, sems, x_first, left, right, write):
        self.place, self.x_first, self.left, self.right, self.write = place, x_first, left, right, write
        self.whole, self.first, self.second, self.near, self.far = refs
        self.send, self.receive = sems
        self.rows, self.columns = self.whole.shape[-2:]

    def axes(self, p):
        place = self.place
        if p not in self.x_first:
            return place.y, place.x, place.y_partner(), place.x_partner()
        return place.x, place.y, place.x_partner(), place.y_partner()

    def copy(self, p, stage):
        place = self.place
        mine, other, partner, second = self.axes(p)
        if stage == 0:
            source, target, device = self.whole.at[p, 1 - mine], self.first.at[p], partner
        elif stage == 1:
            source, target, device = self.first.at[p, :, :, 1 - other], self.second.at[p], second
        elif stage == 2:
            source, target, device = self.second.at[p, :, 1 - place.z0], self.near.at[p], place.near_partner()
        else:
            source, target, device = self.near.at[p, 1 - place.z1], self.far.at[p], place.far_partner()
        index = p
        return remote(source, target, self.send.at[stage, index], self.receive.at[stage, index], device)

    def compute(self, p):
        left, right = self.left(p), self.right(p)
        rows = self.rows

        def one(y, carry):
            for half in range(2):
                span = 4 * rows
                at = pl.ds(pl.multiple_of(y * 8 * rows + half * span, 128), span)
                block = tn(left[:, at], right[...]).astype(LOW)
                for k in range(4):
                    x = k % 2
                    part = block[k * rows : (k + 1) * rows]
                    if p not in self.x_first:
                        self.whole[p, y, half, k // 2, x] = part
                    else:
                        self.whole[p, x, half, k // 2, y] = part
            return carry

        lax.fori_loop(0, 2, one, 0)
        self.copy(p, 0).start()

    def advance(self, p, stage):
        place = self.place
        mine, other, _, _ = self.axes(p)
        wide = jnp.float32
        self.copy(p, stage - 1).wait_recv()
        if stage == 1:

            def add(k, carry):
                a, b, s = k // 4, k // 2 % 2, k % 2
                total = self.first[p, a, b, s].astype(wide) + self.whole[p, mine, a, b, s].astype(wide)
                self.first[p, a, b, s] = total.astype(LOW)
                return carry

            lax.fori_loop(0, 8, add, 0)
        elif stage == 2:

            def add(z, carry):
                a, b = z // 2, z % 2
                total = self.second[p, a, b].astype(wide) + self.first[p, a, b, other].astype(wide)
                self.second[p, a, b] = total.astype(LOW)
                return carry

            lax.fori_loop(0, 4, add, 0)
        elif stage == 3:

            def add(a, carry):
                total = self.near[p, a].astype(wide) + self.second[p, a, place.z0].astype(wide)
                self.near[p, a] = total.astype(LOW)
                return carry

            lax.fori_loop(0, 2, add, 0)
        else:
            self.write(p, self.near[p, place.z1].astype(wide) + self.far[p].astype(wide))
            return
        self.copy(p, stage).start()

    def settle(self, p):
        for stage in range(4):
            self.copy(p, stage).wait_send()


def scatter_scratch(pieces, rows, columns):
    return [
        pltpu.VMEM((pieces, 2, 2, 2, 2, rows, columns), LOW),
        pltpu.VMEM((pieces, 2, 2, 2, rows, columns), LOW),
        pltpu.VMEM((pieces, 2, 2, rows, columns), LOW),
        pltpu.VMEM((pieces, 2, rows, columns), LOW),
        pltpu.VMEM((pieces, rows, columns), LOW),
    ]


class Gather:
    def __init__(self, place, sems):
        self.place = place
        self.send, self.receive = sems

    def copies(self, index, own, full, rows, shared):
        place = self.place
        across = place.dp + 2 - 4 * place.y
        half = rows // 2

        def move(kind, source, target, device):
            return remote(source, target, self.send.at[kind, index], self.receive.at[kind, index], device)

        out = [move(0, own, full(place.dp, 0, rows), place.core_partner())]
        if shared:
            first = place.x * half
            out.append(
                move(1, own.at[pl.ds(pl.multiple_of(first, half), half), :],
                     full(place.dp, first, half), place.y_partner())
            )
            landed = full(across, first, half)
            out.append(move(2, landed, landed, place.x_partner()))
        else:
            out.append(move(1, own, full(place.dp, 0, rows), place.y_partner()))
            out.append(None)
        landed = full(across, 0, rows)
        out.append(move(3, landed, landed, place.core_partner()))
        return out


FRONT_ALONE = (2, 5, 8)
FRONT_ORDER = (
    500, 100, 101, 200, 0, 201, 1, 300, 600, 202, 301, 2, 103, 104, 302, 203, 3, 205,
    204, 106, 303, 107, 404, 405, 206, 208, 207, 406, 408, 407,
)


def front_kernel(
    tokens, gain, ids, w_triple, w_out, w_up,
    o_v, o_k, o_q, o_normed, o_starts, o_triple, o_out, o_up,
    triple_s, part_s, ids_s, bounce, relay, send, receive, x_send, x_recv, z_send, z_recv, ids_send, ids_recv, local_sem,
):
    place = Place()
    exchange_sem = (x_send, x_recv, z_send, z_recv)
    local, width = tokens.shape
    heads_width = o_v.shape[1]
    meet([(place.dp, (place.seq + k) % 8) for k in range(1, 8)] + [place.core_partner(), place.y_partner()])
    gather = Gather(place, (send, receive))

    def columns(weight, at):
        def full(d, first, count):
            return weight.at[pl.ds(pl.multiple_of(d * 256 + first, 128), count), at]

        return full

    half = width // 2
    spans = [
        (2 * width + (1 - place.z1) * half, half), (2 * width + place.z1 * half, half), (width, width), (0, width)
    ]
    spans = [(pl.multiple_of(first, 512), count) for first, count in spans]
    plans = []
    for first, count in spans:
        plans.append((w_triple.at[:, pl.ds(first, count)], columns(triple_s, pl.ds(first, count))))
    plans.append((w_out, columns(o_out, pl.ds(0, width))))
    for k in range(w_up.shape[1] // width):
        plans.append((w_up.at[:, pl.ds(k * width, width)], columns(o_up, pl.ds(k * width, width))))
    alone = FRONT_ALONE
    chunks = [
        gather.copies(n, own, full, 256, n not in alone) for n, (own, full) in enumerate(plans)
    ]
    mine = []
    for n, (own, full) in enumerate(plans):
        chunks[n][1].start()
        chunks[n][0].start()
        target = full(place.dp, 0, 256) if n < 4 else bounce.at[n - 4]
        copy = pltpu.make_async_copy(own, target, local_sem.at[n])
        copy.start()
        mine.append(copy)
        if n == 0:
            news = []
            for k in range(1, 8):
                peer = (place.dp, (place.seq + k) % 8)
                move = remote(ids, ids_s.at[place.seq], ids_send.at[k - 1], ids_recv.at[k - 1], peer)
                move.start()
                news.append(move)
            ids_s[pl.ds(place.seq, 1)] = ids[...].reshape(1, 1, local)

    def norm_rows(n, carry):
        rows = pl.ds(pl.multiple_of(n * 128, 128), 128)
        values = tokens[rows, :].astype(jnp.float32)
        o_normed[rows, :] = (norm_parts(values)[0] * gain[...]).astype(LOW)
        return carry

    moves = []
    exchanges = [
        ToHeads(
            place, part_s.at[t], target, relay.at[t], [sem.at[t] for sem in exchange_sem], local_sem.at[12 + t]
        )
        for t, target in enumerate((o_v, o_k, o_q))
    ]
    far, near = (2, 3), (1, 0)
    steps = ((0, far), (0, near), (1, far + near), (2, far + near))

    def project(n):
        first, count = spans[n]
        t, reach = steps[n]

        def one(c, carry):
            from_at = pl.ds(pl.multiple_of(first + c * 256, 256), 256)
            at = pl.ds(pl.multiple_of(first - (2 - t) * width + c * 256, 256), 256)
            part_s[t, :, at] = jnp.dot(
                o_normed[...], triple_s[:, from_at], preferred_element_type=jnp.float32
            ).astype(LOW)
            return carry

        lax.fori_loop(0, count // 256, one, 0)
        exchanges[t].start(reach)
        at = pl.ds(first, count)
        save = pltpu.make_async_copy(triple_s.at[:, at], o_triple.at[:, at], local_sem.at[15 + n])
        save.start()
        moves.append(save)

    def pass_on(n):
        t, reach = steps[n]
        exchanges[t].pass_on(tuple(m for m in reach if m))

    def forward(n):
        if chunks[n][2] is not None:
            chunks[n][1].wait_recv()
            chunks[n][2].start()

    def across(n):
        (chunks[n][1] if chunks[n][2] is None else chunks[n][2]).wait_recv()
        chunks[n][3].start()

    def finish(n):
        chunks[n][0].wait_recv()
        chunks[n][3].wait_recv()
        mine[n].wait()
        project(n)

    def put_back(n):
        chunks[n][0].wait_recv()
        chunks[n][3].wait_recv()
        mine[n].wait()
        copy = pltpu.make_async_copy(bounce.at[n - 4], plans[n][1](place.dp, 0, 256), local_sem.at[n])
        copy.start()
        moves.append(copy)

    def document_starts_here(_):
        for move in news:
            move.wait()
        every = ids_s[...]
        starts = jnp.zeros_like(every)
        for d in range(1, 8):
            before = jnp.sum((every < d).astype(jnp.int32), axis=2, keepdims=True)
            before = jnp.sum(before, axis=0, keepdims=True)
            starts = jnp.where(every == d, before, starts)
        for b in range(o_starts.shape[0]):
            for piece in range(BQ // 128):
                at = b * BQ + piece * 128
                o_starts[b, :, pl.ds(piece * 128, 128)] = starts[
                    at // local, :, at % local : at % local + 128
                ]

    act = (
        finish, forward, across, pass_on, put_back,
        lambda n: lax.fori_loop(0, local // 128, norm_rows, 0), document_starts_here,
    )
    for code in FRONT_ORDER:
        act[code // 100](code % 100)
    for move in moves:
        move.wait()
    for exchange in exchanges:
        exchange.finish()
    for chunk in chunks:
        for copy in chunk:
            if copy is not None:
                copy.wait_send()


def front(tokens, gain, ids, w_triple, w_out, w_up):
    local, width = tokens.shape
    heads_width = width // 8
    length = local * 8
    hidden = w_up.shape[1]
    any_spec = pl.BlockSpec(memory_space=pl.ANY)
    vmem = pl.BlockSpec(memory_space=pltpu.VMEM)
    dma = pltpu.SemaphoreType.DMA
    one = jax.ShapeDtypeStruct((length, heads_width), LOW)
    return pl.pallas_call(
        front_kernel,
        out_shape=(
            one, one, one,
            jax.ShapeDtypeStruct((local, width), LOW),
            jax.ShapeDtypeStruct((length // BQ, 1, BQ), jnp.int32),
            jax.ShapeDtypeStruct((width, 3 * width), LOW),
            jax.ShapeDtypeStruct((width, width), LOW),
            jax.ShapeDtypeStruct((width, hidden), LOW),
        ),
        in_specs=[vmem] * 3 + [any_spec] * 3,
        out_specs=(any_spec,) * 3 + (vmem,) * 2 + (any_spec,) * 3,
        scratch_shapes=[
            pltpu.VMEM((width, 3 * width), LOW),
            pltpu.VMEM((3, local, width), LOW),
            pltpu.VMEM((8, 1, local), jnp.int32),
            pltpu.VMEM((1 + hidden // width, 256, width), LOW),
            pltpu.VMEM((3, 3, local, heads_width), LOW),
            dma((4, 9)),
            dma((4, 9)),
            *exchange_sems(3),
            dma((7,)),
            dma((7,)),
            dma((20,)),
        ],
        compiler_params=pltpu.CompilerParams(
            collective_id=1, has_side_effects=True, vmem_limit_bytes=VMEM_BYTES
        ),
        name="front",
    )(tokens, gain.reshape(1, width), ids, w_triple, w_out, w_up)


MIDDLE_ALONE = (1, 3)
MIDDLE_X_FIRST = (1, 3)
MIDDLE_ORDER = (
    1100, 500, 601, 1200, 1300, 1400, 700, 701, 502, 702, 703, 1500, 600, 602, 1, 603, 0, 3,
    800, 801, 802, 900, 901, 902, 903, 101, 2, 1000, 1001, 1600, 201, 1700, 103, 100, 301, 1800,
    102, 401, 203, 200, 303, 202, 1900, 300, 403, 302, 400, 402,
)


def middle_kernel(
    u, tokens, cotangent, post_gain, second_gain, mid_gain, w_out, w_up, w_down,
    o_layer, o_grad, o_heads, o_merged, o_second, o_hidden, o_projected, o_gains, o_down,
    out_s, up_s, down_s, merged_s, second_s, unit_s, slope_s, act_s, hidden_s, projected_s, middle_s, far_s,
    layer_s, o_middle, inverse_s, inner_s, relay, grad_s,
    d_left, d_right, d_whole, d_first, d_second, d_near, d_far,
    local_sem, g_send, g_recv, core_send, core_recv, x_send, x_recv, z_send, z_recv, s_send, s_recv,
):
    place = Place()
    local, width = tokens.shape
    hidden = mid_gain.shape[1]
    wide = jnp.float32
    column_peers = [(place.dp, (place.z + k) % 4 * 2 + place.x) for k in range(1, 4)]
    meet(column_peers + [place.x_partner(), place.core_partner(), place.y_partner()])
    exchange_sem = (x_send, x_recv, z_send, z_recv)

    inbound = ToTokens(
        place, u, merged_s, relay.at[0], [sem.at[0] for sem in exchange_sem], local_sem.at[0], (2, 3, 1)
    )
    gather = Gather(place, (g_send, g_recv))
    alone = MIDDLE_ALONE
    chunks, mine = [], []
    for k in range(4):

        def full(d, first, count, k=k):
            return down_s.at[pl.ds(pl.multiple_of(d * 1024 + k * 256 + first, 128), count), :]

        own = w_down.at[pl.ds(k * 256, 256), :]
        chunks.append(gather.copies(k, own, full, 256, k not in alone))
        chunks[k][1].start()
        chunks[k][0].start()
        mine.append(pltpu.make_async_copy(own, full(place.dp, 0, 256), local_sem.at[1 + k]))
        mine[k].start()
    loads = [
        pltpu.make_async_copy(w_out, out_s, local_sem.at[5]),
        pltpu.make_async_copy(w_up, up_s, local_sem.at[6]),
    ]
    for load in loads:
        load.start()
    sems = (local_sem, core_send, core_recv)
    right = share(place, 7, cotangent, cotangent, d_right, local, *sems)
    saves = []

    def save(source, target, index):
        copy = pltpu.make_async_copy(source, target, local_sem.at[index])
        copy.start()
        saves.append(copy)

    def across(k):
        (chunks[k][1] if chunks[k][2] is None else chunks[k][2]).wait_recv()
        chunks[k][3].start()

    def forward(k):
        chunks[k][1].wait_recv()
        chunks[k][2].start()

    gain = mid_gain[...]
    part_one = gain.astype(LOW)
    left_over = gain - part_one.astype(wide)
    part_two = left_over.astype(LOW)
    part_three = (left_over - part_two.astype(wide)).astype(LOW)
    row = lax.broadcasted_iota(jnp.int32, (16, hidden), 0)
    parts = jnp.where(row == 0, part_one.astype(wide), jnp.where(row == 1, part_two.astype(wide), part_three.astype(wide)))
    act_s[pl.ds(local, 16), :] = jnp.where(row < 3, parts, 0.0).astype(LOW)

    def blocks(first, count, body):
        def one(n, carry):
            body(n + first)
            return carry

        lax.fori_loop(0, count, one, 0)

    def span(n, size):
        return pl.ds(pl.multiple_of(n * size, size), size)

    later = {}

    def arrive(_):
        inbound.finish()
        wait_all(loads)
        save(merged_s, o_merged, 8)

    def project(n):
        at = span(n, 512)
        far_s[:, at] = jnp.dot(merged_s[...], out_s[:, at], preferred_element_type=wide)

    def norms(n):
        rows = span(n, 128)
        unit, inverse = norm_parts(far_s[rows, :])
        far_s[rows, :] = unit
        inverse_s[rows, :] = jnp.broadcast_to(inverse, (128, 128))
        middle = tokens[rows, :].astype(wide) + unit * post_gain[...]
        middle_s[rows, :] = middle
        second_s[rows, :] = (norm_parts(middle)[0] * second_gain[...]).astype(LOW)

    def grow(n):
        at = span(n, 512)
        z = jnp.dot(second_s[...], up_s[:, at], preferred_element_type=wide)
        root = 0.7978845608028654
        square = z * z
        half = 0.5 + 0.5 * jnp.tanh(z * (root + (root * 0.044715) * square))
        value = z * half
        unit_s[:, at] = value
        slope_s[:, at] = half + (value - value * half) * (2.0 * root + (6.0 * root * 0.044715) * square)

    def hidden_norm(n):
        rows = span(n, 64)
        unit, inverse = norm_parts(unit_s[rows, :])
        unit_s[rows, :] = unit
        inner_s[rows, :] = jnp.broadcast_to(inverse, (64, 128))
        act_s[rows, :] = (unit * gain).astype(LOW)

    def settle_weights():
        for k in range(4):
            chunks[k][0].wait_recv()
            chunks[k][3].wait_recv()
            mine[k].wait()
        grad_s[...] = jnp.zeros_like(grad_s)

    def shrink(n):
        at = span(n, 512)
        total = jnp.dot(act_s[...], down_s[:, at], preferred_element_type=wide)
        low = cotangent[:, at].astype(wide)
        value = total[:local]
        layer_s[:, at] = (middle_s[:, at] + value).astype(LOW)
        weight = jnp.sum(total[local:], axis=0, keepdims=True)
        first = jnp.sum(low * weight, axis=1, keepdims=True) * (1.0 / hidden)
        second = jnp.sum(low * value, axis=1, keepdims=True) * (1.0 / hidden)
        grad_s[0] = grad_s[0] + jnp.broadcast_to(first, (local, 128))
        grad_s[1] = grad_s[1] + jnp.broadcast_to(second, (local, 128))

    def write_down(p, value):
        o_down[:, pl.ds(p * 256, 256)] = value

    down = Scatter(
        place, (d_whole, d_first, d_second, d_near, d_far), (s_send, s_recv), MIDDLE_X_FIRST,
        lambda p: d_left, lambda p: d_right.at[:, pl.ds(p * 256, 256)], write_down,
    )

    def pull_hidden(n):
        at = span(n, 512)
        grad = nt(cotangent[...], down_s[at, :])
        unit = unit_s[:, at]
        o_gains[3:4, at] = jnp.sum(grad * unit, axis=0, keepdims=True)
        pulled = grad * mid_gain[:, at] - grad_s[0][:, 0:1] - unit * grad_s[1][:, 0:1]
        hidden_s[:, at] = (inner_s[:, 0:1] * pulled * slope_s[:, at]).astype(LOW)

    def pull_second(n):
        at = span(n, 512)
        o_middle[:, at] = nt(hidden_s[...], up_s[at, :])

    def pull_norms(n, totals):
        rows = span(n, 128)
        grad = o_middle[rows, :]
        unit, inverse = norm_parts(middle_s[rows, :])
        grad_middle = cotangent[rows, :].astype(wide) + norm_pull(grad, unit, inverse, second_gain[...])
        o_middle[rows, :] = grad_middle
        outer = far_s[rows, :]
        projected_s[rows, :] = norm_pull(grad_middle, outer, inverse_s[rows, 0:1], post_gain[...]).astype(LOW)
        return (
            totals[0] + jnp.sum(grad_middle * outer, axis=0, keepdims=True),
            totals[1] + jnp.sum(grad * unit, axis=0, keepdims=True),
        )

    def pull_merged(n):
        at = span(n, 512)
        merged_s[:, at] = nt(projected_s[...], out_s[at, :]).astype(LOW)

    def compute(p):
        if later.get("left"):
            wait_all(right)
            wait_all(later.pop("left"))
        down.compute(p)

    def do_norms(_):
        blocks(0, local // 128, norms)
        save(second_s, o_second, 9)

    def do_hidden_norm(_):
        blocks(0, local // 64, hidden_norm)
        later["left"] = share_left(place, 10, act_s, d_left, local, *sems)

    def do_shrink(n):
        if n == 0:
            settle_weights()
        else:
            blocks(n - 1, 1, shrink)
        if n == 2:
            save(layer_s, o_layer, 18)

    def do_pull_hidden(n):
        blocks(n * (hidden // 2048), hidden // 2048, pull_hidden)
        if n == 3:
            save(hidden_s, o_hidden, 15)

    def do_pull_norms(_):
        nothing = jnp.zeros((1, width), wide)
        post, second = lax.fori_loop(0, local // 128, pull_norms, (nothing, nothing))
        o_gains[1:2, 0:width] = post
        o_gains[2:3, 0:width] = second
        save(projected_s, o_projected, 16)
        save(o_middle, o_grad, 19)

    def do_pull_merged(_):
        saves[0].wait()
        blocks(0, width // 512, pull_merged)
        later["out"] = ToHeads(
            place, merged_s, o_heads, relay.at[1], [sem.at[1] for sem in exchange_sem], local_sem.at[17]
        )
        later["out"].start()

    act = (
        compute,
        lambda p: down.advance(p, 1),
        lambda p: down.advance(p, 2),
        lambda p: down.advance(p, 3),
        lambda p: down.advance(p, 4),
        forward,
        across,
        lambda n: blocks(n * (hidden // 2048), hidden // 2048, grow),
        do_shrink,
        do_pull_hidden,
        lambda n: blocks(n, 1, pull_second),
        lambda n: inbound.pass_on(),
        arrive,
        lambda n: blocks(0, width // 512, project),
        do_norms,
        do_hidden_norm,
        do_pull_norms,
        do_pull_merged,
        lambda n: later["out"].pass_on(),
        lambda n: later["out"].finish(),
    )
    for code in MIDDLE_ORDER:
        act[code // 100](code % 100)
    wait_all(saves[1:])
    for p in range(4):
        down.settle(p)
    for chunk in chunks:
        for copy in chunk:
            if copy is not None:
                copy.wait_send()


def middle(u, tokens, cotangent, post_gain, second_gain, mid_gain, w_out, w_up, w_down):
    local, width = tokens.shape
    hidden = w_up.shape[1]
    any_spec = pl.BlockSpec(memory_space=pl.ANY)
    vmem = pl.BlockSpec(memory_space=pltpu.VMEM)
    dma = pltpu.SemaphoreType.DMA
    wide = jnp.float32
    act = jax.ShapeDtypeStruct((local, width), LOW)
    return pl.pallas_call(
        middle_kernel,
        out_shape=(
            act,
            jax.ShapeDtypeStruct((local, width), wide),
            jax.ShapeDtypeStruct((local * 8, width // 8), LOW),
            act,
            act,
            jax.ShapeDtypeStruct((local, hidden), LOW),
            act,
            jax.ShapeDtypeStruct((8, hidden), wide),
            jax.ShapeDtypeStruct((hidden // 32, width), wide),
        ),
        in_specs=[any_spec] + [vmem] * 5 + [any_spec] * 3,
        out_specs=(any_spec,) * 7 + (vmem,) * 2,
        scratch_shapes=[
            pltpu.VMEM((width, width), LOW),
            pltpu.VMEM((width, hidden), LOW),
            pltpu.VMEM((hidden, width), LOW),
            pltpu.VMEM((local, width), LOW),
            pltpu.VMEM((local, width), LOW),
            pltpu.VMEM((local, hidden), wide),
            pltpu.VMEM((local, hidden), wide),
            pltpu.VMEM((local + 16, hidden), LOW),
            pltpu.VMEM((local, hidden), LOW),
            pltpu.VMEM((local, width), LOW),
            pltpu.VMEM((local, width), wide),
            pltpu.VMEM((local, width), wide),
            pltpu.VMEM((local, width), LOW),
            pltpu.VMEM((local, width), wide),
            pltpu.VMEM((local, 128), wide),
            pltpu.VMEM((local, 128), wide),
            pltpu.VMEM((2, 3, local, width // 8), LOW),
            pltpu.VMEM((2, local, 128), wide),
            pltpu.VMEM((2 * local, hidden // 2), LOW),
            pltpu.VMEM((2 * local, width), LOW),
            *scatter_scratch(4, 128, 256),
            dma((20,)),
            dma((4, 4)),
            dma((4, 4)),
            dma((20,)),
            dma((20,)),
            *exchange_sems(2),
            dma((4, 4)),
            dma((4, 4)),
        ],
        compiler_params=pltpu.CompilerParams(
            collective_id=2, has_side_effects=True, vmem_limit_bytes=VMEM_BYTES
        ),
        name="middle",
    )(
        u, tokens, cotangent, post_gain.reshape(1, width), second_gain.reshape(1, width),
        mid_gain.reshape(1, hidden), w_out, w_up, w_down,
    )


HALF = 512
X_FIRST = (2, 3, 9, 13)
TAIL_ORDER = (
    0, 2, 3, 4, 5, 7, 500, 6, 8, 100, 102, 1, 9, 104, 103, 105, 600, 700, 501, 14,
    15, 107, 200, 106, 109, 204, 205, 300, 108, 304, 502, 305, 601, 701, 12, 207, 101, 202, 203, 206,
    13, 307, 400, 404, 303, 208, 114, 602, 702, 800, 900, 306, 308, 403, 10, 201, 407, 209, 302, 11,
    115, 406, 301, 901, 112, 309, 214, 402, 401, 215, 408, 113, 405, 110, 212, 902, 314, 409, 210, 315,
    111, 312, 213, 414, 310, 211, 415, 313, 412, 311, 410, 413, 411,
)


def tail_kernel(
    dq, dk, dv, tokens, gain, middle_in, triple_in, act_up, act_out, act_in, g_up, g_out, gains, scales,
    o_tokens, o_triple, o_out, o_up, o_gains,
    e_left, e_right, e_whole, e_first, e_second, e_near, e_far,
    triple, middle, tokens_s, grad_s, gain_s, gain_r, relay,
    local_sem, core_send, core_recv, x_send, x_recv, z_send, z_recv, s_send, s_recv, gain_send, gain_recv,
):
    place = Place()
    partner = place.core_partner()
    local, width = tokens.shape
    heads_width = dq.shape[1]
    seq_peers = [(place.dp, (place.seq + k) % 8) for k in range(1, 8)]
    dp_peers = [((place.dp + k) % 4, place.seq) for k in range(1, 4)]
    meet(seq_peers + dp_peers)

    def start_exchange(t):
        return ToTokens(
            place, (dv, dk, dq)[t], e_right.at[7 - t, pl.ds(0, local), :], relay.at[t],
            [sem.at[t] for sem in (x_send, x_recv, z_send, z_recv)], local_sem.at[13 + t],
        )

    exchanges = [start_exchange(t) for t in range(3)]

    load_triple = pltpu.make_async_copy(triple_in, triple, local_sem.at[16])
    load_middle = pltpu.make_async_copy(middle_in, middle, local_sem.at[17])

    sems = (local_sem, core_send, core_recv)
    ready = {"up": share_left(place, 0, act_up, e_left.at[0], local, *sems)}
    for k in range(4):
        part = g_up.at[:, pl.ds(k * BLOCK, BLOCK)]
        ready[k] = share(place, 2 + k, part, part, e_right.at[k], local, *sems)
    ready["out"] = share_left(place, 6, act_out, e_left.at[1], local, *sems)
    ready["out"] += share(place, 8, g_out, g_out, e_right.at[4], local, *sems)
    ready["in"] = share_left(place, 9, act_in, e_left.at[2], local, *sems)
    load_triple.start()
    load_middle.start()

    def write(p, value):
        at = pl.ds(p % 2 * HALF, HALF)
        if p < 8:
            o_up[:, pl.ds(p * HALF, HALF)] = value
        elif p < 10:
            o_out[:, at] = value
        else:
            o_triple[:, pl.ds((p - 10) * HALF, HALF)] = value

    engine = Scatter(
        place, (e_whole, e_first, e_second, e_near, e_far), (s_send, s_recv), X_FIRST,
        lambda p: e_left.at[0 if p < 8 else 1 if p < 10 else 2],
        lambda p: e_right.at[p // 2, :, pl.ds(p % 2 * HALF, HALF)], write,
    )
    gain_s[0:3, :] = gains[0:3, 0:width]
    for k in range(gains.shape[1] // width):
        gain_s[3 + k : 4 + k, :] = gains[3:4, pl.ds(k * width, width)]
    gain_s[7:8, :] = jnp.zeros((1, width), jnp.float32)
    gain_s[7:8, 0:128] = scales[...]
    def bring_back(t):
        exchanges[t].finish()
        slot = e_right.at[7 - t]
        move = remote(
            slot.at[pl.ds(0, local), :], slot.at[pl.ds(local, local), :],
            core_send.at[11 + t], core_recv.at[11 + t], partner,
        )
        move.start()
        return move

    def pull_normed(t):
        if t == 0:
            load_triple.wait()

        def one(n, carry):
            rows = pl.ds(pl.multiple_of(n * 256, 256), 256)
            part = nt(e_right[7 - t, pl.ds(0, local), :], triple[rows, pl.ds((2 - t) * width, width)])
            grad_s[:, rows] = part if t == 0 else grad_s[:, rows] + part
            return carry

        lax.fori_loop(0, width // 256, one, 0)

    def norm_rows(n, total):
        rows = pl.ds(pl.multiple_of(n * 128, 128), 128)
        unit, inverse = norm_parts(tokens[rows, :].astype(jnp.float32))
        grad = grad_s[rows, :]
        pulled = norm_pull(grad, unit, inverse, gain[...])
        tokens_s[rows, :] = (middle[rows, :] + pulled).astype(LOW)
        return total + jnp.sum(grad * unit, axis=0, keepdims=True)

    save_tokens = pltpu.make_async_copy(tokens_s, o_tokens, local_sem.at[18])

    def pull_norm(_):
        load_middle.wait()
        gain_s[0:1, :] = lax.fori_loop(0, local // 128, norm_rows, jnp.zeros((1, width), jnp.float32))
        save_tokens.start()

    def gain_moves(peers, first):
        out = [
            remote(gain_s, gain_r.at[first + k], gain_send.at[first + k], gain_recv.at[first + k], peer)
            for k, peer in enumerate(peers)
        ]
        for move in out:
            move.start()
        return out

    gain_steps = {}

    def sum_gains(step):
        if step == 0:
            gain_steps[0] = gain_moves(dp_peers, 0)
        elif step == 1:
            wait_all(gain_steps[0])
            gain_s[...] = gain_s[...] + gain_r[0] + gain_r[1] + gain_r[2]
            o_gains[7:8, :] = gain_s[7:8, 0:128]
            gain_steps[1] = gain_moves(seq_peers, 3)
        else:
            wait_all(gain_steps[1])
            total = gain_s[...]
            for k in range(7):
                total = total + gain_r[3 + k]
            gain_s[...] = total
            device = place.dp * 8 + place.seq
            pick = (
                lax.broadcasted_iota(jnp.int32, (width, 128), 0)
                == device * 32 + lax.broadcasted_iota(jnp.int32, (width, 128), 1)
            ).astype(jnp.float32)
            o_gains[0:3, :] = jnp.dot(
                gain_s[...], pick, preferred_element_type=jnp.float32, precision=lax.Precision.HIGHEST
            )[0:3]
            block = gain_s[:, pl.ds(pl.multiple_of((device % 8) * 128, 128), 128)]
            row = lax.broadcasted_iota(jnp.int32, block.shape, 0)
            o_gains[3:4, :] = jnp.sum(jnp.where(row == 3 + device // 8, block, 0.0), axis=0, keepdims=True)

    backs, waited = {}, set()

    def need(key):
        if key not in waited:
            wait_all(ready[key])
            waited.add(key)

    def compute(p):
        need("up" if p < 8 else "out" if p < 10 else "in")
        if p < 8:
            need(p // 2)
        elif p >= 10 and 7 - p // 2 in backs:
            backs.pop(7 - p // 2).wait()
        engine.compute(p)

    def bring(t):
        backs[t] = bring_back(t)

    act = (
        compute,
        lambda p: engine.advance(p, 1),
        lambda p: engine.advance(p, 2),
        lambda p: engine.advance(p, 3),
        lambda p: engine.advance(p, 4),
        lambda t: exchanges[t].pass_on(),
        bring,
        pull_normed,
        pull_norm,
        sum_gains,
    )
    for code in TAIL_ORDER:
        act[code // 100](code % 100)
    o_gains[4:7, :] = jnp.zeros((3, 128), jnp.float32)
    save_tokens.wait()
    for p in range(16):
        engine.settle(p)


def tail(dqkv, tokens, gain, middle, triple, acts, grads, gains, scales):
    local, width = tokens.shape
    heads_width = dqkv[0].shape[1]
    hidden = grads[0].shape[1]
    any_spec = pl.BlockSpec(memory_space=pl.ANY)
    vmem = pl.BlockSpec(memory_space=pltpu.VMEM)
    wide = jnp.float32
    dma = pltpu.SemaphoreType.DMA
    return pl.pallas_call(
        tail_kernel,
        out_shape=(
            jax.ShapeDtypeStruct((local, width), LOW),
            jax.ShapeDtypeStruct((width // 32, 3 * width), wide),
            jax.ShapeDtypeStruct((width // 32, width), wide),
            jax.ShapeDtypeStruct((width // 32, hidden), wide),
            jax.ShapeDtypeStruct((8, 128), wide),
        ),
        in_specs=[any_spec] * 3 + [vmem] * 2 + [any_spec] * 7 + [vmem] * 2,
        out_specs=(any_spec,) + (vmem,) * 4,
        scratch_shapes=[pltpu.VMEM((3, 2 * local, width // 2), LOW), pltpu.VMEM((8, 2 * local, width), LOW)]
        + scatter_scratch(16, 32, HALF)
        + [
            pltpu.VMEM((width, 3 * width), LOW),
            pltpu.VMEM((local, width), wide),
            pltpu.VMEM((local, width), LOW),
            pltpu.VMEM((local, width), wide),
            pltpu.VMEM((8, width), wide),
            pltpu.VMEM((10, 8, width), wide),
            pltpu.VMEM((3, 3, local, heads_width), LOW),
            dma((20,)),
            dma((20,)),
            dma((20,)),
            *exchange_sems(3),
            dma((4, 16)),
            dma((4, 16)),
            dma((10,)),
            dma((10,)),
        ],
        compiler_params=pltpu.CompilerParams(
            collective_id=3, has_side_effects=True, vmem_limit_bytes=VMEM_BYTES
        ),
        name="tail",
    )(*dqkv, tokens, gain.reshape(1, width), middle, triple, *acts, *grads, gains, scales)


def finish_kernel(count, *refs):
    ins, outs = refs[: count + 1], refs[count + 1 :]
    for k in range(count):
        outs[k][...] = ins[k][...]
    sums = ins[count]
    for row in range(3):
        outs[count + row][...] = sums[row, 0 : outs[count + row].shape[0]]
    outs[count + 3][...] = sums[3]
    row = sums[7:8, :]
    lane = lax.broadcasted_iota(jnp.int32, row.shape, 1)
    heads = outs[count + 4].shape[1]
    for h in range(heads):
        own = (lane >= h * HEAD) & (lane < (h + 1) * HEAD)
        outs[count + 4][:, h : h + 1] = jnp.sum(jnp.where(own, row, 0.0), axis=1, keepdims=True)


def finish(arrays, sums, own, heads):
    vmem = pl.BlockSpec(memory_space=pltpu.VMEM)
    wide = jnp.float32
    shapes = [jax.ShapeDtypeStruct(a.shape, a.dtype) for a in arrays]
    shapes += [jax.ShapeDtypeStruct((own,), wide)] * 3 + [jax.ShapeDtypeStruct((sums.shape[1],), wide), jax.ShapeDtypeStruct((1, heads), wide)]
    return pl.pallas_call(
        functools.partial(finish_kernel, len(arrays)),
        out_shape=tuple(shapes),
        in_specs=[vmem] * (len(arrays) + 1),
        out_specs=(vmem,) * len(shapes),
        name="finish",
    )(*arrays, sums)


def per_device(
    sizes,
    tokens,
    segment_ids,
    first_gain,
    triple_weight,
    head_scale,
    output_weight,
    post_gain,
    second_gain,
    up_weight,
    mid_gain,
    down_weight,
    cotangent,
):
    inputs = tokens[0].astype(jnp.float32)
    width = inputs.shape[1]
    doc_ids = lax.all_gather(segment_ids[0], "seq", axis=0, tiled=True)
    triple_full, output_full = (
        lax.all_gather(triple_weight, "dp", axis=0, tiled=True),
        lax.all_gather(output_weight, "dp", axis=0, tiled=True),
    )
    normed, pull_first = jax.vjp(layer_norm, inputs, first_gain)
    normed_low = normed.astype(jnp.bfloat16)
    triple = jnp.dot(normed_low, triple_full, preferred_element_type=jnp.float32).astype(
        jnp.bfloat16
    )
    queries, keys_all, values_all = (
        lax.all_to_all(triple[:, :width], "seq", split_axis=1, concat_axis=0, tiled=True),
        lax.all_to_all(
            triple[:, width : 2 * width], "seq", split_axis=1, concat_axis=0, tiled=True
        ),
        lax.all_to_all(triple[:, 2 * width :], "seq", split_axis=1, concat_axis=0, tiled=True),
    )
    heads_here = queries.shape[1] // HEAD
    starts = document_starts(doc_ids)
    attended, scaled, logsum = attend_forward(
        queries, keys_all, values_all, starts, head_scale
    )
    merged = lax.all_to_all(scaled, "seq", split_axis=0, concat_axis=1, tiled=True)
    projected = jnp.dot(merged, output_full, preferred_element_type=jnp.float32)
    post_normed, pull_post = jax.vjp(layer_norm, projected, post_gain)
    middle = inputs + post_normed
    second, pull_second = jax.vjp(layer_norm, middle, second_gain)
    second_low = second.astype(jnp.bfloat16)
    feed_up, feed_down = (
        lax.all_gather(up_weight, "dp", axis=0, tiled=True),
        lax.all_gather(down_weight, "dp", axis=0, tiled=True),
    )
    hidden = jnp.dot(second_low, feed_up, preferred_element_type=jnp.float32)
    activated, pull_mid = jax.vjp(gelu_norm, hidden, mid_gain)
    activated_low = activated.astype(jnp.bfloat16)
    layer_out = (
        middle + jnp.dot(activated_low, feed_down, preferred_element_type=jnp.float32)
    ).astype(jnp.bfloat16)
    upstream = cotangent[0]
    grad_act = times_transposed(upstream, feed_down)
    grad_hidden, grad_mid = pull_mid(grad_act)
    grad_hidden_low = grad_hidden.astype(jnp.bfloat16)
    grad_second_in = times_transposed(grad_hidden_low, feed_up)
    grad_middle_part, grad_second = pull_second(grad_second_in)
    grad_middle = upstream.astype(jnp.float32) + grad_middle_part
    grad_projected, grad_post = pull_post(grad_middle)
    grad_projected_low = grad_projected.astype(jnp.bfloat16)
    grad_merged = times_transposed(grad_projected_low, output_full).astype(jnp.bfloat16)
    grad_scaled = lax.all_to_all(
        grad_merged, "seq", split_axis=1, concat_axis=0, tiled=True
    )
    grad_queries, grad_keys, grad_values, scale_lanes = attend_backward(
        queries, keys_all, values_all, attended, grad_scaled, starts, head_scale, logsum
    )
    scale_terms = jnp.sum(scale_lanes.reshape(heads_here, HEAD), axis=1)
    back_queries, back_keys, back_values = (
        lax.all_to_all(
            grad_queries.astype(jnp.bfloat16), "seq", split_axis=0, concat_axis=1, tiled=True
        ),
        lax.all_to_all(
            grad_keys.astype(jnp.bfloat16), "seq", split_axis=0, concat_axis=1, tiled=True
        ),
        lax.all_to_all(
            grad_values.astype(jnp.bfloat16), "seq", split_axis=0, concat_axis=1, tiled=True
        ),
    )
    grad_triple_act = jnp.concatenate((back_queries, back_keys, back_values), axis=1)
    grad_normed = times_transposed(grad_triple_act, triple_full)
    grad_input_part, grad_first = pull_first(grad_normed)
    grad_tokens = (grad_middle + grad_input_part).astype(jnp.bfloat16)
    low = jnp.bfloat16
    grad_down = scatter_rows(transposed_times(activated_low, upstream).astype(low), sizes)
    grad_up = scatter_rows(transposed_times(second_low, grad_hidden_low).astype(low), sizes)
    grad_output = scatter_rows(transposed_times(merged, grad_projected_low).astype(low), sizes)
    gains = jnp.concatenate(
        (
            grad_first[:, None],
            grad_post[:, None],
            grad_second[:, None],
            grad_mid.reshape(width, -1),
        ),
        axis=1,
    )
    gains = jnp.pad(gains, ((0, 0), (0, 128 - gains.shape[1])))
    grad_triple = scatter_rows(
        jnp.concatenate(
            (transposed_times(normed_low, grad_triple_act).astype(low), gains.astype(low)), axis=1
        ),
        sizes,
    )
    gain_sums = grad_triple[:, 3 * width :]
    grad_scale = lax.psum(scale_terms, "dp")
    return (
        layer_out[None],
        grad_tokens[None],
        gain_sums[:, 0],
        grad_triple[:, : 3 * width],
        grad_scale,
        grad_output,
        gain_sums[:, 1],
        gain_sums[:, 2],
        grad_up,
        gain_sums[:, 3 : 3 + mid_gain.shape[0] // width].reshape(-1),
        grad_down,
    )


def per_device_chips(
    sizes,
    tokens,
    segment_ids,
    first_gain,
    triple_weight,
    head_scale,
    output_weight,
    post_gain,
    second_gain,
    up_weight,
    mid_gain,
    down_weight,
    cotangent,
):
    width, hidden = tokens.shape[2], up_weight.shape[1]
    heads_here = width // HEAD // sizes[1]
    values, keys, queries, normed, starts, triple_full, output_full, up_full = front(
        tokens[0], first_gain, segment_ids, triple_weight, output_weight, up_weight
    )
    attended, scaled, logsum = attend_forward(queries, keys, values, starts, head_scale)
    layer_out, grad_middle, grad_scaled, merged, second_low, grad_hidden, grad_projected, gains, grad_down = middle(
        scaled, tokens[0], cotangent[0], post_gain, second_gain, mid_gain, output_full, up_full, down_weight
    )
    grad_queries, grad_keys, grad_values, scale_lanes, layer_out, grad_down = attend_backward(
        queries, keys, values, attended, grad_scaled, starts, head_scale, logsum, (layer_out, grad_down)
    )
    grad_tokens, grad_triple, grad_output, grad_up, sums = tail(
        (grad_queries, grad_keys, grad_values),
        tokens[0],
        first_gain,
        grad_middle,
        triple_full,
        (second_low, merged, normed),
        (grad_hidden, grad_projected),
        gains,
        scale_lanes,
    )
    grad_tokens, grad_triple, grad_output, grad_up, first, post, second, mid, scale = finish(
        (grad_tokens, grad_triple, grad_output, grad_up), sums, width // 32, heads_here
    )
    return (
        layer_out[None],
        grad_tokens[None],
        first,
        grad_triple,
        scale[0],
        grad_output,
        post,
        second,
        grad_up,
        mid,
        grad_down,
    )


def solution(mesh):
    placed = (
        P("dp", "seq", None),
        P("dp", "seq"),
        P(),
        P("dp", None),
        P(),
        P("dp", None),
        P(),
        P(),
        P("dp", None),
        P(),
        P("dp", None),
        P("dp", "seq", None),
    )
    sizes = (mesh.shape["dp"], mesh.shape["seq"])
    program = per_device_chips if sizes == (4, 8) else per_device
    return jax.shard_map(
        functools.partial(program, sizes),
        mesh=mesh,
        in_specs=placed,
        out_specs=(
            P("dp", "seq", None),
            P("dp", "seq", None),
            P(("dp", "seq")),
            P(("dp", "seq"), None),
            P("seq"),
            P(("dp", "seq"), None),
            P(("dp", "seq")),
            P(("dp", "seq")),
            P(("dp", "seq"), None),
            P(("dp", "seq")),
            P(("dp", "seq"), None),
        ),
        check_vma=False,
    )
```
